32 devices in a mesh: clip: 8 (over z, y), win: 4 (over x, core).
Axes of the slice: x: 2, y: 2, z: 4, core: 2. Of those that a mesh axis runs over, the one named last changes fastest.
Arguments:
- tokens: bfloat16 [2, 8, 4, 4, 5, 4, 8, 1024], P(None, 'clip', 'win'), may hold values from -6 to 6
- cond: bfloat16 [2, 8, 1024], P(None, 'clip'), may hold values from -6 to 6
- lengths: int32 [2, 8], P(None, 'clip'), may hold values from 2 to 9, as said below
- ada_w: bfloat16 [1024, 6144], P(('clip', 'win')), may hold values from -0.1875 to 0.1875
- ada_b: bfloat16 [6144], P(('clip', 'win')), may hold values from -3 to 3
- w_qkv: bfloat16 [1024, 3072], P(('clip', 'win')), may hold values from -0.1875 to 0.1875
- w_out: bfloat16 [1024, 1024], P(('clip', 'win')), may hold values from -3.5 to 3.5
- w_up: bfloat16 [1024, 4096], P(('clip', 'win')), may hold values from -0.1875 to 0.1875
- b_up: bfloat16 [4096], P(('clip', 'win')), may hold values from -3 to 3
- w_down: bfloat16 [4096, 1024], P(('clip', 'win')), may hold values from -0.09375 to 0.09375
- b_down: bfloat16 [1024], P(('clip', 'win')), may hold values from -3 to 3
- rel_table: bfloat16 [512, 16], P(('clip', 'win')), may hold values from -4 to 4
- bucket: int32 [2025], replicated, may hold values from 0 to 511
- cotangent: bfloat16 [2, 8, 4, 4, 5, 4, 8, 1024], P(None, 'clip', 'win'), may hold values from -6 to 6
Outputs:
- output: bfloat16 [2, 8, 4, 4, 5, 4, 8, 1024], P(None, 'clip', 'win')
- grad_tokens: bfloat16 [2, 8, 4, 4, 5, 4, 8, 1024], P(None, 'clip', 'win')
- grad_ada_w: float32 [1024, 6144], P(('clip', 'win'))
- grad_ada_b: float32 [6144], P(('clip', 'win'))
- grad_w_qkv: float32 [1024, 3072], P(('clip', 'win'))
- grad_w_out: float32 [1024, 1024], P(('clip', 'win'))
- grad_w_up: float32 [1024, 4096], P(('clip', 'win'))
- grad_b_up: float32 [4096], P(('clip', 'win'))
- grad_w_down: float32 [4096, 1024], P(('clip', 'win'))
- grad_b_down: float32 [1024], P(('clip', 'win'))
- grad_rel_table: float32 [512, 16], P(('clip', 'win'))
The draws below stay inside these ranges and needn't reach their ends.
Inputs may be any that keep to these rules, and one draw needn't show every extreme that they name: `lengths`: in each micro-batch some clip has 9 frames.
All inputs are finite; a program needn't handle non-finite values.
Results may differ from the reference program's by a relative error of at most 0.013.
The reference program's roundings to bfloat16 on the way count: a program that leaves them out, or rounds other values in their place, can miss the bound.
Values may be sent and summed in bfloat16 or wider, within the bound.
No kernel may reach another device: no remote copies, remote signals or barrier semaphores. Data moves between devices by JAX's collectives and lax.ppermute only.
A program may use at most 448 MiB of HBM per device.

```python
import math
import jax
import jax.numpy as jnp
from jax import lax

D = 1024
HEADS = 16
HD = 64
FF = 4096
DC = 1024
NB = 512
TF = 5
WS = 8
WIN_T = 2
MB = 2
RS = 4
SIDE_WINS = 2
BLOCKS = 4
WT = 320
REL = 2025
NCLIP = 8
N_WIN = 4


def draw_lengths(key, part):
    longest = WIN_T * TF - 1
    base_len = jax.random.randint(jax.random.fold_in(key, 11), (MB, NCLIP), 2, longest + 1, dtype=jnp.int32)
    chosen = jax.random.randint(jax.random.fold_in(key, 12), (MB, 1), 0, NCLIP, dtype=jnp.int32)
    return jnp.where(jnp.arange(NCLIP, dtype=jnp.int32)[None, :] == chosen, longest, base_len).astype(jnp.int32)


def with_ends(drawn, rng, least, top_value):
    longest = drawn.shape.index(max(drawn.shape))
    spots = []
    for shift in (0, 1):
        where = [jax.random.randint(jax.random.fold_in(rng, axis), (), 0, length) for axis, length in enumerate(drawn.shape)]
        where[longest] = (where[longest] + shift) % drawn.shape[longest]
        spots.append(tuple(where))
    return drawn.at[spots[0]].set(least).at[spots[1]].set(top_value)


def steps_of(key, shape, shards, smallest, high):
    gain = 1.0
    for dim, parts in shards:
        heights = jax.random.uniform(jax.random.fold_in(jax.random.fold_in(key, 6), dim), (parts,), jnp.float32, smallest / len(shards), high / len(shards))
        gain = gain * jnp.repeat(jnp.exp(heights), shape[dim] // parts).reshape((-1,) + (1,) * (len(shape) - 1 - dim))
    return gain


def centred(stream_key, extent, spread, most, cuts=(), held_as=jnp.bfloat16):
    values = jax.random.normal(stream_key, extent, jnp.float32) * spread
    if len(cuts) > 0:
        values = steps_of(stream_key, extent, cuts, -0.22, 0.18) * values
    return jnp.clip(values, min=-most, max=most).astype(held_as)


def setup_inputs(seed: int = 0) -> dict:
    splits = jax.random.split(jax.random.key(seed), 15)
    return {
        "tokens": centred(splits[0], (MB, NCLIP, N_WIN, BLOCKS, TF, RS, WS, D), 1.0, 6.0, ((1, 8), (2, 4))),
        "cond": centred(splits[1], (MB, NCLIP, DC), 1.0, 6.0, ((1, 8),)),
        "lengths": draw_lengths(jax.random.fold_in(splits[14], 71), 0),
        "ada_w": centred(splits[3], (DC, 6 * D), DC ** -0.5, 0.1875, ((0, 32),)),
        "ada_b": centred(splits[4], (6 * D,), 0.5, 3.0, ((0, 32),)),
        "w_qkv": centred(splits[5], (D, 3 * D), D ** -0.5, 0.1875, ((0, 32),)),
        "w_out": centred(splits[6], (D, D), (max(D // WT, 1)) ** -0.5, 3.5, ((0, 32),)),
        "w_up": centred(splits[7], (D, FF), D ** -0.5, 0.1875, ((0, 32),)),
        "b_up": centred(splits[8], (FF,), 0.5, 3.0, ((0, 32),)),
        "w_down": centred(splits[9], (FF, D), FF ** -0.5, 0.09375, ((0, 32),)),
        "b_down": centred(splits[10], (D,), 0.5, 3.0, ((0, 32),)),
        "rel_table": centred(splits[11], (NB, HEADS), 1.0, 4.0, ((0, 32),)),
        "bucket": with_ends(jax.random.randint(splits[12], (REL,), 0, NB), jax.random.fold_in(splits[12], 1), 0, NB - 1).astype(jnp.int32),
        "cotangent": centred(splits[13], (MB, NCLIP, N_WIN, BLOCKS, TF, RS, WS, D), 1.0, 6.0, ((1, 8), (2, 4))),
    }


@jax.custom_vjp
def low(v):
    return lax.optimization_barrier(v.astype(jnp.bfloat16)).astype(jnp.float32)

@jax.custom_vjp
def low_back(v):
    return v

def low_keep(v):
    return (low(v), None)

def low_pass(kept, grad):
    return (grad,)

def back_keep(v):
    return (v, None)

def back_low(kept, grad):
    return (low(grad),)
low.defvjp(low_keep, low_pass)
low_back.defvjp(back_keep, back_low)
EPSILON = 1e-06
MASKED = -1000000000.0

def relative_index(frames, strip_rows, window_side):
    position = jnp.arange(frames * window_side * window_side, dtype=jnp.int32)
    column = position % window_side
    row_in = position // window_side % strip_rows
    frame_pos = position // (window_side * strip_rows) % frames
    half_idx = position // (window_side * strip_rows * frames)
    row_pos = half_idx * strip_rows + row_in
    span_len = 2 * window_side - 1
    delta_t = frame_pos[:, None] - frame_pos[None, :] + frames - 1
    delta_y = row_pos[:, None] - row_pos[None, :] + window_side - 1
    delta_x = column[:, None] - column[None, :] + window_side - 1
    return ((delta_t * span_len + delta_y) * span_len + delta_x).astype(jnp.int32)

def normalize(values):
    centered = values - lax.optimization_barrier(jnp.mean(values, axis=-1, keepdims=True))
    inv_std = lax.rsqrt(lax.optimization_barrier(jnp.mean(centered * centered, axis=-1, keepdims=True)) + EPSILON)
    return centered * inv_std

def block_layer(window_x, cond_act, length, pair_bucket, ada_w, ada_b, w_qkv, w_out, w_up, b_up, w_down, b_down, rel_table):
    highest = lax.Precision.HIGHEST
    windows_all = window_x.shape[0]
    modulation = jnp.dot(cond_act, ada_w, precision=highest) + ada_b
    shift_one, scale_one, gate_one, shift_two, scale_two, gate_two = jnp.split(modulation, 6)
    block_of = jnp.arange(windows_all, dtype=jnp.int32) // SIDE_WINS
    time_win = block_of // SIDE_WINS
    frame_pos = time_win[:, None] * TF + (jnp.arange(WT, dtype=jnp.int32) // (RS * WS) % TF)[None, :]
    valid_mask = (frame_pos < length).astype(jnp.float32)
    hidden_one = low_back(low(normalize(window_x) * (1.0 + scale_one) + shift_one))
    qkv_rows = low_back(low(jnp.einsum('wpd,de->wpe', hidden_one, w_qkv, precision=highest)))
    qkv_rows = qkv_rows.reshape(windows_all, WT, 3, HEADS, HD)
    query_rows = qkv_rows[:, :, 0]
    key_rows = qkv_rows[:, :, 1]
    value_rows = qkv_rows[:, :, 2]
    rel_bias = jnp.transpose(rel_table[pair_bucket], (2, 0, 1))
    score_scale = 1.0 / math.sqrt(HD)
    scores = low_back(jnp.einsum('wphd,wqhd->whpq', query_rows, key_rows, precision=highest) * score_scale + rel_bias[None])
    scores = jnp.where(valid_mask[:, None, None, :] > 0, scores, MASKED)
    probabilities = jax.nn.softmax(scores, axis=-1)
    attended = low_back(low(jnp.einsum('whpq,wqhd->wphd', low(probabilities), value_rows, precision=highest)))
    attended = attended.reshape(windows_all, WT, D)
    branch = low_back(low(jnp.einsum('wpd,de->wpe', attended, w_out, precision=highest) * valid_mask[..., None]))
    middle = window_x + gate_one * branch
    hidden_two = low(normalize(middle) * (1.0 + scale_two) + shift_two)
    pre_act = low_back(jnp.einsum('wpd,df->wpf', hidden_two, w_up, precision=highest) + b_up)
    activated = low(jax.nn.gelu(pre_act, approximate=True))
    mlp_out = low_back(jnp.einsum('wpf,fd->wpd', activated, w_down, precision=highest) + b_down)
    return middle + valid_mask[..., None] * gate_two * mlp_out

def reference(tokens, cond, lengths, ada_w, ada_b, w_qkv, w_out, w_up, b_up, w_down, b_down, rel_table, bucket, cotangent):
    params = tuple((element.astype(jnp.float32) for element in (ada_w, ada_b, w_qkv, w_out, w_up, b_up, w_down, b_down, rel_table)))
    pair_bucket = jnp.take(bucket, relative_index(TF, RS, WS).reshape(-1)).reshape(WT, WT)
    clip_count = MB * NCLIP

    def to_windows(array):
        permuted = jnp.transpose(array.astype(jnp.float32), (0, 1, 3, 2, 4, 5, 6, 7))
        return permuted.reshape(clip_count, BLOCKS * SIDE_WINS, WT, D)

    def from_windows(array):
        shaped = array.reshape(MB, NCLIP, BLOCKS, N_WIN, TF, RS, WS, D)
        return jnp.transpose(shaped, (0, 1, 3, 2, 4, 5, 6, 7))
    window_in = to_windows(tokens)
    window_cot = to_windows(cotangent)
    cond_all = cond.astype(jnp.float32).reshape(clip_count, DC)
    length_all = lengths.reshape(clip_count).astype(jnp.int32)

    def clip_step(carried, element):
        window_x, cond_row, cot_row, length = element
        cond_act = low(jax.nn.silu(cond_row))

        def forward(window_val, *weights):
            return block_layer(window_val, cond_act, length, pair_bucket, *weights)
        result, pullback = jax.vjp(forward, window_x, *params)
        gradients = pullback(cot_row)
        carried = tuple((running + addend for running, addend in zip(carried, gradients[1:])))
        return (carried, (result.astype(jnp.bfloat16), gradients[0].astype(jnp.bfloat16)))
    initial = tuple((jnp.zeros_like(element) for element in params))
    totals, (outputs, input_grads) = lax.scan(clip_step, initial, (window_in, cond_all, window_cot, length_all))
    return (from_windows(outputs), from_windows(input_grads), totals[0], totals[1], totals[2], totals[3], totals[4], totals[5], totals[6], totals[7], totals[8])
```

```python
import functools
import math

import jax
import jax.numpy as jnp
from jax import lax
from jax.experimental import pallas as pl
from jax.experimental.pallas import tpu as pltpu
from jax.sharding import PartitionSpec as P

HEADS = 16
EPSILON = 1e-06
MASKED = -1000000000.0
F32 = jnp.float32
BF16 = jnp.bfloat16
VMEM_LIMIT = 58 * 1024 * 1024
HIGHEST = lax.Precision.HIGHEST


def dot_nn(a, b):
    return lax.dot_general(a, b, (((1,), (0,)), ((), ())), preferred_element_type=F32)


def dot_nt(a, b):
    return lax.dot_general(a, b, (((1,), (1,)), ((), ())), preferred_element_type=F32)


def dot_tn(a, b):
    return lax.dot_general(a, b, (((0,), (0,)), ((), ())), preferred_element_type=F32)


def params(count):
    return pltpu.CompilerParams(
        dimension_semantics=("arbitrary",) * count, vmem_limit_bytes=VMEM_LIMIT
    )


def cost(flops, size):
    return pl.CostEstimate(flops=flops, bytes_accessed=size, transcendentals=0)


def once(shape, index_map):
    return pl.BlockSpec(shape, index_map, pipeline_mode=pl.Buffered(1))


def normalize(values):
    centered = values - jnp.mean(values, axis=-1, keepdims=True)
    inv = lax.rsqrt(jnp.mean(centered * centered, axis=-1, keepdims=True) + EPSILON)
    return centered * inv, inv


def norm_back(grad, normed, inv):
    return inv * (
        grad
        - jnp.mean(grad, axis=-1, keepdims=True)
        - normed * jnp.mean(grad * normed, axis=-1, keepdims=True)
    )


class Sizes:
    def __init__(self, tokens):
        self.micro, _, _, self.blocks, self.frames, rows, side, self.width = tokens.shape
        self.half = rows * side
        self.cols = self.blocks // 2
        self.strip_rows, self.side = rows, side
        self.used = 2 * self.frames - 1
        self.frame = 2 * self.half
        self.win_rows = self.used * self.frame
        self.rows = self.micro * self.win_rows
        self.lens = (self.frames * self.frame, (self.frames - 1) * self.frame)
        self.head = self.width // HEADS
        self.group = 4
        self.gcols = self.group * self.head
        self.groups = HEADS // self.group


def frame_rows(value):
    return value.reshape(-1, value.shape[-1])


def first_norm(tok, mod, core, sz):
    def kernel(sc_ref, x_ref, mod_ref, own_ref, far_ref):
        shift = mod_ref[0, 0:1, :]
        scale = 1.0 + mod_ref[0, 1:2, :]
        for slot, out_ref in enumerate((own_ref, far_ref)):
            column = sc_ref[0] ^ slot
            for tw in range(2):
                count = sz.frames - tw
                rows = frame_rows(x_ref[0, tw, column, :count].astype(F32))
                normed, _ = normalize(rows)
                hidden = (normed * scale + shift).astype(BF16)
                out_ref[0, tw * sz.frames : tw * sz.frames + count] = hidden.reshape(
                    count, sz.half, sz.width
                )

    strip = (1, 2, 2, sz.frames, sz.half, sz.width)
    piece = (1, sz.used, sz.half, sz.width)
    shape = jax.ShapeDtypeStruct((sz.micro,) + piece[1:], BF16)
    return pl.pallas_call(
        kernel,
        grid_spec=pltpu.PrefetchScalarGridSpec(
            num_scalar_prefetch=1,
            grid=(sz.micro,),
            in_specs=[
                pl.BlockSpec(strip, lambda m, s: (m, 0, 0, 0, 0, 0)),
                pl.BlockSpec((1, 6, sz.width), lambda m, s: (m, 0, 0)),
            ],
            out_specs=[pl.BlockSpec(piece, lambda m, s: (m, 0, 0, 0))] * 2,
        ),
        out_shape=[shape, shape],
        compiler_params=params(1),
        name="first_norm",
    )(core, tok, mod)


def valid_rows(tw, count, length, sz):
    frame = tw * sz.frames + lax.broadcasted_iota(jnp.int32, (count * sz.half, 1), 0) // sz.half
    return (frame < length).astype(F32)


def second_norm(tok, cot, branch_own, branch_far, mod, scalars, sz):
    def kernel(sc_ref, x_ref, c_ref, bo_ref, bf_ref, mod_ref, h_ref, g_ref):
        length = sc_ref[1 + pl.program_id(0)]
        gate1 = mod_ref[0, 2:3, :]
        shift = mod_ref[0, 3:4, :]
        scale = 1.0 + mod_ref[0, 4:5, :]
        gate2 = mod_ref[0, 5:6, :]
        for slot, b_ref in enumerate((bo_ref, bf_ref)):
            column = sc_ref[0] ^ slot
            for tw in range(2):
                count = sz.frames - tw
                span = slice(tw * sz.frames, tw * sz.frames + count)
                rows = frame_rows(x_ref[0, tw, column, :count].astype(F32))
                branch = frame_rows(b_ref[0, span].astype(F32))
                normed, _ = normalize(rows + gate1 * branch)
                h_ref[slot, 0, span] = (
                    (normed * scale + shift).astype(BF16).reshape(count, sz.half, sz.width)
                )
                grad = frame_rows(c_ref[0, tw, column, :count].astype(F32))
                grad = grad * valid_rows(tw, count, length, sz) * gate2
                g_ref[slot, 0, span] = grad.astype(BF16).reshape(count, sz.half, sz.width)

    strip = (1, 2, 2, sz.frames, sz.half, sz.width)
    piece = (1, sz.used, sz.half, sz.width)
    both = (2, 1, sz.used, sz.half, sz.width)
    shape = jax.ShapeDtypeStruct((2, sz.micro, sz.used, sz.half, sz.width), BF16)
    return pl.pallas_call(
        kernel,
        grid_spec=pltpu.PrefetchScalarGridSpec(
            num_scalar_prefetch=1,
            grid=(sz.micro,),
            in_specs=[
                pl.BlockSpec(strip, lambda m, s: (m, 0, 0, 0, 0, 0)),
                pl.BlockSpec(strip, lambda m, s: (m, 0, 0, 0, 0, 0)),
                pl.BlockSpec(piece, lambda m, s: (m, 0, 0, 0)),
                pl.BlockSpec(piece, lambda m, s: (m, 0, 0, 0)),
                pl.BlockSpec((1, 6, sz.width), lambda m, s: (m, 0, 0)),
            ],
            out_specs=[pl.BlockSpec(both, lambda m, s: (0, m, 0, 0, 0))] * 2,
        ),
        out_shape=[shape, shape],
        compiler_params=params(1),
        name="second_norm",
    )(scalars, tok, cot, branch_own, branch_far, mod)


def after_mlp(tok, cot, branch_own, branch_far, mlps, grads, mod, b_down, scalars, sz):
    def kernel(
        sc_ref, x_ref, c_ref, bo_ref, bf_ref, y0_ref, y1_ref, t0_ref, t1_ref, mod_ref, bd_ref,
        out_ref, gm_ref, go_ref, gf_ref, sum_ref,
    ):
        length = sc_ref[1 + pl.program_id(0)]
        gate1 = mod_ref[0, 2:3, :]
        scale = 1.0 + mod_ref[0, 4:5, :]
        gate2 = mod_ref[0, 5:6, :]
        sums = [jnp.zeros((1, sz.width), F32) for _ in range(4)]
        for slot, (b_ref, g_ref) in enumerate(((bo_ref, go_ref), (bf_ref, gf_ref))):
            column = sc_ref[0] ^ slot
            for tw in range(2):
                count = sz.frames - tw
                span = slice(tw * sz.frames, tw * sz.frames + count)
                shape = (count, sz.half, sz.width)
                valid = valid_rows(tw, count, length, sz)
                branch = frame_rows(b_ref[0, span].astype(F32))
                middle = frame_rows(x_ref[0, tw, column, :count].astype(F32)) + gate1 * branch
                normed, inv = normalize(middle)
                y = frame_rows(y0_ref[slot, 0, span] + y1_ref[slot, 0, span]) + bd_ref[0:1, :]
                grad = frame_rows(c_ref[0, tw, column, :count].astype(F32))
                out_ref[0, tw, column, :count] = (
                    (middle + valid * gate2 * y).astype(BF16).reshape(shape)
                )
                two = frame_rows(t0_ref[slot, 0, span] + t1_ref[slot, 0, span])
                gm = grad + norm_back(two * scale, normed, inv)
                gm_ref[slot, 0, span] = gm.reshape(shape)
                g_ref[0, span] = (valid * (gm * gate1)).astype(BF16).reshape(shape)
                for n, term in enumerate((two, two * normed, grad * valid * y, gm * branch)):
                    sums[n] = sums[n] + jnp.sum(term, axis=0, keepdims=True)
            out_ref[0, 1, column, sz.frames - 1] = x_ref[0, 1, column, sz.frames - 1]
        for n in range(4):
            sum_ref[0, n : n + 1, :] = sums[n]

    strip = (1, 2, 2, sz.frames, sz.half, sz.width)
    piece = (1, sz.used, sz.half, sz.width)
    both = (2, 1, sz.used, sz.half, sz.width)
    full = (sz.micro,) + piece[1:]
    at_strip = lambda m, s: (m, 0, 0, 0, 0, 0)
    at_piece = lambda m, s: (m, 0, 0, 0)
    at_both = lambda m, s: (0, m, 0, 0, 0)
    return pl.pallas_call(
        kernel,
        grid_spec=pltpu.PrefetchScalarGridSpec(
            num_scalar_prefetch=1,
            grid=(sz.micro,),
            in_specs=[
                pl.BlockSpec(strip, at_strip),
                pl.BlockSpec(strip, at_strip),
                pl.BlockSpec(piece, at_piece),
                pl.BlockSpec(piece, at_piece),
                pl.BlockSpec(both, at_both),
                pl.BlockSpec(both, at_both),
                pl.BlockSpec(both, at_both),
                pl.BlockSpec(both, at_both),
                pl.BlockSpec((1, 6, sz.width), lambda m, s: (m, 0, 0)),
                pl.BlockSpec((1, sz.width), lambda m, s: (0, 0)),
            ],
            out_specs=[
                pl.BlockSpec(strip, at_strip),
                pl.BlockSpec(both, at_both),
                pl.BlockSpec(piece, at_piece),
                pl.BlockSpec(piece, at_piece),
                pl.BlockSpec((1, 4, sz.width), lambda m, s: (m, 0, 0)),
            ],
        ),
        out_shape=[
            jax.ShapeDtypeStruct(tok.shape, BF16),
            jax.ShapeDtypeStruct((2,) + full, F32),
            jax.ShapeDtypeStruct(full, BF16),
            jax.ShapeDtypeStruct(full, BF16),
            jax.ShapeDtypeStruct((sz.micro, 4, sz.width), F32),
        ],
        compiler_params=params(1),
        name="after_mlp",
    )(scalars, tok, cot, branch_own, branch_far, *mlps, *grads, mod, b_down)


def last_norm(tok, cot, grad_mid, grad_own, grad_far, mod, scalars, sz):
    def kernel(sc_ref, x_ref, c_ref, gm_ref, go_ref, gf_ref, mod_ref, out_ref, sum_ref):
        scale = 1.0 + mod_ref[0, 1:2, :]
        sums = [jnp.zeros((1, sz.width), F32) for _ in range(2)]
        for slot, g_ref in enumerate((go_ref, gf_ref)):
            column = sc_ref[0] ^ slot
            for tw in range(2):
                count = sz.frames - tw
                span = slice(tw * sz.frames, tw * sz.frames + count)
                normed, inv = normalize(frame_rows(x_ref[0, tw, column, :count].astype(F32)))
                one = frame_rows(g_ref[0, span].astype(F32))
                grad = frame_rows(gm_ref[slot, 0, span]) + norm_back(one * scale, normed, inv)
                out_ref[0, tw, column, :count] = grad.astype(BF16).reshape(
                    count, sz.half, sz.width
                )
                for n, term in enumerate((one, one * normed)):
                    sums[n] = sums[n] + jnp.sum(term, axis=0, keepdims=True)
        for slot in range(2):
            out_ref[0, 1, slot, sz.frames - 1] = c_ref[0, 0, slot, 0]
        for n in range(2):
            sum_ref[0, n : n + 1, :] = sums[n]

    strip = (1, 2, 2, sz.frames, sz.half, sz.width)
    tail = (1, 1, 2, 1, sz.half, sz.width)
    piece = (1, sz.used, sz.half, sz.width)
    both = (2, 1, sz.used, sz.half, sz.width)
    return pl.pallas_call(
        kernel,
        grid_spec=pltpu.PrefetchScalarGridSpec(
            num_scalar_prefetch=1,
            grid=(sz.micro,),
            in_specs=[
                pl.BlockSpec(strip, lambda m, s: (m, 0, 0, 0, 0, 0)),
                pl.BlockSpec(tail, lambda m, s: (m, 1, 0, sz.frames - 1, 0, 0)),
                pl.BlockSpec(both, lambda m, s: (0, m, 0, 0, 0)),
                pl.BlockSpec(piece, lambda m, s: (m, 0, 0, 0)),
                pl.BlockSpec(piece, lambda m, s: (m, 0, 0, 0)),
                pl.BlockSpec((1, 6, sz.width), lambda m, s: (m, 0, 0)),
            ],
            out_specs=[
                pl.BlockSpec(strip, lambda m, s: (m, 0, 0, 0, 0, 0)),
                pl.BlockSpec((1, 2, sz.width), lambda m, s: (m, 0, 0)),
            ],
        ),
        out_shape=[
            jax.ShapeDtypeStruct(tok.shape, BF16),
            jax.ShapeDtypeStruct((sz.micro, 2, sz.width), F32),
        ],
        compiler_params=params(1),
        name="last_norm",
    )(scalars, tok, cot, grad_mid, grad_own, grad_far, mod)


class Pieces:
    def __init__(self, arrays):
        self.arrays = arrays
        self.whole = len(arrays) == 1

    def specs(self, columns, index_map):
        if self.whole:
            at = lambda *g: (0, index_map(*g))
            return [pl.BlockSpec((self.arrays[0].shape[0], columns), at)]
        at = lambda *g: (0, 0, 0, 0, index_map(*g))
        shape = self.arrays[0].shape[:-1] + (columns,)
        return [pl.BlockSpec(shape, at)] * 4

    def row_specs(self, columns, row_map, block):
        shape = self.arrays[0].shape[:2] + (1,) + self.arrays[0].shape[3:4] + (columns,)
        return [pl.BlockSpec(shape, lambda *g: (0, 0, row_map(*g), 0, block))] * 4


def place(refs, key, out_ref, columns, pitch=None, offset=0):
    depth, cut = refs[0].shape[2:4]
    pitch = 2 * cut if pitch is None else pitch
    for n, ref in enumerate(refs):
        half, far = n // 2, n % 2
        for i in range(2):
            for j in range(2):
                away = (i * 4 + j * 2 if half == 0 else j * 4 + i * 2) + far
                at = (key ^ away) * pitch + offset + half * cut
                for z in range(depth):
                    rows = pl.ds(pl.multiple_of(z * 8 * pitch + at, cut), cut)
                    out_ref[rows, columns] = ref[i, j, z]


def hand_out(value, start, rows, core, keep_ref, send_ref):
    for parity in range(2):
        for own, ref in ((0, keep_ref), (1, send_ref)):

            @pl.when(core == parity ^ own)
            def _(parity=parity, ref=ref):
                for low in range(parity * rows, value.shape[0], 2 * rows):
                    ref[(start + low) // (2 * rows)] = value[low : low + rows].astype(BF16)


def join_frames(own_ref, far_ref, joined_ref, sz):
    for m in range(sz.micro):
        for f in range(sz.used):
            at = m * sz.win_rows + f * sz.frame
            joined_ref[at : at + sz.half] = own_ref[m, f]
            joined_ref[at + sz.half : at + sz.frame] = far_ref[m, f]


def spread_bias(block_ref, head, bias_ref, sz):
    full = sz.lens[0]
    for t in range(sz.frames):
        low = (sz.frames - 1 - t) * sz.frame
        bias_ref[t * sz.frame : (t + 1) * sz.frame, :] = block_ref[head, :, low : low + full]


def window_rows(m, tw, sz):
    start = pl.multiple_of(m * sz.win_rows + tw * sz.lens[0], sz.frame)
    return pl.ds(start, sz.lens[tw])


def attention(half, own, far, w_qkv, bias, scalars, sz, att_first=None, w_out=None):
    scale = 1.0 / math.sqrt(sz.head)
    last = w_out is not None
    steps = sz.groups // 2
    direct = not w_qkv.whole
    gcols = sz.gcols

    def kernel(sc_ref, own_ref, far_ref, bias_ref, *refs):
        refs = list(refs)
        take = lambda count: [refs.pop(0) for _ in range(count)]
        w_refs = take(len(w_qkv.arrays))
        if last:
            (first_ref,) = take(1)
            out_refs = take(8 if direct else 1)
        qkv_ref, att_ref, w_ref = take(3)
        if last:
            wo_ref, bo_ref, bf_ref = take(3)
        joined, spread = take(2)
        step = pl.program_id(0)
        key = sc_ref[1 + sz.micro]

        @pl.when(step == 0)
        def _():
            join_frames(own_ref, far_ref, joined, sz)

        if direct:
            place(w_refs, key, w_ref, slice(None))
        else:
            w_ref[...] = w_refs[0][...]
        for n in range(3):
            part = dot_nn(joined[...], w_ref[:, n * gcols : (n + 1) * gcols]).astype(BF16)
            qkv_ref[n] = part * scale if n == 0 else part
        for head in range(sz.group):
            lanes = slice(head * sz.head, (head + 1) * sz.head)
            spread_bias(bias_ref, head, spread, sz)

            def one_micro(m, carry, lanes=lanes):
                for tw in range(2):
                    size = sz.lens[tw]
                    rows = window_rows(m, tw, sz)
                    keys_ok = (sc_ref[1 + m] - tw * sz.frames) * sz.frame

                    @pl.when(keys_ok > 0)
                    def _(rows=rows, size=size, keys_ok=keys_ok):
                        scores = dot_nt(qkv_ref[0, rows, lanes], qkv_ref[1, rows, lanes])
                        scores = scores + spread[:size, :size].astype(F32)
                        column = lax.broadcasted_iota(jnp.int32, (1, size), 1)
                        scores = jnp.where(column < keys_ok, scores, MASKED)
                        top = jnp.max(scores, axis=-1, keepdims=True)
                        weight = jnp.exp(scores - top)
                        share = 1.0 / jnp.sum(weight, axis=-1, keepdims=True)
                        probs = (weight * share).astype(BF16)
                        att_ref[rows, lanes] = dot_nn(probs, qkv_ref[2, rows, lanes]).astype(BF16)

                    @pl.when(keys_ok <= 0)
                    def _(rows=rows, size=size):
                        att_ref[rows, lanes] = jnp.zeros((size, sz.head), BF16)

                return carry

            lax.fori_loop(0, sz.micro, one_micro, 0)
        if not last:
            return
        kept, total = take(2)
        for n in range(steps):

            @pl.when(step == n)
            def _(n=n):
                kept[:, n * gcols : (n + 1) * gcols] = att_ref[...]

        @pl.when(step == steps - 1)
        def _():
            if direct:
                place(out_refs[:4], key, wo_ref, slice(0, 2 * gcols))
                place(out_refs[4:], key, wo_ref, slice(2 * gcols, 4 * gcols))
            else:
                wo_ref[...] = out_refs[0][...]
            middle = first_ref.shape[1]
            total[...] = dot_nn(first_ref[...], wo_ref[:middle]) + dot_nn(
                kept[...], wo_ref[middle:]
            )
            for m in range(sz.micro):
                for f in range(sz.used):
                    at = m * sz.win_rows + f * sz.frame
                    valid = (f < sc_ref[1 + m]).astype(F32)
                    bo_ref[m, f] = (total[at : at + sz.half] * valid).astype(BF16)
                    bf_ref[m, f] = (total[at + sz.half : at + sz.frame] * valid).astype(BF16)

    piece = (sz.micro, sz.used, sz.half, sz.width)
    fixed = lambda g, s: (0, 0, 0, 0)
    flat = lambda g, s: (0, 0)
    width, cols = sz.width, sz.width // 2
    in_specs = [
        once(piece, fixed),
        once(piece, fixed),
        pl.BlockSpec((sz.group,) + bias.shape[1:], lambda g, s: (half * steps + g, 0, 0)),
    ] + w_qkv.specs(3 * gcols, lambda g, s: g)
    out_specs = [
        pl.BlockSpec((3, sz.rows, gcols), lambda g, s: (0, 0, g)),
        pl.BlockSpec((sz.rows, gcols), lambda g, s: (0, g)),
        pl.BlockSpec((width, 3 * gcols), lambda g, s: (0, g)),
    ]
    out_shape = [
        jax.ShapeDtypeStruct((3, sz.rows, cols), BF16),
        jax.ShapeDtypeStruct((sz.rows, cols), BF16),
        jax.ShapeDtypeStruct((width, 3 * cols), BF16),
    ]
    scratch = [
        pltpu.VMEM((sz.rows, width), BF16),
        pltpu.VMEM((sz.lens[0], sz.lens[0]), BF16),
    ]
    args = [scalars, own, far, bias, *w_qkv.arrays]
    flops = 6 * sz.rows * width * cols + 4 * sz.rows * sz.lens[0] * cols
    if last:
        in_specs += [once((sz.rows, cols), flat)]
        if direct:
            low = w_out.arrays[0].shape[-1] // (2 * gcols) - 2
            in_specs += w_out.specs(2 * gcols, lambda g, s: low)
            in_specs += w_out.specs(2 * gcols, lambda g, s: low + 1)
            out_args = w_out.arrays * 2
        else:
            in_specs += w_out.specs(width, lambda g, s: 0)
            out_args = w_out.arrays
        out_specs += [pl.BlockSpec((width, width), flat)] + [pl.BlockSpec(piece, fixed)] * 2
        out_shape += [jax.ShapeDtypeStruct((width, width), BF16)]
        out_shape += [jax.ShapeDtypeStruct(piece, BF16)] * 2
        scratch += [pltpu.VMEM((sz.rows, cols), BF16), pltpu.VMEM((sz.rows, width), F32)]
        args += [att_first, *out_args]
        flops += 2 * sz.rows * width * width
    return pl.pallas_call(
        kernel,
        grid_spec=pltpu.PrefetchScalarGridSpec(
            num_scalar_prefetch=1,
            grid=(steps,),
            in_specs=in_specs,
            out_specs=out_specs,
            scratch_shapes=scratch,
        ),
        out_shape=out_shape,
        compiler_params=params(1),
        cost_estimate=cost(3 * flops, 16 * sz.rows * width),
        name="attention" + "_last" * last,
    )(*args)


def grad_shapes(direct, rows, width, columns, sz):
    if not direct:
        return [jax.ShapeDtypeStruct((width, columns), BF16)]
    return [jax.ShapeDtypeStruct((width // (2 * rows), rows, columns), BF16)] * 2


def grad_specs(direct, rows, width, columns, at_row, at_column):
    if not direct:
        return [pl.BlockSpec((width, columns), lambda *g: (at_row(*g), at_column(*g)))]
    shape = (width // (2 * rows), rows, columns)
    return [pl.BlockSpec(shape, lambda *g: (at_row(*g), 0, at_column(*g)))] * 2


def attention_back(half, grad_own, grad_far, own, far, qkv, atts, w_qkv, w_out, bias_t, scalars, sz, shard, carry=None):
    scale = 1.0 / math.sqrt(sz.head)
    last = carry is not None
    steps = sz.groups // 2
    direct = shard is not None
    outs = 2 if direct else 1
    gcols, width = sz.gcols, sz.width
    quarter = width // 4

    def kernel(
        sc_ref, go_ref, gf_ref, own_ref, far_ref, qkv_ref, w_ref, wo_ref, bias_ref, *refs
    ):
        refs = list(refs)
        take = lambda count: [refs.pop(0) for _ in range(count)]
        if last:
            (carry_ref,) = take(1)
        else:
            att_refs = take(2)
        gw_refs = take(outs)
        (fold_ref,) = take(1)
        if last:
            ho_ref, hf_ref = take(2)
        else:
            gwo_refs = take(outs)
            (total,) = take(1)
        grad, hidden_t, grad_att, parts, spread, pair_sum = take(6)
        if last:
            (total,) = take(1)
        step = pl.program_id(0)

        def give(value, start, refs):
            if direct:
                hand_out(value, start, shard, sc_ref[0], *refs)
            else:
                refs[0][start : start + value.shape[0]] = value.astype(BF16)

        @pl.when(step == 0)
        def _():
            join_frames(own_ref, far_ref, grad, sz)
            hidden_t[...] = grad[...].T
            join_frames(go_ref, gf_ref, grad, sz)
            if last:
                total[...] = carry_ref[...]
            else:
                total[...] = jnp.zeros_like(total)

        grad_att[...] = dot_nt(grad[...], wo_ref[...]).astype(BF16)
        full = sz.lens[0]
        for head in range(sz.group):
            lanes = slice(head * sz.head, (head + 1) * sz.head)
            spread_bias(bias_ref, head, spread, sz)
            pair_sum[...] = jnp.zeros((full, full), F32)

            def one_micro(m, carry, head=head, lanes=lanes):
                for tw in range(2):
                    size = sz.lens[tw]
                    rows = window_rows(m, tw, sz)
                    keys_ok = (sc_ref[1 + m] - tw * sz.frames) * sz.frame
                    spot = [
                        slice(n * gcols + head * sz.head, n * gcols + (head + 1) * sz.head)
                        for n in range(3)
                    ]

                    @pl.when(keys_ok > 0)
                    def _(rows=rows, size=size, keys_ok=keys_ok, spot=spot):
                        query = qkv_ref[0, rows, lanes]
                        key = qkv_ref[1, rows, lanes]
                        value = qkv_ref[2, rows, lanes]
                        grad_out = grad_att[rows, lanes]
                        scores = dot_nt(key, query) + spread[:size, :size].astype(F32)
                        row = lax.broadcasted_iota(jnp.int32, (size, 1), 0)
                        scores = jnp.where(row < keys_ok, scores, MASKED)
                        weight = jnp.exp(scores - jnp.max(scores, axis=0, keepdims=True))
                        probs = weight * (1.0 / jnp.sum(weight, axis=0, keepdims=True))
                        grad_probs = dot_nt(value, grad_out)
                        inner = jnp.sum(probs * grad_probs, axis=0, keepdims=True)
                        grad_scores = (probs * (grad_probs - inner)).astype(BF16)
                        pair_sum[:size, :size] += grad_scores.astype(F32)
                        parts[rows, spot[2]] = dot_nn(probs.astype(BF16), grad_out).astype(BF16)
                        parts[rows, spot[1]] = dot_nn(grad_scores, query).astype(BF16)
                        parts[rows, spot[0]] = (dot_tn(grad_scores, key) * scale).astype(BF16)

                    @pl.when(keys_ok <= 0)
                    def _(rows=rows, size=size, spot=spot):
                        for n in range(3):
                            parts[rows, spot[n]] = jnp.zeros((size, sz.head), BF16)

                return carry

            lax.fori_loop(0, sz.micro, one_micro, 0)
            fold_ref[head] = jnp.zeros(fold_ref.shape[1:], F32)
            for t in range(sz.frames):
                low = (sz.frames - 1 - t) * sz.frame
                fold_ref[head, :, low : low + full] += pair_sum[
                    t * sz.frame : (t + 1) * sz.frame, :
                ]
        for n in range(4):
            rows = slice(n * quarter, (n + 1) * quarter)
            give(dot_nn(hidden_t[rows, :], parts[...]), n * quarter, gw_refs)
        total[...] += dot_nt(parts[...], w_ref[...])
        if not last:
            for n, a_ref in enumerate(att_refs):

                @pl.when(step == n)
                def _(a_ref=a_ref):
                    for k in range(2):
                        columns = slice(k * quarter, (k + 1) * quarter)
                        give(dot_tn(a_ref[:, columns], grad[...]), k * quarter, gwo_refs)

            return

        @pl.when(step == steps - 1)
        def _():
            for m in range(sz.micro):
                for f in range(sz.used):
                    at = m * sz.win_rows + f * sz.frame
                    ho_ref[m, f] = total[at : at + sz.half].astype(BF16)
                    hf_ref[m, f] = total[at + sz.half : at + sz.frame].astype(BF16)

    piece = (sz.micro, sz.used, sz.half, width)
    fixed = lambda g, s: (0, 0, 0, 0)
    flat = lambda g, s: (0, 0)
    cols = width // 2
    block_bias = (sz.group,) + bias_t.shape[1:]
    in_specs = [
        once(piece, fixed),
        once(piece, fixed),
        once(piece, fixed),
        once(piece, fixed),
        pl.BlockSpec((3, sz.rows, gcols), lambda g, s: (0, 0, g)),
        pl.BlockSpec((width, 3 * gcols), lambda g, s: (0, g)),
        pl.BlockSpec((gcols, width), lambda g, s: (half * steps + g, 0)),
        pl.BlockSpec(block_bias, lambda g, s: (half * steps + g, 0, 0)),
    ]
    zero = lambda g, s: 0
    along = lambda g, s: g
    out_specs = grad_specs(direct, shard, width, 3 * gcols, zero, along)
    out_specs += [pl.BlockSpec(block_bias, lambda g, s: (g, 0, 0))]
    out_shape = grad_shapes(direct, shard, width, 3 * cols, sz)
    out_shape += [jax.ShapeDtypeStruct((HEADS // 2,) + bias_t.shape[1:], F32)]
    scratch = [
        pltpu.VMEM((sz.rows, width), BF16),
        pltpu.VMEM((width, sz.rows), BF16),
        pltpu.VMEM((sz.rows, gcols), BF16),
        pltpu.VMEM((sz.rows, 3 * gcols), BF16),
        pltpu.VMEM((sz.lens[0], sz.lens[0]), BF16),
        pltpu.VMEM((sz.lens[0], sz.lens[0]), F32),
    ]
    args = [scalars, grad_own, grad_far, own, far, qkv, w_qkv, w_out, bias_t]
    flops = 14 * sz.rows * width * cols + 10 * sz.rows * sz.lens[0] * cols
    if last:
        in_specs += [once((sz.rows, width), flat)]
        out_specs += [pl.BlockSpec(piece, fixed)] * 2
        out_shape += [jax.ShapeDtypeStruct(piece, BF16)] * 2
        scratch += [pltpu.VMEM((sz.rows, width), F32)]
        args += [carry]
    else:
        in_specs += [once((sz.rows, cols), flat)] * 2
        out_specs += grad_specs(direct, shard, cols, width, along, zero)
        out_specs += [once((sz.rows, width), flat)]
        out_shape += grad_shapes(direct, shard, width, width, sz)
        out_shape += [jax.ShapeDtypeStruct((sz.rows, width), F32)]
        args += list(atts)
        flops += 2 * sz.rows * width * width
    return pl.pallas_call(
        kernel,
        grid_spec=pltpu.PrefetchScalarGridSpec(
            num_scalar_prefetch=1,
            grid=(steps,),
            in_specs=in_specs,
            out_specs=out_specs,
            scratch_shapes=scratch,
        ),
        out_shape=out_shape,
        compiler_params=params(1),
        cost_estimate=cost(3 * flops, 24 * sz.rows * width),
        name="attention_back" + "_last" * last,
    )(*args)


GELU_A = math.sqrt(2.0 / math.pi)
GELU_B = 0.044715


def mlp(hidden, grad, w_up, b_up, w_down, scalars, sz, shards):
    chunk = 512
    tiles = 3
    tile = sz.rows // tiles
    inner = b_up.shape[1]
    steps = inner // chunk
    direct = shards is not None
    outs = 2 if direct else 1
    rows, width = sz.rows, sz.width
    quarter = width // 4

    def kernel(sc_ref, h_ref, g_ref, bu_ref, *refs):
        refs = list(refs)
        take = lambda count: [refs.pop(0) for _ in range(count)]
        up_refs = take(4 if direct else 1)
        down_refs = take(8 if direct else 1)
        y_ref, t_ref, gbu_ref, gbd_ref = take(4)
        gwu_refs, gwd_refs = take(outs), take(outs)
        hidden_t, act_s, gpre_s = take(3)
        if direct:
            wu_ref, wd_ref = take(2)
        else:
            wu_ref, wd_ref = up_refs[0], down_refs[0]
        step = pl.program_id(0)

        def give(value, start, shard, refs):
            if direct:
                hand_out(value, start, shard, sc_ref[0], *refs)
            else:
                refs[0][start : start + value.shape[0]] = value.astype(BF16)

        @pl.when(step == 0)
        def _():
            hidden_t[...] = h_ref[...].T
            gbd_ref[...] = jnp.sum(g_ref[...].astype(F32), axis=0, keepdims=True)
            y_ref[...] = jnp.zeros_like(y_ref)
            t_ref[...] = jnp.zeros_like(t_ref)

        if direct:
            key = sc_ref[1 + sz.micro]
            place(up_refs, key, wu_ref, slice(None))
            for part in range(2):
                refs_part = down_refs[4 * part : 4 * part + 4]
                place(refs_part, key, wd_ref, slice(None), shards[1], part * shards[0])
        bias_sum = jnp.zeros((1, chunk), F32)
        for n in range(tiles):
            span = slice(n * tile, (n + 1) * tile)
            pre = dot_nn(h_ref[span], wu_ref[...]) + bu_ref[...]
            grad_act = dot_nt(g_ref[span], wd_ref[...])
            square = pre * pre
            tanh = jnp.tanh(GELU_A * pre * (1.0 + GELU_B * square))
            half = 0.5 * (1.0 + tanh)
            act = (pre * half).astype(BF16)
            slope = half + (0.5 * GELU_A) * pre * (1.0 - tanh * tanh) * (
                1.0 + (3.0 * GELU_B) * square
            )
            grad_pre = (grad_act * slope).astype(BF16)
            act_s[span] = act
            gpre_s[span] = grad_pre
            bias_sum = bias_sum + jnp.sum(grad_pre.astype(F32), axis=0, keepdims=True)
            y_ref[span] += dot_nn(act, wd_ref[...])
            t_ref[span] += dot_nt(grad_pre, wu_ref[...])
        gbu_ref[...] = bias_sum
        for n in range(4):
            span = slice(n * quarter, (n + 1) * quarter)
            give(dot_nn(hidden_t[span, :], gpre_s[...]), n * quarter, shards and shards[0], gwu_refs)
        for n in range(2):
            span = slice(n * quarter, (n + 1) * quarter)
            give(dot_tn(act_s[:, span], g_ref[...]), n * quarter, shards and shards[1], gwd_refs)

    fixed = lambda j, s: (0, 0)
    zero = lambda j, s: 0
    along = lambda j, s: j
    in_specs = [
        once((rows, width), fixed),
        once((rows, width), fixed),
        pl.BlockSpec((1, chunk), lambda j, s: (0, j)),
    ] + w_up.specs(chunk, along)
    args = [scalars, hidden, grad, b_up, *w_up.arrays]
    if direct:
        low = w_down.arrays[0].shape[-1] // width - 2
        for part in range(2):
            in_specs += w_down.row_specs(width, along, low + part)
            args += w_down.arrays
    else:
        in_specs += [pl.BlockSpec((chunk, width), lambda j, s: (j, 0))]
        args += w_down.arrays
    out_specs = [
        pl.BlockSpec((rows, width), fixed),
        pl.BlockSpec((rows, width), fixed),
        pl.BlockSpec((1, chunk), lambda j, s: (0, j)),
        pl.BlockSpec((1, width), fixed),
    ]
    out_specs += grad_specs(direct, shards and shards[0], width, chunk, zero, along)
    out_specs += grad_specs(direct, shards and shards[1], chunk, width, along, zero)
    out_shape = [
        jax.ShapeDtypeStruct((rows, width), F32),
        jax.ShapeDtypeStruct((rows, width), F32),
        jax.ShapeDtypeStruct((1, inner), F32),
        jax.ShapeDtypeStruct((1, width), F32),
    ]
    out_shape += grad_shapes(direct, shards and shards[0], width, inner, sz)
    out_shape += grad_shapes(direct, shards and shards[1], inner, width, sz)
    scratch = [
        pltpu.VMEM((width, rows), BF16),
        pltpu.VMEM((rows, chunk), BF16),
        pltpu.VMEM((rows, chunk), BF16),
    ]
    if direct:
        scratch += [pltpu.VMEM((width, chunk), BF16), pltpu.VMEM((chunk, width), BF16)]
    return pl.pallas_call(
        kernel,
        grid_spec=pltpu.PrefetchScalarGridSpec(
            num_scalar_prefetch=1,
            grid=(steps,),
            in_specs=in_specs,
            out_specs=out_specs,
            scratch_shapes=scratch,
        ),
        out_shape=out_shape,
        compiler_params=params(1),
        cost_estimate=cost(14 * rows * width * inner, 16 * rows * width),
        name="mlp",
    )(*args)


def offset_onehot(core, sz):
    span = 2 * sz.side - 1
    place = jnp.arange(sz.frame, dtype=jnp.int32)
    row = ((place // sz.half) ^ core) * sz.strip_rows + place // sz.side % sz.strip_rows
    column = place % sz.side
    index = (row[:, None] - row[None, :] + sz.side - 1) * span
    index = index + column[:, None] - column[None, :] + sz.side - 1
    return (jnp.arange(span * span, dtype=jnp.int32)[:, None, None] == index[None]).astype(BF16)


def bucket_onehot(bucket, count):
    return (jnp.arange(count, dtype=jnp.int32)[:, None] == bucket[None, :]).astype(BF16)


def bias_blocks(table, bucket, places, sz):
    steps = 2 * sz.frames - 1
    by_offset = dot_tn(table, bucket_onehot(bucket, table.shape[0])).astype(BF16)
    by_offset = by_offset.reshape(HEADS, steps, -1)
    shape = (HEADS, sz.frame, steps * sz.frame)
    forward = jnp.einsum("hkj,jpq->hpkq", by_offset[:, ::-1], places, preferred_element_type=F32)
    backward = jnp.einsum("hkj,jpq->hqkp", by_offset, places, preferred_element_type=F32)
    return forward.astype(BF16).reshape(shape), backward.astype(BF16).reshape(shape)


def split_low(value):
    high = value.astype(BF16)
    return high, (value - high.astype(F32)).astype(BF16)


def table_grad(fold, bucket, places, buckets, sz):
    steps = 2 * sz.frames - 1
    fold = fold.reshape(HEADS, sz.frame, steps, sz.frame)
    by_offset = sum(
        jnp.einsum("hqkp,jpq->hkj", part, places, preferred_element_type=F32)
        for part in split_low(fold)
    ).reshape(HEADS, -1)
    onehot = bucket_onehot(bucket, buckets)
    return sum(dot_nt(onehot, part) for part in split_low(by_offset))


class Net:
    AXES = ("clip", "win")
    X, Y, CORE = 2, 4, 1

    def __init__(self):
        self.count = lax.axis_size(self.AXES)
        self.direct = lax.axis_size("win") == 4 and self.count == 32
        self.deep = self.count // 8
        self.index = lax.axis_index(self.AXES)
        self.z = self.index // 8

    def bit(self, which):
        return self.index // which % 2

    def swap(self, value, which):
        return lax.ppermute(value, self.AXES, [(n, n ^ which) for n in range(self.count)])

    def from_z(self, value, step):
        move = lambda n: (n // 8 - step) % self.deep * 8 + n % 8
        return lax.ppermute(value, self.AXES, [(n, move(n)) for n in range(self.count)])

    def swap_sum(self, value, which):
        return value + self.swap(value, which)


    def gather_clips(self, value):
        along = jnp.stack([value] + [self.from_z(value, k) for k in range(1, self.deep)])
        return jnp.stack([along, self.swap(along, self.Y)], axis=1)

    def scatter_clips(self, value):
        kept = value[:, 0] + self.swap(value[:, 1], self.Y)
        return kept[0] + sum(
            self.from_z(kept[self.deep - k], k) for k in range(1, self.deep)
        )

    def sum_all(self, value):
        for which in (self.CORE, self.X, self.Y):
            value = self.swap_sum(value, which)
        return value + sum(self.from_z(value, k) for k in range(1, self.deep))

    def gather_small(self, value):
        parts = self.gather_clips(value)
        for which in (self.X, self.CORE):
            parts = jnp.stack([parts, self.swap(parts, which)], axis=2 if which == self.X else 3)
        parts = parts.reshape(self.count, -1)
        place = jnp.arange(self.count, dtype=jnp.int32)
        holder = (self.z + place // 8) % self.deep * 8 + (place % 8 ^ self.index % 8)
        pick = (place[:, None] == holder[None, :]).astype(BF16)
        return dot_nn(pick, parts).astype(BF16)


    def gather_rows(self, shard):
        along = [shard] + [self.from_z(shard, k) for k in range(1, self.deep)]
        ready = along[-1]
        along = jnp.concatenate([a[None] for a in along + along[:-1]])
        along = lax.dynamic_slice_in_dim(along, (self.deep - self.z) % self.deep, self.deep, 0)
        cut = shard.shape[0] // 2
        arrays = []
        for half, order in enumerate(((self.X, self.Y), (self.Y, self.X))):
            here = along[:, half * cut : (half + 1) * cut]
            for which in order:
                here = jnp.stack([here, self.swap(here, which)])
            arrays += [here, self.swap(here, self.CORE)]
        return Pieces(arrays), ready


class Scatter:
    def __init__(self, net):
        self.net = net

    @staticmethod
    def add(one, two):
        return (one.astype(F32) + two.astype(F32)).astype(BF16)

    @staticmethod
    def pick(value, at, axis):
        return lax.dynamic_index_in_dim(value, at, axis, keepdims=False)

    def core(self, keep, send):
        got = self.net.swap(send, self.net.CORE)
        total = self.add(keep, got)
        return total.reshape((self.net.deep, 2, 2) + total.shape[1:])

    def second(self, value):
        net = self.net
        cut = value.shape[3] // 2
        first, last = value[..., :cut, :], value[..., cut:, :]
        y, x = net.bit(net.Y), net.bit(net.X)
        got = net.swap(self.pick(first, 1 - y, 1), net.Y), net.swap(self.pick(last, 1 - x, 2), net.X)
        return self.add(self.pick(first, y, 1), got[0]), self.add(self.pick(last, x, 2), got[1])

    def third(self, value):
        net = self.net
        first, last = value
        y, x = net.bit(net.Y), net.bit(net.X)
        got = net.swap(self.pick(first, 1 - x, 1), net.X), net.swap(self.pick(last, 1 - y, 1), net.Y)
        first = self.add(self.pick(first, x, 1), got[0])
        return jnp.concatenate([first, self.add(self.pick(last, y, 1), got[1])], axis=1)

    def fourth(self, value):
        net = self.net
        total = self.pick(value, net.z, 0).astype(F32)
        for k in range(1, net.deep):
            send = self.pick(value, (net.z + net.deep - k) % net.deep, 0)
            total = total + net.from_z(send, k).astype(F32)
        return total


def tie(value, *others):
    return lax.optimization_barrier((value,) + others)[0]


def body(
    tokens, cond, lengths, ada_w, ada_b, w_qkv, w_out, w_up, b_up, w_down, b_down,
    rel_table, bucket, cotangent,
):
    axes = ("clip", "win")
    sz = Sizes(tokens)
    net = Net()
    devices, index = net.count, net.index
    clips = lax.axis_size("clip")
    width = sz.width
    core = lax.axis_index("win") % 2
    swap = [(n, n ^ 1) for n in range(lax.axis_size("win"))]
    scalars = jnp.stack([core] + [lengths[n, 0] for n in range(sz.micro)] + [index % 8])
    strip = (sz.micro, 2, 2, sz.frames, sz.half, width)
    tok = tokens.reshape(strip)
    cot = cotangent.reshape(strip)

    cond_act = jax.nn.silu(cond[:, 0].astype(F32)).astype(BF16)
    rows = ada_w.shape[0]
    if net.direct:
        cond_all = net.gather_clips(cond_act)
    else:
        cond_all = lax.all_gather(cond_act, "clip", axis=0)
    cond_mine = lax.dynamic_slice_in_dim(cond_all, index * rows, rows, cond_all.ndim - 1)
    lead = cond_mine.shape[:-1]
    cond_mine = cond_mine.reshape(clips * sz.micro, rows)
    mod_part = dot_nn(cond_mine, ada_w)
    spread_b = jnp.zeros((mod_part.shape[1],), F32)
    spread_b = lax.dynamic_update_slice(spread_b, ada_b.astype(F32), (index * ada_b.shape[0],))
    mod_part = (mod_part + spread_b[None, :]).reshape(lead + (6 * width,))
    if net.direct:
        mod = net.scatter_clips(mod_part)
        mod = net.swap_sum(net.swap_sum(mod, net.CORE), net.X)
    else:
        mod = lax.psum_scatter(mod_part, "clip", scatter_dimension=0, tiled=False)
        mod = lax.psum(mod, "win")
    mod = mod.reshape(sz.micro, 6, width)

    cols = width // 2
    half_groups = sz.groups // 2
    by_group = w_qkv.reshape(rows, 3, sz.groups, sz.gcols).transpose(0, 2, 1, 3)
    by_group = by_group.reshape(rows, 2, 3 * cols)
    shard_q = [by_group[:, n] for n in range(2)]
    inner = w_up.shape[1]
    per = w_down.shape[0] // 2
    shard_u = w_up.reshape(rows, devices, 2, per)
    shard_u = [shard_u[:, :, n].reshape(rows, inner // 2) for n in range(2)]
    shard_d = [w_down[:per], w_down[per:]]
    small = jnp.concatenate([b_up, b_down, rel_table.reshape(-1)])
    if net.direct:
        fold_d = [d.reshape(2, rows, width) for d in shard_d]
        packs = [
            shard_q[0],
            jnp.concatenate([shard_q[1], w_out], axis=1),
            jnp.concatenate([shard_u[0], fold_d[0][0], fold_d[0][1]], axis=1),
            jnp.concatenate([shard_u[1], fold_d[1][0], fold_d[1][1]], axis=1),
        ]
        small = jnp.pad(small, (0, -small.shape[0] % 128))
        small = net.gather_small(small)
        q_0, ready = net.gather_rows(packs[0])
        q_1, ready = net.gather_rows(tie(packs[1], ready))
        full_q, full_out = [q_0, q_1], q_1
        u_0, ready = net.gather_rows(tie(packs[2], ready, mod))
        u_1, ready = net.gather_rows(tie(packs[3], ready))
        full_u = full_d = [u_0, u_1]
    else:
        gather = lambda v: lax.all_gather(v, axes, axis=0, tiled=True)
        full_q = [Pieces([gather(v)]) for v in shard_q]
        full_out = Pieces([gather(w_out)])
        full_u = [Pieces([gather(v)]) for v in shard_u]
        full_d = [Pieces([gather(v)]) for v in shard_d]
        small = gather(small[None])
    n_up, n_down = b_up.shape[0], b_down.shape[0]
    n_small = n_up + n_down + rel_table.size
    full_bup = small[:, :n_up].astype(F32).reshape(devices, 2, per)
    full_bup = [full_bup[:, n].reshape(1, inner // 2) for n in range(2)]
    full_bdown = small[:, n_up : n_up + n_down].astype(F32).reshape(1, width)
    table = small[:, n_up + n_down : n_small].reshape(-1, HEADS)
    places = offset_onehot(core, sz)
    bias, bias_t = bias_blocks(table, bucket, places, sz)

    own, send = first_norm(tok, mod, scalars, sz)
    far = lax.ppermute(send, "win", swap)
    qkv_0, att_0, wide_0 = attention(0, own, far, full_q[0], bias, scalars, sz)
    qkv_1, att_1, wide_1, wide_out, branch_own, branch_send = attention(
        1, own, far, full_q[1], bias, scalars, sz, att_0, full_out
    )
    branch_far = lax.ppermute(branch_send, "win", swap)
    hidden_two, grad_mlp = second_norm(tok, cot, branch_own, branch_far, mod, scalars, sz)
    flat = (sz.rows, width)
    both = (2, sz.micro, sz.used, sz.half, width)
    hidden_two, grad_mlp = hidden_two.reshape(flat), grad_mlp.reshape(flat)
    shards = (rows, per) if net.direct else None
    mlps = [
        mlp(hidden_two, grad_mlp, full_u[n], full_bup[n], full_d[n], scalars, sz, shards)
        for n in range(2)
    ]

    scat = Scatter(net)
    output, grad_mid, grad_own, grad_send, sums_two = after_mlp(
        tok, cot, branch_own, branch_far, [v[0].reshape(both) for v in mlps],
        [v[1].reshape(both) for v in mlps], mod, full_bdown, scalars, sz,
    )
    grad_far = lax.ppermute(grad_send, "win", swap)
    if net.direct:
        inner_terms = []
        for v in mlps:
            up, down = scat.core(*v[4:6]), scat.core(*v[6:8])
            inner_terms += [up, down[..., :rows, :], down[..., rows:, :]]
        terms = jnp.concatenate(inner_terms, axis=-1)
        grad_far = tie(grad_far, terms)
    g_q0, fold_0, g_out, carry = unpack(
        attention_back(
            0, grad_own, grad_far, own, far, qkv_0, (att_0, att_1), wide_0, wide_out, bias_t,
            scalars, sz, rows if net.direct else None,
        ),
        net.direct,
    )
    if net.direct:
        terms = scat.second(terms)
        carry = tie(carry, *terms)
    g_q1, fold_1, hid_own, hid_send = unpack(
        attention_back(
            1, grad_own, grad_far, own, far, qkv_1, None, wide_1, wide_out, bias_t, scalars, sz,
            rows if net.direct else None, carry,
        ),
        net.direct,
    )
    hid_far = lax.ppermute(hid_send, "win", swap)
    if net.direct:
        terms = scat.third(terms)
        hid_far = tie(hid_far, terms)
    grad_in, sums_one = last_norm(tok, cot, grad_mid, hid_own, hid_far, mod, scalars, sz)

    grad_mod = jnp.concatenate(
        [sums_one, sums_two[:, 3:4], sums_two[:, 0:3]], axis=1
    ).reshape(sz.micro, 6 * width)
    if net.direct:
        grad_mod = net.swap_sum(net.swap_sum(grad_mod, net.CORE), net.X)
        mod_all = net.gather_clips(grad_mod)
    else:
        mod_all = lax.all_gather(lax.psum(grad_mod, "win"), "clip", axis=0)
    mod_all = mod_all.reshape(clips * sz.micro, -1)
    grad_ada_w = lax.dot_general(
        cond_mine.astype(F32), mod_all, (((0,), (0,)), ((), ())),
        precision=HIGHEST, preferred_element_type=F32,
    )
    grad_ada_b = lax.dynamic_slice_in_dim(
        jnp.sum(mod_all, axis=0), index * ada_b.shape[0], ada_b.shape[0]
    )
    g_table = table_grad(
        jnp.concatenate([fold_0, fold_1]), bucket, places, table.shape[0], sz
    ).reshape(devices, -1)
    g_bup = jnp.stack([v[2].reshape(devices, per) for v in mlps], axis=1).reshape(devices, -1)
    g_bdown = mlps[0][3].reshape(devices, -1)
    g_small = jnp.concatenate([g_bup, g_bdown, g_table], axis=1)
    if net.direct:
        g_small = lax.dynamic_index_in_dim(net.sum_all(g_small), index, 0, keepdims=False)
        terms_att = jnp.concatenate([scat.core(*v) for v in (g_q0, g_q1, g_out)], axis=-1)
        terms_att = scat.third(scat.second(terms_att))
        terms = scat.fourth(terms)
        terms_att = scat.fourth(terms_att)
        r_u, r_d = [], []
        for n in range(2):
            mine = terms[:, n * inner : (n + 1) * inner]
            r_u.append(mine[:, : inner // 2])
            r_d += [mine[:, inner // 2 : inner // 2 + width], mine[:, inner // 2 + width :]]
        r_q = [terms_att[:, n * 3 * cols : (n + 1) * 3 * cols] for n in range(2)]
        r_out = terms_att[:, 6 * cols :]
    else:
        scatter = lambda v: lax.psum_scatter(
            v[0].astype(F32), axes, scatter_dimension=0, tiled=True
        )
        g_small = lax.psum_scatter(g_small, axes, scatter_dimension=0, tiled=False)
        r_u = [scatter(v[4:5]) for v in mlps]
        r_d = [scatter(v[5:6]) for v in mlps]
        r_q, r_out = [scatter(v) for v in (g_q0, g_q1)], scatter(g_out)
    r_up = jnp.stack([v.reshape(rows, devices, per) for v in r_u], axis=2).reshape(rows, inner)
    r_down = jnp.concatenate(r_d)
    r_qkv = jnp.stack([v.reshape(rows, half_groups, 3, sz.gcols) for v in r_q], axis=1)
    r_qkv = r_qkv.reshape(rows, sz.groups, 3, sz.gcols).transpose(0, 2, 1, 3)
    r_qkv = r_qkv.reshape(rows, 3 * width)
    return (
        output.reshape(tokens.shape), grad_in.reshape(tokens.shape), grad_ada_w, grad_ada_b,
        r_qkv, r_out, r_up, g_small[:n_up], r_down, g_small[n_up : n_up + n_down],
        g_small[n_up + n_down :].reshape(rel_table.shape),
    )


def unpack(results, direct):
    results = list(results)
    count = 2 if direct else 1
    out = [results[:count], results[count]]
    results = results[count + 1 :]
    if len(results) == count + 1:
        if results[0].ndim == (3 if direct else 2):
            return out + [results[:count], results[count]]
    return out + results


def solution(mesh):
    weights = P(("clip", "win"), None)
    vector = P(("clip", "win"))
    strips = P(None, "clip", "win", None, None, None, None, None)
    return jax.shard_map(
        body,
        mesh=mesh,
        in_specs=(
            strips, P(None, "clip", None), P(None, "clip"), weights, vector, weights, weights,
            weights, vector, weights, vector, weights, P(), strips,
        ),
        out_specs=(
            strips, strips, weights, vector, weights, weights, weights, vector, weights, vector,
            weights,
        ),
        check_vma=False,
    )
```

```python
import functools
import math

import jax
import jax.numpy as jnp
from jax import lax
from jax.experimental import pallas as pl
from jax.experimental.pallas import tpu as pltpu
from jax.sharding import PartitionSpec as P

HEADS = 16
EPSILON = 1e-06
MASKED = -1000000000.0
F32 = jnp.float32
BF16 = jnp.bfloat16
VMEM_LIMIT = 58 * 1024 * 1024
HIGHEST = lax.Precision.HIGHEST


def dot_nn(a, b):
    return lax.dot_general(a, b, (((1,), (0,)), ((), ())), preferred_element_type=F32)


def dot_nt(a, b):
    return lax.dot_general(a, b, (((1,), (1,)), ((), ())), preferred_element_type=F32)


def dot_tn(a, b):
    return lax.dot_general(a, b, (((0,), (0,)), ((), ())), preferred_element_type=F32)


def params(count):
    return pltpu.CompilerParams(
        dimension_semantics=("arbitrary",) * count, vmem_limit_bytes=VMEM_LIMIT
    )


def cost(flops, size):
    return pl.CostEstimate(flops=flops, bytes_accessed=size, transcendentals=0)


def once(shape, index_map):
    return pl.BlockSpec(shape, index_map, pipeline_mode=pl.Buffered(1))


def normalize(values):
    centered = values - jnp.mean(values, axis=-1, keepdims=True)
    inv = lax.rsqrt(jnp.mean(centered * centered, axis=-1, keepdims=True) + EPSILON)
    return centered * inv, inv


def norm_back(grad, normed, inv):
    return inv * (
        grad
        - jnp.mean(grad, axis=-1, keepdims=True)
        - normed * jnp.mean(grad * normed, axis=-1, keepdims=True)
    )


class Sizes:
    def __init__(self, tokens):
        self.micro, _, _, self.blocks, self.frames, rows, side, self.width = tokens.shape
        self.half = rows * side
        self.cols = self.blocks // 2
        self.strip_rows, self.side = rows, side
        self.used = 2 * self.frames - 1
        self.frame = 2 * self.half
        self.win_rows = self.used * self.frame
        self.rows = self.micro * self.win_rows
        self.lens = (self.frames * self.frame, (self.frames - 1) * self.frame)
        self.head = self.width // HEADS
        self.group = 4
        self.gcols = self.group * self.head
        self.groups = HEADS // self.group


def frame_rows(value):
    return value.reshape(-1, value.shape[-1])


def first_norm(tok, mod, core, sz):
    def kernel(sc_ref, x_ref, mod_ref, own_ref, far_ref):
        shift = mod_ref[0, 0:1, :]
        scale = 1.0 + mod_ref[0, 1:2, :]
        for slot, out_ref in enumerate((own_ref, far_ref)):
            column = sc_ref[0] ^ slot
            for tw in range(2):
                count = sz.frames - tw
                rows = frame_rows(x_ref[0, tw, column, :count].astype(F32))
                normed, _ = normalize(rows)
                hidden = (normed * scale + shift).astype(BF16)
                out_ref[0, tw * sz.frames : tw * sz.frames + count] = hidden.reshape(
                    count, sz.half, sz.width
                )

    strip = (1, 2, 2, sz.frames, sz.half, sz.width)
    piece = (1, sz.used, sz.half, sz.width)
    shape = jax.ShapeDtypeStruct((sz.micro,) + piece[1:], BF16)
    return pl.pallas_call(
        kernel,
        grid_spec=pltpu.PrefetchScalarGridSpec(
            num_scalar_prefetch=1,
            grid=(sz.micro,),
            in_specs=[
                pl.BlockSpec(strip, lambda m, s: (m, 0, 0, 0, 0, 0)),
                pl.BlockSpec((1, 6, sz.width), lambda m, s: (m, 0, 0)),
            ],
            out_specs=[pl.BlockSpec(piece, lambda m, s: (m, 0, 0, 0))] * 2,
        ),
        out_shape=[shape, shape],
        compiler_params=params(1),
        name="first_norm",
    )(core, tok, mod)


def valid_rows(tw, count, length, sz):
    frame = tw * sz.frames + lax.broadcasted_iota(jnp.int32, (count * sz.half, 1), 0) // sz.half
    return (frame < length).astype(F32)


def second_norm(tok, cot, branch_own, branch_far, mod, scalars, sz):
    def kernel(sc_ref, x_ref, c_ref, bo_ref, bf_ref, mod_ref, h_ref, g_ref):
        length = sc_ref[1 + pl.program_id(0)]
        gate1 = mod_ref[0, 2:3, :]
        shift = mod_ref[0, 3:4, :]
        scale = 1.0 + mod_ref[0, 4:5, :]
        gate2 = mod_ref[0, 5:6, :]
        for slot, b_ref in enumerate((bo_ref, bf_ref)):
            column = sc_ref[0] ^ slot
            for tw in range(2):
                count = sz.frames - tw
                span = slice(tw * sz.frames, tw * sz.frames + count)
                rows = frame_rows(x_ref[0, tw, column, :count].astype(F32))
                branch = frame_rows(b_ref[0, span].astype(F32))
                normed, _ = normalize(rows + gate1 * branch)
                h_ref[slot, 0, span] = (
                    (normed * scale + shift).astype(BF16).reshape(count, sz.half, sz.width)
                )
                grad = frame_rows(c_ref[0, tw, column, :count].astype(F32))
                grad = grad * valid_rows(tw, count, length, sz) * gate2
                g_ref[slot, 0, span] = grad.astype(BF16).reshape(count, sz.half, sz.width)

    strip = (1, 2, 2, sz.frames, sz.half, sz.width)
    piece = (1, sz.used, sz.half, sz.width)
    both = (2, 1, sz.used, sz.half, sz.width)
    shape = jax.ShapeDtypeStruct((2, sz.micro, sz.used, sz.half, sz.width), BF16)
    return pl.pallas_call(
        kernel,
        grid_spec=pltpu.PrefetchScalarGridSpec(
            num_scalar_prefetch=1,
            grid=(sz.micro,),
            in_specs=[
                pl.BlockSpec(strip, lambda m, s: (m, 0, 0, 0, 0, 0)),
                pl.BlockSpec(strip, lambda m, s: (m, 0, 0, 0, 0, 0)),
                pl.BlockSpec(piece, lambda m, s: (m, 0, 0, 0)),
                pl.BlockSpec(piece, lambda m, s: (m, 0, 0, 0)),
                pl.BlockSpec((1, 6, sz.width), lambda m, s: (m, 0, 0)),
            ],
            out_specs=[pl.BlockSpec(both, lambda m, s: (0, m, 0, 0, 0))] * 2,
        ),
        out_shape=[shape, shape],
        compiler_params=params(1),
        name="second_norm",
    )(scalars, tok, cot, branch_own, branch_far, mod)


def after_mlp(tok, cot, branch_own, branch_far, mlps, grads, mod, b_down, scalars, sz):
    def kernel(
        sc_ref, x_ref, c_ref, bo_ref, bf_ref, y0_ref, y1_ref, t0_ref, t1_ref, mod_ref, bd_ref,
        out_ref, gm_ref, go_ref, gf_ref, sum_ref,
    ):
        length = sc_ref[1 + pl.program_id(0)]
        gate1 = mod_ref[0, 2:3, :]
        scale = 1.0 + mod_ref[0, 4:5, :]
        gate2 = mod_ref[0, 5:6, :]
        sums = [jnp.zeros((1, sz.width), F32) for _ in range(4)]
        for slot, (b_ref, g_ref) in enumerate(((bo_ref, go_ref), (bf_ref, gf_ref))):
            column = sc_ref[0] ^ slot
            for tw in range(2):
                count = sz.frames - tw
                span = slice(tw * sz.frames, tw * sz.frames + count)
                shape = (count, sz.half, sz.width)
                valid = valid_rows(tw, count, length, sz)
                branch = frame_rows(b_ref[0, span].astype(F32))
                middle = frame_rows(x_ref[0, tw, column, :count].astype(F32)) + gate1 * branch
                normed, inv = normalize(middle)
                y = frame_rows(y0_ref[slot, 0, span] + y1_ref[slot, 0, span]) + bd_ref[0:1, :]
                grad = frame_rows(c_ref[0, tw, column, :count].astype(F32))
                out_ref[0, tw, column, :count] = (
                    (middle + valid * gate2 * y).astype(BF16).reshape(shape)
                )
                two = frame_rows(t0_ref[slot, 0, span] + t1_ref[slot, 0, span])
                gm = grad + norm_back(two * scale, normed, inv)
                gm_ref[slot, 0, span] = gm.reshape(shape)
                g_ref[0, span] = (valid * (gm * gate1)).astype(BF16).reshape(shape)
                for n, term in enumerate((two, two * normed, grad * valid * y, gm * branch)):
                    sums[n] = sums[n] + jnp.sum(term, axis=0, keepdims=True)
            out_ref[0, 1, column, sz.frames - 1] = x_ref[0, 1, column, sz.frames - 1]
        for n in range(4):
            sum_ref[0, n : n + 1, :] = sums[n]

    strip = (1, 2, 2, sz.frames, sz.half, sz.width)
    piece = (1, sz.used, sz.half, sz.width)
    both = (2, 1, sz.used, sz.half, sz.width)
    full = (sz.micro,) + piece[1:]
    at_strip = lambda m, s: (m, 0, 0, 0, 0, 0)
    at_piece = lambda m, s: (m, 0, 0, 0)
    at_both = lambda m, s: (0, m, 0, 0, 0)
    return pl.pallas_call(
        kernel,
        grid_spec=pltpu.PrefetchScalarGridSpec(
            num_scalar_prefetch=1,
            grid=(sz.micro,),
            in_specs=[
                pl.BlockSpec(strip, at_strip),
                pl.BlockSpec(strip, at_strip),
                pl.BlockSpec(piece, at_piece),
                pl.BlockSpec(piece, at_piece),
                pl.BlockSpec(both, at_both),
                pl.BlockSpec(both, at_both),
                pl.BlockSpec(both, at_both),
                pl.BlockSpec(both, at_both),
                pl.BlockSpec((1, 6, sz.width), lambda m, s: (m, 0, 0)),
                pl.BlockSpec((1, sz.width), lambda m, s: (0, 0)),
            ],
            out_specs=[
                pl.BlockSpec(strip, at_strip),
                pl.BlockSpec(both, at_both),
                pl.BlockSpec(piece, at_piece),
                pl.BlockSpec(piece, at_piece),
                pl.BlockSpec((1, 4, sz.width), lambda m, s: (m, 0, 0)),
            ],
        ),
        out_shape=[
            jax.ShapeDtypeStruct(tok.shape, BF16),
            jax.ShapeDtypeStruct((2,) + full, F32),
            jax.ShapeDtypeStruct(full, BF16),
            jax.ShapeDtypeStruct(full, BF16),
            jax.ShapeDtypeStruct((sz.micro, 4, sz.width), F32),
        ],
        compiler_params=params(1),
        name="after_mlp",
    )(scalars, tok, cot, branch_own, branch_far, *mlps, *grads, mod, b_down)


def last_norm(tok, cot, grad_mid, grad_own, grad_far, mod, scalars, sz):
    def kernel(sc_ref, x_ref, c_ref, gm_ref, go_ref, gf_ref, mod_ref, out_ref, sum_ref):
        scale = 1.0 + mod_ref[0, 1:2, :]
        sums = [jnp.zeros((1, sz.width), F32) for _ in range(2)]
        for slot, g_ref in enumerate((go_ref, gf_ref)):
            column = sc_ref[0] ^ slot
            for tw in range(2):
                count = sz.frames - tw
                span = slice(tw * sz.frames, tw * sz.frames + count)
                normed, inv = normalize(frame_rows(x_ref[0, tw, column, :count].astype(F32)))
                one = frame_rows(g_ref[0, span].astype(F32))
                grad = frame_rows(gm_ref[slot, 0, span]) + norm_back(one * scale, normed, inv)
                out_ref[0, tw, column, :count] = grad.astype(BF16).reshape(
                    count, sz.half, sz.width
                )
                for n, term in enumerate((one, one * normed)):
                    sums[n] = sums[n] + jnp.sum(term, axis=0, keepdims=True)
        for slot in range(2):
            out_ref[0, 1, slot, sz.frames - 1] = c_ref[0, 0, slot, 0]
        for n in range(2):
            sum_ref[0, n : n + 1, :] = sums[n]

    strip = (1, 2, 2, sz.frames, sz.half, sz.width)
    tail = (1, 1, 2, 1, sz.half, sz.width)
    piece = (1, sz.used, sz.half, sz.width)
    both = (2, 1, sz.used, sz.half, sz.width)
    return pl.pallas_call(
        kernel,
        grid_spec=pltpu.PrefetchScalarGridSpec(
            num_scalar_prefetch=1,
            grid=(sz.micro,),
            in_specs=[
                pl.BlockSpec(strip, lambda m, s: (m, 0, 0, 0, 0, 0)),
                pl.BlockSpec(tail, lambda m, s: (m, 1, 0, sz.frames - 1, 0, 0)),
                pl.BlockSpec(both, lambda m, s: (0, m, 0, 0, 0)),
                pl.BlockSpec(piece, lambda m, s: (m, 0, 0, 0)),
                pl.BlockSpec(piece, lambda m, s: (m, 0, 0, 0)),
                pl.BlockSpec((1, 6, sz.width), lambda m, s: (m, 0, 0)),
            ],
            out_specs=[
                pl.BlockSpec(strip, lambda m, s: (m, 0, 0, 0, 0, 0)),
                pl.BlockSpec((1, 2, sz.width), lambda m, s: (m, 0, 0)),
            ],
        ),
        out_shape=[
            jax.ShapeDtypeStruct(tok.shape, BF16),
            jax.ShapeDtypeStruct((sz.micro, 2, sz.width), F32),
        ],
        compiler_params=params(1),
        name="last_norm",
    )(scalars, tok, cot, grad_mid, grad_own, grad_far, mod)


class Pieces:
    def __init__(self, arrays):
        self.arrays = arrays
        self.whole = len(arrays) == 1

    def specs(self, columns, index_map):
        if self.whole:
            at = lambda *g: (0, index_map(*g))
            return [pl.BlockSpec((self.arrays[0].shape[0], columns), at)]
        at = lambda *g: (0, 0, 0, 0, index_map(*g))
        shape = self.arrays[0].shape[:-1] + (columns,)
        return [pl.BlockSpec(shape, at)] * 4


def pieces_of(refs, key, z_here):
    depth = refs[0].shape[2]
    for z in range(depth):
        for n in range(4):
            half, far = n // 2, n % 2
            for i in range(2):
                for j in range(2):
                    away = (i * 4 + j * 2 if half == 0 else j * 4 + i * 2) + far
                    yield (z_here + z) % depth, key ^ away, half, refs[n].at[i, j, z]


def place(refs, key, z_here, out_ref, columns=slice(None), source=slice(None)):
    if len(refs) == 1:
        out_ref[:, columns] = refs[0][:, source]
        return
    for z, at, half, piece in pieces_of(refs, key, z_here):
        cut = piece.shape[0]
        row = pl.multiple_of((z * 8 + at) * (2 * cut) + half * cut, cut)
        out_ref[pl.ds(row, cut), columns] = piece[:, source]


def place_inner(refs, key, z_here, out_ref, source):
    size = source.stop - source.start
    if len(refs) == 1:
        cut = out_ref.shape[0] // 32
        for n in range(64):
            at, half = n // 2, n % 2
            to = (at % 2) * (16 * cut) + at // 2 * cut
            out_ref[to : to + cut, half * size : (half + 1) * size] = refs[0][
                n * cut : (n + 1) * cut, source
            ]
        return
    for z, at, half, piece in pieces_of(refs, key, z_here):
        cut = piece.shape[0]
        row = pl.multiple_of((at % 2) * (16 * cut) + (z * 4 + at // 2) * cut, cut)
        out_ref[pl.ds(row, cut), half * size : (half + 1) * size] = piece[:, source]


def turn(value, out_ref, core, shard, start=0):
    turned = value.T
    if shard is None:
        out_ref[start : start + turned.shape[0]] = turned
        return
    height = out_ref.shape[0]
    for n in range(turned.shape[0] // shard):
        at = start // shard + n
        at = (core ^ (at % 2)) * (height // 2) + at // 2 * shard
        out_ref[pl.ds(pl.multiple_of(at, shard), shard), :] = turned[n * shard : (n + 1) * shard]


def give(refs, half, low, value, start=0):
    value = value.astype(BF16)
    columns = slice(start, start + value.shape[1])
    if len(refs) == 1:
        low = half * (refs[0].shape[0] // 2) + low
        refs[0][low : low + value.shape[0], columns] = value
        return
    rows = refs[half].shape[1]
    refs[half][low // rows : (low + value.shape[0]) // rows, :, columns] = value.reshape(
        value.shape[0] // rows, rows, value.shape[1]
    )


def grad_shapes(direct, rows, height, columns):
    if not direct:
        return [jax.ShapeDtypeStruct((height, columns), BF16)]
    return [jax.ShapeDtypeStruct((height // (2 * rows), rows, columns), BF16)] * 2


def grad_specs(direct, rows, height, columns, at_column):
    if not direct:
        return [pl.BlockSpec((height, columns), lambda *g: (0, at_column(*g)))]
    shape = (height // (2 * rows), rows, columns)
    return [pl.BlockSpec(shape, lambda *g: (0, 0, at_column(*g)))] * 2


def join_frames(own_ref, far_ref, joined_ref, sz):
    for m in range(sz.micro):
        for f in range(sz.used):
            at = m * sz.win_rows + f * sz.frame
            joined_ref[at : at + sz.half] = own_ref[m, f]
            joined_ref[at + sz.half : at + sz.frame] = far_ref[m, f]


def spread_bias(block_ref, head, bias_ref, sz):
    full = sz.lens[0]
    for t in range(sz.frames):
        low = (sz.frames - 1 - t) * sz.frame
        bias_ref[t * sz.frame : (t + 1) * sz.frame, :] = block_ref[head, :, low : low + full]


def window_rows(m, tw, sz):
    start = pl.multiple_of(m * sz.win_rows + tw * sz.lens[0], sz.frame)
    return pl.ds(start, sz.lens[tw])


def attention(half, own, far, w_qkv, bias, scalars, sz, att_first=None, w_out=None):
    scale = 1.0 / math.sqrt(sz.head)
    last = w_out is not None
    steps = sz.groups // 2
    gcols = sz.gcols
    joint = w_out is w_qkv
    n_out = 2 * len(w_qkv.arrays) if joint else 1

    def kernel(sc_ref, own_ref, far_ref, bias_ref, *refs):
        refs = list(refs)
        take = lambda count: [refs.pop(0) for _ in range(count)]
        w_refs = take(len(w_qkv.arrays))
        if last:
            (first_ref,) = take(1)
            out_refs = take(n_out)
        qkv_ref, att_ref, w_ref = take(3)
        if last:
            wo_ref, bo_ref, bf_ref = take(3)
        joined, spread = take(2)
        step = pl.program_id(0)
        key, z_here = sc_ref[1 + sz.micro], sc_ref[2 + sz.micro]

        @pl.when(step == 0)
        def _():
            join_frames(own_ref, far_ref, joined, sz)

        place(w_refs, key, z_here, w_ref)
        for n in range(3):
            part = dot_nn(joined[...], w_ref[:, n * gcols : (n + 1) * gcols]).astype(BF16)
            qkv_ref[n] = part * scale if n == 0 else part
        for head in range(sz.group):
            spread_bias(bias_ref, head, spread.at[head], sz)

        def one_micro(m, carry):
            for tw in range(2):
                size = sz.lens[tw]
                rows = window_rows(m, tw, sz)
                keys_ok = (sc_ref[1 + m] - tw * sz.frames) * sz.frame

                @pl.when(keys_ok > 0)
                def _(rows=rows, size=size, keys_ok=keys_ok):
                    column = lax.broadcasted_iota(jnp.int32, (1, size), 1)
                    for head in range(sz.group):
                        lanes = slice(head * sz.head, (head + 1) * sz.head)
                        scores = dot_nt(qkv_ref[0, rows, lanes], qkv_ref[1, rows, lanes])
                        scores = scores + spread[head, :size, :size].astype(F32)
                        scores = jnp.where(column < keys_ok, scores, MASKED)
                        top = jnp.max(scores, axis=-1, keepdims=True)
                        weight = jnp.exp(scores - top)
                        share = 1.0 / jnp.sum(weight, axis=-1, keepdims=True)
                        probs = (weight * share).astype(BF16)
                        att_ref[rows, lanes] = dot_nn(probs, qkv_ref[2, rows, lanes]).astype(BF16)

                @pl.when(keys_ok <= 0)
                def _(rows=rows, size=size):
                    att_ref[rows, :] = jnp.zeros((size, gcols), BF16)

            return carry

        lax.fori_loop(0, sz.micro, one_micro, 0)
        if not last:
            return
        kept, total = take(2)
        for n in range(steps):

            @pl.when(step == n)
            def _(n=n):
                kept[:, n * gcols : (n + 1) * gcols] = att_ref[...]

        @pl.when(step == steps - 1)
        def _():
            if joint:
                place(out_refs[: n_out // 2], key, z_here, wo_ref, slice(0, 2 * gcols))
                place(out_refs[n_out // 2 :], key, z_here, wo_ref, slice(2 * gcols, 4 * gcols))
            else:
                place(out_refs, key, z_here, wo_ref)
            middle = first_ref.shape[1]
            total[...] = dot_nn(first_ref[...], wo_ref[:middle]) + dot_nn(
                kept[...], wo_ref[middle:]
            )
            for m in range(sz.micro):
                for f in range(sz.used):
                    at = m * sz.win_rows + f * sz.frame
                    valid = (f < sc_ref[1 + m]).astype(F32)
                    bo_ref[m, f] = (total[at : at + sz.half] * valid).astype(BF16)
                    bf_ref[m, f] = (total[at + sz.half : at + sz.frame] * valid).astype(BF16)

    piece = (sz.micro, sz.used, sz.half, sz.width)
    fixed = lambda g, s: (0, 0, 0, 0)
    flat = lambda g, s: (0, 0)
    width, cols = sz.width, sz.width // 2
    in_specs = [
        once(piece, fixed),
        once(piece, fixed),
        pl.BlockSpec((sz.group,) + bias.shape[1:], lambda g, s: (half * steps + g, 0, 0)),
    ] + w_qkv.specs(3 * gcols, lambda g, s: g)
    out_specs = [
        pl.BlockSpec((3, sz.rows, gcols), lambda g, s: (0, 0, g)),
        pl.BlockSpec((sz.rows, gcols), lambda g, s: (0, g)),
        pl.BlockSpec((width, 3 * gcols), lambda g, s: (0, g)),
    ]
    out_shape = [
        jax.ShapeDtypeStruct((3, sz.rows, cols), BF16),
        jax.ShapeDtypeStruct((sz.rows, cols), BF16),
        jax.ShapeDtypeStruct((width, 3 * cols), BF16),
    ]
    scratch = [
        pltpu.VMEM((sz.rows, width), BF16),
        pltpu.VMEM((sz.group, sz.lens[0], sz.lens[0]), BF16),
    ]
    args = [scalars, own, far, bias, *w_qkv.arrays]
    flops = 6 * sz.rows * width * cols + 4 * sz.rows * sz.lens[0] * cols
    if last:
        in_specs += [once((sz.rows, cols), flat)]
        if joint:
            low = w_out.arrays[0].shape[-1] // (2 * gcols) - 2
            in_specs += w_out.specs(2 * gcols, lambda g, s: low)
            in_specs += w_out.specs(2 * gcols, lambda g, s: low + 1)
            out_args = w_out.arrays * 2
        else:
            in_specs += w_out.specs(width, lambda g, s: 0)
            out_args = w_out.arrays
        out_specs += [pl.BlockSpec((width, width), flat)] + [pl.BlockSpec(piece, fixed)] * 2
        out_shape += [jax.ShapeDtypeStruct((width, width), BF16)]
        out_shape += [jax.ShapeDtypeStruct(piece, BF16)] * 2
        scratch += [pltpu.VMEM((sz.rows, cols), BF16), pltpu.VMEM((sz.rows, width), F32)]
        args += [att_first, *out_args]
        flops += 2 * sz.rows * width * width
    return pl.pallas_call(
        kernel,
        grid_spec=pltpu.PrefetchScalarGridSpec(
            num_scalar_prefetch=1,
            grid=(steps,),
            in_specs=in_specs,
            out_specs=out_specs,
            scratch_shapes=scratch,
        ),
        out_shape=out_shape,
        compiler_params=params(1),
        cost_estimate=cost(3 * flops, 16 * sz.rows * width),
        name="attention" + "_last" * last,
    )(*args)


def attention_back(half, grad_own, grad_far, own, far, qkv, atts, w_qkv, w_out, bias_t, scalars, sz, shard, carry=None):
    scale = 1.0 / math.sqrt(sz.head)
    last = carry is not None
    steps = sz.groups // 2
    direct = shard is not None
    outs = 2 if direct else 1
    gcols, width = sz.gcols, sz.width
    quarter = width // 4

    def kernel(
        sc_ref, go_ref, gf_ref, own_ref, far_ref, qkv_ref, w_ref, wo_ref, bias_ref, *refs
    ):
        refs = list(refs)
        take = lambda count: [refs.pop(0) for _ in range(count)]
        if last:
            (carry_ref,) = take(1)
        else:
            att_refs = take(2)
        gw_refs = take(outs)
        (fold_ref,) = take(1)
        if last:
            ho_ref, hf_ref = take(2)
        else:
            gwo_refs = gw_refs if direct else take(1)
            (total,) = take(1)
        grad, hidden_t, grad_att, parts, spread, pair_sum = take(6)
        if last:
            (total,) = take(1)
        else:
            (turned,) = take(1)
        step = pl.program_id(0)

        @pl.when(step == 0)
        def _():
            join_frames(own_ref, far_ref, grad, sz)
            turn(grad[...], hidden_t, sc_ref[0], shard)
            join_frames(go_ref, gf_ref, grad, sz)
            if last:
                total[...] = carry_ref[...]
            else:
                total[...] = jnp.zeros_like(total)
                for n, a_ref in enumerate(att_refs):
                    turn(a_ref[...], turned, sc_ref[0], shard, n * a_ref.shape[1])

        grad_att[...] = dot_nt(grad[...], wo_ref[...]).astype(BF16)
        full = sz.lens[0]
        for head in range(sz.group):
            spread_bias(bias_ref, head, spread.at[head], sz)
            pair_sum[head] = jnp.zeros((full, full), F32)

        def one_micro(m, carry):
            for tw in range(2):
                size = sz.lens[tw]
                rows = window_rows(m, tw, sz)
                keys_ok = (sc_ref[1 + m] - tw * sz.frames) * sz.frame

                @pl.when(keys_ok > 0)
                def _(rows=rows, size=size, keys_ok=keys_ok):
                    row = lax.broadcasted_iota(jnp.int32, (size, 1), 0)
                    for head in range(sz.group):
                        lanes = slice(head * sz.head, (head + 1) * sz.head)
                        spot = [slice(n * gcols + lanes.start, n * gcols + lanes.stop) for n in range(3)]
                        query = qkv_ref[0, rows, lanes]
                        key = qkv_ref[1, rows, lanes]
                        value = qkv_ref[2, rows, lanes]
                        grad_out = grad_att[rows, lanes]
                        scores = dot_nt(key, query) + spread[head, :size, :size].astype(F32)
                        scores = jnp.where(row < keys_ok, scores, MASKED)
                        weight = jnp.exp(scores - jnp.max(scores, axis=0, keepdims=True))
                        probs = weight * (1.0 / jnp.sum(weight, axis=0, keepdims=True))
                        grad_probs = dot_nt(value, grad_out)
                        inner = jnp.sum(probs * grad_probs, axis=0, keepdims=True)
                        grad_scores = (probs * (grad_probs - inner)).astype(BF16)
                        pair_sum[head, :size, :size] += grad_scores.astype(F32)
                        parts[rows, spot[2]] = dot_nn(probs.astype(BF16), grad_out).astype(BF16)
                        parts[rows, spot[1]] = dot_nn(grad_scores, query).astype(BF16)
                        parts[rows, spot[0]] = (dot_tn(grad_scores, key) * scale).astype(BF16)

                @pl.when(keys_ok <= 0)
                def _(rows=rows, size=size):
                    parts[rows, :] = jnp.zeros((size, 3 * gcols), BF16)

            return carry

        lax.fori_loop(0, sz.micro, one_micro, 0)
        for head in range(sz.group):
            fold_ref[head] = jnp.zeros(fold_ref.shape[1:], F32)
            for t in range(sz.frames):
                low = (sz.frames - 1 - t) * sz.frame
                fold_ref[head, :, low : low + full] += pair_sum[
                    head, t * sz.frame : (t + 1) * sz.frame, :
                ]
        for n in range(4):
            rows = slice(n * quarter, (n + 1) * quarter)
            give(gw_refs, n // 2, n % 2 * quarter, dot_nn(hidden_t[rows, :], parts[...]))
        total[...] += dot_nt(parts[...], w_ref[...])
        if not last:
            columns = pl.ds(pl.multiple_of(step * 2 * gcols, 2 * gcols), 2 * gcols)
            for n in range(4):
                rows = slice(n * quarter, (n + 1) * quarter)
                value = dot_nn(turned[rows, :], grad[:, columns])
                give(gwo_refs, n // 2, n % 2 * quarter, value, 3 * gcols if direct else 0)
            return

        @pl.when(step == steps - 1)
        def _():
            for m in range(sz.micro):
                for f in range(sz.used):
                    at = m * sz.win_rows + f * sz.frame
                    ho_ref[m, f] = total[at : at + sz.half].astype(BF16)
                    hf_ref[m, f] = total[at + sz.half : at + sz.frame].astype(BF16)

    piece = (sz.micro, sz.used, sz.half, width)
    fixed = lambda g, s: (0, 0, 0, 0)
    flat = lambda g, s: (0, 0)
    cols = width // 2
    block_bias = (sz.group,) + bias_t.shape[1:]
    in_specs = [
        once(piece, fixed),
        once(piece, fixed),
        once(piece, fixed),
        once(piece, fixed),
        pl.BlockSpec((3, sz.rows, gcols), lambda g, s: (0, 0, g)),
        pl.BlockSpec((width, 3 * gcols), lambda g, s: (0, g)),
        pl.BlockSpec((gcols, width), lambda g, s: (half * steps + g, 0)),
        pl.BlockSpec(block_bias, lambda g, s: (half * steps + g, 0, 0)),
    ]
    along = lambda g, s: g
    wide = 3 * gcols if last or not direct else 5 * gcols
    out_specs = grad_specs(direct, shard, width, wide, along)
    out_specs += [pl.BlockSpec(block_bias, lambda g, s: (g, 0, 0))]
    out_shape = grad_shapes(direct, shard, width, steps * wide)
    out_shape += [jax.ShapeDtypeStruct((HEADS // 2,) + bias_t.shape[1:], F32)]
    scratch = [
        pltpu.VMEM((sz.rows, width), BF16),
        pltpu.VMEM((width, sz.rows), BF16),
        pltpu.VMEM((sz.rows, gcols), BF16),
        pltpu.VMEM((sz.rows, 3 * gcols), BF16),
        pltpu.VMEM((sz.group, sz.lens[0], sz.lens[0]), BF16),
        pltpu.VMEM((sz.group, sz.lens[0], sz.lens[0]), F32),
    ]
    args = [scalars, grad_own, grad_far, own, far, qkv, w_qkv, w_out, bias_t]
    flops = 14 * sz.rows * width * cols + 10 * sz.rows * sz.lens[0] * cols
    if last:
        in_specs += [once((sz.rows, width), flat)]
        out_specs += [pl.BlockSpec(piece, fixed)] * 2
        out_shape += [jax.ShapeDtypeStruct(piece, BF16)] * 2
        scratch += [pltpu.VMEM((sz.rows, width), F32)]
        args += [carry]
    else:
        in_specs += [once((sz.rows, cols), flat)] * 2
        if not direct:
            out_specs += grad_specs(direct, shard, width, 2 * gcols, along)
            out_shape += grad_shapes(direct, shard, width, width)
        out_specs += [once((sz.rows, width), flat)]
        out_shape += [jax.ShapeDtypeStruct((sz.rows, width), F32)]
        scratch += [pltpu.VMEM((width, sz.rows), BF16)]
        args += list(atts)
        flops += 2 * sz.rows * width * width
    return pl.pallas_call(
        kernel,
        grid_spec=pltpu.PrefetchScalarGridSpec(
            num_scalar_prefetch=1,
            grid=(steps,),
            in_specs=in_specs,
            out_specs=out_specs,
            scratch_shapes=scratch,
        ),
        out_shape=out_shape,
        compiler_params=params(1),
        cost_estimate=cost(3 * flops, 24 * sz.rows * width),
        name="attention_back" + "_last" * last,
    )(*args)


GELU_A = math.sqrt(2.0 / math.pi)
GELU_B = 0.044715
MLP_TILES = 3
CHUNK = 512


def mlp(hidden, grad, weights, b_up, scalars, sz, shard, inner_first):
    chunk = CHUNK
    tiles = MLP_TILES
    tile = sz.rows // tiles
    inner = b_up.shape[1]
    steps = inner // chunk
    packed = len(weights) == 1
    direct = shard is not None
    rows, width = sz.rows, sz.width
    quarter = width // 4
    n_up = len(weights[0].arrays)
    copied = n_up == 4

    def kernel(sc_ref, h_ref, g_ref, bu_ref, *refs):
        refs = list(refs)
        take = lambda count: [refs.pop(0) for _ in range(count)]
        up_refs = take(n_up)
        down_refs = up_refs if packed else take(1)
        y_ref, t_ref, gbu_ref = take(3)
        if inner_first:
            (gbd_ref,) = take(1)
        gw_refs = take(2 if direct else 1)
        gwd_refs = gw_refs if packed else take(1)
        hidden_t, act_s, gpre_s = take(3)
        step = pl.program_id(0)
        key, z_here = sc_ref[1 + sz.micro], sc_ref[2 + sz.micro]

        @pl.when(step == 0)
        def _():
            turn(h_ref[...], hidden_t, sc_ref[0], shard)
            if inner_first:
                gbd_ref[...] = jnp.sum(g_ref[...].astype(F32), axis=0, keepdims=True)
            y_ref[...] = jnp.zeros_like(y_ref)
            t_ref[...] = jnp.zeros_like(t_ref)

        if packed:
            (wd_ref,) = take(1)
            place_inner(down_refs, key, z_here, wd_ref, slice(chunk, chunk + width // 2))
        else:
            wd_ref = down_refs[0]
        if copied:
            (wu_ref,) = take(1)
            place(up_refs, key, z_here, wu_ref, source=slice(0, chunk))
        else:
            wu_ref = up_refs[0]
        bias_sum = jnp.zeros((1, chunk), F32)
        for n in range(tiles):
            span = slice(n * tile, (n + 1) * tile)
            pre = dot_nn(h_ref[span], wu_ref[:, :chunk]) + bu_ref[...]
            grad_act = dot_nt(g_ref[span], wd_ref[...])
            square = pre * pre
            tanh = jnp.tanh(GELU_A * pre * (1.0 + GELU_B * square))
            half = 0.5 * (1.0 + tanh)
            act = (pre * half).astype(BF16)
            slope = half + (0.5 * GELU_A) * pre * (1.0 - tanh * tanh) * (
                1.0 + (3.0 * GELU_B) * square
            )
            grad_pre = (grad_act * slope).astype(BF16)
            act_s[0, span] = act[:, : chunk // 2]
            act_s[1, span] = act[:, chunk // 2 :]
            gpre_s[span] = grad_pre
            bias_sum = bias_sum + jnp.sum(grad_pre.astype(F32), axis=0, keepdims=True)
            y_ref[span] += dot_nn(act, wd_ref[...])
            t_ref[span] += dot_nt(grad_pre, wu_ref[:, :chunk])
        gbu_ref[...] = bias_sum
        for n in range(4):
            span = slice(n * quarter, (n + 1) * quarter)
            give(gw_refs, n // 2, n % 2 * quarter, dot_nn(hidden_t[span, :], gpre_s[...]))
        for n in range(2):
            source = sc_ref[0] ^ n if direct else n
            value = dot_tn(act_s[source], g_ref[...])
            if not packed:
                give(gwd_refs, n, 0, value)
                continue
            value = value.astype(BF16)
            cut = chunk // 32
            for half in range(2):
                part = value[:, half * width // 2 : (half + 1) * width // 2]
                if direct:
                    gw_refs[n][:, half * cut : (half + 1) * cut, chunk:] = part.reshape(
                        16, cut, width // 2
                    )
                    continue
                for k in range(16):
                    to = (2 * k + n) * 2 * cut + half * cut
                    gw_refs[0][to : to + cut, chunk:] = part[k * cut : (k + 1) * cut]

    fixed = lambda j, s: (0, 0)
    along = lambda j, s: j
    in_specs = [
        once((rows, width), fixed),
        once((rows, width), fixed),
        pl.BlockSpec((1, chunk), lambda j, s: (0, j)),
    ]
    args = [scalars, hidden, grad, b_up]
    out_specs = [
        pl.BlockSpec((rows, width), fixed),
        pl.BlockSpec((rows, width), fixed),
        pl.BlockSpec((1, chunk), lambda j, s: (0, j)),
    ]
    out_shape = [
        jax.ShapeDtypeStruct((rows, width), F32),
        jax.ShapeDtypeStruct((rows, width), F32),
        jax.ShapeDtypeStruct((1, inner), F32),
    ]
    if inner_first:
        out_specs += [pl.BlockSpec((1, width), fixed)]
        out_shape += [jax.ShapeDtypeStruct((1, width), F32)]
    if packed:
        wide = chunk + width // 2
        in_specs += weights[0].specs(wide, along)
        args += weights[0].arrays
        out_specs += grad_specs(direct, shard, width, wide, along)
        out_shape += grad_shapes(direct, shard, width, steps * wide)
    else:
        in_specs += weights[0].specs(chunk, along)
        in_specs += [pl.BlockSpec((chunk, width), lambda j, s: (j, 0))]
        args += [weights[0].arrays[0], weights[1].arrays[0]]
        out_specs += grad_specs(False, None, width, chunk, along)
        out_specs += [pl.BlockSpec((chunk, width), lambda j, s: (j, 0))]
        out_shape += grad_shapes(False, None, width, inner)
        out_shape += grad_shapes(False, None, inner, width)
    scratch = [
        pltpu.VMEM((width, rows), BF16),
        pltpu.VMEM((2, rows, chunk // 2), BF16),
        pltpu.VMEM((rows, chunk), BF16),
    ]
    if packed:
        scratch += [pltpu.VMEM((chunk, width), BF16)]
    if copied:
        scratch += [pltpu.VMEM((width, chunk), BF16)]
    return pl.pallas_call(
        kernel,
        grid_spec=pltpu.PrefetchScalarGridSpec(
            num_scalar_prefetch=1,
            grid=(steps,),
            in_specs=in_specs,
            out_specs=out_specs,
            scratch_shapes=scratch,
        ),
        out_shape=out_shape,
        compiler_params=params(1),
        cost_estimate=cost(14 * rows * width * inner, 16 * rows * width),
        name="mlp",
    )(*args)


def offset_onehot(core, sz):
    span = 2 * sz.side - 1
    place = jnp.arange(sz.frame, dtype=jnp.int32)
    row = ((place // sz.half) ^ core) * sz.strip_rows + place // sz.side % sz.strip_rows
    column = place % sz.side
    index = (row[:, None] - row[None, :] + sz.side - 1) * span
    index = index + column[:, None] - column[None, :] + sz.side - 1
    return (jnp.arange(span * span, dtype=jnp.int32)[:, None, None] == index[None]).astype(BF16)


def bucket_onehot(bucket, count):
    return (jnp.arange(count, dtype=jnp.int32)[:, None] == bucket[None, :]).astype(BF16)


def bias_blocks(table, bucket, places, sz):
    steps = 2 * sz.frames - 1
    by_offset = dot_tn(table, bucket_onehot(bucket, table.shape[0])).astype(BF16)
    by_offset = by_offset.reshape(HEADS, steps, -1)
    shape = (HEADS, sz.frame, steps * sz.frame)
    forward = jnp.einsum("hkj,jpq->hpkq", by_offset[:, ::-1], places, preferred_element_type=F32)
    backward = jnp.einsum("hkj,jpq->hqkp", by_offset, places, preferred_element_type=F32)
    return forward.astype(BF16).reshape(shape), backward.astype(BF16).reshape(shape)


def split_low(value):
    high = value.astype(BF16)
    return high, (value - high.astype(F32)).astype(BF16)


def offset_grad(fold, places, sz):
    steps = 2 * sz.frames - 1
    fold = fold.reshape(-1, sz.frame, steps, sz.frame)
    return sum(
        jnp.einsum("hqkp,jpq->hkj", part, places, preferred_element_type=F32)
        for part in split_low(fold)
    ).reshape(fold.shape[0], -1)


def table_grad(by_offset, bucket, buckets):
    onehot = bucket_onehot(bucket, buckets)
    return sum(dot_nt(onehot, part) for part in split_low(by_offset))


class Net:
    AXES = ("clip", "win")
    X, Y, CORE = 2, 4, 1

    def __init__(self):
        self.count = lax.axis_size(self.AXES)
        self.direct = lax.axis_size("win") == 4 and self.count == 32
        self.deep = self.count // 8
        self.index = lax.axis_index(self.AXES)
        self.z = self.index // 8

    def bit(self, which):
        return self.index // which % 2

    def swap(self, value, which):
        return lax.ppermute(value, self.AXES, [(n, n ^ which) for n in range(self.count)])

    def from_z(self, value, step):
        move = lambda n: (n // 8 - step) % self.deep * 8 + n % 8
        return lax.ppermute(value, self.AXES, [(n, move(n)) for n in range(self.count)])

    def swap_sum(self, value, which):
        return value + self.swap(value, which)


    def gather_clips(self, value):
        along = jnp.stack([value] + [self.from_z(value, k) for k in range(1, self.deep)])
        return jnp.stack([along, self.swap(along, self.Y)], axis=1)

    def scatter_clips(self, value, notes):
        got = self.swap(value[:, 1], self.Y)
        notes.append(got)
        kept = value[:, 0] + got
        got = [self.from_z(kept[self.deep - k], k) for k in range(1, self.deep)]
        notes.append(got[-1])
        return kept[0] + sum(got)

    def gather_pairs(self, value):
        parts = value
        for which in (self.X, self.CORE):
            parts = jnp.stack([parts, self.swap(parts, which)], axis=2 if which == self.X else 3)
        parts = parts.reshape(self.count, -1)
        place = jnp.arange(self.count, dtype=jnp.int32)
        holder = (self.z + place // 8) % self.deep * 8 + (place % 8 ^ self.index % 8)
        pick = (place[:, None] == holder[None, :]).astype(BF16)
        return dot_nn(pick, parts).astype(BF16)


def cut_rows(parts):
    rows, columns = parts[0].shape
    half = rows // 2

    def kernel(*refs):
        ins, outs = refs[:-2], refs[-2:]
        for n, ref in enumerate(ins):
            for k, out in enumerate(outs):
                out[n] = ref[k * half : (k + 1) * half]

    return pl.pallas_call(
        kernel,
        out_shape=[jax.ShapeDtypeStruct((len(parts), half, columns), BF16)] * 2,
        compiler_params=pltpu.CompilerParams(vmem_limit_bytes=VMEM_LIMIT),
        cost_estimate=cost(0, 4 * len(parts) * rows * columns),
        name="cut_rows",
    )(*parts)


class Gather:
    def __init__(self, net, shard):
        self.net = net
        self.got = [net.from_z(shard, k) for k in range(1, net.deep)]
        self.shard = shard
        self.halves = None

    def along_z(self):
        self.halves = cut_rows([self.shard] + list(self.got))

    def start(self, first):
        net = self.net
        order = (net.X, net.Y) if first else (net.Y, net.X)
        self.got = [net.swap(v, which) for v, which in zip(self.halves, order)]

    def join(self):
        self.halves = [jnp.stack(pair) for pair in zip(self.halves, self.got)]

    def tie(self, *others):
        self.got = list(lax.optimization_barrier((*self.got, *others))[: len(self.got)])

    def core(self):
        net = self.net
        self.got = [net.swap(v, net.CORE) for v in self.halves]

    def pieces(self):
        return Pieces([self.halves[0], self.got[0], self.halves[1], self.got[1]])


def add_bf16(one, two):
    return (one.astype(F32) + two.astype(F32)).astype(BF16)


class Scatter:
    def __init__(self, net, pair):
        self.net = net
        keep, send = [v.reshape((net.deep, 4) + v.shape[1:]) for v in pair]
        self.keep = [keep]
        self.got = [net.swap(send, net.CORE)]
        self.bits = jnp.stack([net.bit(net.Y), net.bit(net.X), net.z])
        self.rows, self.columns = keep.shape[2:]

    def tie(self, *others):
        self.got = list(lax.optimization_barrier((*self.got, *others))[: len(self.got)])

    def tie_keep(self, *others):
        self.keep = list(lax.optimization_barrier((*self.keep, *others))[: len(self.keep)])

    def second(self):
        net, cut = self.net, self.rows // 2

        def kernel(sc_ref, keep, got, *outs):
            for half in range(2):
                span = slice(half * cut, (half + 1) * cut)
                for role in range(2):
                    for other in range(2):
                        near = sc_ref[half] ^ role
                        at = near * 2 + other if half == 0 else other * 2 + near
                        outs[2 * half + role][0, other] = add_bf16(keep[0, at, span], got[0, at, span])

        block = (1,) + self.keep[0].shape[1:]
        out = (2, cut, self.columns)
        made = pl.pallas_call(
            kernel,
            grid_spec=pltpu.PrefetchScalarGridSpec(
                num_scalar_prefetch=1,
                grid=(net.deep,),
                in_specs=[pl.BlockSpec(block, lambda z, s: (z, 0, 0, 0))] * 2,
                out_specs=[pl.BlockSpec((1,) + out, lambda z, s: (z, 0, 0, 0))] * 4,
            ),
            out_shape=[jax.ShapeDtypeStruct((net.deep,) + out, BF16)] * 4,
            compiler_params=params(1),
            cost_estimate=cost(0, 6 * self.keep[0].size),
            name="add_cores",
        )(self.bits, *self.keep, *self.got)
        self.keep = [made[0], made[2]]
        self.got = [net.swap(made[1], net.Y), net.swap(made[3], net.X)]

    def third(self):
        net, cut = self.net, self.rows // 2

        def kernel(sc_ref, k0, k1, g0, g1, *outs):
            for half, (keep, got) in enumerate(((k0, g0), (k1, g1))):
                for role in range(2):
                    at = sc_ref[1 - half] ^ role
                    outs[2 * half + role][...] = add_bf16(keep[:, at], got[:, at])

        out = jax.ShapeDtypeStruct((net.deep, cut, self.columns), BF16)
        made = self.call(kernel, [*self.keep, *self.got], [out] * 4, "add_second")
        self.keep = [made[0], made[2]]
        self.got = [net.swap(made[1], net.X), net.swap(made[3], net.Y)]

    def fourth(self, *joined):
        net, rows, cut = self.net, self.rows, self.rows // 2
        group = (self,) + joined
        widths = [v.columns for v in group]

        def kernel(sc_ref, *refs):
            ins, outs = refs[: 4 * len(group)], refs[4 * len(group) :]
            for away, out in enumerate(outs):
                at = (sc_ref[2] + net.deep - away) % net.deep
                low = 0
                for n, size in enumerate(widths):
                    k0, k1, g0, g1 = ins[4 * n : 4 * n + 4]
                    out[:cut, low : low + size] = add_bf16(k0[at], g0[at])
                    out[cut:, low : low + size] = add_bf16(k1[at], g1[at])
                    low += size

        out = jax.ShapeDtypeStruct((rows, sum(widths)), BF16)
        args = [v for one in group for v in (*one.keep, *one.got)]
        made = self.call(kernel, args, [out] * net.deep, "add_third")
        self.keep = [made[0]]
        self.got = [net.from_z(made[k], k) for k in range(1, net.deep)]

    def total(self):
        return self.keep[0].astype(F32) + sum(v.astype(F32) for v in self.got)

    def call(self, kernel, args, outs, name):
        return pl.pallas_call(
            kernel,
            grid_spec=pltpu.PrefetchScalarGridSpec(
                num_scalar_prefetch=1,
                grid=(1,),
                in_specs=[pl.BlockSpec(memory_space=pltpu.VMEM)] * len(args),
                out_specs=[pl.BlockSpec(memory_space=pltpu.VMEM)] * len(outs),
            ),
            out_shape=outs,
            compiler_params=params(1),
            cost_estimate=cost(0, 6 * sum(v.size for v in args)),
            name=name,
        )(self.bits, *args)


def tie(value, *others):
    return lax.optimization_barrier((value,) + others)[0]


def tie2(values, others):
    return lax.optimization_barrier((*values, *others))[: len(values)]


def body(
    tokens, cond, lengths, ada_w, ada_b, w_qkv, w_out, w_up, b_up, w_down, b_down,
    rel_table, bucket, cotangent,
):
    axes = ("clip", "win")
    sz = Sizes(tokens)
    net = Net()
    devices, index = net.count, net.index
    clips = lax.axis_size("clip")
    width = sz.width
    core = lax.axis_index("win") % 2
    swap = [(n, n ^ 1) for n in range(lax.axis_size("win"))]
    flags = [core] + [lengths[n, 0] for n in range(sz.micro)]
    scalars = jnp.stack(flags + [index % 8, index // 8])
    strip = (sz.micro, 2, 2, sz.frames, sz.half, width)
    tok = tokens.reshape(strip)
    cot = cotangent.reshape(strip)

    cond_act = jax.nn.silu(cond[:, 0].astype(F32)).astype(BF16)
    rows = ada_w.shape[0]
    small = jnp.concatenate([b_up, b_down, rel_table.reshape(-1)])
    n_cond = cond_act.size
    if net.direct:
        early = jnp.concatenate([cond_act.reshape(-1), small])
        early = net.gather_clips(jnp.pad(early, (0, -early.size % 128)))
        cond_all = early[:, :, :n_cond].reshape(early.shape[:2] + cond_act.shape)
    else:
        cond_all = lax.all_gather(cond_act, "clip", axis=0)
    cond_mine = lax.dynamic_slice_in_dim(cond_all, index * rows, rows, cond_all.ndim - 1)
    lead = cond_mine.shape[:-1]
    cond_mine = cond_mine.reshape(clips * sz.micro, rows)
    mod_part = dot_nn(cond_mine, ada_w)
    spread_b = jnp.zeros((mod_part.shape[1],), F32)
    spread_b = lax.dynamic_update_slice(spread_b, ada_b.astype(F32), (index * ada_b.shape[0],))
    mod_part = (mod_part + spread_b[None, :]).reshape(lead + (6 * width,))
    notes = []
    if net.direct:
        mod = net.scatter_clips(mod_part, notes)
        mod = net.swap_sum(net.swap_sum(mod, net.CORE), net.X)
    else:
        mod = lax.psum_scatter(mod_part, "clip", scatter_dimension=0, tiled=False)
        mod = lax.psum(mod, "win")
    mod = mod.reshape(sz.micro, 6, width)

    cols = width // 2
    half_groups = sz.groups // 2
    by_group = w_qkv.reshape(rows, 3, sz.groups, sz.gcols).transpose(0, 2, 1, 3)
    by_group = by_group.reshape(rows, 2, 3 * cols)
    shard_q = [by_group[:, n] for n in range(2)]
    inner = w_up.shape[1]
    per = w_down.shape[0] // 2
    thin = CHUNK // devices

    def inner_order(value):
        if not net.direct:
            value = value.reshape(-1, devices, 2, per).transpose(2, 0, 1, 3)
        else:
            value = value.reshape(-1, devices // 2, 2, 2, per // thin, thin)
            value = value.transpose(3, 0, 4, 2, 1, 5)
        return value.reshape(2, -1, inner // 2)

    def inner_back(halves):
        value = jnp.stack(halves)
        if not net.direct:
            value = value.reshape(2, -1, devices, per).transpose(1, 2, 0, 3)
        else:
            value = value.reshape(2, -1, per // thin, 2, devices // 2, thin)
            value = value.transpose(1, 4, 3, 0, 2, 5)
        return value.reshape(-1, inner)

    def pack_inner(up, down):
        down = down.reshape(per // thin, thin, 2, width // 2).transpose(2, 1, 0, 3)
        down = down.reshape(rows, per // thin, width // 2)
        return jnp.concatenate([up.reshape(rows, -1, CHUNK), down], axis=2).reshape(rows, -1)

    def unpack_inner(value):
        value = value.reshape(rows, per // thin, -1)
        down = value[:, :, CHUNK:].reshape(2, thin, per // thin, width // 2)
        return value[:, :, :CHUNK].reshape(rows, -1), down.transpose(2, 1, 0, 3).reshape(per, width)

    shard_u = inner_order(w_up)
    shard_d = [w_down[:per], w_down[per:]]
    gather = lambda v: lax.all_gather(v, axes, axis=0, tiled=True)
    if net.direct:
        packs = [
            shard_q[0],
            jnp.concatenate([shard_q[1], w_out], axis=1),
            pack_inner(shard_u[0], shard_d[0]),
            pack_inner(shard_u[1], shard_d[1]),
        ]
        rest_q = gather(packs[1])
        one = Gather(net, packs[0])
        one.along_z()
        one.halves = tie2(one.halves, [mod_part])
        one.start(True)
        one.join()
        one.halves = tie2(one.halves, notes[:1])
        one.start(False)
        one.join()
        one.halves = tie2(one.halves, notes[1:])
        one.core()
        small = net.gather_pairs(tie(early[:, :, n_cond:], *notes))
        three = Gather(net, tie(packs[2], *notes))
        full_q = [one.pieces(), Pieces([rest_q])]
        full_out = full_q[1]
        rest = gather(tie(packs[3], early))
    else:
        full_q = [Pieces([gather(v)]) for v in shard_q]
        full_out = Pieces([gather(w_out)])
        full_i = [[Pieces([gather(u)]), Pieces([gather(d)])] for u, d in zip(shard_u, shard_d)]
        small = gather(small[None])
    n_up, n_down = b_up.shape[0], b_down.shape[0]
    n_small = n_up + n_down + rel_table.size
    full_bup = inner_order(small[:, :n_up].astype(F32).reshape(1, inner))
    full_bdown = small[:, n_up : n_up + n_down].astype(F32).reshape(1, width)
    table = small[:, n_up + n_down : n_small].reshape(-1, HEADS)
    places = offset_onehot(core, sz)
    bias, bias_t = lax.optimization_barrier(bias_blocks(table, bucket, places, sz))

    own, send = first_norm(tok, mod, scalars, sz)
    far = lax.ppermute(send, "win", swap)
    if net.direct:
        three.along_z()
        three.start(True)
        far = tie(far, *three.halves)
    qkv_0, att_0, wide_0 = attention(0, own, far, full_q[0], bias, scalars, sz)
    if net.direct:
        three.tie(att_0)
        three.join()
        three.start(False)
        att_0 = tie(att_0, *three.halves)
    qkv_1, att_1, wide_1, wide_out, branch_own, branch_send = attention(
        1, own, far, full_q[1], bias, scalars, sz, att_0, full_out
    )
    branch_far = lax.ppermute(branch_send, "win", swap)
    hidden_two, grad_mlp = second_norm(tok, cot, branch_own, branch_far, mod, scalars, sz)
    flat = (sz.rows, width)
    both = (2, sz.micro, sz.used, sz.half, width)
    hidden_two, grad_mlp = hidden_two.reshape(flat), grad_mlp.reshape(flat)
    if net.direct:
        three.tie(branch_own)
        three.join()
        three.core()
        full_i = [[three.pieces()], [Pieces([rest])]]
    mlps = []
    for n in range(2):
        shard = rows if net.direct and n == 1 else None
        mlps.append(
            mlp(hidden_two, grad_mlp, full_i[n], full_bup[n], scalars, sz, shard, n == 0)
        )
        if net.direct and n == 0:
            pack, hidden_two = lax.optimization_barrier((mlps[0][4], hidden_two))
            r_first = lax.psum_scatter(pack, axes, scatter_dimension=0, tiled=True).astype(F32)

    if net.direct:
        second = Scatter(net, mlps[1][3:5])
    output, grad_mid, grad_own, grad_send, sums_two = after_mlp(
        tok, cot, branch_own, branch_far, [v[0].reshape(both) for v in mlps],
        [v[1].reshape(both) for v in mlps], mod, full_bdown, scalars, sz,
    )
    grad_far = lax.ppermute(grad_send, "win", swap)
    if net.direct:
        second.tie(grad_own)
        second.second()
        grad_own = tie(grad_own, *second.keep)
    shard = rows if net.direct else None
    *g_0, carry = attention_back(
        0, grad_own, grad_far, own, far, qkv_0, (att_0, att_1), wide_0, wide_out, bias_t,
        scalars, sz, shard,
    )
    if net.direct:
        second.tie(carry)
        second.third()
        g_0 = lax.optimization_barrier((*g_0, *second.keep))[: len(g_0)]
        heads_0 = Scatter(net, g_0[:2])
        heads_0.second()
        carry = tie(carry, *heads_0.keep)
        fold_0 = g_0[2]
    else:
        fold_0 = g_0[1]
    *g_1, fold_1, hid_own, hid_send = attention_back(
        1, grad_own, grad_far, own, far, qkv_1, None, wide_1, wide_out, bias_t, scalars, sz,
        shard, carry,
    )
    if net.direct:
        second.tie(hid_own)
        second.fourth()
        heads_0.tie(hid_own)
        heads_0.third()
        g_1 = tie2(g_1, second.keep + heads_0.keep)
        hid_send = tie(hid_send, *second.keep, *heads_0.keep)
        heads_1 = Scatter(net, g_1)
        hid_far = lax.ppermute(hid_send, "win", swap)
        heads_1.second()
        hid_far = tie(hid_far, *heads_1.keep)
    else:
        hid_far = lax.ppermute(hid_send, "win", swap)
    grad_in, sums_one = last_norm(tok, cot, grad_mid, hid_own, hid_far, mod, scalars, sz)
    if net.direct:
        heads_1.tie(sums_one)
        heads_1.third()
        sums_one = tie(sums_one, *heads_1.keep)

    grad_mod = jnp.concatenate(
        [sums_one, sums_two[:, 3:4], sums_two[:, 0:3]], axis=1
    ).reshape(sz.micro, 6 * width)
    by_offset = jnp.concatenate([offset_grad(fold, places, sz) for fold in (fold_0, fold_1)])
    g_table = table_grad(by_offset, bucket, table.shape[0]).reshape(devices, -1)
    g_bup = inner_back([v[2] for v in mlps]).reshape(devices, -1)
    g_bdown = mlps[0][3].reshape(devices, -1)
    g_small = jnp.concatenate([g_bup, g_bdown, g_table], axis=1)
    if net.direct:
        every = jnp.concatenate([grad_mod.reshape(-1), g_small.reshape(-1)])
        every = net.gather_clips(net.swap_sum(net.swap_sum(every, net.CORE), net.X))
        mod_all = every[:, :, : grad_mod.size]
        g_small = jnp.sum(every[:, :, grad_mod.size :], axis=(0, 1)).reshape(g_small.shape)
        g_small = lax.dynamic_index_in_dim(g_small, index, 0, keepdims=False)
    else:
        mod_all = lax.all_gather(lax.psum(grad_mod, "win"), "clip", axis=0)
        g_small = lax.psum_scatter(g_small, axes, scatter_dimension=0, tiled=False)
    mod_all = mod_all.reshape(clips * sz.micro, -1)
    grad_ada_w = lax.dot_general(
        cond_mine.astype(F32), mod_all, (((0,), (0,)), ((), ())),
        precision=HIGHEST, preferred_element_type=F32,
    )
    grad_ada_b = lax.dynamic_slice_in_dim(
        jnp.sum(mod_all, axis=0), index * ada_b.shape[0], ada_b.shape[0]
    )
    if net.direct:
        heads_1.fourth(heads_0)
        r_u, r_d = zip(unpack_inner(r_first), unpack_inner(second.total()))
        mine = heads_1.total()
        r_q = [mine[:, 3 * cols :].reshape(rows, half_groups, -1), mine[:, : 3 * cols]]
        r_out = r_q[0][:, :, 3 * sz.gcols :].reshape(rows, width)
        r_q[0] = r_q[0][:, :, : 3 * sz.gcols]
    else:
        scatter = lambda v: lax.psum_scatter(
            v.astype(F32), axes, scatter_dimension=0, tiled=True
        )
        r_u = [scatter(v[-2]) for v in mlps]
        r_d = [scatter(v[-1]) for v in mlps]
        r_q, r_out = [scatter(g_0[0]), scatter(g_1[0])], scatter(g_0[2])
    r_up = inner_back(r_u)
    r_down = jnp.concatenate(r_d)
    r_qkv = jnp.stack([v.reshape(rows, half_groups, 3, sz.gcols) for v in r_q], axis=1)
    r_qkv = r_qkv.reshape(rows, sz.groups, 3, sz.gcols).transpose(0, 2, 1, 3)
    r_qkv = r_qkv.reshape(rows, 3 * width)
    return (
        output.reshape(tokens.shape), grad_in.reshape(tokens.shape), grad_ada_w, grad_ada_b,
        r_qkv, r_out, r_up, g_small[:n_up], r_down, g_small[n_up : n_up + n_down],
        g_small[n_up + n_down :].reshape(rel_table.shape),
    )


def solution(mesh):
    weights = P(("clip", "win"), None)
    vector = P(("clip", "win"))
    strips = P(None, "clip", "win", None, None, None, None, None)
    return jax.shard_map(
        body,
        mesh=mesh,
        in_specs=(
            strips, P(None, "clip", None), P(None, "clip"), weights, vector, weights, weights,
            weights, vector, weights, vector, weights, P(), strips,
        ),
        out_specs=(
            strips, strips, weights, vector, weights, weights, weights, vector, weights, vector,
            weights,
        ),
        check_vma=False,
    )
```

```python
import functools
import math

import jax
import jax.numpy as jnp
from jax import lax
from jax.experimental import pallas as pl
from jax.experimental.pallas import tpu as pltpu
from jax.sharding import PartitionSpec as P

HEADS = 16
EPSILON = 1e-06
MASKED = -1000000000.0
F32 = jnp.float32
BF16 = jnp.bfloat16
VMEM_LIMIT = 58 * 1024 * 1024
HIGHEST = lax.Precision.HIGHEST


def dot_nn(a, b):
    return lax.dot_general(a, b, (((1,), (0,)), ((), ())), preferred_element_type=F32)


def dot_nt(a, b):
    return lax.dot_general(a, b, (((1,), (1,)), ((), ())), preferred_element_type=F32)


def dot_tn(a, b):
    return lax.dot_general(a, b, (((0,), (0,)), ((), ())), preferred_element_type=F32)


def params(count):
    return pltpu.CompilerParams(
        dimension_semantics=("arbitrary",) * count, vmem_limit_bytes=VMEM_LIMIT
    )


def cost(flops, size):
    return pl.CostEstimate(flops=flops, bytes_accessed=size, transcendentals=0)


def once(shape, index_map):
    return pl.BlockSpec(shape, index_map, pipeline_mode=pl.Buffered(1))


def normalize(values):
    centered = values - jnp.mean(values, axis=-1, keepdims=True)
    inv = lax.rsqrt(jnp.mean(centered * centered, axis=-1, keepdims=True) + EPSILON)
    return centered * inv, inv


def norm_back(grad, normed, inv):
    return inv * (
        grad
        - jnp.mean(grad, axis=-1, keepdims=True)
        - normed * jnp.mean(grad * normed, axis=-1, keepdims=True)
    )


class Sizes:
    def __init__(self, tokens):
        self.micro, _, _, self.blocks, self.frames, rows, side, self.width = tokens.shape
        self.half = rows * side
        self.cols = self.blocks // 2
        self.strip_rows, self.side = rows, side
        self.used = 2 * self.frames - 1
        self.frame = 2 * self.half
        self.win_rows = self.used * self.frame
        self.rows = self.micro * self.win_rows
        self.lens = (self.frames * self.frame, (self.frames - 1) * self.frame)
        self.head = self.width // HEADS
        self.group = 4
        self.gcols = self.group * self.head
        self.groups = HEADS // self.group


def frame_rows(value):
    return value.reshape(-1, value.shape[-1])


def first_norm(tok, mod, core, sz):
    def kernel(sc_ref, x_ref, mod_ref, own_ref, far_ref):
        shift = mod_ref[0, 0:1, :]
        scale = 1.0 + mod_ref[0, 1:2, :]
        for slot, out_ref in enumerate((own_ref, far_ref)):
            column = sc_ref[0] ^ slot
            for tw in range(2):
                count = sz.frames - tw
                rows = frame_rows(x_ref[0, tw, column, :count].astype(F32))
                normed, _ = normalize(rows)
                hidden = (normed * scale + shift).astype(BF16)
                out_ref[0, tw * sz.frames : tw * sz.frames + count] = hidden.reshape(
                    count, sz.half, sz.width
                )

    strip = (1, 2, 2, sz.frames, sz.half, sz.width)
    piece = (1, sz.used, sz.half, sz.width)
    shape = jax.ShapeDtypeStruct((sz.micro,) + piece[1:], BF16)
    return pl.pallas_call(
        kernel,
        grid_spec=pltpu.PrefetchScalarGridSpec(
            num_scalar_prefetch=1,
            grid=(sz.micro,),
            in_specs=[
                pl.BlockSpec(strip, lambda m, s: (m, 0, 0, 0, 0, 0)),
                pl.BlockSpec((1, 6, sz.width), lambda m, s: (m, 0, 0)),
            ],
            out_specs=[pl.BlockSpec(piece, lambda m, s: (m, 0, 0, 0))] * 2,
        ),
        out_shape=[shape, shape],
        compiler_params=params(1),
        name="first_norm",
    )(core, tok, mod)


def valid_rows(tw, count, length, sz):
    frame = tw * sz.frames + lax.broadcasted_iota(jnp.int32, (count * sz.half, 1), 0) // sz.half
    return (frame < length).astype(F32)


def second_norm(tok, cot, branch_own, branch_far, mod, scalars, sz):
    def kernel(sc_ref, x_ref, c_ref, bo_ref, bf_ref, mod_ref, h_ref, g_ref):
        length = sc_ref[1 + pl.program_id(0)]
        gate1 = mod_ref[0, 2:3, :]
        shift = mod_ref[0, 3:4, :]
        scale = 1.0 + mod_ref[0, 4:5, :]
        gate2 = mod_ref[0, 5:6, :]
        for slot, b_ref in enumerate((bo_ref, bf_ref)):
            column = sc_ref[0] ^ slot
            for tw in range(2):
                count = sz.frames - tw
                span = slice(tw * sz.frames, tw * sz.frames + count)
                rows = frame_rows(x_ref[0, tw, column, :count].astype(F32))
                branch = frame_rows(b_ref[0, span].astype(F32))
                normed, _ = normalize(rows + gate1 * branch)
                h_ref[slot, 0, span] = (
                    (normed * scale + shift).astype(BF16).reshape(count, sz.half, sz.width)
                )
                grad = frame_rows(c_ref[0, tw, column, :count].astype(F32))
                grad = grad * valid_rows(tw, count, length, sz) * gate2
                g_ref[slot, 0, span] = grad.astype(BF16).reshape(count, sz.half, sz.width)

    strip = (1, 2, 2, sz.frames, sz.half, sz.width)
    piece = (1, sz.used, sz.half, sz.width)
    both = (2, 1, sz.used, sz.half, sz.width)
    shape = jax.ShapeDtypeStruct((2, sz.micro, sz.used, sz.half, sz.width), BF16)
    return pl.pallas_call(
        kernel,
        grid_spec=pltpu.PrefetchScalarGridSpec(
            num_scalar_prefetch=1,
            grid=(sz.micro,),
            in_specs=[
                pl.BlockSpec(strip, lambda m, s: (m, 0, 0, 0, 0, 0)),
                pl.BlockSpec(strip, lambda m, s: (m, 0, 0, 0, 0, 0)),
                pl.BlockSpec(piece, lambda m, s: (m, 0, 0, 0)),
                pl.BlockSpec(piece, lambda m, s: (m, 0, 0, 0)),
                pl.BlockSpec((1, 6, sz.width), lambda m, s: (m, 0, 0)),
            ],
            out_specs=[pl.BlockSpec(both, lambda m, s: (0, m, 0, 0, 0))] * 2,
        ),
        out_shape=[shape, shape],
        compiler_params=params(1),
        name="second_norm",
    )(scalars, tok, cot, branch_own, branch_far, mod)


def after_mlp(tok, cot, branch_own, branch_far, mlps, grads, mod, b_down, scalars, sz):
    def kernel(
        sc_ref, x_ref, c_ref, bo_ref, bf_ref, y0_ref, y1_ref, t0_ref, t1_ref, mod_ref, bd_ref,
        out_ref, gm_ref, go_ref, gf_ref, sum_ref,
    ):
        length = sc_ref[1 + pl.program_id(0)]
        gate1 = mod_ref[0, 2:3, :]
        scale = 1.0 + mod_ref[0, 4:5, :]
        gate2 = mod_ref[0, 5:6, :]
        sums = [jnp.zeros((1, sz.width), F32) for _ in range(4)]
        for slot, (b_ref, g_ref) in enumerate(((bo_ref, go_ref), (bf_ref, gf_ref))):
            column = sc_ref[0] ^ slot
            for tw in range(2):
                count = sz.frames - tw
                span = slice(tw * sz.frames, tw * sz.frames + count)
                shape = (count, sz.half, sz.width)
                valid = valid_rows(tw, count, length, sz)
                branch = frame_rows(b_ref[0, span].astype(F32))
                middle = frame_rows(x_ref[0, tw, column, :count].astype(F32)) + gate1 * branch
                normed, inv = normalize(middle)
                y = frame_rows(y0_ref[slot, 0, span] + y1_ref[slot, 0, span]) + bd_ref[0:1, :]
                grad = frame_rows(c_ref[0, tw, column, :count].astype(F32))
                out_ref[0, tw, column, :count] = (
                    (middle + valid * gate2 * y).astype(BF16).reshape(shape)
                )
                two = frame_rows(t0_ref[slot, 0, span] + t1_ref[slot, 0, span])
                gm = grad + norm_back(two * scale, normed, inv)
                gm_ref[slot, 0, span] = gm.reshape(shape)
                g_ref[0, span] = (valid * (gm * gate1)).astype(BF16).reshape(shape)
                for n, term in enumerate((two, two * normed, grad * valid * y, gm * branch)):
                    sums[n] = sums[n] + jnp.sum(term, axis=0, keepdims=True)
            out_ref[0, 1, column, sz.frames - 1] = x_ref[0, 1, column, sz.frames - 1]
        for n in range(4):
            sum_ref[0, n : n + 1, :] = sums[n]

    strip = (1, 2, 2, sz.frames, sz.half, sz.width)
    piece = (1, sz.used, sz.half, sz.width)
    both = (2, 1, sz.used, sz.half, sz.width)
    full = (sz.micro,) + piece[1:]
    at_strip = lambda m, s: (m, 0, 0, 0, 0, 0)
    at_piece = lambda m, s: (m, 0, 0, 0)
    at_both = lambda m, s: (0, m, 0, 0, 0)
    return pl.pallas_call(
        kernel,
        grid_spec=pltpu.PrefetchScalarGridSpec(
            num_scalar_prefetch=1,
            grid=(sz.micro,),
            in_specs=[
                pl.BlockSpec(strip, at_strip),
                pl.BlockSpec(strip, at_strip),
                pl.BlockSpec(piece, at_piece),
                pl.BlockSpec(piece, at_piece),
                pl.BlockSpec(both, at_both),
                pl.BlockSpec(both, at_both),
                pl.BlockSpec(both, at_both),
                pl.BlockSpec(both, at_both),
                pl.BlockSpec((1, 6, sz.width), lambda m, s: (m, 0, 0)),
                pl.BlockSpec((1, sz.width), lambda m, s: (0, 0)),
            ],
            out_specs=[
                pl.BlockSpec(strip, at_strip),
                pl.BlockSpec(both, at_both),
                pl.BlockSpec(piece, at_piece),
                pl.BlockSpec(piece, at_piece),
                pl.BlockSpec((1, 4, sz.width), lambda m, s: (m, 0, 0)),
            ],
        ),
        out_shape=[
            jax.ShapeDtypeStruct(tok.shape, BF16),
            jax.ShapeDtypeStruct((2,) + full, F32),
            jax.ShapeDtypeStruct(full, BF16),
            jax.ShapeDtypeStruct(full, BF16),
            jax.ShapeDtypeStruct((sz.micro, 4, sz.width), F32),
        ],
        compiler_params=params(1),
        name="after_mlp",
    )(scalars, tok, cot, branch_own, branch_far, *mlps, *grads, mod, b_down)


def last_norm(tok, cot, grad_mid, grad_own, grad_far, mod, scalars, sz):
    def kernel(sc_ref, x_ref, c_ref, gm_ref, go_ref, gf_ref, mod_ref, out_ref, sum_ref):
        scale = 1.0 + mod_ref[0, 1:2, :]
        sums = [jnp.zeros((1, sz.width), F32) for _ in range(2)]
        for slot, g_ref in enumerate((go_ref, gf_ref)):
            column = sc_ref[0] ^ slot
            for tw in range(2):
                count = sz.frames - tw
                span = slice(tw * sz.frames, tw * sz.frames + count)
                normed, inv = normalize(frame_rows(x_ref[0, tw, column, :count].astype(F32)))
                one = frame_rows(g_ref[0, span].astype(F32))
                grad = frame_rows(gm_ref[slot, 0, span]) + norm_back(one * scale, normed, inv)
                out_ref[0, tw, column, :count] = grad.astype(BF16).reshape(
                    count, sz.half, sz.width
                )
                for n, term in enumerate((one, one * normed)):
                    sums[n] = sums[n] + jnp.sum(term, axis=0, keepdims=True)
        for slot in range(2):
            out_ref[0, 1, slot, sz.frames - 1] = c_ref[0, 0, slot, 0]
        for n in range(2):
            sum_ref[0, n : n + 1, :] = sums[n]

    strip = (1, 2, 2, sz.frames, sz.half, sz.width)
    tail = (1, 1, 2, 1, sz.half, sz.width)
    piece = (1, sz.used, sz.half, sz.width)
    both = (2, 1, sz.used, sz.half, sz.width)
    return pl.pallas_call(
        kernel,
        grid_spec=pltpu.PrefetchScalarGridSpec(
            num_scalar_prefetch=1,
            grid=(sz.micro,),
            in_specs=[
                pl.BlockSpec(strip, lambda m, s: (m, 0, 0, 0, 0, 0)),
                pl.BlockSpec(tail, lambda m, s: (m, 1, 0, sz.frames - 1, 0, 0)),
                pl.BlockSpec(both, lambda m, s: (0, m, 0, 0, 0)),
                pl.BlockSpec(piece, lambda m, s: (m, 0, 0, 0)),
                pl.BlockSpec(piece, lambda m, s: (m, 0, 0, 0)),
                pl.BlockSpec((1, 6, sz.width), lambda m, s: (m, 0, 0)),
            ],
            out_specs=[
                pl.BlockSpec(strip, lambda m, s: (m, 0, 0, 0, 0, 0)),
                pl.BlockSpec((1, 2, sz.width), lambda m, s: (m, 0, 0)),
            ],
        ),
        out_shape=[
            jax.ShapeDtypeStruct(tok.shape, BF16),
            jax.ShapeDtypeStruct((sz.micro, 2, sz.width), F32),
        ],
        compiler_params=params(1),
        name="last_norm",
    )(scalars, tok, cot, grad_mid, grad_own, grad_far, mod)


class Pieces:
    def __init__(self, arrays):
        self.arrays = arrays
        self.whole = len(arrays) == 1

    def specs(self, columns, index_map):
        if self.whole:
            at = lambda *g: (0, index_map(*g))
            return [pl.BlockSpec((self.arrays[0].shape[0], columns), at)]
        at = lambda *g: (0, 0, 0, index_map(*g))
        shape = self.arrays[0].shape[:-1] + (columns,)
        return [pl.BlockSpec(shape, at)] * 8


def pieces_of(refs, key, z_here):
    depth = refs[0].shape[1]
    for z in range(depth):
        for n in range(8):
            half, far, i = n // 4, n // 2 % 2, n % 2
            for j in range(2):
                away = (i * 4 + j * 2 if half == 0 else i * 2 + j * 4) + far
                yield (z_here + z) % depth, key ^ away, half, refs[n].at[j, z]


def place(refs, key, z_here, out_ref, columns=slice(None), source=slice(None)):
    if len(refs) == 1:
        out_ref[:, columns] = refs[0][:, source]
        return
    for z, at, half, piece in pieces_of(refs, key, z_here):
        cut = piece.shape[0]
        row = pl.multiple_of((z * 8 + at) * (2 * cut) + half * cut, cut)
        out_ref[pl.ds(row, cut), columns] = piece[:, source]


def place_inner(refs, key, z_here, out_ref, source):
    size = source.stop - source.start
    if len(refs) == 1:
        cut = out_ref.shape[0] // 32
        for n in range(64):
            at, half = n // 2, n % 2
            to = (at % 2) * (16 * cut) + at // 2 * cut
            out_ref[to : to + cut, half * size : (half + 1) * size] = refs[0][
                n * cut : (n + 1) * cut, source
            ]
        return
    for z, at, half, piece in pieces_of(refs, key, z_here):
        cut = piece.shape[0]
        row = pl.multiple_of((at % 2) * (16 * cut) + (z * 4 + at // 2) * cut, cut)
        out_ref[pl.ds(row, cut), half * size : (half + 1) * size] = piece[:, source]


def turn(value, out_ref, core, shard, start=0):
    turned = value.T
    if shard is None:
        out_ref[start : start + turned.shape[0]] = turned
        return
    height = out_ref.shape[0]
    for n in range(turned.shape[0] // shard):
        at = start // shard + n
        at = (core ^ (at % 2)) * (height // 2) + at // 2 * shard
        out_ref[pl.ds(pl.multiple_of(at, shard), shard), :] = turned[n * shard : (n + 1) * shard]


def give(refs, half, low, value, start=0):
    value = value.astype(BF16)
    columns = slice(start, start + value.shape[1])
    if len(refs) == 1:
        low = half * (refs[0].shape[0] // 2) + low
        refs[0][low : low + value.shape[0], columns] = value
        return
    rows = refs[half].shape[1]
    refs[half][low // rows : (low + value.shape[0]) // rows, :, columns] = value.reshape(
        value.shape[0] // rows, rows, value.shape[1]
    )


def grad_shapes(direct, rows, height, columns):
    if not direct:
        return [jax.ShapeDtypeStruct((height, columns), BF16)]
    return [jax.ShapeDtypeStruct((height // (2 * rows), rows, columns), BF16)] * 2


def grad_specs(direct, rows, height, columns, at_column):
    if not direct:
        return [pl.BlockSpec((height, columns), lambda *g: (0, at_column(*g)))]
    shape = (height // (2 * rows), rows, columns)
    return [pl.BlockSpec(shape, lambda *g: (0, 0, at_column(*g)))] * 2


def join_frames(own_ref, far_ref, joined_ref, sz):
    for m in range(sz.micro):
        for f in range(sz.used):
            at = m * sz.win_rows + f * sz.frame
            joined_ref[at : at + sz.half] = own_ref[m, f]
            joined_ref[at + sz.half : at + sz.frame] = far_ref[m, f]


def spread_bias(block_ref, head, bias_ref, sz, turned=False):
    size = sz.frame
    for step in range(2 * sz.frames - 1):
        block = block_ref[head, step]
        if turned:
            block = block.T
        for key in range(sz.frames):
            query = key + step - (sz.frames - 1)
            if 0 <= query < sz.frames:
                row, column = (key, query) if turned else (query, key)
                bias_ref[row * size : (row + 1) * size, column * size : (column + 1) * size] = block


def window_rows(m, tw, sz):
    start = pl.multiple_of(m * sz.win_rows + tw * sz.lens[0], sz.frame)
    return pl.ds(start, sz.lens[tw])


def attention(half, own, far, w_qkv, bias, scalars, sz, first=None, w_out=None):
    scale = 1.0 / math.sqrt(sz.head)
    last = w_out is not None
    steps = sz.groups // 2
    gcols = sz.gcols
    joint = w_out is w_qkv
    n_out = 2 * len(w_qkv.arrays) if joint else 1

    def kernel(sc_ref, own_ref, far_ref, bias_ref, *refs):
        refs = list(refs)
        take = lambda count: [refs.pop(0) for _ in range(count)]
        w_refs = take(len(w_qkv.arrays))
        if last:
            (first_ref,) = take(1)
            out_refs = take(n_out)
            take(2)
        qkv_ref, w_ref, att_ref = take(3)
        if last:
            wo_ref, bo_ref, bf_ref = take(3)
        joined, spread = take(2)
        step = pl.program_id(0)
        key, z_here = sc_ref[1 + sz.micro], sc_ref[2 + sz.micro]

        @pl.when(step == 0)
        def _():
            join_frames(own_ref, far_ref, joined, sz)

        place(w_refs, key, z_here, w_ref)
        for n in range(3):
            part = dot_nn(joined[...], w_ref[:, n * gcols : (n + 1) * gcols]).astype(BF16)
            qkv_ref[n] = part * scale if n == 0 else part
        for head in range(sz.group):
            spread_bias(bias_ref, head, spread.at[head], sz)

        def one_micro(m, carry):
            for tw in range(2):
                size = sz.lens[tw]
                rows = window_rows(m, tw, sz)
                keys_ok = (sc_ref[1 + m] - tw * sz.frames) * sz.frame

                @pl.when(keys_ok > 0)
                def _(rows=rows, size=size, keys_ok=keys_ok):
                    column = lax.broadcasted_iota(jnp.int32, (1, size), 1)
                    for head in range(sz.group):
                        lanes = slice(head * sz.head, (head + 1) * sz.head)
                        scores = dot_nt(qkv_ref[0, rows, lanes], qkv_ref[1, rows, lanes])
                        scores = scores + spread[head, :size, :size].astype(F32)
                        scores = jnp.where(column < keys_ok, scores, MASKED)
                        top = jnp.max(scores, axis=-1, keepdims=True)
                        weight = jnp.exp(scores - top)
                        share = 1.0 / jnp.sum(weight, axis=-1, keepdims=True)
                        probs = (weight * share).astype(BF16)
                        att_ref[rows, lanes] = dot_nn(probs, qkv_ref[2, rows, lanes]).astype(BF16)

                @pl.when(keys_ok <= 0)
                def _(rows=rows, size=size):
                    att_ref[rows, :] = jnp.zeros((size, gcols), BF16)

            return carry

        lax.fori_loop(0, sz.micro, one_micro, 0)
        if not last:
            return
        kept, total = take(2)
        for n in range(steps):

            @pl.when(step == n)
            def _(n=n):
                kept[:, n * gcols : (n + 1) * gcols] = att_ref[...]

        @pl.when(step == steps - 1)
        def _():
            if joint:
                place(out_refs[: n_out // 2], key, z_here, wo_ref, slice(0, 2 * gcols))
                place(out_refs[n_out // 2 :], key, z_here, wo_ref, slice(2 * gcols, 4 * gcols))
            else:
                place(out_refs, key, z_here, wo_ref)
            middle = first_ref.shape[1]
            total[...] = dot_nn(first_ref[...], wo_ref[:middle]) + dot_nn(
                kept[...], wo_ref[middle:]
            )
            for m in range(sz.micro):
                for f in range(sz.used):
                    at = m * sz.win_rows + f * sz.frame
                    valid = (f < sc_ref[1 + m]).astype(F32)
                    bo_ref[m, f] = (total[at : at + sz.half] * valid).astype(BF16)
                    bf_ref[m, f] = (total[at + sz.half : at + sz.frame] * valid).astype(BF16)

    piece = (sz.micro, sz.used, sz.half, sz.width)
    fixed = lambda g, s: (0, 0, 0, 0)
    flat = lambda g, s: (0, 0)
    width, cols = sz.width, sz.width // 2
    in_specs = [
        once(piece, fixed),
        once(piece, fixed),
        pl.BlockSpec((sz.group,) + bias.shape[1:], lambda g, s: (half * steps + g, 0, 0, 0)),
    ] + w_qkv.specs(3 * gcols, lambda g, s: g)
    out_specs = [
        pl.BlockSpec((3, sz.rows, gcols), lambda g, s: (0, 0, half * steps + g)),
        pl.BlockSpec((width, 3 * gcols), lambda g, s: (0, half * steps + g)),
        pl.BlockSpec((sz.rows, gcols), lambda g, s: (0, g)),
    ]
    out_shape = [
        jax.ShapeDtypeStruct((3, sz.rows, width), BF16),
        jax.ShapeDtypeStruct((width, 3 * width), BF16),
        jax.ShapeDtypeStruct((sz.rows, cols), BF16),
    ]
    aliases = {}
    scratch = [
        pltpu.VMEM((sz.rows, width), BF16),
        pltpu.VMEM((sz.group, sz.lens[0], sz.lens[0]), BF16),
    ]
    args = [scalars, own, far, bias, *w_qkv.arrays]
    flops = 6 * sz.rows * width * cols + 4 * sz.rows * sz.lens[0] * cols
    if last:
        in_specs += [once((sz.rows, cols), flat)]
        if joint:
            low = w_out.arrays[0].shape[-1] // (2 * gcols) - 2
            in_specs += w_out.specs(2 * gcols, lambda g, s: low)
            in_specs += w_out.specs(2 * gcols, lambda g, s: low + 1)
            out_args = w_out.arrays * 2
        else:
            in_specs += w_out.specs(width, lambda g, s: 0)
            out_args = w_out.arrays
        out_specs += [pl.BlockSpec((width, width), flat)] + [pl.BlockSpec(piece, fixed)] * 2
        out_shape += [jax.ShapeDtypeStruct((width, width), BF16)]
        out_shape += [jax.ShapeDtypeStruct(piece, BF16)] * 2
        scratch += [pltpu.VMEM((sz.rows, cols), BF16), pltpu.VMEM((sz.rows, width), F32)]
        args += [first[2], *out_args]
        aliases = {len(args): 0, len(args) + 1: 1}
        in_specs += [pl.BlockSpec(memory_space=pl.ANY)] * 2
        args += first[:2]
        flops += 2 * sz.rows * width * width
    return pl.pallas_call(
        kernel,
        grid_spec=pltpu.PrefetchScalarGridSpec(
            num_scalar_prefetch=1,
            grid=(steps,),
            in_specs=in_specs,
            out_specs=out_specs,
            scratch_shapes=scratch,
        ),
        out_shape=out_shape,
        input_output_aliases=aliases,
        compiler_params=params(1),
        cost_estimate=cost(3 * flops, 16 * sz.rows * width),
        name="attention" + "_last" * last,
    )(*args)


def attention_back(grad_own, grad_far, own, far, qkv, atts, w_qkv, w_out, bias, scalars, sz, shard):
    scale = 1.0 / math.sqrt(sz.head)
    steps = sz.groups
    direct = shard is not None
    outs = 2 if direct else 1
    gcols, width = sz.gcols, sz.width
    quarter = width // 4

    def kernel(
        sc_ref, go_ref, gf_ref, own_ref, far_ref, qkv_ref, w_ref, wo_ref, bias_ref, *refs
    ):
        refs = list(refs)
        take = lambda count: [refs.pop(0) for _ in range(count)]
        att_refs = take(2)
        gw_refs = take(outs)
        gwo_refs = gw_refs if direct else take(1)
        fold_ref, ho_ref, hf_ref = take(3)
        grad, hidden_t, grad_att, parts, spread, pair_sum, total, turned = take(8)
        step = pl.program_id(0)

        @pl.when(step == 0)
        def _():
            join_frames(own_ref, far_ref, grad, sz)
            turn(grad[...], hidden_t, sc_ref[0], shard)
            join_frames(go_ref, gf_ref, grad, sz)
            total[...] = jnp.zeros_like(total)
            for n, a_ref in enumerate(att_refs):
                turn(a_ref[...], turned, sc_ref[0], shard, n * a_ref.shape[1])

        grad_att[...] = dot_nt(grad[...], wo_ref[...]).astype(BF16)
        full = sz.lens[0]
        for head in range(sz.group):
            spread_bias(bias_ref, head, spread.at[head], sz, True)
            pair_sum[head] = jnp.zeros((full, full), F32)

        def one_micro(m, carry):
            for tw in range(2):
                size = sz.lens[tw]
                rows = window_rows(m, tw, sz)
                keys_ok = (sc_ref[1 + m] - tw * sz.frames) * sz.frame

                @pl.when(keys_ok > 0)
                def _(rows=rows, size=size, keys_ok=keys_ok):
                    row = lax.broadcasted_iota(jnp.int32, (size, 1), 0)
                    for head in range(sz.group):
                        lanes = slice(head * sz.head, (head + 1) * sz.head)
                        spot = [slice(n * gcols + lanes.start, n * gcols + lanes.stop) for n in range(3)]
                        query = qkv_ref[0, rows, lanes]
                        key = qkv_ref[1, rows, lanes]
                        value = qkv_ref[2, rows, lanes]
                        grad_out = grad_att[rows, lanes]
                        scores = dot_nt(key, query) + spread[head, :size, :size].astype(F32)
                        scores = jnp.where(row < keys_ok, scores, MASKED)
                        weight = jnp.exp(scores - jnp.max(scores, axis=0, keepdims=True))
                        probs = weight * (1.0 / jnp.sum(weight, axis=0, keepdims=True))
                        grad_probs = dot_nt(value, grad_out)
                        inner = jnp.sum(probs * grad_probs, axis=0, keepdims=True)
                        grad_scores = (probs * (grad_probs - inner)).astype(BF16)
                        pair_sum[head, :size, :size] += grad_scores.astype(F32)
                        parts[rows, spot[2]] = dot_nn(probs.astype(BF16), grad_out).astype(BF16)
                        parts[rows, spot[1]] = dot_nn(grad_scores, query).astype(BF16)
                        parts[rows, spot[0]] = (dot_tn(grad_scores, key) * scale).astype(BF16)

                @pl.when(keys_ok <= 0)
                def _(rows=rows, size=size):
                    parts[rows, :] = jnp.zeros((size, 3 * gcols), BF16)

            return carry

        lax.fori_loop(0, sz.micro, one_micro, 0)
        for head in range(sz.group):
            fold_ref[head] = jnp.zeros(fold_ref.shape[1:], F32)
            for t in range(sz.frames):
                low = (sz.frames - 1 - t) * sz.frame
                fold_ref[head, :, low : low + full] += pair_sum[
                    head, t * sz.frame : (t + 1) * sz.frame, :
                ]
        for n in range(4):
            rows = slice(n * quarter, (n + 1) * quarter)
            give(gw_refs, n // 2, n % 2 * quarter, dot_nn(hidden_t[rows, :], parts[...]))
        total[...] += dot_nt(parts[...], w_ref[...])
        columns = pl.ds(pl.multiple_of(step * gcols, gcols), gcols)
        for n in range(4):
            rows = slice(n * quarter, (n + 1) * quarter)
            value = dot_nn(turned[rows, :], grad[:, columns])
            give(gwo_refs, n // 2, n % 2 * quarter, value, 3 * gcols if direct else 0)

        @pl.when(step == steps - 1)
        def _():
            for m in range(sz.micro):
                for f in range(sz.used):
                    at = m * sz.win_rows + f * sz.frame
                    ho_ref[m, f] = total[at : at + sz.half].astype(BF16)
                    hf_ref[m, f] = total[at + sz.half : at + sz.frame].astype(BF16)

    piece = (sz.micro, sz.used, sz.half, width)
    fixed = lambda g, s: (0, 0, 0, 0)
    flat = lambda g, s: (0, 0)
    cols = width // 2
    fold = (sz.frame, (2 * sz.frames - 1) * sz.frame)
    in_specs = [
        once(piece, fixed),
        once(piece, fixed),
        once(piece, fixed),
        once(piece, fixed),
        pl.BlockSpec((3, sz.rows, gcols), lambda g, s: (0, 0, g)),
        pl.BlockSpec((width, 3 * gcols), lambda g, s: (0, g)),
        pl.BlockSpec((gcols, width), lambda g, s: (g, 0)),
        pl.BlockSpec((sz.group,) + bias.shape[1:], lambda g, s: (g, 0, 0, 0)),
    ]
    along = lambda g, s: g
    wide = 4 * gcols if direct else 3 * gcols
    out_specs = grad_specs(direct, shard, width, wide, along)
    if not direct:
        out_specs += grad_specs(direct, shard, width, gcols, along)
    out_specs += [pl.BlockSpec((sz.group,) + fold, lambda g, s: (g, 0, 0))]
    out_specs += [pl.BlockSpec(piece, fixed)] * 2
    out_shape = grad_shapes(direct, shard, width, steps * wide)
    if not direct:
        out_shape += grad_shapes(direct, shard, width, width)
    out_shape += [jax.ShapeDtypeStruct((HEADS,) + fold, F32)]
    out_shape += [jax.ShapeDtypeStruct(piece, BF16)] * 2
    scratch = [
        pltpu.VMEM((sz.rows, width), BF16),
        pltpu.VMEM((width, sz.rows), BF16),
        pltpu.VMEM((sz.rows, gcols), BF16),
        pltpu.VMEM((sz.rows, 3 * gcols), BF16),
        pltpu.VMEM((sz.group, sz.lens[0], sz.lens[0]), BF16),
        pltpu.VMEM((sz.group, sz.lens[0], sz.lens[0]), F32),
    ]
    args = [scalars, grad_own, grad_far, own, far, qkv, w_qkv, w_out, bias]
    flops = 16 * sz.rows * width * width + 10 * sz.rows * sz.lens[0] * width
    in_specs += [once((sz.rows, cols), flat)] * 2
    scratch += [pltpu.VMEM((sz.rows, width), F32), pltpu.VMEM((width, sz.rows), BF16)]
    args += list(atts)
    return pl.pallas_call(
        kernel,
        grid_spec=pltpu.PrefetchScalarGridSpec(
            num_scalar_prefetch=1,
            grid=(steps,),
            in_specs=in_specs,
            out_specs=out_specs,
            scratch_shapes=scratch,
        ),
        out_shape=out_shape,
        compiler_params=params(1),
        cost_estimate=cost(3 * flops, 24 * sz.rows * width),
        name="attention_back",
    )(*args)


GELU_A = math.sqrt(2.0 / math.pi)
GELU_B = 0.044715
MLP_TILES = 3
CHUNK = 512


def mlp(hidden, grad, weights, b_up, scalars, sz, shard, inner_first):
    chunk = CHUNK
    tiles = MLP_TILES
    tile = sz.rows // tiles
    inner = b_up.shape[1]
    steps = inner // chunk
    packed = len(weights) == 1
    direct = shard is not None
    rows, width = sz.rows, sz.width
    quarter = width // 4
    n_up = len(weights[0].arrays)
    copied = n_up > 1

    def kernel(sc_ref, h_ref, g_ref, bu_ref, *refs):
        refs = list(refs)
        take = lambda count: [refs.pop(0) for _ in range(count)]
        up_refs = take(n_up)
        down_refs = up_refs if packed else take(1)
        y_ref, t_ref, gbu_ref = take(3)
        if inner_first:
            (gbd_ref,) = take(1)
        gw_refs = take(2 if direct else 1)
        gwd_refs = gw_refs if packed else take(1)
        hidden_t, act_s, gpre_s = take(3)
        step = pl.program_id(0)
        key, z_here = sc_ref[1 + sz.micro], sc_ref[2 + sz.micro]

        @pl.when(step == 0)
        def _():
            turn(h_ref[...], hidden_t, sc_ref[0], shard)
            if inner_first:
                gbd_ref[...] = jnp.sum(g_ref[...].astype(F32), axis=0, keepdims=True)
            y_ref[...] = jnp.zeros_like(y_ref)
            t_ref[...] = jnp.zeros_like(t_ref)

        if packed:
            (wd_ref,) = take(1)
            place_inner(down_refs, key, z_here, wd_ref, slice(chunk, chunk + width // 2))
        else:
            wd_ref = down_refs[0]
        if copied:
            (wu_ref,) = take(1)
            place(up_refs, key, z_here, wu_ref, source=slice(0, chunk))
        else:
            wu_ref = up_refs[0]
        bias_sum = jnp.zeros((1, chunk), F32)
        for n in range(tiles):
            span = slice(n * tile, (n + 1) * tile)
            pre = dot_nn(h_ref[span], wu_ref[:, :chunk]) + bu_ref[...]
            grad_act = dot_nt(g_ref[span], wd_ref[...])
            square = pre * pre
            tanh = jnp.tanh(GELU_A * pre * (1.0 + GELU_B * square))
            half = 0.5 * (1.0 + tanh)
            act = (pre * half).astype(BF16)
            slope = half + (0.5 * GELU_A) * pre * (1.0 - tanh * tanh) * (
                1.0 + (3.0 * GELU_B) * square
            )
            grad_pre = (grad_act * slope).astype(BF16)
            act_s[0, span] = act[:, : chunk // 2]
            act_s[1, span] = act[:, chunk // 2 :]
            gpre_s[span] = grad_pre
            bias_sum = bias_sum + jnp.sum(grad_pre.astype(F32), axis=0, keepdims=True)
            y_ref[span] += dot_nn(act, wd_ref[...])
            t_ref[span] += dot_nt(grad_pre, wu_ref[:, :chunk])
        gbu_ref[...] = bias_sum
        for n in range(4):
            span = slice(n * quarter, (n + 1) * quarter)
            give(gw_refs, n // 2, n % 2 * quarter, dot_nn(hidden_t[span, :], gpre_s[...]))
        for n in range(2):
            source = sc_ref[0] ^ n if direct else n
            value = dot_tn(act_s[source], g_ref[...])
            if not packed:
                give(gwd_refs, n, 0, value)
                continue
            value = value.astype(BF16)
            cut = chunk // 32
            for half in range(2):
                part = value[:, half * width // 2 : (half + 1) * width // 2]
                if direct:
                    gw_refs[n][:, half * cut : (half + 1) * cut, chunk:] = part.reshape(
                        16, cut, width // 2
                    )
                    continue
                for k in range(16):
                    to = (2 * k + n) * 2 * cut + half * cut
                    gw_refs[0][to : to + cut, chunk:] = part[k * cut : (k + 1) * cut]

    fixed = lambda j, s: (0, 0)
    along = lambda j, s: j
    in_specs = [
        once((rows, width), fixed),
        once((rows, width), fixed),
        pl.BlockSpec((1, chunk), lambda j, s: (0, j)),
    ]
    args = [scalars, hidden, grad, b_up]
    out_specs = [
        pl.BlockSpec((rows, width), fixed),
        pl.BlockSpec((rows, width), fixed),
        pl.BlockSpec((1, chunk), lambda j, s: (0, j)),
    ]
    out_shape = [
        jax.ShapeDtypeStruct((rows, width), F32),
        jax.ShapeDtypeStruct((rows, width), F32),
        jax.ShapeDtypeStruct((1, inner), F32),
    ]
    if inner_first:
        out_specs += [pl.BlockSpec((1, width), fixed)]
        out_shape += [jax.ShapeDtypeStruct((1, width), F32)]
    if packed:
        wide = chunk + width // 2
        in_specs += weights[0].specs(wide, along)
        args += weights[0].arrays
        out_specs += grad_specs(direct, shard, width, wide, along)
        out_shape += grad_shapes(direct, shard, width, steps * wide)
    else:
        in_specs += weights[0].specs(chunk, along)
        in_specs += [pl.BlockSpec((chunk, width), lambda j, s: (j, 0))]
        args += [weights[0].arrays[0], weights[1].arrays[0]]
        out_specs += grad_specs(False, None, width, chunk, along)
        out_specs += [pl.BlockSpec((chunk, width), lambda j, s: (j, 0))]
        out_shape += grad_shapes(False, None, width, inner)
        out_shape += grad_shapes(False, None, inner, width)
    scratch = [
        pltpu.VMEM((width, rows), BF16),
        pltpu.VMEM((2, rows, chunk // 2), BF16),
        pltpu.VMEM((rows, chunk), BF16),
    ]
    if packed:
        scratch += [pltpu.VMEM((chunk, width), BF16)]
    if copied:
        scratch += [pltpu.VMEM((width, chunk), BF16)]
    return pl.pallas_call(
        kernel,
        grid_spec=pltpu.PrefetchScalarGridSpec(
            num_scalar_prefetch=1,
            grid=(steps,),
            in_specs=in_specs,
            out_specs=out_specs,
            scratch_shapes=scratch,
        ),
        out_shape=out_shape,
        compiler_params=params(1),
        cost_estimate=cost(14 * rows * width * inner, 16 * rows * width),
        name="mlp",
    )(*args)


def offset_onehot(core, sz):
    span = 2 * sz.side - 1
    place = jnp.arange(sz.frame, dtype=jnp.int32)
    row = ((place // sz.half) ^ core) * sz.strip_rows + place // sz.side % sz.strip_rows
    column = place % sz.side
    index = (row[:, None] - row[None, :] + sz.side - 1) * span
    index = index + column[:, None] - column[None, :] + sz.side - 1
    return (jnp.arange(span * span, dtype=jnp.int32)[:, None, None] == index[None]).astype(BF16)


def bucket_onehot(bucket, count):
    return (jnp.arange(count, dtype=jnp.int32)[:, None] == bucket[None, :]).astype(BF16)


def bias_blocks(table, bucket, places, sz):
    by_offset = dot_tn(table, bucket_onehot(bucket, table.shape[0])).astype(BF16)
    by_offset = by_offset.reshape(HEADS * (2 * sz.frames - 1), -1)
    blocks = dot_nn(by_offset, places.reshape(places.shape[0], -1)).astype(BF16)
    return blocks.reshape(HEADS, -1, sz.frame, sz.frame)


def split_low(value):
    high = value.astype(BF16)
    return high, (value - high.astype(F32)).astype(BF16)


def offset_grad(fold, places, sz):
    steps = 2 * sz.frames - 1
    fold = fold.reshape(-1, sz.frame, steps, sz.frame)
    return sum(
        jnp.einsum("hqkp,jpq->hkj", part, places, preferred_element_type=F32)
        for part in split_low(fold)
    ).reshape(fold.shape[0], -1)


def table_grad(by_offset, bucket, buckets):
    onehot = bucket_onehot(bucket, buckets)
    return sum(dot_nt(onehot, part) for part in split_low(by_offset))


class Net:
    AXES = ("clip", "win")
    X, Y, CORE = 2, 4, 1

    def __init__(self):
        self.count = lax.axis_size(self.AXES)
        self.direct = lax.axis_size("win") == 4 and self.count == 32
        self.deep = self.count // 8
        self.index = lax.axis_index(self.AXES)
        self.z = self.index // 8

    def bit(self, which):
        return self.index // which % 2

    def swap(self, value, which):
        return lax.ppermute(value, self.AXES, [(n, n ^ which) for n in range(self.count)])

    def from_z(self, value, step):
        move = lambda n: (n // 8 - step) % self.deep * 8 + n % 8
        return lax.ppermute(value, self.AXES, [(n, move(n)) for n in range(self.count)])

    def swap_sum(self, value, which):
        return value + self.swap(value, which)


    def gather_clips(self, value):
        along = jnp.stack([value] + [self.from_z(value, k) for k in range(1, self.deep)])
        return jnp.stack([along, self.swap(along, self.Y)], axis=1)

    def scatter_clips(self, value, notes):
        got = self.swap(value[:, 1], self.Y)
        notes.append(got)
        kept = value[:, 0] + got
        got = [self.from_z(kept[self.deep - k], k) for k in range(1, self.deep)]
        notes.append(got[-1])
        return kept[0] + sum(got)

    def gather_pairs(self, value):
        parts = value
        for which in (self.X, self.CORE):
            parts = jnp.stack([parts, self.swap(parts, which)], axis=2 if which == self.X else 3)
        parts = parts.reshape(self.count, -1)
        place = jnp.arange(self.count, dtype=jnp.int32)
        holder = (self.z + place // 8) % self.deep * 8 + (place % 8 ^ self.index % 8)
        pick = (place[:, None] == holder[None, :]).astype(BF16)
        return dot_nn(pick, parts).astype(BF16)


def cut_rows(parts, widths):
    rows, columns = parts[0].shape
    half = rows // 2

    def kernel(*refs):
        ins, outs = refs[: len(parts)], refs[len(parts) :]
        for n, ref in enumerate(ins):
            low = 0
            for k, size in enumerate(widths):
                for side in range(2):
                    outs[2 * k + side][n] = ref[side * half : (side + 1) * half, low : low + size]
                low += size

    return pl.pallas_call(
        kernel,
        out_shape=[
            jax.ShapeDtypeStruct((len(parts), half, size), BF16) for size in widths for _ in range(2)
        ],
        compiler_params=pltpu.CompilerParams(vmem_limit_bytes=VMEM_LIMIT),
        cost_estimate=cost(0, 4 * len(parts) * rows * columns),
        name="cut_rows",
    )(*parts)


class Gather:
    def __init__(self, net, halves):
        self.net = net
        self.halves = list(halves)
        self.got = []

    @staticmethod
    def along_z(net, shards):
        both = jnp.concatenate(shards, axis=1)
        return Gather.cut(net, both, Gather.send_z(net, both), [v.shape[1] for v in shards])

    @staticmethod
    def send_z(net, shard):
        return [net.from_z(shard, k) for k in range(1, net.deep)]

    @staticmethod
    def cut(net, shard, got, widths):
        made = cut_rows([shard] + list(got), widths)
        return [Gather(net, made[2 * n : 2 * n + 2]) for n in range(len(widths))]

    def start(self, first):
        net = self.net
        order = (net.X, net.Y) if first else (net.Y, net.X)
        self.got = [net.swap(v, which) for v, which in zip(self.halves, order)]

    def join(self):
        self.halves = [jnp.stack(pair) for pair in zip(self.halves, self.got)]

    def tie(self, *others):
        self.got = list(lax.optimization_barrier((*self.got, *others))[: len(self.got)])

    def core(self):
        net = self.net
        self.halves = [v for pair in zip(self.halves, self.got) for v in pair]
        self.got = [net.swap(v, net.CORE) for v in self.halves]

    def pieces(self):
        near, far = self.halves, self.got
        return Pieces([*near[:2], *far[:2], *near[2:], *far[2:]])


def add_bf16(one, two):
    return (one.astype(F32) + two.astype(F32)).astype(BF16)


class Scatter:
    def __init__(self, net, pair):
        self.net = net
        keep, send = [v.reshape((net.deep, 4) + v.shape[1:]) for v in pair]
        self.keep = [keep]
        self.got = [net.swap(send, net.CORE)]
        self.bits = jnp.stack([net.bit(net.Y), net.bit(net.X), net.z])
        self.rows, self.columns = keep.shape[2:]

    def tie(self, *others):
        self.got = list(lax.optimization_barrier((*self.got, *others))[: len(self.got)])

    def tie_keep(self, *others):
        self.keep = list(lax.optimization_barrier((*self.keep, *others))[: len(self.keep)])

    def second(self):
        net, cut = self.net, self.rows // 2

        def kernel(sc_ref, keep, got, *outs):
            for half in range(2):
                span = slice(half * cut, (half + 1) * cut)
                for role in range(2):
                    for other in range(2):
                        near = sc_ref[half] ^ role
                        at = near * 2 + other if half == 0 else other * 2 + near
                        outs[2 * half + role][0, other] = add_bf16(keep[0, at, span], got[0, at, span])

        spans = 1
        block = (1,) + self.keep[0].shape[1:3] + (self.columns // spans,)
        out = (2, cut, self.columns // spans)
        made = pl.pallas_call(
            kernel,
            grid_spec=pltpu.PrefetchScalarGridSpec(
                num_scalar_prefetch=1,
                grid=(net.deep, spans),
                in_specs=[pl.BlockSpec(block, lambda z, n, s: (z, 0, 0, n))] * 2,
                out_specs=[pl.BlockSpec((1,) + out, lambda z, n, s: (z, 0, 0, n))] * 4,
            ),
            out_shape=[jax.ShapeDtypeStruct((net.deep, 2, cut, self.columns), BF16)] * 4,
            compiler_params=params(2),
            cost_estimate=cost(0, 6 * self.keep[0].size),
            name="add_cores",
        )(self.bits, *self.keep, *self.got)
        self.keep = [made[0], made[2]]
        self.got = [net.swap(made[1], net.Y), net.swap(made[3], net.X)]

    def third(self):
        net, cut = self.net, self.rows // 2

        def kernel(sc_ref, k0, k1, g0, g1, *outs):
            for half, (keep, got) in enumerate(((k0, g0), (k1, g1))):
                for role in range(2):
                    at = sc_ref[1 - half] ^ role
                    outs[2 * half + role][...] = add_bf16(keep[:, at], got[:, at])

        out = jax.ShapeDtypeStruct((net.deep, cut, self.columns), BF16)
        made = self.call(kernel, [*self.keep, *self.got], [out] * 4, "add_second")
        self.keep = [made[0], made[2]]
        self.got = [net.swap(made[1], net.X), net.swap(made[3], net.Y)]

    def fourth(self):
        net, rows, cut = self.net, self.rows, self.rows // 2

        def kernel(sc_ref, k0, k1, g0, g1, *outs):
            for away, out in enumerate(outs):
                at = (sc_ref[2] + net.deep - away) % net.deep
                out[:cut] = add_bf16(k0[at], g0[at])
                out[cut:] = add_bf16(k1[at], g1[at])

        out = jax.ShapeDtypeStruct((rows, self.columns), BF16)
        made = self.call(kernel, [*self.keep, *self.got], [out] * net.deep, "add_third")
        self.keep = [made[0]]
        self.got = [net.from_z(made[k], k) for k in range(1, net.deep)]

    def total(self):
        return self.keep[0].astype(F32) + sum(v.astype(F32) for v in self.got)

    def call(self, kernel, args, outs, name):
        return pl.pallas_call(
            kernel,
            grid_spec=pltpu.PrefetchScalarGridSpec(
                num_scalar_prefetch=1,
                grid=(1,),
                in_specs=[pl.BlockSpec(memory_space=pltpu.VMEM)] * len(args),
                out_specs=[pl.BlockSpec(memory_space=pltpu.VMEM)] * len(outs),
            ),
            out_shape=outs,
            compiler_params=params(1),
            cost_estimate=cost(0, 6 * sum(v.size for v in args)),
            name=name,
        )(self.bits, *args)


def tie(value, *others):
    return lax.optimization_barrier((value,) + others)[0]


def tie2(values, others):
    return lax.optimization_barrier((*values, *others))[: len(values)]


def body(
    tokens, cond, lengths, ada_w, ada_b, w_qkv, w_out, w_up, b_up, w_down, b_down,
    rel_table, bucket, cotangent,
):
    axes = ("clip", "win")
    sz = Sizes(tokens)
    net = Net()
    devices, index = net.count, net.index
    clips = lax.axis_size("clip")
    width = sz.width
    core = lax.axis_index("win") % 2
    swap = [(n, n ^ 1) for n in range(lax.axis_size("win"))]
    place_in = jnp.arange(3 + sz.micro, dtype=jnp.int32)
    scalars = jnp.where(place_in == 0, core, jnp.where(place_in == 1 + sz.micro, index % 8, index // 8))
    for n in range(sz.micro):
        scalars = jnp.where(place_in == 1 + n, lengths[n, 0], scalars)
    strip = (sz.micro, 2, 2, sz.frames, sz.half, width)
    tok = tokens.reshape(strip)
    cot = cotangent.reshape(strip)

    cond_act = jax.nn.silu(cond[:, 0].astype(F32)).astype(BF16)
    rows = ada_w.shape[0]
    small = jnp.concatenate([b_up, b_down, rel_table.reshape(-1)])
    n_cond = cond_act.size
    if net.direct:
        early = jnp.concatenate([cond_act.reshape(-1), small])
        early = net.gather_clips(jnp.pad(early, (0, -early.size % 128)))
        cond_all = early[:, :, :n_cond].reshape(early.shape[:2] + cond_act.shape)
    else:
        cond_all = lax.all_gather(cond_act, "clip", axis=0)
    cond_mine = lax.dynamic_slice_in_dim(cond_all, index * rows, rows, cond_all.ndim - 1)
    lead = cond_mine.shape[:-1]
    cond_mine = cond_mine.reshape(clips * sz.micro, rows)
    mod_part = dot_nn(cond_mine, ada_w)
    spread_b = jnp.zeros((mod_part.shape[1],), F32)
    spread_b = lax.dynamic_update_slice(spread_b, ada_b.astype(F32), (index * ada_b.shape[0],))
    mod_part = (mod_part + spread_b[None, :]).reshape(lead + (6 * width,))
    notes = []
    if net.direct:
        mod = net.scatter_clips(mod_part, notes)
        mod = net.swap_sum(net.swap_sum(mod, net.CORE), net.X)
    else:
        mod = lax.psum_scatter(mod_part, "clip", scatter_dimension=0, tiled=False)
        mod = lax.psum(mod, "win")
    mod = mod.reshape(sz.micro, 6, width)

    cols = width // 2
    by_group = w_qkv.reshape(rows, 3, sz.groups, sz.gcols).transpose(0, 2, 1, 3)
    by_group = by_group.reshape(rows, 2, 3 * cols)
    shard_q = [by_group[:, n] for n in range(2)]
    inner = w_up.shape[1]
    per = w_down.shape[0] // 2
    thin = CHUNK // devices

    def inner_order(value):
        if not net.direct:
            value = value.reshape(-1, devices, 2, per).transpose(2, 0, 1, 3)
        else:
            value = value.reshape(-1, devices // 2, 2, 2, per // thin, thin)
            value = value.transpose(3, 0, 4, 2, 1, 5)
        return value.reshape(2, -1, inner // 2)

    def inner_back(halves):
        value = jnp.stack(halves)
        if not net.direct:
            value = value.reshape(2, -1, devices, per).transpose(1, 2, 0, 3)
        else:
            value = value.reshape(2, -1, per // thin, 2, devices // 2, thin)
            value = value.transpose(1, 4, 3, 0, 2, 5)
        return value.reshape(-1, inner)

    def pack_inner(up, down):
        down = down.reshape(per // thin, thin, 2, width // 2).transpose(2, 1, 0, 3)
        down = down.reshape(rows, per // thin, width // 2)
        return jnp.concatenate([up.reshape(rows, -1, CHUNK), down], axis=2).reshape(rows, -1)

    def unpack_inner(value):
        value = value.reshape(rows, per // thin, -1)
        down = value[:, :, CHUNK:].reshape(2, thin, per // thin, width // 2)
        return value[:, :, :CHUNK].reshape(rows, -1), down.transpose(2, 1, 0, 3).reshape(per, width)

    shard_u = inner_order(w_up)
    shard_d = [w_down[:per], w_down[per:]]
    gather = lambda v: lax.all_gather(v, axes, axis=0, tiled=True)
    if net.direct:
        packs = [
            shard_q[0],
            jnp.concatenate([shard_q[1], w_out], axis=1),
            pack_inner(shard_u[1], shard_d[1]),
            pack_inner(shard_u[0], shard_d[0]),
        ]
        rest_q = gather(packs[1])
        rest = gather(tie(packs[2], early))
        (one,) = Gather.along_z(net, [packs[0]])
        small = net.gather_pairs(tie(early[:, :, n_cond:], *notes))
        one.halves = tie2(one.halves, [mod_part])
        one.start(True)
        one.join()
        one.halves = tie2(one.halves, notes[:1])
        one.start(False)
        three_pack = tie(packs[3], notes[0])
        three_got = tie2(Gather.send_z(net, three_pack), one.got)
        (three,) = Gather.cut(net, three_pack, three_got, [packs[3].shape[1]])
        one.core()
        full_q = [one.pieces(), Pieces([rest_q])]
        full_out = full_q[1]
    else:
        full_q = [Pieces([gather(v)]) for v in shard_q]
        full_out = Pieces([gather(w_out)])
        full_i = [[Pieces([gather(u)]), Pieces([gather(d)])] for u, d in zip(shard_u, shard_d)]
        small = gather(small[None])
    n_up, n_down = b_up.shape[0], b_down.shape[0]
    n_small = n_up + n_down + rel_table.size
    full_bup = inner_order(small[:, :n_up].astype(F32).reshape(1, inner))
    full_bdown = small[:, n_up : n_up + n_down].astype(F32).reshape(1, width)
    table = small[:, n_up + n_down : n_small].reshape(-1, HEADS)
    places = offset_onehot(core, sz)
    bias = bias_blocks(table, bucket, places, sz)

    if net.direct:
        mod = tie(mod, bias, *three.halves)
    own, send = first_norm(tok, mod, scalars, sz)
    far = lax.ppermute(send, "win", swap)
    if net.direct:
        three.start(True)
    first = attention(0, own, far, full_q[0], bias, scalars, sz)
    if net.direct:
        three.tie(first[2])
        three.join()
        three.start(False)
        first = tie2(first, three.halves)
    qkv, wide, att_1, wide_out, branch_own, branch_send = attention(
        1, own, far, full_q[1], bias, scalars, sz, first, full_out
    )
    if net.direct:
        three.tie(branch_own)
        branch_send = tie(branch_send, *three.got)
    branch_far = lax.ppermute(branch_send, "win", swap)
    hidden_two, grad_mlp = second_norm(tok, cot, branch_own, branch_far, mod, scalars, sz)
    flat = (sz.rows, width)
    both = (2, sz.micro, sz.used, sz.half, width)
    hidden_two, grad_mlp = hidden_two.reshape(flat), grad_mlp.reshape(flat)
    if net.direct:
        three.tie(branch_far)
        three.halves = tie2(three.halves, [branch_far])
        three.core()
        full_i = [[three.pieces()], [Pieces([rest])]]
    mlps = []
    for n in range(2):
        shard = rows if net.direct and n == 1 else None
        mlps.append(
            mlp(hidden_two, grad_mlp, full_i[n], full_bup[n], scalars, sz, shard, n == 0)
        )
        if net.direct and n == 0:
            pack, hidden_two = lax.optimization_barrier((mlps[0][4], hidden_two))
            r_first = lax.psum_scatter(pack, axes, scatter_dimension=0, tiled=True).astype(F32)

    if net.direct:
        second = Scatter(net, mlps[1][3:5])
    output, grad_mid, grad_own, grad_send, sums_two = after_mlp(
        tok, cot, branch_own, branch_far, [v[0].reshape(both) for v in mlps],
        [v[1].reshape(both) for v in mlps], mod, full_bdown, scalars, sz,
    )
    grad_far = lax.ppermute(grad_send, "win", swap)
    if net.direct:
        second.tie(grad_own)
        second.second()
        grad_own = tie(grad_own, *second.keep)
    *g_att, fold, hid_own, hid_send = attention_back(
        grad_own, grad_far, own, far, qkv, (first[2], att_1), wide, wide_out, bias, scalars, sz,
        rows if net.direct else None,
    )
    if net.direct:
        second.tie(hid_own)
        g_att = tie2(g_att, second.got)
        hid_send = tie(hid_send, *second.got)
        heads = Scatter(net, g_att)
        hid_far = lax.ppermute(hid_send, "win", swap)
        second.third()
        heads.tie(*second.keep)
        heads.second()
        hid_far = tie(hid_far, r_first, *heads.keep)
    else:
        hid_far = lax.ppermute(hid_send, "win", swap)
    grad_in, sums_one = last_norm(tok, cot, grad_mid, hid_own, hid_far, mod, scalars, sz)
    if net.direct:
        second.tie(sums_one)
        second.fourth()
        sums_one, fold = lax.optimization_barrier((sums_one, fold, *second.keep))[:2]

    grad_mod = jnp.concatenate(
        [sums_one, sums_two[:, 3:4], sums_two[:, 0:3]], axis=1
    ).reshape(sz.micro, 6 * width)
    g_table = table_grad(offset_grad(fold, places, sz), bucket, table.shape[0]).reshape(devices, -1)
    if net.direct:
        heads.tie(g_table)
        heads.third()
        second.tie(*heads.keep)
        r_second = second.total()
        g_table = tie(g_table, r_second)
    g_bup = inner_back([v[2] for v in mlps]).reshape(devices, -1)
    g_bdown = mlps[0][3].reshape(devices, -1)
    g_small = jnp.concatenate([g_bup, g_bdown, g_table], axis=1)
    if net.direct:
        every = jnp.concatenate([grad_mod.reshape(-1), g_small.reshape(-1)])
        every = net.swap_sum(net.swap_sum(every, net.CORE), net.X)
        heads.tie(every)
        heads.fourth()
        every = net.gather_clips(tie(every, *heads.keep))
        mod_all = every[:, :, : grad_mod.size]
        g_small = jnp.sum(every[:, :, grad_mod.size :], axis=(0, 1)).reshape(g_small.shape)
        g_small = lax.dynamic_index_in_dim(g_small, index, 0, keepdims=False)
    else:
        mod_all = lax.all_gather(lax.psum(grad_mod, "win"), "clip", axis=0)
        g_small = lax.psum_scatter(g_small, axes, scatter_dimension=0, tiled=False)
    mod_all = mod_all.reshape(clips * sz.micro, -1)
    grad_ada_w = lax.dot_general(
        cond_mine.astype(F32), mod_all, (((0,), (0,)), ((), ())),
        precision=HIGHEST, preferred_element_type=F32,
    )
    grad_ada_b = lax.dynamic_slice_in_dim(
        jnp.sum(mod_all, axis=0), index * ada_b.shape[0], ada_b.shape[0]
    )
    if net.direct:
        r_u, r_d = zip(unpack_inner(r_first), unpack_inner(r_second))
        mine = heads.total().reshape(rows, sz.groups, -1)
        r_qkv = mine[:, :, : 3 * sz.gcols]
        r_out = mine[:, :, 3 * sz.gcols :].reshape(rows, width)
    else:
        scatter = lambda v: lax.psum_scatter(
            v.astype(F32), axes, scatter_dimension=0, tiled=True
        )
        r_u = [scatter(v[-2]) for v in mlps]
        r_d = [scatter(v[-1]) for v in mlps]
        r_qkv, r_out = scatter(g_att[0]), scatter(g_att[1])
    r_up = inner_back(r_u)
    r_down = jnp.concatenate(r_d)
    r_qkv = r_qkv.reshape(rows, sz.groups, 3, sz.gcols).transpose(0, 2, 1, 3)
    r_qkv = r_qkv.reshape(rows, 3 * width)
    return (
        output.reshape(tokens.shape), grad_in.reshape(tokens.shape), grad_ada_w, grad_ada_b,
        r_qkv, r_out, r_up, g_small[:n_up], r_down, g_small[n_up : n_up + n_down],
        g_small[n_up + n_down :].reshape(rel_table.shape),
    )


def solution(mesh):
    weights = P(("clip", "win"), None)
    vector = P(("clip", "win"))
    strips = P(None, "clip", "win", None, None, None, None, None)
    return jax.shard_map(
        body,
        mesh=mesh,
        in_specs=(
            strips, P(None, "clip", None), P(None, "clip"), weights, vector, weights, weights,
            weights, vector, weights, vector, weights, P(), strips,
        ),
        out_specs=(
            strips, strips, weights, vector, weights, weights, weights, vector, weights, vector,
            weights,
        ),
        check_vma=False,
    )
```

```python
import functools
import math

import jax
import jax.numpy as jnp
from jax import lax
from jax.experimental import pallas as pl
from jax.experimental.pallas import tpu as pltpu
from jax.sharding import PartitionSpec as P

HEADS = 16
EPSILON = 1e-06
MASKED = -1000000000.0
F32 = jnp.float32
BF16 = jnp.bfloat16
VMEM_LIMIT = 58 * 1024 * 1024
HIGHEST = lax.Precision.HIGHEST


def dot_nn(a, b):
    return lax.dot_general(a, b, (((1,), (0,)), ((), ())), preferred_element_type=F32)


def dot_nt(a, b):
    return lax.dot_general(a, b, (((1,), (1,)), ((), ())), preferred_element_type=F32)


def dot_tn(a, b):
    return lax.dot_general(a, b, (((0,), (0,)), ((), ())), preferred_element_type=F32)


def params(count):
    return pltpu.CompilerParams(
        dimension_semantics=("arbitrary",) * count, vmem_limit_bytes=VMEM_LIMIT
    )


def cost(flops, size):
    return pl.CostEstimate(flops=flops, bytes_accessed=size, transcendentals=0)


def once(shape, index_map):
    return pl.BlockSpec(shape, index_map, pipeline_mode=pl.Buffered(1))


def normalize(values):
    centered = values - jnp.mean(values, axis=-1, keepdims=True)
    inv = lax.rsqrt(jnp.mean(centered * centered, axis=-1, keepdims=True) + EPSILON)
    return centered * inv, inv


def norm_back(grad, normed, inv):
    return inv * (
        grad
        - jnp.mean(grad, axis=-1, keepdims=True)
        - normed * jnp.mean(grad * normed, axis=-1, keepdims=True)
    )


class Sizes:
    def __init__(self, tokens):
        self.micro, _, _, self.blocks, self.frames, rows, side, self.width = tokens.shape
        self.half = rows * side
        self.cols = self.blocks // 2
        self.strip_rows, self.side = rows, side
        self.used = 2 * self.frames - 1
        self.frame = 2 * self.half
        self.win_rows = self.used * self.frame
        self.rows = self.micro * self.win_rows
        self.lens = (self.frames * self.frame, (self.frames - 1) * self.frame)
        self.head = self.width // HEADS
        self.group = 4
        self.gcols = self.group * self.head
        self.groups = HEADS // self.group


def each_frame(body, sz):
    for tw in range(2):

        def step(t, carry, tw=tw):
            body(tw, t, tw * sz.frames + t)
            return carry

        lax.fori_loop(0, sz.frames - tw, step, 0, unroll=True)


def fold_rows(value):
    return jnp.sum(value.reshape(-1, 8, value.shape[-1]), axis=0)


def first_norm(tok, mod, core, sz):
    def kernel(sc_ref, x_ref, mod_ref, own_ref, far_ref):
        shift = mod_ref[0, 0:1, :]
        scale = 1.0 + mod_ref[0, 1:2, :]
        for slot, out_ref in enumerate((own_ref, far_ref)):
            column = sc_ref[0] ^ slot

            def one(tw, t, f, column=column, out_ref=out_ref):
                normed, _ = normalize(x_ref[0, tw, column, t].astype(F32))
                out_ref[0, f] = (normed * scale + shift).astype(BF16)

            each_frame(one, sz)

    strip = (1, 2, 2, sz.frames, sz.half, sz.width)
    piece = (1, sz.used, sz.half, sz.width)
    shape = jax.ShapeDtypeStruct((sz.micro,) + piece[1:], BF16)
    return pl.pallas_call(
        kernel,
        grid_spec=pltpu.PrefetchScalarGridSpec(
            num_scalar_prefetch=1,
            grid=(sz.micro,),
            in_specs=[
                pl.BlockSpec(strip, lambda m, s: (m, 0, 0, 0, 0, 0)),
                pl.BlockSpec((1, 6, sz.width), lambda m, s: (m, 0, 0)),
            ],
            out_specs=[pl.BlockSpec(piece, lambda m, s: (m, 0, 0, 0))] * 2,
        ),
        out_shape=[shape, shape],
        compiler_params=params(1),
        name="first_norm",
    )(core, tok, mod)


def second_norm(tok, cot, branch_own, branch_far, mod, scalars, sz):
    def kernel(sc_ref, x_ref, c_ref, bo_ref, bf_ref, mod_ref, h_ref, g_ref):
        length = sc_ref[1 + pl.program_id(0)]
        gate1 = mod_ref[0, 2:3, :]
        shift = mod_ref[0, 3:4, :]
        scale = 1.0 + mod_ref[0, 4:5, :]
        gate2 = mod_ref[0, 5:6, :]
        for slot, b_ref in enumerate((bo_ref, bf_ref)):
            column = sc_ref[0] ^ slot

            def one(tw, t, f, slot=slot, column=column, b_ref=b_ref):
                rows = x_ref[0, tw, column, t].astype(F32) + gate1 * b_ref[0, f].astype(F32)
                normed, _ = normalize(rows)
                h_ref[slot, 0, f] = (normed * scale + shift).astype(BF16)
                valid = (f < length).astype(F32)
                g_ref[slot, 0, f] = (c_ref[0, tw, column, t].astype(F32) * (valid * gate2)).astype(BF16)

            each_frame(one, sz)

    strip = (1, 2, 2, sz.frames, sz.half, sz.width)
    piece = (1, sz.used, sz.half, sz.width)
    both = (2, 1, sz.used, sz.half, sz.width)
    shape = jax.ShapeDtypeStruct((2, sz.micro, sz.used, sz.half, sz.width), BF16)
    return pl.pallas_call(
        kernel,
        grid_spec=pltpu.PrefetchScalarGridSpec(
            num_scalar_prefetch=1,
            grid=(sz.micro,),
            in_specs=[
                pl.BlockSpec(strip, lambda m, s: (m, 0, 0, 0, 0, 0)),
                pl.BlockSpec(strip, lambda m, s: (m, 0, 0, 0, 0, 0)),
                pl.BlockSpec(piece, lambda m, s: (m, 0, 0, 0)),
                pl.BlockSpec(piece, lambda m, s: (m, 0, 0, 0)),
                pl.BlockSpec((1, 6, sz.width), lambda m, s: (m, 0, 0)),
            ],
            out_specs=[pl.BlockSpec(both, lambda m, s: (0, m, 0, 0, 0))] * 2,
        ),
        out_shape=[shape, shape],
        compiler_params=params(1),
        name="second_norm",
    )(scalars, tok, cot, branch_own, branch_far, mod)


def after_mlp(tok, cot, branch_own, branch_far, mlps, grads, mod, b_down, scalars, sz):
    def kernel(
        sc_ref, x_ref, c_ref, bo_ref, bf_ref, y0_ref, y1_ref, t0_ref, t1_ref, mod_ref, bd_ref,
        out_ref, gm_ref, go_ref, gf_ref, sum_ref, sums,
    ):
        length = sc_ref[1 + pl.program_id(0)]
        gate1 = mod_ref[0, 2:3, :]
        scale = 1.0 + mod_ref[0, 4:5, :]
        gate2 = mod_ref[0, 5:6, :]
        sums[...] = jnp.zeros_like(sums)
        for slot, (b_ref, g_ref) in enumerate(((bo_ref, go_ref), (bf_ref, gf_ref))):
            column = sc_ref[0] ^ slot

            def one(tw, t, f, slot=slot, column=column, b_ref=b_ref, g_ref=g_ref):
                valid = (f < length).astype(F32)
                branch = b_ref[0, f].astype(F32)
                middle = x_ref[0, tw, column, t].astype(F32) + gate1 * branch
                normed, inv = normalize(middle)
                y = y0_ref[slot, 0, f] + y1_ref[slot, 0, f] + bd_ref[0:1, :]
                grad = c_ref[0, tw, column, t].astype(F32)
                out_ref[0, tw, column, t] = (middle + valid * gate2 * y).astype(BF16)
                two = t0_ref[slot, 0, f] + t1_ref[slot, 0, f]
                gm = grad + norm_back(two * scale, normed, inv)
                gm_ref[slot, 0, f] = gm
                g_ref[0, f] = (valid * (gm * gate1)).astype(BF16)
                for n, term in enumerate((two, two * normed, grad * valid * y, gm * branch)):
                    sums[n] += fold_rows(term)

            each_frame(one, sz)
            out_ref[0, 1, column, sz.frames - 1] = x_ref[0, 1, column, sz.frames - 1]
        for n in range(4):
            sum_ref[0, n : n + 1, :] = jnp.sum(sums[n], axis=0, keepdims=True)

    strip = (1, 2, 2, sz.frames, sz.half, sz.width)
    piece = (1, sz.used, sz.half, sz.width)
    both = (2, 1, sz.used, sz.half, sz.width)
    full = (sz.micro,) + piece[1:]
    at_strip = lambda m, s: (m, 0, 0, 0, 0, 0)
    at_piece = lambda m, s: (m, 0, 0, 0)
    at_both = lambda m, s: (0, m, 0, 0, 0)
    return pl.pallas_call(
        kernel,
        grid_spec=pltpu.PrefetchScalarGridSpec(
            num_scalar_prefetch=1,
            grid=(sz.micro,),
            in_specs=[
                pl.BlockSpec(strip, at_strip),
                pl.BlockSpec(strip, at_strip),
                pl.BlockSpec(piece, at_piece),
                pl.BlockSpec(piece, at_piece),
                pl.BlockSpec(both, at_both),
                pl.BlockSpec(both, at_both),
                pl.BlockSpec(both, at_both),
                pl.BlockSpec(both, at_both),
                pl.BlockSpec((1, 6, sz.width), lambda m, s: (m, 0, 0)),
                pl.BlockSpec((1, sz.width), lambda m, s: (0, 0)),
            ],
            out_specs=[
                pl.BlockSpec(strip, at_strip),
                pl.BlockSpec(both, at_both),
                pl.BlockSpec(piece, at_piece),
                pl.BlockSpec(piece, at_piece),
                pl.BlockSpec((1, 4, sz.width), lambda m, s: (m, 0, 0)),
            ],
            scratch_shapes=[pltpu.VMEM((4, 8, sz.width), F32)],
        ),
        out_shape=[
            jax.ShapeDtypeStruct(tok.shape, BF16),
            jax.ShapeDtypeStruct((2,) + full, F32),
            jax.ShapeDtypeStruct(full, BF16),
            jax.ShapeDtypeStruct(full, BF16),
            jax.ShapeDtypeStruct((sz.micro, 4, sz.width), F32),
        ],
        compiler_params=params(1),
        name="after_mlp",
    )(scalars, tok, cot, branch_own, branch_far, *mlps, *grads, mod, b_down)


def last_norm(tok, cot, grad_mid, grad_own, grad_far, mod, scalars, sz):
    def kernel(sc_ref, x_ref, c_ref, gm_ref, go_ref, gf_ref, mod_ref, out_ref, sum_ref, sums):
        scale = 1.0 + mod_ref[0, 1:2, :]
        sums[...] = jnp.zeros_like(sums)
        for slot, g_ref in enumerate((go_ref, gf_ref)):
            column = sc_ref[0] ^ slot

            def one(tw, t, f, slot=slot, column=column, g_ref=g_ref):
                normed, inv = normalize(x_ref[0, tw, column, t].astype(F32))
                grad = g_ref[0, f].astype(F32)
                total = gm_ref[slot, 0, f] + norm_back(grad * scale, normed, inv)
                out_ref[0, tw, column, t] = total.astype(BF16)
                sums[0] += fold_rows(grad)
                sums[1] += fold_rows(grad * normed)

            each_frame(one, sz)
        for slot in range(2):
            out_ref[0, 1, slot, sz.frames - 1] = c_ref[0, 0, slot, 0]
        for n in range(2):
            sum_ref[0, n : n + 1, :] = jnp.sum(sums[n], axis=0, keepdims=True)

    strip = (1, 2, 2, sz.frames, sz.half, sz.width)
    tail = (1, 1, 2, 1, sz.half, sz.width)
    piece = (1, sz.used, sz.half, sz.width)
    both = (2, 1, sz.used, sz.half, sz.width)
    return pl.pallas_call(
        kernel,
        grid_spec=pltpu.PrefetchScalarGridSpec(
            num_scalar_prefetch=1,
            grid=(sz.micro,),
            in_specs=[
                pl.BlockSpec(strip, lambda m, s: (m, 0, 0, 0, 0, 0)),
                pl.BlockSpec(tail, lambda m, s: (m, 1, 0, sz.frames - 1, 0, 0)),
                pl.BlockSpec(both, lambda m, s: (0, m, 0, 0, 0)),
                pl.BlockSpec(piece, lambda m, s: (m, 0, 0, 0)),
                pl.BlockSpec(piece, lambda m, s: (m, 0, 0, 0)),
                pl.BlockSpec((1, 6, sz.width), lambda m, s: (m, 0, 0)),
            ],
            out_specs=[
                pl.BlockSpec(strip, lambda m, s: (m, 0, 0, 0, 0, 0)),
                pl.BlockSpec((1, 2, sz.width), lambda m, s: (m, 0, 0)),
            ],
            scratch_shapes=[pltpu.VMEM((2, 8, sz.width), F32)],
        ),
        out_shape=[
            jax.ShapeDtypeStruct(tok.shape, BF16),
            jax.ShapeDtypeStruct((sz.micro, 2, sz.width), F32),
        ],
        compiler_params=params(1),
        name="last_norm",
    )(scalars, tok, cot, grad_mid, grad_own, grad_far, mod)


class Pieces:
    def __init__(self, arrays):
        self.arrays = arrays
        self.whole = len(arrays) == 1

    def specs(self, columns, index_map):
        if self.whole:
            at = lambda *g: (0, index_map(*g))
            return [pl.BlockSpec((self.arrays[0].shape[0], columns), at)]
        at = lambda *g: (0, 0, 0, index_map(*g))
        shape = self.arrays[0].shape[:-1] + (columns,)
        return [pl.BlockSpec(shape, at)] * 8


def pieces_of(refs, key, z_here):
    depth = refs[0].shape[1]
    for z in range(depth):
        for n in range(8):
            half, far, i = n // 4, n // 2 % 2, n % 2
            for j in range(2):
                away = (i * 4 + j * 2 if half == 0 else i * 2 + j * 4) + far
                yield (z_here + z) % depth, key ^ away, half, refs[n].at[j, z]


def place(refs, key, z_here, out_ref, columns=slice(None), source=slice(None)):
    if len(refs) == 1:
        out_ref[:, columns] = refs[0][:, source]
        return
    for z, at, half, piece in pieces_of(refs, key, z_here):
        cut = piece.shape[0]
        row = pl.multiple_of((z * 8 + at) * (2 * cut) + half * cut, cut)
        out_ref[pl.ds(row, cut), columns] = piece[:, source]


def place_inner(refs, key, z_here, out_ref, source):
    size = source.stop - source.start
    if len(refs) == 1:
        cut = out_ref.shape[0] // 32
        for n in range(64):
            at, half = n // 2, n % 2
            to = (at % 2) * (16 * cut) + at // 2 * cut
            out_ref[to : to + cut, half * size : (half + 1) * size] = refs[0][
                n * cut : (n + 1) * cut, source
            ]
        return
    for z, at, half, piece in pieces_of(refs, key, z_here):
        cut = piece.shape[0]
        row = pl.multiple_of((at % 2) * (16 * cut) + (z * 4 + at // 2) * cut, cut)
        out_ref[pl.ds(row, cut), half * size : (half + 1) * size] = piece[:, source]


def turn(value, out_ref, core, shard, start=0):
    turned = value.T
    if shard is None:
        out_ref[start : start + turned.shape[0]] = turned
        return
    height = out_ref.shape[0]
    for n in range(turned.shape[0] // shard):
        at = start // shard + n
        at = (core ^ (at % 2)) * (height // 2) + at // 2 * shard
        out_ref[pl.ds(pl.multiple_of(at, shard), shard), :] = turned[n * shard : (n + 1) * shard]


def give(refs, half, low, value, start=0):
    value = value.astype(BF16)
    columns = slice(start, start + value.shape[1])
    if len(refs) == 1:
        low = half * (refs[0].shape[0] // 2) + low
        refs[0][low : low + value.shape[0], columns] = value
        return
    rows = refs[half].shape[1]
    refs[half][low // rows : (low + value.shape[0]) // rows, :, columns] = value.reshape(
        value.shape[0] // rows, rows, value.shape[1]
    )


def grad_shapes(direct, rows, height, columns):
    if not direct:
        return [jax.ShapeDtypeStruct((height, columns), BF16)]
    return [jax.ShapeDtypeStruct((height // (2 * rows), rows, columns), BF16)] * 2


def grad_specs(direct, rows, height, columns, at_column):
    if not direct:
        return [pl.BlockSpec((height, columns), lambda *g: (0, at_column(*g)))]
    shape = (height // (2 * rows), rows, columns)
    return [pl.BlockSpec(shape, lambda *g: (0, 0, at_column(*g)))] * 2


def join_frames(own_ref, far_ref, joined_ref, sz):
    for m in range(sz.micro):
        for f in range(sz.used):
            at = m * sz.win_rows + f * sz.frame
            joined_ref[at : at + sz.half] = own_ref[m, f]
            joined_ref[at + sz.half : at + sz.frame] = far_ref[m, f]


def spread_bias(block_ref, head, bias_ref, sz, turned=False):
    size = sz.frame
    for step in range(2 * sz.frames - 1):
        block = block_ref[head, step]
        if turned:
            block = block.T
        for key in range(sz.frames):
            query = key + step - (sz.frames - 1)
            if 0 <= query < sz.frames:
                row, column = (key, query) if turned else (query, key)
                bias_ref[row * size : (row + 1) * size, column * size : (column + 1) * size] = block


def window_rows(m, tw, sz):
    start = pl.multiple_of(m * sz.win_rows + tw * sz.lens[0], sz.frame)
    return pl.ds(start, sz.lens[tw])


def attention(half, own, far, w_qkv, bias, scalars, sz, first=None, w_out=None):
    scale = 1.0 / math.sqrt(sz.head)
    last = w_out is not None
    steps = sz.groups // 2
    gcols = sz.gcols
    joint = w_out is w_qkv
    n_out = 2 * len(w_qkv.arrays) if joint else 1

    def kernel(sc_ref, own_ref, far_ref, bias_ref, *refs):
        refs = list(refs)
        take = lambda count: [refs.pop(0) for _ in range(count)]
        w_refs = take(len(w_qkv.arrays))
        if last:
            (first_ref,) = take(1)
            out_refs = take(n_out)
            take(2)
        qkv_ref, w_ref, att_ref = take(3)
        if last:
            wo_ref, bo_ref, bf_ref = take(3)
        joined, spread = take(2)
        step = pl.program_id(0)
        key, z_here = sc_ref[1 + sz.micro], sc_ref[2 + sz.micro]

        @pl.when(step == 0)
        def _():
            join_frames(own_ref, far_ref, joined, sz)

        place(w_refs, key, z_here, w_ref)
        for n in range(3):
            part = dot_nn(joined[...], w_ref[:, n * gcols : (n + 1) * gcols]).astype(BF16)
            qkv_ref[n] = part * scale if n == 0 else part
        for head in range(sz.group):
            spread_bias(bias_ref, head, spread.at[head], sz)

        def one_micro(m, carry):
            for tw in range(2):
                size = sz.lens[tw]
                rows = window_rows(m, tw, sz)
                keys_ok = (sc_ref[1 + m] - tw * sz.frames) * sz.frame

                @pl.when(keys_ok > 0)
                def _(rows=rows, size=size, keys_ok=keys_ok):
                    column = lax.broadcasted_iota(jnp.int32, (1, size), 1)
                    for head in range(sz.group):
                        lanes = slice(head * sz.head, (head + 1) * sz.head)
                        scores = dot_nt(qkv_ref[0, rows, lanes], qkv_ref[1, rows, lanes])
                        scores = scores + spread[head, :size, :size].astype(F32)
                        scores = jnp.where(column < keys_ok, scores, MASKED)
                        top = jnp.max(scores, axis=-1, keepdims=True)
                        weight = jnp.exp(scores - top)
                        share = 1.0 / jnp.sum(weight, axis=-1, keepdims=True)
                        probs = (weight * share).astype(BF16)
                        att_ref[rows, lanes] = dot_nn(probs, qkv_ref[2, rows, lanes]).astype(BF16)

                @pl.when(keys_ok <= 0)
                def _(rows=rows, size=size):
                    att_ref[rows, :] = jnp.zeros((size, gcols), BF16)

            return carry

        lax.fori_loop(0, sz.micro, one_micro, 0)
        if not last:
            return
        kept, total = take(2)
        for n in range(steps):

            @pl.when(step == n)
            def _(n=n):
                kept[:, n * gcols : (n + 1) * gcols] = att_ref[...]

        @pl.when(step == steps - 1)
        def _():
            if joint:
                place(out_refs[: n_out // 2], key, z_here, wo_ref, slice(0, 2 * gcols))
                place(out_refs[n_out // 2 :], key, z_here, wo_ref, slice(2 * gcols, 4 * gcols))
            else:
                place(out_refs, key, z_here, wo_ref)
            middle = first_ref.shape[1]
            total[...] = dot_nn(first_ref[...], wo_ref[:middle]) + dot_nn(
                kept[...], wo_ref[middle:]
            )
            for m in range(sz.micro):
                for f in range(sz.used):
                    at = m * sz.win_rows + f * sz.frame
                    valid = (f < sc_ref[1 + m]).astype(F32)
                    bo_ref[m, f] = (total[at : at + sz.half] * valid).astype(BF16)
                    bf_ref[m, f] = (total[at + sz.half : at + sz.frame] * valid).astype(BF16)

    piece = (sz.micro, sz.used, sz.half, sz.width)
    fixed = lambda g, s: (0, 0, 0, 0)
    flat = lambda g, s: (0, 0)
    width, cols = sz.width, sz.width // 2
    in_specs = [
        once(piece, fixed),
        once(piece, fixed),
        pl.BlockSpec((sz.group,) + bias.shape[1:], lambda g, s: (half * steps + g, 0, 0, 0)),
    ] + w_qkv.specs(3 * gcols, lambda g, s: g)
    out_specs = [
        pl.BlockSpec((3, sz.rows, gcols), lambda g, s: (0, 0, half * steps + g)),
        pl.BlockSpec((width, 3 * gcols), lambda g, s: (0, half * steps + g)),
        pl.BlockSpec((sz.rows, gcols), lambda g, s: (0, g)),
    ]
    out_shape = [
        jax.ShapeDtypeStruct((3, sz.rows, width), BF16),
        jax.ShapeDtypeStruct((width, 3 * width), BF16),
        jax.ShapeDtypeStruct((sz.rows, cols), BF16),
    ]
    aliases = {}
    scratch = [
        pltpu.VMEM((sz.rows, width), BF16),
        pltpu.VMEM((sz.group, sz.lens[0], sz.lens[0]), BF16),
    ]
    args = [scalars, own, far, bias, *w_qkv.arrays]
    flops = 6 * sz.rows * width * cols + 4 * sz.rows * sz.lens[0] * cols
    if last:
        in_specs += [once((sz.rows, cols), flat)]
        if joint:
            low = w_out.arrays[0].shape[-1] // (2 * gcols) - 2
            in_specs += w_out.specs(2 * gcols, lambda g, s: low)
            in_specs += w_out.specs(2 * gcols, lambda g, s: low + 1)
            out_args = w_out.arrays * 2
        else:
            in_specs += w_out.specs(width, lambda g, s: 0)
            out_args = w_out.arrays
        out_specs += [pl.BlockSpec((width, width), flat)] + [pl.BlockSpec(piece, fixed)] * 2
        out_shape += [jax.ShapeDtypeStruct((width, width), BF16)]
        out_shape += [jax.ShapeDtypeStruct(piece, BF16)] * 2
        scratch += [pltpu.VMEM((sz.rows, cols), BF16), pltpu.VMEM((sz.rows, width), F32)]
        args += [first[2], *out_args]
        aliases = {len(args): 0, len(args) + 1: 1}
        in_specs += [pl.BlockSpec(memory_space=pl.ANY)] * 2
        args += first[:2]
        flops += 2 * sz.rows * width * width
    return pl.pallas_call(
        kernel,
        grid_spec=pltpu.PrefetchScalarGridSpec(
            num_scalar_prefetch=1,
            grid=(steps,),
            in_specs=in_specs,
            out_specs=out_specs,
            scratch_shapes=scratch,
        ),
        out_shape=out_shape,
        input_output_aliases=aliases,
        compiler_params=params(1),
        cost_estimate=cost(3 * flops, 16 * sz.rows * width),
        name="attention" + "_last" * last,
    )(*args)


def attention_back(grad_own, grad_far, own, far, qkv, atts, w_qkv, w_out, bias, scalars, sz, shard):
    scale = 1.0 / math.sqrt(sz.head)
    steps = sz.groups
    direct = shard is not None
    outs = 2 if direct else 1
    gcols, width = sz.gcols, sz.width
    quarter = width // 4

    def kernel(
        sc_ref, go_ref, gf_ref, own_ref, far_ref, qkv_ref, w_ref, wo_ref, bias_ref, *refs
    ):
        refs = list(refs)
        take = lambda count: [refs.pop(0) for _ in range(count)]
        att_refs = take(2)
        gw_refs = take(outs)
        gwo_refs = gw_refs if direct else take(1)
        fold_ref, ho_ref, hf_ref = take(3)
        grad, hidden_t, grad_att, parts, spread, pair_sum, total, turned = take(8)
        (folded,) = take(1)
        step = pl.program_id(0)

        @pl.when(step == 0)
        def _():
            join_frames(own_ref, far_ref, grad, sz)
            turn(grad[...], hidden_t, sc_ref[0], shard)
            join_frames(go_ref, gf_ref, grad, sz)
            total[...] = jnp.zeros_like(total)
            for n, a_ref in enumerate(att_refs):
                turn(a_ref[...], turned, sc_ref[0], shard, n * a_ref.shape[1])

        grad_att[...] = dot_nt(grad[...], wo_ref[...]).astype(BF16)
        full = sz.lens[0]
        for head in range(sz.group):
            spread_bias(bias_ref, head, spread.at[head], sz, True)
            pair_sum[head] = jnp.zeros((full, full), F32)

        def one_micro(m, carry):
            for tw in range(2):
                size = sz.lens[tw]
                rows = window_rows(m, tw, sz)
                keys_ok = (sc_ref[1 + m] - tw * sz.frames) * sz.frame

                @pl.when(keys_ok > 0)
                def _(rows=rows, size=size, keys_ok=keys_ok):
                    row = lax.broadcasted_iota(jnp.int32, (size, 1), 0)
                    for head in range(sz.group):
                        lanes = slice(head * sz.head, (head + 1) * sz.head)
                        spot = [slice(n * gcols + lanes.start, n * gcols + lanes.stop) for n in range(3)]
                        query = qkv_ref[0, rows, lanes]
                        key = qkv_ref[1, rows, lanes]
                        value = qkv_ref[2, rows, lanes]
                        grad_out = grad_att[rows, lanes]
                        scores = dot_nt(key, query) + spread[head, :size, :size].astype(F32)
                        scores = jnp.where(row < keys_ok, scores, MASKED)
                        weight = jnp.exp(scores - jnp.max(scores, axis=0, keepdims=True))
                        probs = weight * (1.0 / jnp.sum(weight, axis=0, keepdims=True))
                        grad_probs = dot_nt(value, grad_out)
                        inner = jnp.sum(probs * grad_probs, axis=0, keepdims=True)
                        grad_scores = (probs * (grad_probs - inner)).astype(BF16)
                        pair_sum[head, :size, :size] += grad_scores.astype(F32)
                        parts[rows, spot[2]] = dot_nn(probs.astype(BF16), grad_out).astype(BF16)
                        parts[rows, spot[1]] = dot_nn(grad_scores, query).astype(BF16)
                        parts[rows, spot[0]] = (dot_tn(grad_scores, key) * scale).astype(BF16)

                @pl.when(keys_ok <= 0)
                def _(rows=rows, size=size):
                    parts[rows, :] = jnp.zeros((size, 3 * gcols), BF16)

            return carry

        lax.fori_loop(0, sz.micro, one_micro, 0)
        for head in range(sz.group):
            folded[...] = jnp.zeros_like(folded)
            for t in range(sz.frames):
                low = (sz.frames - 1 - t) * sz.frame
                folded[:, low : low + full] += pair_sum[head, t * sz.frame : (t + 1) * sz.frame, :]
            fold_ref[head] = folded[...].astype(BF16)
        for n in range(4):
            rows = slice(n * quarter, (n + 1) * quarter)
            give(gw_refs, n // 2, n % 2 * quarter, dot_nn(hidden_t[rows, :], parts[...]))
        total[...] += dot_nt(parts[...], w_ref[...])
        columns = pl.ds(pl.multiple_of(step * gcols, gcols), gcols)
        for n in range(4):
            rows = slice(n * quarter, (n + 1) * quarter)
            value = dot_nn(turned[rows, :], grad[:, columns])
            give(gwo_refs, n // 2, n % 2 * quarter, value, 3 * gcols if direct else 0)

        @pl.when(step == steps - 1)
        def _():
            for m in range(sz.micro):
                for f in range(sz.used):
                    at = m * sz.win_rows + f * sz.frame
                    ho_ref[m, f] = total[at : at + sz.half].astype(BF16)
                    hf_ref[m, f] = total[at + sz.half : at + sz.frame].astype(BF16)

    piece = (sz.micro, sz.used, sz.half, width)
    fixed = lambda g, s: (0, 0, 0, 0)
    flat = lambda g, s: (0, 0)
    cols = width // 2
    fold = (sz.frame, (2 * sz.frames - 1) * sz.frame)
    in_specs = [
        once(piece, fixed),
        once(piece, fixed),
        once(piece, fixed),
        once(piece, fixed),
        pl.BlockSpec((3, sz.rows, gcols), lambda g, s: (0, 0, g)),
        pl.BlockSpec((width, 3 * gcols), lambda g, s: (0, g)),
        pl.BlockSpec((gcols, width), lambda g, s: (g, 0)),
        pl.BlockSpec((sz.group,) + bias.shape[1:], lambda g, s: (g, 0, 0, 0)),
    ]
    along = lambda g, s: g
    wide = 4 * gcols if direct else 3 * gcols
    out_specs = grad_specs(direct, shard, width, wide, along)
    if not direct:
        out_specs += grad_specs(direct, shard, width, gcols, along)
    out_specs += [pl.BlockSpec((sz.group,) + fold, lambda g, s: (g, 0, 0))]
    out_specs += [pl.BlockSpec(piece, fixed)] * 2
    out_shape = grad_shapes(direct, shard, width, steps * wide)
    if not direct:
        out_shape += grad_shapes(direct, shard, width, width)
    out_shape += [jax.ShapeDtypeStruct((HEADS,) + fold, BF16)]
    out_shape += [jax.ShapeDtypeStruct(piece, BF16)] * 2
    scratch = [
        pltpu.VMEM((sz.rows, width), BF16),
        pltpu.VMEM((width, sz.rows), BF16),
        pltpu.VMEM((sz.rows, gcols), BF16),
        pltpu.VMEM((sz.rows, 3 * gcols), BF16),
        pltpu.VMEM((sz.group, sz.lens[0], sz.lens[0]), BF16),
        pltpu.VMEM((sz.group, sz.lens[0], sz.lens[0]), F32),
    ]
    args = [scalars, grad_own, grad_far, own, far, qkv, w_qkv, w_out, bias]
    flops = 16 * sz.rows * width * width + 10 * sz.rows * sz.lens[0] * width
    in_specs += [once((sz.rows, cols), flat)] * 2
    scratch += [pltpu.VMEM((sz.rows, width), F32), pltpu.VMEM((width, sz.rows), BF16)]
    scratch += [pltpu.VMEM(fold, F32)]
    args += list(atts)
    return pl.pallas_call(
        kernel,
        grid_spec=pltpu.PrefetchScalarGridSpec(
            num_scalar_prefetch=1,
            grid=(steps,),
            in_specs=in_specs,
            out_specs=out_specs,
            scratch_shapes=scratch,
        ),
        out_shape=out_shape,
        compiler_params=params(1),
        cost_estimate=cost(3 * flops, 24 * sz.rows * width),
        name="attention_back",
    )(*args)


GELU_A = math.sqrt(2.0 / math.pi)
GELU_B = 0.044715
MLP_TILES = 3
CHUNK = 512


def mlp(hidden, grad, weights, b_up, scalars, sz, shard, inner_first):
    chunk = CHUNK
    tiles = MLP_TILES
    tile = sz.rows // tiles
    inner = b_up.shape[1]
    steps = inner // chunk
    packed = len(weights) == 1
    direct = shard is not None
    rows, width = sz.rows, sz.width
    quarter = width // 4
    n_up = len(weights[0].arrays)
    copied = n_up > 1

    def kernel(sc_ref, h_ref, g_ref, bu_ref, *refs):
        refs = list(refs)
        take = lambda count: [refs.pop(0) for _ in range(count)]
        up_refs = take(n_up)
        down_refs = up_refs if packed else take(1)
        y_ref, t_ref, gbu_ref = take(3)
        if inner_first:
            (gbd_ref,) = take(1)
        gw_refs = take(2 if direct else 1)
        gwd_refs = gw_refs if packed else take(1)
        hidden_t, act_s, gpre_s = take(3)
        step = pl.program_id(0)
        key, z_here = sc_ref[1 + sz.micro], sc_ref[2 + sz.micro]

        @pl.when(step == 0)
        def _():
            turn(h_ref[...], hidden_t, sc_ref[0], shard)
            if inner_first:
                gbd_ref[...] = jnp.sum(g_ref[...].astype(F32), axis=0, keepdims=True)
            y_ref[...] = jnp.zeros_like(y_ref)
            t_ref[...] = jnp.zeros_like(t_ref)

        if packed:
            (wd_ref,) = take(1)
            place_inner(down_refs, key, z_here, wd_ref, slice(chunk, chunk + width // 2))
        else:
            wd_ref = down_refs[0]
        if copied:
            (wu_ref,) = take(1)
            place(up_refs, key, z_here, wu_ref, source=slice(0, chunk))
        else:
            wu_ref = up_refs[0]
        bias_sum = jnp.zeros((1, chunk), F32)
        for n in range(tiles):
            span = slice(n * tile, (n + 1) * tile)
            pre = dot_nn(h_ref[span], wu_ref[:, :chunk]) + bu_ref[...]
            grad_act = dot_nt(g_ref[span], wd_ref[...])
            square = pre * pre
            tanh = jnp.tanh(GELU_A * pre * (1.0 + GELU_B * square))
            half = 0.5 * (1.0 + tanh)
            act = (pre * half).astype(BF16)
            slope = half + (0.5 * GELU_A) * pre * (1.0 - tanh * tanh) * (
                1.0 + (3.0 * GELU_B) * square
            )
            grad_pre = (grad_act * slope).astype(BF16)
            act_s[0, span] = act[:, : chunk // 2]
            act_s[1, span] = act[:, chunk // 2 :]
            gpre_s[span] = grad_pre
            bias_sum = bias_sum + jnp.sum(grad_pre.astype(F32), axis=0, keepdims=True)
            y_ref[span] += dot_nn(act, wd_ref[...])
            t_ref[span] += dot_nt(grad_pre, wu_ref[:, :chunk])
        gbu_ref[...] = bias_sum
        for n in range(4):
            span = slice(n * quarter, (n + 1) * quarter)
            give(gw_refs, n // 2, n % 2 * quarter, dot_nn(hidden_t[span, :], gpre_s[...]))
        for n in range(2):
            source = sc_ref[0] ^ n if direct else n
            value = dot_tn(act_s[source], g_ref[...])
            if not packed:
                give(gwd_refs, n, 0, value)
                continue
            value = value.astype(BF16)
            cut = chunk // 32
            for half in range(2):
                part = value[:, half * width // 2 : (half + 1) * width // 2]
                if direct:
                    gw_refs[n][:, half * cut : (half + 1) * cut, chunk:] = part.reshape(
                        16, cut, width // 2
                    )
                    continue
                for k in range(16):
                    to = (2 * k + n) * 2 * cut + half * cut
                    gw_refs[0][to : to + cut, chunk:] = part[k * cut : (k + 1) * cut]

    fixed = lambda j, s: (0, 0)
    along = lambda j, s: j
    in_specs = [
        once((rows, width), fixed),
        once((rows, width), fixed),
        pl.BlockSpec((1, chunk), lambda j, s: (0, j)),
    ]
    args = [scalars, hidden, grad, b_up]
    out_specs = [
        pl.BlockSpec((rows, width), fixed),
        pl.BlockSpec((rows, width), fixed),
        pl.BlockSpec((1, chunk), lambda j, s: (0, j)),
    ]
    out_shape = [
        jax.ShapeDtypeStruct((rows, width), F32),
        jax.ShapeDtypeStruct((rows, width), F32),
        jax.ShapeDtypeStruct((1, inner), F32),
    ]
    if inner_first:
        out_specs += [pl.BlockSpec((1, width), fixed)]
        out_shape += [jax.ShapeDtypeStruct((1, width), F32)]
    if packed:
        wide = chunk + width // 2
        in_specs += weights[0].specs(wide, along)
        args += weights[0].arrays
        out_specs += grad_specs(direct, shard, width, wide, along)
        out_shape += grad_shapes(direct, shard, width, steps * wide)
    else:
        in_specs += weights[0].specs(chunk, along)
        in_specs += [pl.BlockSpec((chunk, width), lambda j, s: (j, 0))]
        args += [weights[0].arrays[0], weights[1].arrays[0]]
        out_specs += grad_specs(False, None, width, chunk, along)
        out_specs += [pl.BlockSpec((chunk, width), lambda j, s: (j, 0))]
        out_shape += grad_shapes(False, None, width, inner)
        out_shape += grad_shapes(False, None, inner, width)
    scratch = [
        pltpu.VMEM((width, rows), BF16),
        pltpu.VMEM((2, rows, chunk // 2), BF16),
        pltpu.VMEM((rows, chunk), BF16),
    ]
    if packed:
        scratch += [pltpu.VMEM((chunk, width), BF16)]
    if copied:
        scratch += [pltpu.VMEM((width, chunk), BF16)]
    return pl.pallas_call(
        kernel,
        grid_spec=pltpu.PrefetchScalarGridSpec(
            num_scalar_prefetch=1,
            grid=(steps,),
            in_specs=in_specs,
            out_specs=out_specs,
            scratch_shapes=scratch,
        ),
        out_shape=out_shape,
        compiler_params=params(1),
        cost_estimate=cost(14 * rows * width * inner, 16 * rows * width),
        name="mlp",
    )(*args)


def offset_onehot(core, sz):
    span = 2 * sz.side - 1
    place = jnp.arange(sz.frame, dtype=jnp.int32)
    row = ((place // sz.half) ^ core) * sz.strip_rows + place // sz.side % sz.strip_rows
    column = place % sz.side
    index = (row[:, None] - row[None, :] + sz.side - 1) * span
    index = index + column[:, None] - column[None, :] + sz.side - 1
    return (jnp.arange(span * span, dtype=jnp.int32)[:, None, None] == index[None]).astype(BF16)


def bucket_onehot(bucket, count):
    return (jnp.arange(count, dtype=jnp.int32)[:, None] == bucket[None, :]).astype(BF16)


def bias_blocks(table, bucket, places, sz):
    by_offset = dot_tn(table, bucket_onehot(bucket, table.shape[0])).astype(BF16)
    by_offset = by_offset.reshape(HEADS * (2 * sz.frames - 1), -1)
    blocks = dot_nn(by_offset, places.reshape(places.shape[0], -1)).astype(BF16)
    return blocks.reshape(HEADS, -1, sz.frame, sz.frame)


def split_low(value):
    high = value.astype(BF16)
    return high, (value - high.astype(F32)).astype(BF16)


def offset_grad(fold, places, sz):
    steps = 2 * sz.frames - 1
    fold = fold.reshape(-1, sz.frame, steps, sz.frame)
    made = jnp.einsum("hqkp,jpq->hkj", fold, places, preferred_element_type=F32)
    return made.reshape(fold.shape[0], -1)


def table_grad(by_offset, bucket, buckets):
    onehot = bucket_onehot(bucket, buckets)
    return sum(dot_nt(onehot, part) for part in split_low(by_offset))


class Net:
    AXES = ("clip", "win")
    X, Y, CORE = 2, 4, 1

    def __init__(self):
        self.count = lax.axis_size(self.AXES)
        self.direct = lax.axis_size("win") == 4 and self.count == 32
        self.deep = self.count // 8
        self.index = lax.axis_index(self.AXES)
        self.z = self.index // 8

    def bit(self, which):
        return self.index // which % 2

    def swap(self, value, which):
        return lax.ppermute(value, self.AXES, [(n, n ^ which) for n in range(self.count)])

    def from_z(self, value, step):
        move = lambda n: (n // 8 - step) % self.deep * 8 + n % 8
        return lax.ppermute(value, self.AXES, [(n, move(n)) for n in range(self.count)])

    def swap_sum(self, value, which):
        return value + self.swap(value, which)


    def gather_clips(self, value):
        along = jnp.stack([value] + [self.from_z(value, k) for k in range(1, self.deep)])
        return jnp.stack([along, self.swap(along, self.Y)], axis=1)

    def scatter_clips(self, value, notes):
        got = self.swap(value[:, 1], self.Y)
        notes.append(got)
        kept = value[:, 0] + got
        got = [self.from_z(kept[self.deep - k], k) for k in range(1, self.deep)]
        notes.append(got[-1])
        return kept[0] + sum(got)

    def share(self, value, count, scatter):
        deep = self.deep
        got = self.swap(value, self.Y)
        clips = jnp.stack([value[:count], got[:count]])
        rest = (value[count:] + got[count:]).reshape(deep, -1)
        pick = lambda at: lax.dynamic_index_in_dim(rest, at % deep, 0, keepdims=False)
        sends = [
            jnp.concatenate([clips.reshape(-1), pick(self.z + deep - k)]).astype(BF16)
            for k in range(1, deep)
        ]
        sends = tie2(sends, scatter.got[:1])
        got = [self.from_z(send, k).astype(F32) for k, send in enumerate(sends, 1)]
        clips = jnp.stack([clips] + [v[: 2 * count].reshape(2, count) for v in got])
        rest = (pick(self.z) + sum(v[2 * count :] for v in got)).reshape(8, -1)
        return clips, lax.dynamic_index_in_dim(rest, self.index % 8, 0, keepdims=False)

    def gather_pairs(self, value):
        parts = value
        for which in (self.X, self.CORE):
            parts = jnp.stack([parts, self.swap(parts, which)], axis=2 if which == self.X else 3)
        parts = parts.reshape(self.count, -1)
        place = jnp.arange(self.count, dtype=jnp.int32)
        holder = (self.z + place // 8) % self.deep * 8 + (place % 8 ^ self.index % 8)
        pick = (place[:, None] == holder[None, :]).astype(BF16)
        return dot_nn(pick, parts).astype(BF16)


def cut_rows(parts, widths):
    rows, columns = parts[0].shape
    half = rows // 2

    def kernel(*refs):
        ins, outs = refs[: len(parts)], refs[len(parts) :]
        for n, ref in enumerate(ins):
            low = 0
            for k, size in enumerate(widths):
                for side in range(2):
                    outs[2 * k + side][n] = ref[side * half : (side + 1) * half, low : low + size]
                low += size

    return pl.pallas_call(
        kernel,
        out_shape=[
            jax.ShapeDtypeStruct((len(parts), half, size), BF16) for size in widths for _ in range(2)
        ],
        compiler_params=pltpu.CompilerParams(vmem_limit_bytes=VMEM_LIMIT),
        cost_estimate=cost(0, 4 * len(parts) * rows * columns),
        name="cut_rows",
    )(*parts)


class Gather:
    def __init__(self, net, halves):
        self.net = net
        self.halves = list(halves)
        self.got = []

    @staticmethod
    def along_z(net, shards):
        both = jnp.concatenate(shards, axis=1)
        return Gather.cut(net, both, Gather.send_z(net, both), [v.shape[1] for v in shards])

    @staticmethod
    def send_z(net, shard):
        return [net.from_z(shard, k) for k in range(1, net.deep)]

    @staticmethod
    def cut(net, shard, got, widths):
        made = cut_rows([shard] + list(got), widths)
        return [Gather(net, made[2 * n : 2 * n + 2]) for n in range(len(widths))]

    def start(self, first):
        net = self.net
        order = (net.X, net.Y) if first else (net.Y, net.X)
        self.got = [net.swap(v, which) for v, which in zip(self.halves, order)]

    def join(self):
        self.halves = [jnp.stack(pair) for pair in zip(self.halves, self.got)]

    def tie(self, *others):
        self.got = list(lax.optimization_barrier((*self.got, *others))[: len(self.got)])

    def core(self):
        net = self.net
        self.halves = [v for pair in zip(self.halves, self.got) for v in pair]
        self.got = [net.swap(v, net.CORE) for v in self.halves]

    def pieces(self):
        near, far = self.halves, self.got
        return Pieces([*near[:2], *far[:2], *near[2:], *far[2:]])


def add_bf16(one, two):
    return (one.astype(F32) + two.astype(F32)).astype(BF16)


class Scatter:
    def __init__(self, net, pair):
        self.net = net
        keep, send = [v.reshape((net.deep, 4) + v.shape[1:]) for v in pair]
        self.keep = [keep]
        self.got = [net.swap(send, net.CORE)]
        self.bits = jnp.stack([net.bit(net.Y), net.bit(net.X), net.z])
        self.rows, self.columns = keep.shape[2:]

    def tie(self, *others):
        self.got = list(lax.optimization_barrier((*self.got, *others))[: len(self.got)])

    def tie_keep(self, *others):
        self.keep = list(lax.optimization_barrier((*self.keep, *others))[: len(self.keep)])

    def second(self):
        net, cut = self.net, self.rows // 2

        def kernel(sc_ref, keep, got, *outs):
            for half in range(2):
                span = slice(half * cut, (half + 1) * cut)
                for role in range(2):
                    for other in range(2):
                        near = sc_ref[half] ^ role
                        at = near * 2 + other if half == 0 else other * 2 + near
                        outs[2 * half + role][0, other] = add_bf16(keep[0, at, span], got[0, at, span])

        spans = 1
        block = (1,) + self.keep[0].shape[1:3] + (self.columns // spans,)
        out = (2, cut, self.columns // spans)
        made = pl.pallas_call(
            kernel,
            grid_spec=pltpu.PrefetchScalarGridSpec(
                num_scalar_prefetch=1,
                grid=(net.deep, spans),
                in_specs=[pl.BlockSpec(block, lambda z, n, s: (z, 0, 0, n))] * 2,
                out_specs=[pl.BlockSpec((1,) + out, lambda z, n, s: (z, 0, 0, n))] * 4,
            ),
            out_shape=[jax.ShapeDtypeStruct((net.deep, 2, cut, self.columns), BF16)] * 4,
            compiler_params=params(2),
            cost_estimate=cost(0, 6 * self.keep[0].size),
            name="add_cores",
        )(self.bits, *self.keep, *self.got)
        self.keep = [made[0], made[2]]
        self.got = [net.swap(made[1], net.Y), net.swap(made[3], net.X)]

    def third(self):
        net, cut = self.net, self.rows // 2

        def kernel(sc_ref, k0, k1, g0, g1, *outs):
            for half, (keep, got) in enumerate(((k0, g0), (k1, g1))):
                for role in range(2):
                    at = sc_ref[1 - half] ^ role
                    outs[2 * half + role][...] = add_bf16(keep[:, at], got[:, at])

        out = jax.ShapeDtypeStruct((net.deep, cut, self.columns), BF16)
        made = self.call(kernel, [*self.keep, *self.got], [out] * 4, "add_second")
        self.keep = [made[0], made[2]]
        self.got = [net.swap(made[1], net.X), net.swap(made[3], net.Y)]

    def fourth(self):
        net, rows, cut = self.net, self.rows, self.rows // 2

        def kernel(sc_ref, k0, k1, g0, g1, *outs):
            for away, out in enumerate(outs):
                at = (sc_ref[2] + net.deep - away) % net.deep
                out[:cut] = add_bf16(k0[at], g0[at])
                out[cut:] = add_bf16(k1[at], g1[at])

        out = jax.ShapeDtypeStruct((rows, self.columns), BF16)
        made = self.call(kernel, [*self.keep, *self.got], [out] * net.deep, "add_third")
        self.keep = [made[0]]
        self.got = [net.from_z(made[k], k) for k in range(1, net.deep)]

    def total(self):
        return self.keep[0].astype(F32) + sum(v.astype(F32) for v in self.got)

    def total_heads(self, sz):
        size = sz.gcols

        def kernel(sc_ref, own, g0, g1, g2, qkv_ref, out_ref):
            for g in range(sz.groups):
                for n in range(4):
                    low = (4 * g + n) * size
                    total = sum(v[:, low : low + size].astype(F32) for v in (own, g0, g1, g2))
                    if n < 3:
                        low = n * sz.width + g * size
                        qkv_ref[:, low : low + size] = total
                    else:
                        out_ref[:, g * size : (g + 1) * size] = total

        outs = [jax.ShapeDtypeStruct((self.rows, k * sz.width), F32) for k in (3, 1)]
        return self.call(kernel, [*self.keep, *self.got], outs, "total_heads")

    def call(self, kernel, args, outs, name):
        return pl.pallas_call(
            kernel,
            grid_spec=pltpu.PrefetchScalarGridSpec(
                num_scalar_prefetch=1,
                grid=(1,),
                in_specs=[pl.BlockSpec(memory_space=pltpu.VMEM)] * len(args),
                out_specs=[pl.BlockSpec(memory_space=pltpu.VMEM)] * len(outs),
            ),
            out_shape=outs,
            compiler_params=params(1),
            cost_estimate=cost(0, 6 * sum(v.size for v in args)),
            name=name,
        )(self.bits, *args)


def tie(value, *others):
    return lax.optimization_barrier((value,) + others)[0]


def tie2(values, others):
    return lax.optimization_barrier((*values, *others))[: len(values)]


def body(
    tokens, cond, lengths, ada_w, ada_b, w_qkv, w_out, w_up, b_up, w_down, b_down,
    rel_table, bucket, cotangent,
):
    axes = ("clip", "win")
    sz = Sizes(tokens)
    net = Net()
    devices, index = net.count, net.index
    clips = lax.axis_size("clip")
    width = sz.width
    core = lax.axis_index("win") % 2
    swap = [(n, n ^ 1) for n in range(lax.axis_size("win"))]
    place_in = jnp.arange(3 + sz.micro, dtype=jnp.int32)
    scalars = jnp.where(place_in == 0, core, jnp.where(place_in == 1 + sz.micro, index % 8, index // 8))
    for n in range(sz.micro):
        scalars = jnp.where(place_in == 1 + n, lengths[n, 0], scalars)
    strip = (sz.micro, 2, 2, sz.frames, sz.half, width)
    tok = tokens.reshape(strip)
    cot = cotangent.reshape(strip)

    cond_act = jax.nn.silu(cond[:, 0].astype(F32)).astype(BF16)
    rows = ada_w.shape[0]
    small = jnp.concatenate([b_up, b_down, rel_table.reshape(-1)])
    n_cond = cond_act.size
    if net.direct:
        early = jnp.concatenate([cond_act.reshape(-1), small])
        early = net.gather_clips(jnp.pad(early, (0, -early.size % 128)))
        cond_all = early[:, :, :n_cond].reshape(early.shape[:2] + cond_act.shape)
    else:
        cond_all = lax.all_gather(cond_act, "clip", axis=0)
    cond_mine = lax.dynamic_slice_in_dim(cond_all, index * rows, rows, cond_all.ndim - 1)
    lead = cond_mine.shape[:-1]
    cond_mine = cond_mine.reshape(clips * sz.micro, rows)
    mod_part = dot_nn(cond_mine, ada_w)
    spread_b = jnp.zeros((mod_part.shape[1],), F32)
    spread_b = lax.dynamic_update_slice(spread_b, ada_b.astype(F32), (index * ada_b.shape[0],))
    mod_part = (mod_part + spread_b[None, :]).reshape(lead + (6 * width,))
    notes = []
    if net.direct:
        mod = net.scatter_clips(mod_part, notes)
        mod = net.swap_sum(net.swap_sum(mod, net.CORE), net.X)
    else:
        mod = lax.psum_scatter(mod_part, "clip", scatter_dimension=0, tiled=False)
        mod = lax.psum(mod, "win")
    mod = mod.reshape(sz.micro, 6, width)

    cols = width // 2
    by_group = w_qkv.reshape(rows, 3, sz.groups, sz.gcols).transpose(0, 2, 1, 3)
    by_group = by_group.reshape(rows, 2, 3 * cols)
    shard_q = [by_group[:, n] for n in range(2)]
    inner = w_up.shape[1]
    per = w_down.shape[0] // 2
    thin = CHUNK // devices

    def inner_order(value):
        if not net.direct:
            value = value.reshape(-1, devices, 2, per).transpose(2, 0, 1, 3)
        else:
            value = value.reshape(-1, devices // 2, 2, 2, per // thin, thin)
            value = value.transpose(3, 0, 4, 2, 1, 5)
        return value.reshape(2, -1, inner // 2)

    def inner_back(halves):
        value = jnp.stack(halves)
        if not net.direct:
            value = value.reshape(2, -1, devices, per).transpose(1, 2, 0, 3)
        else:
            value = value.reshape(2, -1, per // thin, 2, devices // 2, thin)
            value = value.transpose(1, 4, 3, 0, 2, 5)
        return value.reshape(-1, inner)

    def pack_inner(up, down):
        down = down.reshape(per // thin, thin, 2, width // 2).transpose(2, 1, 0, 3)
        down = down.reshape(rows, per // thin, width // 2)
        return jnp.concatenate([up.reshape(rows, -1, CHUNK), down], axis=2).reshape(rows, -1)

    def unpack_inner(value):
        value = value.reshape(rows, per // thin, -1)
        down = value[:, :, CHUNK:].reshape(2, thin, per // thin, width // 2)
        return value[:, :, :CHUNK].reshape(rows, -1), down.transpose(2, 1, 0, 3).reshape(per, width)

    shard_u = inner_order(w_up)
    shard_d = [w_down[:per], w_down[per:]]
    gather = lambda v: lax.all_gather(v, axes, axis=0, tiled=True)
    if net.direct:
        packs = [
            shard_q[0],
            jnp.concatenate([shard_q[1], w_out], axis=1),
            pack_inner(shard_u[1], shard_d[1]),
            pack_inner(shard_u[0], shard_d[0]),
        ]
        rest_q = gather(packs[1])
        rest = gather(tie(packs[2], early))
        (one,) = Gather.along_z(net, [packs[0]])
        small = net.gather_pairs(tie(early[:, :, n_cond:], *notes))
        one.halves = tie2(one.halves, [mod_part])
        one.start(True)
        one.join()
        one.halves = tie2(one.halves, notes[:1])
        one.start(False)
        three_pack = tie(packs[3], notes[0])
        three_got = tie2(Gather.send_z(net, three_pack), one.got)
        (three,) = Gather.cut(net, three_pack, three_got, [packs[3].shape[1]])
        one.core()
        full_q = [one.pieces(), Pieces([rest_q])]
        full_out = full_q[1]
    else:
        full_q = [Pieces([gather(v)]) for v in shard_q]
        full_out = Pieces([gather(w_out)])
        full_i = [[Pieces([gather(u)]), Pieces([gather(d)])] for u, d in zip(shard_u, shard_d)]
        small = gather(small[None])
    n_up, n_down = b_up.shape[0], b_down.shape[0]
    n_small = n_up + n_down + rel_table.size
    full_bup = inner_order(small[:, :n_up].astype(F32).reshape(1, inner))
    full_bdown = small[:, n_up : n_up + n_down].astype(F32).reshape(1, width)
    table = small[:, n_up + n_down : n_small].reshape(-1, HEADS)
    places = offset_onehot(core, sz)
    bias = bias_blocks(table, bucket, places, sz)

    if net.direct:
        mod = tie(mod, bias, *three.halves)
    own, send = first_norm(tok, mod, scalars, sz)
    far = lax.ppermute(send, "win", swap)
    if net.direct:
        three.start(True)
    first = attention(0, own, far, full_q[0], bias, scalars, sz)
    if net.direct:
        three.tie(first[2])
        three.join()
        three.start(False)
        first = tie2(first, three.halves)
    qkv, wide, att_1, wide_out, branch_own, branch_send = attention(
        1, own, far, full_q[1], bias, scalars, sz, first, full_out
    )
    if net.direct:
        three.tie(branch_own)
        branch_send = tie(branch_send, *three.got)
    branch_far = lax.ppermute(branch_send, "win", swap)
    hidden_two, grad_mlp = second_norm(tok, cot, branch_own, branch_far, mod, scalars, sz)
    flat = (sz.rows, width)
    both = (2, sz.micro, sz.used, sz.half, width)
    hidden_two, grad_mlp = hidden_two.reshape(flat), grad_mlp.reshape(flat)
    if net.direct:
        three.tie(branch_far)
        three.halves = tie2(three.halves, [branch_far])
        three.core()
        full_i = [[three.pieces()], [Pieces([rest])]]
    mlps = []
    for n in range(2):
        shard = rows if net.direct and n == 1 else None
        mlps.append(
            mlp(hidden_two, grad_mlp, full_i[n], full_bup[n], scalars, sz, shard, n == 0)
        )
        if net.direct and n == 0:
            pack, hidden_two = lax.optimization_barrier((mlps[0][4], hidden_two))
            r_first = lax.psum_scatter(pack, axes, scatter_dimension=0, tiled=True).astype(F32)

    if net.direct:
        second = Scatter(net, mlps[1][3:5])
    output, grad_mid, grad_own, grad_send, sums_two = after_mlp(
        tok, cot, branch_own, branch_far, [v[0].reshape(both) for v in mlps],
        [v[1].reshape(both) for v in mlps], mod, full_bdown, scalars, sz,
    )
    grad_far = lax.ppermute(grad_send, "win", swap)
    if net.direct:
        second.tie(grad_own)
        second.second()
        grad_own = tie(grad_own, *second.keep)
    *g_att, fold, hid_own, hid_send = attention_back(
        grad_own, grad_far, own, far, qkv, (first[2], att_1), wide, wide_out, bias, scalars, sz,
        rows if net.direct else None,
    )
    if net.direct:
        second.tie(hid_own)
        g_att = tie2(g_att, second.got)
        hid_send = tie(hid_send, *second.got)
        heads = Scatter(net, g_att)
        hid_far = lax.ppermute(hid_send, "win", swap)
        second.third()
        heads.tie(*second.keep)
        heads.second()
        hid_far = tie(hid_far, r_first, *heads.keep)
    else:
        hid_far = lax.ppermute(hid_send, "win", swap)
    grad_in, sums_one = last_norm(tok, cot, grad_mid, hid_own, hid_far, mod, scalars, sz)
    if net.direct:
        second.tie(sums_one)
        second.fourth()
        sums_one, fold = lax.optimization_barrier((sums_one, fold, *second.keep))[:2]

    grad_mod = jnp.concatenate(
        [sums_one, sums_two[:, 3:4], sums_two[:, 0:3]], axis=1
    ).reshape(sz.micro, 6 * width)
    g_table = table_grad(offset_grad(fold, places, sz), bucket, table.shape[0]).reshape(devices, -1)
    if net.direct:
        heads.tie(g_table)
        heads.third()
        second.tie(*heads.keep)
        r_second = second.total()
        g_table = tie(g_table, r_second)
    g_bup = inner_back([v[2] for v in mlps]).reshape(devices, -1)
    g_bdown = mlps[0][3].reshape(devices, -1)
    g_small = jnp.concatenate([g_bup, g_bdown, g_table], axis=1)
    if net.direct:
        every = jnp.concatenate([grad_mod.reshape(-1), g_small.reshape(-1)])
        every = net.swap_sum(net.swap_sum(every, net.CORE), net.X)
        heads.tie(every)
        heads.fourth()
        mod_all, g_small = net.share(tie(every, *heads.keep), grad_mod.size, heads)
    else:
        mod_all = lax.all_gather(lax.psum(grad_mod, "win"), "clip", axis=0)
        g_small = lax.psum_scatter(g_small, axes, scatter_dimension=0, tiled=False)
    mod_all = mod_all.reshape(clips * sz.micro, -1)
    grad_ada_w = lax.dot_general(
        cond_mine.astype(F32), mod_all, (((0,), (0,)), ((), ())),
        precision=HIGHEST, preferred_element_type=F32,
    )
    grad_ada_b = lax.dynamic_slice_in_dim(
        jnp.sum(mod_all, axis=0), index * ada_b.shape[0], ada_b.shape[0]
    )
    if net.direct:
        r_u, r_d = zip(unpack_inner(r_first), unpack_inner(r_second))
        r_qkv, r_out = heads.total_heads(sz)
    else:
        scatter = lambda v: lax.psum_scatter(
            v.astype(F32), axes, scatter_dimension=0, tiled=True
        )
        r_u = [scatter(v[-2]) for v in mlps]
        r_d = [scatter(v[-1]) for v in mlps]
        r_qkv, r_out = scatter(g_att[0]), scatter(g_att[1])
        r_qkv = r_qkv.reshape(rows, sz.groups, 3, sz.gcols).transpose(0, 2, 1, 3)
        r_qkv = r_qkv.reshape(rows, 3 * width)
    r_up = inner_back(r_u)
    r_down = jnp.concatenate(r_d)
    return (
        output.reshape(tokens.shape), grad_in.reshape(tokens.shape), grad_ada_w, grad_ada_b,
        r_qkv, r_out, r_up, g_small[:n_up], r_down, g_small[n_up : n_up + n_down],
        g_small[n_up + n_down :].reshape(rel_table.shape),
    )


def solution(mesh):
    weights = P(("clip", "win"), None)
    vector = P(("clip", "win"))
    strips = P(None, "clip", "win", None, None, None, None, None)
    return jax.shard_map(
        body,
        mesh=mesh,
        in_specs=(
            strips, P(None, "clip", None), P(None, "clip"), weights, vector, weights, weights,
            weights, vector, weights, vector, weights, P(), strips,
        ),
        out_specs=(
            strips, strips, weights, vector, weights, weights, weights, vector, weights, vector,
            weights,
        ),
        check_vma=False,
    )
```

```python
import functools
import math

import jax
import jax.numpy as jnp
from jax import lax
from jax.experimental import pallas as pl
from jax.experimental.pallas import tpu as pltpu
from jax.sharding import PartitionSpec as P

HEADS = 16
EPSILON = 1e-06
MASKED = -1000000000.0
F32 = jnp.float32
BF16 = jnp.bfloat16
VMEM_LIMIT = 58 * 1024 * 1024
HIGHEST = lax.Precision.HIGHEST


def dot_nn(a, b):
    return lax.dot_general(a, b, (((1,), (0,)), ((), ())), preferred_element_type=F32)


def dot_nt(a, b):
    return lax.dot_general(a, b, (((1,), (1,)), ((), ())), preferred_element_type=F32)


def dot_tn(a, b):
    return lax.dot_general(a, b, (((0,), (0,)), ((), ())), preferred_element_type=F32)


def params(count):
    return pltpu.CompilerParams(
        dimension_semantics=("arbitrary",) * count, vmem_limit_bytes=VMEM_LIMIT
    )


def cost(flops, size):
    return pl.CostEstimate(flops=flops, bytes_accessed=size, transcendentals=0)


def once(shape, index_map):
    return pl.BlockSpec(shape, index_map, pipeline_mode=pl.Buffered(1))


def normalize(values):
    centered = values - jnp.mean(values, axis=-1, keepdims=True)
    inv = lax.rsqrt(jnp.mean(centered * centered, axis=-1, keepdims=True) + EPSILON)
    return centered * inv, inv


def norm_back(grad, normed, inv):
    return inv * (
        grad
        - jnp.mean(grad, axis=-1, keepdims=True)
        - normed * jnp.mean(grad * normed, axis=-1, keepdims=True)
    )


class Sizes:
    def __init__(self, tokens):
        self.micro, _, _, self.blocks, self.frames, rows, side, self.width = tokens.shape
        self.half = rows * side
        self.cols = self.blocks // 2
        self.strip_rows, self.side = rows, side
        self.used = 2 * self.frames - 1
        self.frame = 2 * self.half
        self.win_rows = self.used * self.frame
        self.rows = self.micro * self.win_rows
        self.lens = (self.frames * self.frame, (self.frames - 1) * self.frame)
        self.head = self.width // HEADS
        self.group = 4
        self.gcols = self.group * self.head
        self.groups = HEADS // self.group


def each_frame(body, sz):
    for tw in range(2):

        def step(t, carry, tw=tw):
            body(tw, t, tw * sz.frames + t)
            return carry

        lax.fori_loop(0, sz.frames - tw, step, 0, unroll=True)


def fold_rows(value):
    return jnp.sum(value.reshape(-1, 8, value.shape[-1]), axis=0)


def first_norm(tok, mod, core, sz):
    def kernel(sc_ref, x_ref, mod_ref, own_ref, far_ref):
        shift = mod_ref[0, 0:1, :]
        scale = 1.0 + mod_ref[0, 1:2, :]
        for slot, out_ref in enumerate((own_ref, far_ref)):
            column = sc_ref[0] ^ slot

            def one(tw, t, f, column=column, out_ref=out_ref):
                normed, _ = normalize(x_ref[0, tw, column, t].astype(F32))
                out_ref[0, f] = (normed * scale + shift).astype(BF16)

            each_frame(one, sz)

    strip = (1, 2, 2, sz.frames, sz.half, sz.width)
    piece = (1, sz.used, sz.half, sz.width)
    shape = jax.ShapeDtypeStruct((sz.micro,) + piece[1:], BF16)
    return pl.pallas_call(
        kernel,
        grid_spec=pltpu.PrefetchScalarGridSpec(
            num_scalar_prefetch=1,
            grid=(sz.micro,),
            in_specs=[
                pl.BlockSpec(strip, lambda m, s: (m, 0, 0, 0, 0, 0)),
                pl.BlockSpec((1, 6, sz.width), lambda m, s: (m, 0, 0)),
            ],
            out_specs=[pl.BlockSpec(piece, lambda m, s: (m, 0, 0, 0))] * 2,
        ),
        out_shape=[shape, shape],
        compiler_params=params(1),
        name="first_norm",
    )(core, tok, mod)


def second_norm(tok, cot, branch_own, branch_far, mod, scalars, sz):
    def kernel(sc_ref, x_ref, c_ref, bo_ref, bf_ref, mod_ref, h_ref, g_ref):
        length = sc_ref[1 + pl.program_id(0)]
        gate1 = mod_ref[0, 2:3, :]
        shift = mod_ref[0, 3:4, :]
        scale = 1.0 + mod_ref[0, 4:5, :]
        gate2 = mod_ref[0, 5:6, :]
        for slot, b_ref in enumerate((bo_ref, bf_ref)):
            column = sc_ref[0] ^ slot

            def one(tw, t, f, slot=slot, column=column, b_ref=b_ref):
                rows = x_ref[0, tw, column, t].astype(F32) + gate1 * b_ref[0, f].astype(F32)
                normed, _ = normalize(rows)
                h_ref[slot, 0, f] = (normed * scale + shift).astype(BF16)
                valid = (f < length).astype(F32)
                g_ref[slot, 0, f] = (c_ref[0, tw, column, t].astype(F32) * (valid * gate2)).astype(BF16)

            each_frame(one, sz)

    strip = (1, 2, 2, sz.frames, sz.half, sz.width)
    piece = (1, sz.used, sz.half, sz.width)
    both = (2, 1, sz.used, sz.half, sz.width)
    shape = jax.ShapeDtypeStruct((2, sz.micro, sz.used, sz.half, sz.width), BF16)
    return pl.pallas_call(
        kernel,
        grid_spec=pltpu.PrefetchScalarGridSpec(
            num_scalar_prefetch=1,
            grid=(sz.micro,),
            in_specs=[
                pl.BlockSpec(strip, lambda m, s: (m, 0, 0, 0, 0, 0)),
                pl.BlockSpec(strip, lambda m, s: (m, 0, 0, 0, 0, 0)),
                pl.BlockSpec(piece, lambda m, s: (m, 0, 0, 0)),
                pl.BlockSpec(piece, lambda m, s: (m, 0, 0, 0)),
                pl.BlockSpec((1, 6, sz.width), lambda m, s: (m, 0, 0)),
            ],
            out_specs=[pl.BlockSpec(both, lambda m, s: (0, m, 0, 0, 0))] * 2,
        ),
        out_shape=[shape, shape],
        compiler_params=params(1),
        name="second_norm",
    )(scalars, tok, cot, branch_own, branch_far, mod)


def after_mlp(tok, cot, branch_own, branch_far, mlps, grads, mod, b_down, scalars, sz):
    def kernel(
        sc_ref, x_ref, c_ref, bo_ref, bf_ref, y0_ref, y1_ref, t0_ref, t1_ref, mod_ref, bd_ref,
        out_ref, gm_ref, go_ref, gf_ref, sum_ref, sums,
    ):
        length = sc_ref[1 + pl.program_id(0)]
        gate1 = mod_ref[0, 2:3, :]
        scale = 1.0 + mod_ref[0, 4:5, :]
        gate2 = mod_ref[0, 5:6, :]
        sums[...] = jnp.zeros_like(sums)
        for slot, (b_ref, g_ref) in enumerate(((bo_ref, go_ref), (bf_ref, gf_ref))):
            column = sc_ref[0] ^ slot

            def one(tw, t, f, slot=slot, column=column, b_ref=b_ref, g_ref=g_ref):
                valid = (f < length).astype(F32)
                branch = b_ref[0, f].astype(F32)
                middle = x_ref[0, tw, column, t].astype(F32) + gate1 * branch
                normed, inv = normalize(middle)
                y = y0_ref[slot, 0, f] + y1_ref[slot, 0, f] + bd_ref[0:1, :]
                grad = c_ref[0, tw, column, t].astype(F32)
                out_ref[0, tw, column, t] = (middle + valid * gate2 * y).astype(BF16)
                two = t0_ref[slot, 0, f] + t1_ref[slot, 0, f]
                gm = grad + norm_back(two * scale, normed, inv)
                gm_ref[slot, 0, f] = gm
                g_ref[0, f] = (valid * (gm * gate1)).astype(BF16)
                for n, term in enumerate((two, two * normed, grad * valid * y, gm * branch)):
                    sums[n] += fold_rows(term)

            each_frame(one, sz)
            out_ref[0, 1, column, sz.frames - 1] = x_ref[0, 1, column, sz.frames - 1]
        for n in range(4):
            sum_ref[0, n : n + 1, :] = jnp.sum(sums[n], axis=0, keepdims=True)

    strip = (1, 2, 2, sz.frames, sz.half, sz.width)
    piece = (1, sz.used, sz.half, sz.width)
    both = (2, 1, sz.used, sz.half, sz.width)
    full = (sz.micro,) + piece[1:]
    at_strip = lambda m, s: (m, 0, 0, 0, 0, 0)
    at_piece = lambda m, s: (m, 0, 0, 0)
    at_both = lambda m, s: (0, m, 0, 0, 0)
    return pl.pallas_call(
        kernel,
        grid_spec=pltpu.PrefetchScalarGridSpec(
            num_scalar_prefetch=1,
            grid=(sz.micro,),
            in_specs=[
                pl.BlockSpec(strip, at_strip),
                pl.BlockSpec(strip, at_strip),
                pl.BlockSpec(piece, at_piece),
                pl.BlockSpec(piece, at_piece),
                pl.BlockSpec(both, at_both),
                pl.BlockSpec(both, at_both),
                pl.BlockSpec(both, at_both),
                pl.BlockSpec(both, at_both),
                pl.BlockSpec((1, 6, sz.width), lambda m, s: (m, 0, 0)),
                pl.BlockSpec((1, sz.width), lambda m, s: (0, 0)),
            ],
            out_specs=[
                pl.BlockSpec(strip, at_strip),
                pl.BlockSpec(both, at_both),
                pl.BlockSpec(piece, at_piece),
                pl.BlockSpec(piece, at_piece),
                pl.BlockSpec((1, 4, sz.width), lambda m, s: (m, 0, 0)),
            ],
            scratch_shapes=[pltpu.VMEM((4, 8, sz.width), F32)],
        ),
        out_shape=[
            jax.ShapeDtypeStruct(tok.shape, BF16),
            jax.ShapeDtypeStruct((2,) + full, F32),
            jax.ShapeDtypeStruct(full, BF16),
            jax.ShapeDtypeStruct(full, BF16),
            jax.ShapeDtypeStruct((sz.micro, 4, sz.width), F32),
        ],
        compiler_params=params(1),
        name="after_mlp",
    )(scalars, tok, cot, branch_own, branch_far, *mlps, *grads, mod, b_down)


def last_norm(tok, cot, grad_mid, grad_own, grad_far, mod, scalars, sz):
    def kernel(sc_ref, x_ref, c_ref, gm_ref, go_ref, gf_ref, mod_ref, out_ref, sum_ref, sums):
        scale = 1.0 + mod_ref[0, 1:2, :]
        sums[...] = jnp.zeros_like(sums)
        for slot, g_ref in enumerate((go_ref, gf_ref)):
            column = sc_ref[0] ^ slot

            def one(tw, t, f, slot=slot, column=column, g_ref=g_ref):
                normed, inv = normalize(x_ref[0, tw, column, t].astype(F32))
                grad = g_ref[0, f].astype(F32)
                total = gm_ref[slot, 0, f] + norm_back(grad * scale, normed, inv)
                out_ref[0, tw, column, t] = total.astype(BF16)
                sums[0] += fold_rows(grad)
                sums[1] += fold_rows(grad * normed)

            each_frame(one, sz)
        for slot in range(2):
            out_ref[0, 1, slot, sz.frames - 1] = c_ref[0, 0, slot, 0]
        for n in range(2):
            sum_ref[0, n : n + 1, :] = jnp.sum(sums[n], axis=0, keepdims=True)

    strip = (1, 2, 2, sz.frames, sz.half, sz.width)
    tail = (1, 1, 2, 1, sz.half, sz.width)
    piece = (1, sz.used, sz.half, sz.width)
    both = (2, 1, sz.used, sz.half, sz.width)
    return pl.pallas_call(
        kernel,
        grid_spec=pltpu.PrefetchScalarGridSpec(
            num_scalar_prefetch=1,
            grid=(sz.micro,),
            in_specs=[
                pl.BlockSpec(strip, lambda m, s: (m, 0, 0, 0, 0, 0)),
                pl.BlockSpec(tail, lambda m, s: (m, 1, 0, sz.frames - 1, 0, 0)),
                pl.BlockSpec(both, lambda m, s: (0, m, 0, 0, 0)),
                pl.BlockSpec(piece, lambda m, s: (m, 0, 0, 0)),
                pl.BlockSpec(piece, lambda m, s: (m, 0, 0, 0)),
                pl.BlockSpec((1, 6, sz.width), lambda m, s: (m, 0, 0)),
            ],
            out_specs=[
                pl.BlockSpec(strip, lambda m, s: (m, 0, 0, 0, 0, 0)),
                pl.BlockSpec((1, 2, sz.width), lambda m, s: (m, 0, 0)),
            ],
            scratch_shapes=[pltpu.VMEM((2, 8, sz.width), F32)],
        ),
        out_shape=[
            jax.ShapeDtypeStruct(tok.shape, BF16),
            jax.ShapeDtypeStruct((sz.micro, 2, sz.width), F32),
        ],
        compiler_params=params(1),
        name="last_norm",
    )(scalars, tok, cot, grad_mid, grad_own, grad_far, mod)


class Pieces:
    def __init__(self, arrays):
        self.arrays = arrays
        self.whole = len(arrays) == 1

    def specs(self, columns, index_map):
        if self.whole:
            at = lambda *g: (0, index_map(*g))
            return [pl.BlockSpec((self.arrays[0].shape[0], columns), at)]
        at = lambda *g: (0, 0, 0, index_map(*g))
        shape = self.arrays[0].shape[:-1] + (columns,)
        return [pl.BlockSpec(shape, at)] * 8


def pieces_of(refs, key, z_here):
    depth = refs[0].shape[1]
    for z in range(depth):
        for n in range(8):
            half, far, i = n // 4, n // 2 % 2, n % 2
            for j in range(2):
                away = (i * 4 + j * 2 if half == 0 else i * 2 + j * 4) + far
                yield (z_here + z) % depth, key ^ away, half, refs[n].at[j, z]


def place(refs, key, z_here, out_ref, columns=slice(None), source=slice(None)):
    if len(refs) == 1:
        out_ref[:, columns] = refs[0][:, source]
        return
    for z, at, half, piece in pieces_of(refs, key, z_here):
        cut = piece.shape[0]
        row = pl.multiple_of((z * 8 + at) * (2 * cut) + half * cut, cut)
        out_ref[pl.ds(row, cut), columns] = piece[:, source]


def place_inner(refs, key, z_here, out_ref, source):
    size = source.stop - source.start
    if len(refs) == 1:
        cut = out_ref.shape[0] // 32
        for n in range(64):
            at, half = n // 2, n % 2
            to = (at % 2) * (16 * cut) + at // 2 * cut
            out_ref[to : to + cut, half * size : (half + 1) * size] = refs[0][
                n * cut : (n + 1) * cut, source
            ]
        return
    for z, at, half, piece in pieces_of(refs, key, z_here):
        cut = piece.shape[0]
        row = pl.multiple_of((at % 2) * (16 * cut) + (z * 4 + at // 2) * cut, cut)
        out_ref[pl.ds(row, cut), half * size : (half + 1) * size] = piece[:, source]


def turn(value, out_ref, core, shard, start=0):
    turned = value.T
    if shard is None:
        out_ref[start : start + turned.shape[0]] = turned
        return
    height = out_ref.shape[0]
    for n in range(turned.shape[0] // shard):
        at = start // shard + n
        at = (core ^ (at % 2)) * (height // 2) + at // 2 * shard
        out_ref[pl.ds(pl.multiple_of(at, shard), shard), :] = turned[n * shard : (n + 1) * shard]


def give(refs, half, low, value, start=0):
    value = value.astype(BF16)
    columns = slice(start, start + value.shape[1])
    if len(refs) == 1:
        low = half * (refs[0].shape[0] // 2) + low
        refs[0][low : low + value.shape[0], columns] = value
        return
    rows = refs[half].shape[1]
    refs[half][low // rows : (low + value.shape[0]) // rows, :, columns] = value.reshape(
        value.shape[0] // rows, rows, value.shape[1]
    )


def grad_shapes(direct, rows, height, columns):
    if not direct:
        return [jax.ShapeDtypeStruct((height, columns), BF16)]
    return [jax.ShapeDtypeStruct((height // (2 * rows), rows, columns), BF16)] * 2


def grad_specs(direct, rows, height, columns, at_column):
    if not direct:
        return [pl.BlockSpec((height, columns), lambda *g: (0, at_column(*g)))]
    shape = (height // (2 * rows), rows, columns)
    return [pl.BlockSpec(shape, lambda *g: (0, 0, at_column(*g)))] * 2


def join_frames(own_ref, far_ref, joined_ref, sz):
    for m in range(sz.micro):
        for f in range(sz.used):
            at = m * sz.win_rows + f * sz.frame
            joined_ref[at : at + sz.half] = own_ref[m, f]
            joined_ref[at + sz.half : at + sz.frame] = far_ref[m, f]


def spread_bias(block_ref, head, bias_ref, sz, turned=False):
    size = sz.frame
    for step in range(2 * sz.frames - 1):
        block = block_ref[head, step]
        if turned:
            block = block.T
        for key in range(sz.frames):
            query = key + step - (sz.frames - 1)
            if 0 <= query < sz.frames:
                row, column = (key, query) if turned else (query, key)
                bias_ref[row * size : (row + 1) * size, column * size : (column + 1) * size] = block


def window_rows(m, tw, sz):
    start = pl.multiple_of(m * sz.win_rows + tw * sz.lens[0], sz.frame)
    return pl.ds(start, sz.lens[tw])


def attention(half, own, far, w_qkv, bias, scalars, sz, first=None, w_out=None):
    scale = 1.0 / math.sqrt(sz.head)
    last = w_out is not None
    steps = sz.groups // 2
    gcols = sz.gcols
    joint = w_out is w_qkv
    n_out = 2 * len(w_qkv.arrays) if joint else 1

    def kernel(sc_ref, own_ref, far_ref, bias_ref, *refs):
        refs = list(refs)
        take = lambda count: [refs.pop(0) for _ in range(count)]
        w_refs = take(len(w_qkv.arrays))
        if last:
            (first_ref,) = take(1)
            out_refs = take(n_out)
            take(2)
        qkv_ref, w_ref, att_ref = take(3)
        if last:
            wo_ref, bo_ref, bf_ref = take(3)
        joined, spread = take(2)
        step = pl.program_id(0)
        key, z_here = sc_ref[1 + sz.micro], sc_ref[2 + sz.micro]

        @pl.when(step == 0)
        def _():
            join_frames(own_ref, far_ref, joined, sz)

        place(w_refs, key, z_here, w_ref)
        for n in range(3):
            part = dot_nn(joined[...], w_ref[:, n * gcols : (n + 1) * gcols]).astype(BF16)
            qkv_ref[n] = part * scale if n == 0 else part
        for head in range(sz.group):
            spread_bias(bias_ref, head, spread.at[head], sz)

        def one_micro(m, carry):
            for tw in range(2):
                size = sz.lens[tw]
                rows = window_rows(m, tw, sz)
                keys_ok = (sc_ref[1 + m] - tw * sz.frames) * sz.frame

                @pl.when(keys_ok > 0)
                def _(rows=rows, size=size, keys_ok=keys_ok):
                    column = lax.broadcasted_iota(jnp.int32, (1, size), 1)
                    for head in range(sz.group):
                        lanes = slice(head * sz.head, (head + 1) * sz.head)
                        scores = dot_nt(qkv_ref[0, rows, lanes], qkv_ref[1, rows, lanes])
                        scores = scores + spread[head, :size, :size].astype(F32)
                        scores = jnp.where(column < keys_ok, scores, MASKED)
                        top = jnp.max(scores, axis=-1, keepdims=True)
                        weight = jnp.exp(scores - top)
                        share = 1.0 / jnp.sum(weight, axis=-1, keepdims=True)
                        probs = (weight * share).astype(BF16)
                        att_ref[rows, lanes] = dot_nn(probs, qkv_ref[2, rows, lanes]).astype(BF16)

                @pl.when(keys_ok <= 0)
                def _(rows=rows, size=size):
                    att_ref[rows, :] = jnp.zeros((size, gcols), BF16)

            return carry

        lax.fori_loop(0, sz.micro, one_micro, 0)
        if not last:
            return
        kept, total = take(2)
        for n in range(steps):

            @pl.when(step == n)
            def _(n=n):
                kept[:, n * gcols : (n + 1) * gcols] = att_ref[...]

        @pl.when(step == steps - 1)
        def _():
            if joint:
                place(out_refs[: n_out // 2], key, z_here, wo_ref, slice(0, 2 * gcols))
                place(out_refs[n_out // 2 :], key, z_here, wo_ref, slice(2 * gcols, 4 * gcols))
            else:
                place(out_refs, key, z_here, wo_ref)
            middle = first_ref.shape[1]
            total[...] = dot_nn(first_ref[...], wo_ref[:middle]) + dot_nn(
                kept[...], wo_ref[middle:]
            )
            for m in range(sz.micro):
                for f in range(sz.used):
                    at = m * sz.win_rows + f * sz.frame
                    valid = (f < sc_ref[1 + m]).astype(F32)
                    bo_ref[m, f] = (total[at : at + sz.half] * valid).astype(BF16)
                    bf_ref[m, f] = (total[at + sz.half : at + sz.frame] * valid).astype(BF16)

    piece = (sz.micro, sz.used, sz.half, sz.width)
    fixed = lambda g, s: (0, 0, 0, 0)
    flat = lambda g, s: (0, 0)
    width, cols = sz.width, sz.width // 2
    in_specs = [
        once(piece, fixed),
        once(piece, fixed),
        pl.BlockSpec((sz.group,) + bias.shape[1:], lambda g, s: (half * steps + g, 0, 0, 0)),
    ] + w_qkv.specs(3 * gcols, lambda g, s: g)
    out_specs = [
        pl.BlockSpec((3, sz.rows, gcols), lambda g, s: (0, 0, half * steps + g)),
        pl.BlockSpec((width, 3 * gcols), lambda g, s: (0, half * steps + g)),
        pl.BlockSpec((sz.rows, gcols), lambda g, s: (0, g)),
    ]
    out_shape = [
        jax.ShapeDtypeStruct((3, sz.rows, width), BF16),
        jax.ShapeDtypeStruct((width, 3 * width), BF16),
        jax.ShapeDtypeStruct((sz.rows, cols), BF16),
    ]
    aliases = {}
    scratch = [
        pltpu.VMEM((sz.rows, width), BF16),
        pltpu.VMEM((sz.group, sz.lens[0], sz.lens[0]), BF16),
    ]
    args = [scalars, own, far, bias, *w_qkv.arrays]
    flops = 6 * sz.rows * width * cols + 4 * sz.rows * sz.lens[0] * cols
    if last:
        in_specs += [once((sz.rows, cols), flat)]
        if joint:
            low = w_out.arrays[0].shape[-1] // (2 * gcols) - 2
            in_specs += w_out.specs(2 * gcols, lambda g, s: low)
            in_specs += w_out.specs(2 * gcols, lambda g, s: low + 1)
            out_args = w_out.arrays * 2
        else:
            in_specs += w_out.specs(width, lambda g, s: 0)
            out_args = w_out.arrays
        out_specs += [pl.BlockSpec((width, width), flat)] + [pl.BlockSpec(piece, fixed)] * 2
        out_shape += [jax.ShapeDtypeStruct((width, width), BF16)]
        out_shape += [jax.ShapeDtypeStruct(piece, BF16)] * 2
        scratch += [pltpu.VMEM((sz.rows, cols), BF16), pltpu.VMEM((sz.rows, width), F32)]
        args += [first[2], *out_args]
        aliases = {len(args): 0, len(args) + 1: 1}
        in_specs += [pl.BlockSpec(memory_space=pl.ANY)] * 2
        args += first[:2]
        flops += 2 * sz.rows * width * width
    return pl.pallas_call(
        kernel,
        grid_spec=pltpu.PrefetchScalarGridSpec(
            num_scalar_prefetch=1,
            grid=(steps,),
            in_specs=in_specs,
            out_specs=out_specs,
            scratch_shapes=scratch,
        ),
        out_shape=out_shape,
        input_output_aliases=aliases,
        compiler_params=params(1),
        cost_estimate=cost(3 * flops, 16 * sz.rows * width),
        name="attention" + "_last" * last,
    )(*args)


def attention_back(grad_own, grad_far, own, far, qkv, atts, w_qkv, w_out, bias, scalars, sz, shard):
    scale = 1.0 / math.sqrt(sz.head)
    steps = sz.groups
    direct = shard is not None
    outs = 2 if direct else 1
    gcols, width = sz.gcols, sz.width
    quarter = width // 4

    def kernel(
        sc_ref, go_ref, gf_ref, own_ref, far_ref, qkv_ref, w_ref, wo_ref, bias_ref, *refs
    ):
        refs = list(refs)
        take = lambda count: [refs.pop(0) for _ in range(count)]
        att_refs = take(2)
        gw_refs = take(outs)
        gwo_refs = gw_refs if direct else take(1)
        fold_ref, ho_ref, hf_ref = take(3)
        grad, hidden_t, grad_att, parts, spread, pair_sum, total, turned = take(8)
        (folded,) = take(1)
        step = pl.program_id(0)

        @pl.when(step == 0)
        def _():
            join_frames(own_ref, far_ref, grad, sz)
            turn(grad[...], hidden_t, sc_ref[0], shard)
            join_frames(go_ref, gf_ref, grad, sz)
            total[...] = jnp.zeros_like(total)
            for n, a_ref in enumerate(att_refs):
                turn(a_ref[...], turned, sc_ref[0], shard, n * a_ref.shape[1])

        grad_att[...] = dot_nt(grad[...], wo_ref[...]).astype(BF16)
        full = sz.lens[0]
        for head in range(sz.group):
            spread_bias(bias_ref, head, spread.at[head], sz, True)
            pair_sum[head] = jnp.zeros((full, full), F32)

        def one_micro(m, carry):
            for tw in range(2):
                size = sz.lens[tw]
                rows = window_rows(m, tw, sz)
                keys_ok = (sc_ref[1 + m] - tw * sz.frames) * sz.frame

                @pl.when(keys_ok > 0)
                def _(rows=rows, size=size, keys_ok=keys_ok):
                    row = lax.broadcasted_iota(jnp.int32, (size, 1), 0)
                    for head in range(sz.group):
                        lanes = slice(head * sz.head, (head + 1) * sz.head)
                        spot = [slice(n * gcols + lanes.start, n * gcols + lanes.stop) for n in range(3)]
                        query = qkv_ref[0, rows, lanes]
                        key = qkv_ref[1, rows, lanes]
                        value = qkv_ref[2, rows, lanes]
                        grad_out = grad_att[rows, lanes]
                        scores = dot_nt(key, query) + spread[head, :size, :size].astype(F32)
                        scores = jnp.where(row < keys_ok, scores, MASKED)
                        weight = jnp.exp(scores - jnp.max(scores, axis=0, keepdims=True))
                        probs = weight * (1.0 / jnp.sum(weight, axis=0, keepdims=True))
                        grad_probs = dot_nt(value, grad_out)
                        inner = jnp.sum(probs * grad_probs, axis=0, keepdims=True)
                        grad_scores = (probs * (grad_probs - inner)).astype(BF16)
                        pair_sum[head, :size, :size] += grad_scores.astype(F32)
                        parts[rows, spot[2]] = dot_nn(probs.astype(BF16), grad_out).astype(BF16)
                        parts[rows, spot[1]] = dot_nn(grad_scores, query).astype(BF16)
                        parts[rows, spot[0]] = (dot_tn(grad_scores, key) * scale).astype(BF16)

                @pl.when(keys_ok <= 0)
                def _(rows=rows, size=size):
                    parts[rows, :] = jnp.zeros((size, 3 * gcols), BF16)

            return carry

        lax.fori_loop(0, sz.micro, one_micro, 0)
        for head in range(sz.group):
            folded[...] = jnp.zeros_like(folded)
            for t in range(sz.frames):
                low = (sz.frames - 1 - t) * sz.frame
                folded[:, low : low + full] += pair_sum[head, t * sz.frame : (t + 1) * sz.frame, :]
            fold_ref[head] = folded[...].astype(BF16)
        for n in range(4):
            rows = slice(n * quarter, (n + 1) * quarter)
            give(gw_refs, n // 2, n % 2 * quarter, dot_nn(hidden_t[rows, :], parts[...]))
        total[...] += dot_nt(parts[...], w_ref[...])
        columns = pl.ds(pl.multiple_of(step * gcols, gcols), gcols)
        for n in range(4):
            rows = slice(n * quarter, (n + 1) * quarter)
            value = dot_nn(turned[rows, :], grad[:, columns])
            give(gwo_refs, n // 2, n % 2 * quarter, value, 3 * gcols if direct else 0)

        @pl.when(step == steps - 1)
        def _():
            for m in range(sz.micro):
                for f in range(sz.used):
                    at = m * sz.win_rows + f * sz.frame
                    ho_ref[m, f] = total[at : at + sz.half].astype(BF16)
                    hf_ref[m, f] = total[at + sz.half : at + sz.frame].astype(BF16)

    piece = (sz.micro, sz.used, sz.half, width)
    fixed = lambda g, s: (0, 0, 0, 0)
    flat = lambda g, s: (0, 0)
    cols = width // 2
    fold = (sz.frame, (2 * sz.frames - 1) * sz.frame)
    in_specs = [
        once(piece, fixed),
        once(piece, fixed),
        once(piece, fixed),
        once(piece, fixed),
        pl.BlockSpec((3, sz.rows, gcols), lambda g, s: (0, 0, g)),
        pl.BlockSpec((width, 3 * gcols), lambda g, s: (0, g)),
        pl.BlockSpec((gcols, width), lambda g, s: (g, 0)),
        pl.BlockSpec((sz.group,) + bias.shape[1:], lambda g, s: (g, 0, 0, 0)),
    ]
    along = lambda g, s: g
    wide = 4 * gcols if direct else 3 * gcols
    out_specs = grad_specs(direct, shard, width, wide, along)
    if not direct:
        out_specs += grad_specs(direct, shard, width, gcols, along)
    out_specs += [pl.BlockSpec((sz.group,) + fold, lambda g, s: (g, 0, 0))]
    out_specs += [pl.BlockSpec(piece, fixed)] * 2
    out_shape = grad_shapes(direct, shard, width, steps * wide)
    if not direct:
        out_shape += grad_shapes(direct, shard, width, width)
    out_shape += [jax.ShapeDtypeStruct((HEADS,) + fold, BF16)]
    out_shape += [jax.ShapeDtypeStruct(piece, BF16)] * 2
    scratch = [
        pltpu.VMEM((sz.rows, width), BF16),
        pltpu.VMEM((width, sz.rows), BF16),
        pltpu.VMEM((sz.rows, gcols), BF16),
        pltpu.VMEM((sz.rows, 3 * gcols), BF16),
        pltpu.VMEM((sz.group, sz.lens[0], sz.lens[0]), BF16),
        pltpu.VMEM((sz.group, sz.lens[0], sz.lens[0]), F32),
    ]
    args = [scalars, grad_own, grad_far, own, far, qkv, w_qkv, w_out, bias]
    flops = 16 * sz.rows * width * width + 10 * sz.rows * sz.lens[0] * width
    in_specs += [once((sz.rows, cols), flat)] * 2
    scratch += [pltpu.VMEM((sz.rows, width), F32), pltpu.VMEM((width, sz.rows), BF16)]
    scratch += [pltpu.VMEM(fold, F32)]
    args += list(atts)
    return pl.pallas_call(
        kernel,
        grid_spec=pltpu.PrefetchScalarGridSpec(
            num_scalar_prefetch=1,
            grid=(steps,),
            in_specs=in_specs,
            out_specs=out_specs,
            scratch_shapes=scratch,
        ),
        out_shape=out_shape,
        compiler_params=params(1),
        cost_estimate=cost(3 * flops, 24 * sz.rows * width),
        name="attention_back",
    )(*args)


GELU_A = math.sqrt(2.0 / math.pi)
GELU_B = 0.044715
MLP_TILES = 3
CHUNK = 512


def mlp(hidden, grad, weights, b_up, scalars, sz, shard, inner_first):
    chunk = CHUNK
    tiles = MLP_TILES
    tile = sz.rows // tiles
    inner = b_up.shape[1]
    steps = inner // chunk
    packed = len(weights) == 1
    direct = shard is not None
    rows, width = sz.rows, sz.width
    quarter = width // 4
    n_up = len(weights[0].arrays)
    copied = n_up > 1

    def kernel(sc_ref, h_ref, g_ref, bu_ref, *refs):
        refs = list(refs)
        take = lambda count: [refs.pop(0) for _ in range(count)]
        up_refs = take(n_up)
        down_refs = up_refs if packed else take(1)
        y_ref, t_ref, gbu_ref = take(3)
        if inner_first:
            (gbd_ref,) = take(1)
        gw_refs = take(2 if direct else 1)
        gwd_refs = gw_refs if packed else take(1)
        hidden_t, act_s, gpre_s = take(3)
        step = pl.program_id(0)
        key, z_here = sc_ref[1 + sz.micro], sc_ref[2 + sz.micro]

        @pl.when(step == 0)
        def _():
            turn(h_ref[...], hidden_t, sc_ref[0], shard)
            if inner_first:
                gbd_ref[...] = jnp.sum(g_ref[...].astype(F32), axis=0, keepdims=True)
            y_ref[...] = jnp.zeros_like(y_ref)
            t_ref[...] = jnp.zeros_like(t_ref)

        if packed:
            (wd_ref,) = take(1)
            place_inner(down_refs, key, z_here, wd_ref, slice(chunk, chunk + width // 2))
        else:
            wd_ref = down_refs[0]
        if copied:
            (wu_ref,) = take(1)
            place(up_refs, key, z_here, wu_ref, source=slice(0, chunk))
        else:
            wu_ref = up_refs[0]
        bias_sum = jnp.zeros((1, chunk), F32)
        for n in range(tiles):
            span = slice(n * tile, (n + 1) * tile)
            pre = dot_nn(h_ref[span], wu_ref[:, :chunk]) + bu_ref[...]
            grad_act = dot_nt(g_ref[span], wd_ref[...])
            square = pre * pre
            tanh = jnp.tanh(GELU_A * pre * (1.0 + GELU_B * square))
            half = 0.5 * (1.0 + tanh)
            act = (pre * half).astype(BF16)
            slope = half + (0.5 * GELU_A) * pre * (1.0 - tanh * tanh) * (
                1.0 + (3.0 * GELU_B) * square
            )
            grad_pre = (grad_act * slope).astype(BF16)
            act_s[0, span] = act[:, : chunk // 2]
            act_s[1, span] = act[:, chunk // 2 :]
            gpre_s[span] = grad_pre
            bias_sum = bias_sum + jnp.sum(grad_pre.astype(F32), axis=0, keepdims=True)
            y_ref[span] += dot_nn(act, wd_ref[...])
            t_ref[span] += dot_nt(grad_pre, wu_ref[:, :chunk])
        gbu_ref[...] = bias_sum
        for n in range(4):
            span = slice(n * quarter, (n + 1) * quarter)
            give(gw_refs, n // 2, n % 2 * quarter, dot_nn(hidden_t[span, :], gpre_s[...]))
        for n in range(2):
            source = sc_ref[0] ^ n if direct else n
            value = dot_tn(act_s[source], g_ref[...])
            if not packed:
                give(gwd_refs, n, 0, value)
                continue
            value = value.astype(BF16)
            cut = chunk // 32
            for half in range(2):
                part = value[:, half * width // 2 : (half + 1) * width // 2]
                if direct:
                    gw_refs[n][:, half * cut : (half + 1) * cut, chunk:] = part.reshape(
                        16, cut, width // 2
                    )
                    continue
                for k in range(16):
                    to = (2 * k + n) * 2 * cut + half * cut
                    gw_refs[0][to : to + cut, chunk:] = part[k * cut : (k + 1) * cut]

    fixed = lambda j, s: (0, 0)
    along = lambda j, s: j
    in_specs = [
        once((rows, width), fixed),
        once((rows, width), fixed),
        pl.BlockSpec((1, chunk), lambda j, s: (0, j)),
    ]
    args = [scalars, hidden, grad, b_up]
    out_specs = [
        pl.BlockSpec((rows, width), fixed),
        pl.BlockSpec((rows, width), fixed),
        pl.BlockSpec((1, chunk), lambda j, s: (0, j)),
    ]
    out_shape = [
        jax.ShapeDtypeStruct((rows, width), F32),
        jax.ShapeDtypeStruct((rows, width), F32),
        jax.ShapeDtypeStruct((1, inner), F32),
    ]
    if inner_first:
        out_specs += [pl.BlockSpec((1, width), fixed)]
        out_shape += [jax.ShapeDtypeStruct((1, width), F32)]
    if packed:
        wide = chunk + width // 2
        in_specs += weights[0].specs(wide, along)
        args += weights[0].arrays
        out_specs += grad_specs(direct, shard, width, wide, along)
        out_shape += grad_shapes(direct, shard, width, steps * wide)
    else:
        in_specs += weights[0].specs(chunk, along)
        in_specs += [pl.BlockSpec((chunk, width), lambda j, s: (j, 0))]
        args += [weights[0].arrays[0], weights[1].arrays[0]]
        out_specs += grad_specs(False, None, width, chunk, along)
        out_specs += [pl.BlockSpec((chunk, width), lambda j, s: (j, 0))]
        out_shape += grad_shapes(False, None, width, inner)
        out_shape += grad_shapes(False, None, inner, width)
    scratch = [
        pltpu.VMEM((width, rows), BF16),
        pltpu.VMEM((2, rows, chunk // 2), BF16),
        pltpu.VMEM((rows, chunk), BF16),
    ]
    if packed:
        scratch += [pltpu.VMEM((chunk, width), BF16)]
    if copied:
        scratch += [pltpu.VMEM((width, chunk), BF16)]
    return pl.pallas_call(
        kernel,
        grid_spec=pltpu.PrefetchScalarGridSpec(
            num_scalar_prefetch=1,
            grid=(steps,),
            in_specs=in_specs,
            out_specs=out_specs,
            scratch_shapes=scratch,
        ),
        out_shape=out_shape,
        compiler_params=params(1),
        cost_estimate=cost(14 * rows * width * inner, 16 * rows * width),
        name="mlp",
    )(*args)


def offset_onehot(core, sz):
    span = 2 * sz.side - 1
    place = jnp.arange(sz.frame, dtype=jnp.int32)
    row = ((place // sz.half) ^ core) * sz.strip_rows + place // sz.side % sz.strip_rows
    column = place % sz.side
    index = (row[:, None] - row[None, :] + sz.side - 1) * span
    index = index + column[:, None] - column[None, :] + sz.side - 1
    return (jnp.arange(span * span, dtype=jnp.int32)[:, None, None] == index[None]).astype(BF16)


def bucket_onehot(bucket, count):
    return (jnp.arange(count, dtype=jnp.int32)[:, None] == bucket[None, :]).astype(BF16)


def bias_blocks(table, bucket, places, sz):
    by_offset = dot_tn(table, bucket_onehot(bucket, table.shape[0])).astype(BF16)
    by_offset = by_offset.reshape(HEADS * (2 * sz.frames - 1), -1)
    blocks = dot_nn(by_offset, places.reshape(places.shape[0], -1)).astype(BF16)
    return blocks.reshape(HEADS, -1, sz.frame, sz.frame)


def split_low(value):
    high = value.astype(BF16)
    return high, (value - high.astype(F32)).astype(BF16)


def offset_grad(fold, places, sz):
    steps = 2 * sz.frames - 1
    fold = fold.reshape(-1, sz.frame, steps, sz.frame)
    made = jnp.einsum("hqkp,jpq->hkj", fold, places, preferred_element_type=F32)
    return made.reshape(fold.shape[0], -1)


def table_grad(by_offset, bucket, buckets):
    onehot = bucket_onehot(bucket, buckets)
    return sum(dot_nt(onehot, part) for part in split_low(by_offset))


class Net:
    AXES = ("clip", "win")
    X, Y, CORE = 2, 4, 1

    def __init__(self):
        self.count = lax.axis_size(self.AXES)
        self.direct = lax.axis_size("win") == 4 and self.count == 32
        self.deep = self.count // 8
        self.index = lax.axis_index(self.AXES)
        self.z = self.index // 8

    def bit(self, which):
        return self.index // which % 2

    def swap(self, value, which):
        return lax.ppermute(value, self.AXES, [(n, n ^ which) for n in range(self.count)])

    def from_z(self, value, step):
        move = lambda n: (n // 8 - step) % self.deep * 8 + n % 8
        return lax.ppermute(value, self.AXES, [(n, move(n)) for n in range(self.count)])

    def swap_sum(self, value, which):
        return value + self.swap(value, which)


    def gather_clips(self, value):
        along = jnp.stack([value] + [self.from_z(value, k) for k in range(1, self.deep)])
        return jnp.stack([along, self.swap(along, self.Y)], axis=1)

    def scatter_clips(self, value, notes):
        got = self.swap(value[:, 1], self.Y)
        notes.append(got)
        kept = value[:, 0] + got
        got = [self.from_z(kept[self.deep - k], k) for k in range(1, self.deep)]
        notes.append(got[-1])
        return kept[0] + sum(got)

    def share(self, value, count, scatter):
        deep = self.deep
        got = self.swap(value, self.Y)
        clips = jnp.stack([value[:count], got[:count]])
        rest = (value[count:] + got[count:]).reshape(deep, -1)
        pick = lambda at: lax.dynamic_index_in_dim(rest, at % deep, 0, keepdims=False)
        sends = [
            jnp.concatenate([clips.reshape(-1), pick(self.z + deep - k)]).astype(BF16)
            for k in range(1, deep)
        ]
        sends = tie2(sends, scatter.got[:1])
        got = [self.from_z(send, k).astype(F32) for k, send in enumerate(sends, 1)]
        clips = jnp.stack([clips] + [v[: 2 * count].reshape(2, count) for v in got])
        rest = (pick(self.z) + sum(v[2 * count :] for v in got)).reshape(8, -1)
        return clips, lax.dynamic_index_in_dim(rest, self.index % 8, 0, keepdims=False)

    def gather_pairs(self, value):
        parts = value
        for which in (self.X, self.CORE):
            parts = jnp.stack([parts, self.swap(parts, which)], axis=2 if which == self.X else 3)
        parts = parts.reshape(self.count, -1)
        place = jnp.arange(self.count, dtype=jnp.int32)
        holder = (self.z + place // 8) % self.deep * 8 + (place % 8 ^ self.index % 8)
        pick = (place[:, None] == holder[None, :]).astype(BF16)
        return dot_nn(pick, parts).astype(BF16)


def cut_rows(parts, widths):
    rows, columns = parts[0].shape
    half = rows // 2

    def kernel(*refs):
        ins, outs = refs[: len(parts)], refs[len(parts) :]
        for n, ref in enumerate(ins):
            low = 0
            for k, size in enumerate(widths):
                for side in range(2):
                    outs[2 * k + side][n] = ref[side * half : (side + 1) * half, low : low + size]
                low += size

    return pl.pallas_call(
        kernel,
        out_shape=[
            jax.ShapeDtypeStruct((len(parts), half, size), BF16) for size in widths for _ in range(2)
        ],
        compiler_params=pltpu.CompilerParams(vmem_limit_bytes=VMEM_LIMIT),
        cost_estimate=cost(0, 4 * len(parts) * rows * columns),
        name="cut_rows",
    )(*parts)


class Gather:
    def __init__(self, net, halves):
        self.net = net
        self.halves = list(halves)
        self.got = []

    @staticmethod
    def along_z(net, shards):
        both = jnp.concatenate(shards, axis=1)
        return Gather.cut(net, both, Gather.send_z(net, both), [v.shape[1] for v in shards])

    @staticmethod
    def send_z(net, shard):
        return [net.from_z(shard, k) for k in range(1, net.deep)]

    @staticmethod
    def cut(net, shard, got, widths):
        made = cut_rows([shard] + list(got), widths)
        return [Gather(net, made[2 * n : 2 * n + 2]) for n in range(len(widths))]

    def start(self, first):
        net = self.net
        order = (net.X, net.Y) if first else (net.Y, net.X)
        self.got = [net.swap(v, which) for v, which in zip(self.halves, order)]

    def join(self):
        self.halves = [jnp.stack(pair) for pair in zip(self.halves, self.got)]

    def tie(self, *others):
        self.got = list(lax.optimization_barrier((*self.got, *others))[: len(self.got)])

    def core(self):
        net = self.net
        self.halves = [v for pair in zip(self.halves, self.got) for v in pair]
        self.got = [net.swap(v, net.CORE) for v in self.halves]

    def pieces(self):
        near, far = self.halves, self.got
        return Pieces([*near[:2], *far[:2], *near[2:], *far[2:]])


def add_bf16(one, two):
    return (one.astype(F32) + two.astype(F32)).astype(BF16)


class Scatter:
    def __init__(self, net, pair):
        self.net = net
        keep, send = [v.reshape((net.deep, 4) + v.shape[1:]) for v in pair]
        self.keep = [keep]
        self.got = [net.swap(send, net.CORE)]
        self.bits = jnp.stack([net.bit(net.Y), net.bit(net.X), net.z])
        self.rows, self.columns = keep.shape[2:]

    def tie(self, *others):
        self.got = list(lax.optimization_barrier((*self.got, *others))[: len(self.got)])

    def tie_keep(self, *others):
        self.keep = list(lax.optimization_barrier((*self.keep, *others))[: len(self.keep)])

    def second(self):
        net, cut = self.net, self.rows // 2

        def kernel(sc_ref, keep, got, *outs):
            for half in range(2):
                span = slice(half * cut, (half + 1) * cut)
                for role in range(2):
                    for other in range(2):
                        near = sc_ref[half] ^ role
                        at = near * 2 + other if half == 0 else other * 2 + near
                        outs[2 * half + role][0, other] = add_bf16(keep[0, at, span], got[0, at, span])

        spans = 1
        block = (1,) + self.keep[0].shape[1:3] + (self.columns // spans,)
        out = (2, cut, self.columns // spans)
        made = pl.pallas_call(
            kernel,
            grid_spec=pltpu.PrefetchScalarGridSpec(
                num_scalar_prefetch=1,
                grid=(net.deep, spans),
                in_specs=[pl.BlockSpec(block, lambda z, n, s: (z, 0, 0, n))] * 2,
                out_specs=[pl.BlockSpec((1,) + out, lambda z, n, s: (z, 0, 0, n))] * 4,
            ),
            out_shape=[jax.ShapeDtypeStruct((net.deep, 2, cut, self.columns), BF16)] * 4,
            compiler_params=params(2),
            cost_estimate=cost(0, 6 * self.keep[0].size),
            name="add_cores",
        )(self.bits, *self.keep, *self.got)
        self.keep = [made[0], made[2]]
        self.got = [net.swap(made[1], net.Y), net.swap(made[3], net.X)]

    def third(self):
        net, cut = self.net, self.rows // 2

        def kernel(sc_ref, k0, k1, g0, g1, *outs):
            for half, (keep, got) in enumerate(((k0, g0), (k1, g1))):
                for role in range(2):
                    at = sc_ref[1 - half] ^ role
                    outs[2 * half + role][...] = add_bf16(keep[:, at], got[:, at])

        out = jax.ShapeDtypeStruct((net.deep, cut, self.columns), BF16)
        made = self.call(kernel, [*self.keep, *self.got], [out] * 4, "add_second")
        self.keep = [made[0], made[2]]
        self.got = [net.swap(made[1], net.X), net.swap(made[3], net.Y)]

    def fourth(self):
        net, rows, cut = self.net, self.rows, self.rows // 2

        def kernel(sc_ref, k0, k1, g0, g1, *outs):
            for away, out in enumerate(outs):
                at = (sc_ref[2] + net.deep - away) % net.deep
                out[:cut] = add_bf16(k0[at], g0[at])
                out[cut:] = add_bf16(k1[at], g1[at])

        out = jax.ShapeDtypeStruct((rows, self.columns), BF16)
        made = self.call(kernel, [*self.keep, *self.got], [out] * net.deep, "add_third")
        self.keep = [made[0]]
        self.got = [net.from_z(made[k], k) for k in range(1, net.deep)]

    def total(self):
        return self.keep[0].astype(F32) + sum(v.astype(F32) for v in self.got)

    def total_heads(self, sz):
        size = sz.gcols

        def kernel(sc_ref, own, g0, g1, g2, qkv_ref, out_ref):
            for g in range(sz.groups):
                for n in range(4):
                    low = (4 * g + n) * size
                    total = sum(v[:, low : low + size].astype(F32) for v in (own, g0, g1, g2))
                    if n < 3:
                        low = n * sz.width + g * size
                        qkv_ref[:, low : low + size] = total
                    else:
                        out_ref[:, g * size : (g + 1) * size] = total

        outs = [jax.ShapeDtypeStruct((self.rows, k * sz.width), F32) for k in (3, 1)]
        return self.call(kernel, [*self.keep, *self.got], outs, "total_heads")

    def call(self, kernel, args, outs, name):
        return pl.pallas_call(
            kernel,
            grid_spec=pltpu.PrefetchScalarGridSpec(
                num_scalar_prefetch=1,
                grid=(1,),
                in_specs=[pl.BlockSpec(memory_space=pltpu.VMEM)] * len(args),
                out_specs=[pl.BlockSpec(memory_space=pltpu.VMEM)] * len(outs),
            ),
            out_shape=outs,
            compiler_params=params(1),
            cost_estimate=cost(0, 6 * sum(v.size for v in args)),
            name=name,
        )(self.bits, *args)


def tie(value, *others):
    return lax.optimization_barrier((value,) + others)[0]


def tie2(values, others):
    return lax.optimization_barrier((*values, *others))[: len(values)]


def body(
    tokens, cond, lengths, ada_w, ada_b, w_qkv, w_out, w_up, b_up, w_down, b_down,
    rel_table, bucket, cotangent,
):
    axes = ("clip", "win")
    sz = Sizes(tokens)
    net = Net()
    devices, index = net.count, net.index
    clips = lax.axis_size("clip")
    width = sz.width
    core = lax.axis_index("win") % 2
    swap = [(n, n ^ 1) for n in range(lax.axis_size("win"))]
    place_in = jnp.arange(3 + sz.micro, dtype=jnp.int32)
    scalars = jnp.where(place_in == 0, core, jnp.where(place_in == 1 + sz.micro, index % 8, index // 8))
    for n in range(sz.micro):
        scalars = jnp.where(place_in == 1 + n, lengths[n, 0], scalars)
    strip = (sz.micro, 2, 2, sz.frames, sz.half, width)
    tok = tokens.reshape(strip)
    cot = cotangent.reshape(strip)

    cond_act = jax.nn.silu(cond[:, 0].astype(F32)).astype(BF16)
    rows = ada_w.shape[0]
    small = jnp.concatenate([b_up, b_down, rel_table.reshape(-1)])
    n_cond = cond_act.size
    if net.direct:
        early = jnp.concatenate([cond_act.reshape(-1), small])
        early = net.gather_clips(jnp.pad(early, (0, -early.size % 128)))
        cond_all = early[:, :, :n_cond].reshape(early.shape[:2] + cond_act.shape)
    else:
        cond_all = lax.all_gather(cond_act, "clip", axis=0)
    cond_mine = lax.dynamic_slice_in_dim(cond_all, index * rows, rows, cond_all.ndim - 1)
    lead = cond_mine.shape[:-1]
    cond_mine = cond_mine.reshape(clips * sz.micro, rows)
    mod_part = dot_nn(cond_mine, ada_w)
    spread_b = jnp.zeros((mod_part.shape[1],), F32)
    spread_b = lax.dynamic_update_slice(spread_b, ada_b.astype(F32), (index * ada_b.shape[0],))
    mod_part = (mod_part + spread_b[None, :]).reshape(lead + (6 * width,))
    notes = []
    if net.direct:
        mod = net.scatter_clips(mod_part, notes)
        mod = net.swap_sum(net.swap_sum(mod, net.CORE), net.X)
    else:
        mod = lax.psum_scatter(mod_part, "clip", scatter_dimension=0, tiled=False)
        mod = lax.psum(mod, "win")
    mod = mod.reshape(sz.micro, 6, width)

    cols = width // 2
    by_group = w_qkv.reshape(rows, 3, sz.groups, sz.gcols).transpose(0, 2, 1, 3)
    by_group = by_group.reshape(rows, 2, 3 * cols)
    shard_q = [by_group[:, n] for n in range(2)]
    inner = w_up.shape[1]
    per = w_down.shape[0] // 2
    thin = CHUNK // devices

    def inner_order(value):
        if not net.direct:
            value = value.reshape(-1, devices, 2, per).transpose(2, 0, 1, 3)
        else:
            value = value.reshape(-1, devices // 2, 2, 2, per // thin, thin)
            value = value.transpose(3, 0, 4, 2, 1, 5)
        return value.reshape(2, -1, inner // 2)

    def inner_back(halves):
        value = jnp.stack(halves)
        if not net.direct:
            value = value.reshape(2, -1, devices, per).transpose(1, 2, 0, 3)
        else:
            value = value.reshape(2, -1, per // thin, 2, devices // 2, thin)
            value = value.transpose(1, 4, 3, 0, 2, 5)
        return value.reshape(-1, inner)

    def pack_inner(up, down):
        down = down.reshape(per // thin, thin, 2, width // 2).transpose(2, 1, 0, 3)
        down = down.reshape(rows, per // thin, width // 2)
        return jnp.concatenate([up.reshape(rows, -1, CHUNK), down], axis=2).reshape(rows, -1)

    def unpack_inner(value):
        value = value.reshape(rows, per // thin, -1)
        down = value[:, :, CHUNK:].reshape(2, thin, per // thin, width // 2)
        return value[:, :, :CHUNK].reshape(rows, -1), down.transpose(2, 1, 0, 3).reshape(per, width)

    shard_u = inner_order(w_up)
    shard_d = [w_down[:per], w_down[per:]]
    gather = lambda v: lax.all_gather(v, axes, axis=0, tiled=True)
    if net.direct:
        packs = [
            shard_q[0],
            jnp.concatenate([shard_q[1], w_out], axis=1),
            pack_inner(shard_u[1], shard_d[1]),
            pack_inner(shard_u[0], shard_d[0]),
        ]
        rest_q = gather(packs[1])
        rest = gather(tie(packs[2], early))
        (one,) = Gather.along_z(net, [packs[0]])
        small = net.gather_pairs(tie(early[:, :, n_cond:], *notes))
        one.halves = tie2(one.halves, [mod_part])
        one.start(True)
        one.join()
        one.halves = tie2(one.halves, notes[:1])
        one.start(False)
        three_pack = tie(packs[3], notes[0])
        three_got = tie2(Gather.send_z(net, three_pack), one.got)
        (three,) = Gather.cut(net, three_pack, three_got, [packs[3].shape[1]])
        one.core()
        full_q = [one.pieces(), Pieces([rest_q])]
        full_out = full_q[1]
    else:
        full_q = [Pieces([gather(v)]) for v in shard_q]
        full_out = Pieces([gather(w_out)])
        full_i = [[Pieces([gather(u)]), Pieces([gather(d)])] for u, d in zip(shard_u, shard_d)]
        small = gather(small[None])
    n_up, n_down = b_up.shape[0], b_down.shape[0]
    n_small = n_up + n_down + rel_table.size
    full_bup = inner_order(small[:, :n_up].astype(F32).reshape(1, inner))
    full_bdown = small[:, n_up : n_up + n_down].astype(F32).reshape(1, width)
    table = small[:, n_up + n_down : n_small].reshape(-1, HEADS)
    places = offset_onehot(core, sz)
    bias = bias_blocks(table, bucket, places, sz)

    if net.direct:
        mod = tie(mod, bias, *three.halves)
    own, send = first_norm(tok, mod, scalars, sz)
    far = lax.ppermute(send, "win", swap)
    if net.direct:
        three.start(True)
    first = attention(0, own, far, full_q[0], bias, scalars, sz)
    if net.direct:
        three.tie(first[2])
        three.join()
        three.start(False)
        first = tie2(first, three.halves)
    qkv, wide, att_1, wide_out, branch_own, branch_send = attention(
        1, own, far, full_q[1], bias, scalars, sz, first, full_out
    )
    if net.direct:
        three.tie(branch_own)
        branch_send = tie(branch_send, *three.got)
    branch_far = lax.ppermute(branch_send, "win", swap)
    hidden_two, grad_mlp = second_norm(tok, cot, branch_own, branch_far, mod, scalars, sz)
    flat = (sz.rows, width)
    both = (2, sz.micro, sz.used, sz.half, width)
    hidden_two, grad_mlp = hidden_two.reshape(flat), grad_mlp.reshape(flat)
    if net.direct:
        three.tie(branch_far)
        three.halves = tie2(three.halves, [branch_far])
        three.core()
        full_i = [[three.pieces()], [Pieces([rest])]]
    mlps = []
    for n in range(2):
        shard = rows if net.direct and n == 1 else None
        mlps.append(
            mlp(hidden_two, grad_mlp, full_i[n], full_bup[n], scalars, sz, shard, n == 0)
        )
        if net.direct and n == 0:
            pack, hidden_two = lax.optimization_barrier((mlps[0][4], hidden_two))
            r_first = lax.psum_scatter(pack, axes, scatter_dimension=0, tiled=True).astype(F32)

    if net.direct:
        second = Scatter(net, mlps[1][3:5])
    output, grad_mid, grad_own, grad_send, sums_two = after_mlp(
        tok, cot, branch_own, branch_far, [v[0].reshape(both) for v in mlps],
        [v[1].reshape(both) for v in mlps], mod, full_bdown, scalars, sz,
    )
    grad_far = lax.ppermute(grad_send, "win", swap)
    if net.direct:
        second.tie(grad_own)
        second.second()
        grad_own = tie(grad_own, *second.keep)
    *g_att, fold, hid_own, hid_send = attention_back(
        grad_own, grad_far, own, far, qkv, (first[2], att_1), wide, wide_out, bias, scalars, sz,
        rows if net.direct else None,
    )
    if net.direct:
        second.tie(hid_own)
        g_att = tie2(g_att, second.got)
        hid_send = tie(hid_send, *second.got)
        heads = Scatter(net, g_att)
        hid_far = lax.ppermute(hid_send, "win", swap)
        second.third()
        heads.tie(*second.keep)
        heads.second()
        hid_far = tie(hid_far, *heads.keep)
    else:
        hid_far = lax.ppermute(hid_send, "win", swap)
    grad_in, sums_one = last_norm(tok, cot, grad_mid, hid_own, hid_far, mod, scalars, sz)
    if net.direct:
        second.tie(sums_one, r_first)
        second.fourth()
        sums_one, fold = lax.optimization_barrier((sums_one, fold, *second.keep))[:2]

    grad_mod = jnp.concatenate(
        [sums_one, sums_two[:, 3:4], sums_two[:, 0:3]], axis=1
    ).reshape(sz.micro, 6 * width)
    g_table = table_grad(offset_grad(fold, places, sz), bucket, table.shape[0]).reshape(devices, -1)
    if net.direct:
        heads.tie(g_table)
        heads.third()
        second.tie(*heads.keep)
        r_second = second.total()
        g_table = tie(g_table, r_second)
    g_bup = inner_back([v[2] for v in mlps]).reshape(devices, -1)
    g_bdown = mlps[0][3].reshape(devices, -1)
    g_small = jnp.concatenate([g_bup, g_bdown, g_table], axis=1)
    if net.direct:
        every = jnp.concatenate([grad_mod.reshape(-1), g_small.reshape(-1)])
        every = net.swap_sum(net.swap_sum(every, net.CORE), net.X)
        heads.tie(every)
        heads.fourth()
        mod_all, g_small = net.share(tie(every, *heads.keep), grad_mod.size, heads)
    else:
        mod_all = lax.all_gather(lax.psum(grad_mod, "win"), "clip", axis=0)
        g_small = lax.psum_scatter(g_small, axes, scatter_dimension=0, tiled=False)
    mod_all = mod_all.reshape(clips * sz.micro, -1)
    grad_ada_w = lax.dot_general(
        cond_mine.astype(F32), mod_all, (((0,), (0,)), ((), ())),
        precision=HIGHEST, preferred_element_type=F32,
    )
    grad_ada_b = lax.dynamic_slice_in_dim(
        jnp.sum(mod_all, axis=0), index * ada_b.shape[0], ada_b.shape[0]
    )
    if net.direct:
        r_u, r_d = zip(unpack_inner(r_first), unpack_inner(r_second))
        r_qkv, r_out = heads.total_heads(sz)
    else:
        scatter = lambda v: lax.psum_scatter(
            v.astype(F32), axes, scatter_dimension=0, tiled=True
        )
        r_u = [scatter(v[-2]) for v in mlps]
        r_d = [scatter(v[-1]) for v in mlps]
        r_qkv, r_out = scatter(g_att[0]), scatter(g_att[1])
        r_qkv = r_qkv.reshape(rows, sz.groups, 3, sz.gcols).transpose(0, 2, 1, 3)
        r_qkv = r_qkv.reshape(rows, 3 * width)
    r_up = inner_back(r_u)
    r_down = jnp.concatenate(r_d)
    return (
        output.reshape(tokens.shape), grad_in.reshape(tokens.shape), grad_ada_w, grad_ada_b,
        r_qkv, r_out, r_up, g_small[:n_up], r_down, g_small[n_up : n_up + n_down],
        g_small[n_up + n_down :].reshape(rel_table.shape),
    )


def solution(mesh):
    weights = P(("clip", "win"), None)
    vector = P(("clip", "win"))
    strips = P(None, "clip", "win", None, None, None, None, None)
    return jax.shard_map(
        body,
        mesh=mesh,
        in_specs=(
            strips, P(None, "clip", None), P(None, "clip"), weights, vector, weights, weights,
            weights, vector, weights, vector, weights, P(), strips,
        ),
        out_specs=(
            strips, strips, weights, vector, weights, weights, weights, vector, weights, vector,
            weights,
        ),
        check_vma=False,
    )
```

```python
import functools
import math

import jax
import jax.numpy as jnp
from jax import lax
from jax.experimental import pallas as pl
from jax.experimental.pallas import tpu as pltpu
from jax.sharding import PartitionSpec as P

HEADS = 16
EPSILON = 1e-06
MASKED = -1000000000.0
F32 = jnp.float32
BF16 = jnp.bfloat16
VMEM_LIMIT = 58 * 1024 * 1024
HIGHEST = lax.Precision.HIGHEST


def dot_nn(a, b):
    return lax.dot_general(a, b, (((1,), (0,)), ((), ())), preferred_element_type=F32)


def dot_nt(a, b):
    return lax.dot_general(a, b, (((1,), (1,)), ((), ())), preferred_element_type=F32)


def dot_tn(a, b):
    return lax.dot_general(a, b, (((0,), (0,)), ((), ())), preferred_element_type=F32)


def params(count):
    return pltpu.CompilerParams(
        dimension_semantics=("arbitrary",) * count, vmem_limit_bytes=VMEM_LIMIT
    )


def cost(flops, size):
    return pl.CostEstimate(flops=flops, bytes_accessed=size, transcendentals=0)


def once(shape, index_map):
    return pl.BlockSpec(shape, index_map, pipeline_mode=pl.Buffered(1))


def normalize(values):
    centered = values - jnp.mean(values, axis=-1, keepdims=True)
    inv = lax.rsqrt(jnp.mean(centered * centered, axis=-1, keepdims=True) + EPSILON)
    return centered * inv, inv


def norm_back(grad, normed, inv):
    return inv * (
        grad
        - jnp.mean(grad, axis=-1, keepdims=True)
        - normed * jnp.mean(grad * normed, axis=-1, keepdims=True)
    )


class Sizes:
    def __init__(self, tokens):
        self.micro, _, _, self.blocks, self.frames, rows, side, self.width = tokens.shape
        self.half = rows * side
        self.cols = self.blocks // 2
        self.strip_rows, self.side = rows, side
        self.used = 2 * self.frames - 1
        self.frame = 2 * self.half
        self.win_rows = self.used * self.frame
        self.rows = self.micro * self.win_rows
        self.lens = (self.frames * self.frame, (self.frames - 1) * self.frame)
        self.head = self.width // HEADS
        self.group = 4
        self.gcols = self.group * self.head
        self.groups = HEADS // self.group


def each_frame(body, sz):
    for tw in range(2):

        def step(t, carry, tw=tw):
            body(tw, t, tw * sz.frames + t)
            return carry

        lax.fori_loop(0, sz.frames - tw, step, 0, unroll=True)


def fold_rows(value):
    return jnp.sum(value.reshape(-1, 8, value.shape[-1]), axis=0)


def first_norm(tok, mod, core, sz):
    def kernel(sc_ref, x_ref, mod_ref, own_ref, far_ref):
        shift = mod_ref[0, 0:1, :]
        scale = 1.0 + mod_ref[0, 1:2, :]
        for slot, out_ref in enumerate((own_ref, far_ref)):
            column = sc_ref[0] ^ slot

            def one(tw, t, f, column=column, out_ref=out_ref):
                normed, _ = normalize(x_ref[0, tw, column, t].astype(F32))
                out_ref[0, f] = (normed * scale + shift).astype(BF16)

            each_frame(one, sz)

    strip = (1, 2, 2, sz.frames, sz.half, sz.width)
    piece = (1, sz.used, sz.half, sz.width)
    shape = jax.ShapeDtypeStruct((sz.micro,) + piece[1:], BF16)
    return pl.pallas_call(
        kernel,
        grid_spec=pltpu.PrefetchScalarGridSpec(
            num_scalar_prefetch=1,
            grid=(sz.micro,),
            in_specs=[
                pl.BlockSpec(strip, lambda m, s: (m, 0, 0, 0, 0, 0)),
                pl.BlockSpec((1, 6, sz.width), lambda m, s: (m, 0, 0)),
            ],
            out_specs=[pl.BlockSpec(piece, lambda m, s: (m, 0, 0, 0))] * 2,
        ),
        out_shape=[shape, shape],
        compiler_params=params(1),
        name="first_norm",
    )(core, tok, mod)


def second_norm(tok, cot, branch_own, branch_far, mod, scalars, sz):
    def kernel(sc_ref, x_ref, c_ref, bo_ref, bf_ref, mod_ref, h_ref, g_ref):
        length = sc_ref[1 + pl.program_id(0)]
        gate1 = mod_ref[0, 2:3, :]
        shift = mod_ref[0, 3:4, :]
        scale = 1.0 + mod_ref[0, 4:5, :]
        gate2 = mod_ref[0, 5:6, :]
        for slot, b_ref in enumerate((bo_ref, bf_ref)):
            column = sc_ref[0] ^ slot

            def one(tw, t, f, slot=slot, column=column, b_ref=b_ref):
                rows = x_ref[0, tw, column, t].astype(F32) + gate1 * b_ref[0, f].astype(F32)
                normed, _ = normalize(rows)
                h_ref[slot, 0, f] = (normed * scale + shift).astype(BF16)
                valid = (f < length).astype(F32)
                g_ref[slot, 0, f] = (c_ref[0, tw, column, t].astype(F32) * (valid * gate2)).astype(BF16)

            each_frame(one, sz)

    strip = (1, 2, 2, sz.frames, sz.half, sz.width)
    piece = (1, sz.used, sz.half, sz.width)
    both = (2, 1, sz.used, sz.half, sz.width)
    shape = jax.ShapeDtypeStruct((2, sz.micro, sz.used, sz.half, sz.width), BF16)
    return pl.pallas_call(
        kernel,
        grid_spec=pltpu.PrefetchScalarGridSpec(
            num_scalar_prefetch=1,
            grid=(sz.micro,),
            in_specs=[
                pl.BlockSpec(strip, lambda m, s: (m, 0, 0, 0, 0, 0)),
                pl.BlockSpec(strip, lambda m, s: (m, 0, 0, 0, 0, 0)),
                pl.BlockSpec(piece, lambda m, s: (m, 0, 0, 0)),
                pl.BlockSpec(piece, lambda m, s: (m, 0, 0, 0)),
                pl.BlockSpec((1, 6, sz.width), lambda m, s: (m, 0, 0)),
            ],
            out_specs=[pl.BlockSpec(both, lambda m, s: (0, m, 0, 0, 0))] * 2,
        ),
        out_shape=[shape, shape],
        compiler_params=params(1),
        name="second_norm",
    )(scalars, tok, cot, branch_own, branch_far, mod)


def after_mlp(tok, cot, branch_own, branch_far, mlps, grads, mod, b_down, scalars, sz):
    def kernel(
        sc_ref, x_ref, c_ref, bo_ref, bf_ref, y0_ref, y1_ref, t0_ref, t1_ref, mod_ref, bd_ref,
        out_ref, gm_ref, go_ref, gf_ref, sum_ref, sums,
    ):
        length = sc_ref[1 + pl.program_id(0)]
        gate1 = mod_ref[0, 2:3, :]
        scale = 1.0 + mod_ref[0, 4:5, :]
        gate2 = mod_ref[0, 5:6, :]
        sums[...] = jnp.zeros_like(sums)
        for slot, (b_ref, g_ref) in enumerate(((bo_ref, go_ref), (bf_ref, gf_ref))):
            column = sc_ref[0] ^ slot

            def one(tw, t, f, slot=slot, column=column, b_ref=b_ref, g_ref=g_ref):
                valid = (f < length).astype(F32)
                branch = b_ref[0, f].astype(F32)
                middle = x_ref[0, tw, column, t].astype(F32) + gate1 * branch
                normed, inv = normalize(middle)
                y = y0_ref[slot, 0, f] + y1_ref[slot, 0, f] + bd_ref[0:1, :]
                grad = c_ref[0, tw, column, t].astype(F32)
                out_ref[0, tw, column, t] = (middle + valid * gate2 * y).astype(BF16)
                two = t0_ref[slot, 0, f] + t1_ref[slot, 0, f]
                gm = grad + norm_back(two * scale, normed, inv)
                gm_ref[slot, 0, f] = gm.astype(BF16)
                g_ref[0, f] = (valid * (gm * gate1)).astype(BF16)
                for n, term in enumerate((two, two * normed, grad * valid * y, gm * branch)):
                    sums[n] += fold_rows(term)

            each_frame(one, sz)
            out_ref[0, 1, column, sz.frames - 1] = x_ref[0, 1, column, sz.frames - 1]
        for n in range(4):
            sum_ref[0, n : n + 1, :] = jnp.sum(sums[n], axis=0, keepdims=True)

    strip = (1, 2, 2, sz.frames, sz.half, sz.width)
    piece = (1, sz.used, sz.half, sz.width)
    both = (2, 1, sz.used, sz.half, sz.width)
    full = (sz.micro,) + piece[1:]
    at_strip = lambda m, s: (m, 0, 0, 0, 0, 0)
    at_piece = lambda m, s: (m, 0, 0, 0)
    at_both = lambda m, s: (0, m, 0, 0, 0)
    return pl.pallas_call(
        kernel,
        grid_spec=pltpu.PrefetchScalarGridSpec(
            num_scalar_prefetch=1,
            grid=(sz.micro,),
            in_specs=[
                pl.BlockSpec(strip, at_strip),
                pl.BlockSpec(strip, at_strip),
                pl.BlockSpec(piece, at_piece),
                pl.BlockSpec(piece, at_piece),
                pl.BlockSpec(both, at_both),
                pl.BlockSpec(both, at_both),
                pl.BlockSpec(both, at_both),
                pl.BlockSpec(both, at_both),
                pl.BlockSpec((1, 6, sz.width), lambda m, s: (m, 0, 0)),
                pl.BlockSpec((1, sz.width), lambda m, s: (0, 0)),
            ],
            out_specs=[
                pl.BlockSpec(strip, at_strip),
                pl.BlockSpec(both, at_both),
                pl.BlockSpec(piece, at_piece),
                pl.BlockSpec(piece, at_piece),
                pl.BlockSpec((1, 4, sz.width), lambda m, s: (m, 0, 0)),
            ],
            scratch_shapes=[pltpu.VMEM((4, 8, sz.width), F32)],
        ),
        out_shape=[
            jax.ShapeDtypeStruct(tok.shape, BF16),
            jax.ShapeDtypeStruct((2,) + full, BF16),
            jax.ShapeDtypeStruct(full, BF16),
            jax.ShapeDtypeStruct(full, BF16),
            jax.ShapeDtypeStruct((sz.micro, 4, sz.width), F32),
        ],
        compiler_params=params(1),
        name="after_mlp",
    )(scalars, tok, cot, branch_own, branch_far, *mlps, *grads, mod, b_down)


def last_norm(tok, cot, grad_mid, grad_own, grad_far, mod, scalars, sz):
    def kernel(sc_ref, x_ref, c_ref, gm_ref, go_ref, gf_ref, mod_ref, out_ref, sum_ref, sums):
        scale = 1.0 + mod_ref[0, 1:2, :]
        sums[...] = jnp.zeros_like(sums)
        for slot, g_ref in enumerate((go_ref, gf_ref)):
            column = sc_ref[0] ^ slot

            def one(tw, t, f, slot=slot, column=column, g_ref=g_ref):
                normed, inv = normalize(x_ref[0, tw, column, t].astype(F32))
                grad = g_ref[0, f].astype(F32)
                total = gm_ref[slot, 0, f].astype(F32) + norm_back(grad * scale, normed, inv)
                out_ref[0, tw, column, t] = total.astype(BF16)
                sums[0] += fold_rows(grad)
                sums[1] += fold_rows(grad * normed)

            each_frame(one, sz)
        for slot in range(2):
            out_ref[0, 1, slot, sz.frames - 1] = c_ref[0, 0, slot, 0]
        for n in range(2):
            sum_ref[0, n : n + 1, :] = jnp.sum(sums[n], axis=0, keepdims=True)

    strip = (1, 2, 2, sz.frames, sz.half, sz.width)
    tail = (1, 1, 2, 1, sz.half, sz.width)
    piece = (1, sz.used, sz.half, sz.width)
    both = (2, 1, sz.used, sz.half, sz.width)
    return pl.pallas_call(
        kernel,
        grid_spec=pltpu.PrefetchScalarGridSpec(
            num_scalar_prefetch=1,
            grid=(sz.micro,),
            in_specs=[
                pl.BlockSpec(strip, lambda m, s: (m, 0, 0, 0, 0, 0)),
                pl.BlockSpec(tail, lambda m, s: (m, 1, 0, sz.frames - 1, 0, 0)),
                pl.BlockSpec(both, lambda m, s: (0, m, 0, 0, 0)),
                pl.BlockSpec(piece, lambda m, s: (m, 0, 0, 0)),
                pl.BlockSpec(piece, lambda m, s: (m, 0, 0, 0)),
                pl.BlockSpec((1, 6, sz.width), lambda m, s: (m, 0, 0)),
            ],
            out_specs=[
                pl.BlockSpec(strip, lambda m, s: (m, 0, 0, 0, 0, 0)),
                pl.BlockSpec((1, 2, sz.width), lambda m, s: (m, 0, 0)),
            ],
            scratch_shapes=[pltpu.VMEM((2, 8, sz.width), F32)],
        ),
        out_shape=[
            jax.ShapeDtypeStruct(tok.shape, BF16),
            jax.ShapeDtypeStruct((sz.micro, 2, sz.width), F32),
        ],
        compiler_params=params(1),
        name="last_norm",
    )(scalars, tok, cot, grad_mid, grad_own, grad_far, mod)


class Pieces:
    def __init__(self, arrays):
        self.arrays = arrays
        self.whole = len(arrays) == 1

    def specs(self, columns, index_map):
        if self.whole:
            at = lambda *g: (0, index_map(*g))
            return [pl.BlockSpec((self.arrays[0].shape[0], columns), at)]
        at = lambda *g: (0, 0, 0, index_map(*g))
        shape = self.arrays[0].shape[:-1] + (columns,)
        return [pl.BlockSpec(shape, at)] * 8


def pieces_of(refs, key, z_here):
    depth = refs[0].shape[1]
    for z in range(depth):
        for n in range(8):
            half, far, i = n // 4, n // 2 % 2, n % 2
            for j in range(2):
                away = (i * 4 + j * 2 if half == 0 else i * 2 + j * 4) + far
                yield (z_here + z) % depth, key ^ away, half, refs[n].at[j, z]


def place(refs, key, z_here, out_ref, columns=slice(None), source=slice(None)):
    if len(refs) == 1:
        out_ref[:, columns] = refs[0][:, source]
        return
    for z, at, half, piece in pieces_of(refs, key, z_here):
        cut = piece.shape[0]
        row = pl.multiple_of((z * 8 + at) * (2 * cut) + half * cut, cut)
        out_ref[pl.ds(row, cut), columns] = piece[:, source]


def place_inner(refs, key, z_here, out_ref, source):
    size = source.stop - source.start
    if len(refs) == 1:
        cut = out_ref.shape[0] // 32
        for n in range(64):
            at, half = n // 2, n % 2
            to = (at % 2) * (16 * cut) + at // 2 * cut
            out_ref[to : to + cut, half * size : (half + 1) * size] = refs[0][
                n * cut : (n + 1) * cut, source
            ]
        return
    for z, at, half, piece in pieces_of(refs, key, z_here):
        cut = piece.shape[0]
        row = pl.multiple_of((at % 2) * (16 * cut) + (z * 4 + at // 2) * cut, cut)
        out_ref[pl.ds(row, cut), half * size : (half + 1) * size] = piece[:, source]


def turn(value, out_ref, core, shard, start=0):
    turned = value.T
    if shard is None:
        out_ref[start : start + turned.shape[0]] = turned
        return
    height = out_ref.shape[0]
    for n in range(turned.shape[0] // shard):
        at = start // shard + n
        at = (core ^ (at % 2)) * (height // 2) + at // 2 * shard
        out_ref[pl.ds(pl.multiple_of(at, shard), shard), :] = turned[n * shard : (n + 1) * shard]


def give(refs, half, low, value, start=0):
    value = value.astype(BF16)
    columns = slice(start, start + value.shape[1])
    if len(refs) == 1:
        low = half * (refs[0].shape[0] // 2) + low
        refs[0][low : low + value.shape[0], columns] = value
        return
    rows = refs[half].shape[1]
    refs[half][low // rows : (low + value.shape[0]) // rows, :, columns] = value.reshape(
        value.shape[0] // rows, rows, value.shape[1]
    )


def grad_shapes(direct, rows, height, columns):
    if not direct:
        return [jax.ShapeDtypeStruct((height, columns), BF16)]
    return [jax.ShapeDtypeStruct((height // (2 * rows), rows, columns), BF16)] * 2


def grad_specs(direct, rows, height, columns, at_column):
    if not direct:
        return [pl.BlockSpec((height, columns), lambda *g: (0, at_column(*g)))]
    shape = (height // (2 * rows), rows, columns)
    return [pl.BlockSpec(shape, lambda *g: (0, 0, at_column(*g)))] * 2


def join_frames(own_ref, far_ref, joined_ref, sz):
    for m in range(sz.micro):
        for f in range(sz.used):
            at = m * sz.win_rows + f * sz.frame
            joined_ref[at : at + sz.half] = own_ref[m, f]
            joined_ref[at + sz.half : at + sz.frame] = far_ref[m, f]


def spread_bias(block_ref, head, bias_ref, sz, turned=False):
    size = sz.frame
    for step in range(2 * sz.frames - 1):
        block = block_ref[head, step]
        if turned:
            block = block.T
        for key in range(sz.frames):
            query = key + step - (sz.frames - 1)
            if 0 <= query < sz.frames:
                row, column = (key, query) if turned else (query, key)
                bias_ref[row * size : (row + 1) * size, column * size : (column + 1) * size] = block


def window_rows(m, tw, sz):
    start = pl.multiple_of(m * sz.win_rows + tw * sz.lens[0], sz.frame)
    return pl.ds(start, sz.lens[tw])


def attention(half, own, far, w_qkv, bias, scalars, sz, first=None, w_out=None):
    scale = 1.0 / math.sqrt(sz.head)
    last = w_out is not None
    steps = sz.groups // 2
    gcols = sz.gcols
    joint = w_out is w_qkv
    n_out = 2 * len(w_qkv.arrays) if joint else 1

    def kernel(sc_ref, own_ref, far_ref, bias_ref, *refs):
        refs = list(refs)
        take = lambda count: [refs.pop(0) for _ in range(count)]
        w_refs = take(len(w_qkv.arrays))
        if last:
            (first_ref,) = take(1)
            out_refs = take(n_out)
            take(2)
        qkv_ref, w_ref, att_ref = take(3)
        if last:
            wo_ref, bo_ref, bf_ref = take(3)
        joined, spread = take(2)
        step = pl.program_id(0)
        key, z_here = sc_ref[1 + sz.micro], sc_ref[2 + sz.micro]

        @pl.when(step == 0)
        def _():
            join_frames(own_ref, far_ref, joined, sz)

        place(w_refs, key, z_here, w_ref)
        for n in range(3):
            part = dot_nn(joined[...], w_ref[:, n * gcols : (n + 1) * gcols]).astype(BF16)
            qkv_ref[n] = part * scale if n == 0 else part
        for head in range(sz.group):
            spread_bias(bias_ref, head, spread.at[head], sz)

        def one_micro(m, carry):
            for tw in range(2):
                size = sz.lens[tw]
                rows = window_rows(m, tw, sz)
                keys_ok = (sc_ref[1 + m] - tw * sz.frames) * sz.frame

                @pl.when(keys_ok > 0)
                def _(rows=rows, size=size, keys_ok=keys_ok):
                    column = lax.broadcasted_iota(jnp.int32, (1, size), 1)
                    for head in range(sz.group):
                        lanes = slice(head * sz.head, (head + 1) * sz.head)
                        scores = dot_nt(qkv_ref[0, rows, lanes], qkv_ref[1, rows, lanes])
                        scores = scores + spread[head, :size, :size].astype(F32)
                        scores = jnp.where(column < keys_ok, scores, MASKED)
                        top = jnp.max(scores, axis=-1, keepdims=True)
                        weight = jnp.exp(scores - top)
                        share = 1.0 / jnp.sum(weight, axis=-1, keepdims=True)
                        probs = (weight * share).astype(BF16)
                        att_ref[rows, lanes] = dot_nn(probs, qkv_ref[2, rows, lanes]).astype(BF16)

                @pl.when(keys_ok <= 0)
                def _(rows=rows, size=size):
                    att_ref[rows, :] = jnp.zeros((size, gcols), BF16)

            return carry

        lax.fori_loop(0, sz.micro, one_micro, 0)
        if not last:
            return
        kept, total = take(2)
        for n in range(steps):

            @pl.when(step == n)
            def _(n=n):
                kept[:, n * gcols : (n + 1) * gcols] = att_ref[...]

        @pl.when(step == steps - 1)
        def _():
            if joint:
                place(out_refs[: n_out // 2], key, z_here, wo_ref, slice(0, 2 * gcols))
                place(out_refs[n_out // 2 :], key, z_here, wo_ref, slice(2 * gcols, 4 * gcols))
            else:
                place(out_refs, key, z_here, wo_ref)
            middle = first_ref.shape[1]
            total[...] = dot_nn(first_ref[...], wo_ref[:middle]) + dot_nn(
                kept[...], wo_ref[middle:]
            )
            for m in range(sz.micro):
                for f in range(sz.used):
                    at = m * sz.win_rows + f * sz.frame
                    valid = (f < sc_ref[1 + m]).astype(F32)
                    bo_ref[m, f] = (total[at : at + sz.half] * valid).astype(BF16)
                    bf_ref[m, f] = (total[at + sz.half : at + sz.frame] * valid).astype(BF16)

    piece = (sz.micro, sz.used, sz.half, sz.width)
    fixed = lambda g, s: (0, 0, 0, 0)
    flat = lambda g, s: (0, 0)
    width, cols = sz.width, sz.width // 2
    in_specs = [
        once(piece, fixed),
        once(piece, fixed),
        pl.BlockSpec((sz.group,) + bias.shape[1:], lambda g, s: (half * steps + g, 0, 0, 0)),
    ] + w_qkv.specs(3 * gcols, lambda g, s: g)
    out_specs = [
        pl.BlockSpec((3, sz.rows, gcols), lambda g, s: (0, 0, half * steps + g)),
        pl.BlockSpec((width, 3 * gcols), lambda g, s: (0, half * steps + g)),
        pl.BlockSpec((sz.rows, gcols), lambda g, s: (0, g)),
    ]
    out_shape = [
        jax.ShapeDtypeStruct((3, sz.rows, width), BF16),
        jax.ShapeDtypeStruct((width, 3 * width), BF16),
        jax.ShapeDtypeStruct((sz.rows, cols), BF16),
    ]
    aliases = {}
    scratch = [
        pltpu.VMEM((sz.rows, width), BF16),
        pltpu.VMEM((sz.group, sz.lens[0], sz.lens[0]), BF16),
    ]
    args = [scalars, own, far, bias, *w_qkv.arrays]
    flops = 6 * sz.rows * width * cols + 4 * sz.rows * sz.lens[0] * cols
    if last:
        in_specs += [once((sz.rows, cols), flat)]
        if joint:
            low = w_out.arrays[0].shape[-1] // (2 * gcols) - 2
            in_specs += w_out.specs(2 * gcols, lambda g, s: low)
            in_specs += w_out.specs(2 * gcols, lambda g, s: low + 1)
            out_args = w_out.arrays * 2
        else:
            in_specs += w_out.specs(width, lambda g, s: 0)
            out_args = w_out.arrays
        out_specs += [pl.BlockSpec((width, width), flat)] + [pl.BlockSpec(piece, fixed)] * 2
        out_shape += [jax.ShapeDtypeStruct((width, width), BF16)]
        out_shape += [jax.ShapeDtypeStruct(piece, BF16)] * 2
        scratch += [pltpu.VMEM((sz.rows, cols), BF16), pltpu.VMEM((sz.rows, width), F32)]
        args += [first[2], *out_args]
        aliases = {len(args): 0, len(args) + 1: 1}
        in_specs += [pl.BlockSpec(memory_space=pl.ANY)] * 2
        args += first[:2]
        flops += 2 * sz.rows * width * width
    return pl.pallas_call(
        kernel,
        grid_spec=pltpu.PrefetchScalarGridSpec(
            num_scalar_prefetch=1,
            grid=(steps,),
            in_specs=in_specs,
            out_specs=out_specs,
            scratch_shapes=scratch,
        ),
        out_shape=out_shape,
        input_output_aliases=aliases,
        compiler_params=params(1),
        cost_estimate=cost(3 * flops, 16 * sz.rows * width),
        name="attention" + "_last" * last,
    )(*args)


def attention_back(grad_own, grad_far, own, far, qkv, atts, w_qkv, w_out, bias, scalars, sz, shard):
    scale = 1.0 / math.sqrt(sz.head)
    steps = sz.groups
    direct = shard is not None
    outs = 2 if direct else 1
    gcols, width = sz.gcols, sz.width
    quarter = width // 4

    def kernel(
        sc_ref, go_ref, gf_ref, own_ref, far_ref, qkv_ref, w_ref, wo_ref, bias_ref, *refs
    ):
        refs = list(refs)
        take = lambda count: [refs.pop(0) for _ in range(count)]
        att_refs = take(2)
        gw_refs = take(outs)
        gwo_refs = gw_refs if direct else take(1)
        fold_ref, ho_ref, hf_ref = take(3)
        grad, hidden_t, grad_att, parts, spread, pair_sum, total, turned = take(8)
        (folded,) = take(1)
        step = pl.program_id(0)

        @pl.when(step == 0)
        def _():
            join_frames(own_ref, far_ref, grad, sz)
            turn(grad[...], hidden_t, sc_ref[0], shard)
            join_frames(go_ref, gf_ref, grad, sz)
            total[...] = jnp.zeros_like(total)
            for n, a_ref in enumerate(att_refs):
                turn(a_ref[...], turned, sc_ref[0], shard, n * a_ref.shape[1])

        grad_att[...] = dot_nt(grad[...], wo_ref[...]).astype(BF16)
        full = sz.lens[0]
        for head in range(sz.group):
            spread_bias(bias_ref, head, spread.at[head], sz, True)
            pair_sum[head] = jnp.zeros((full, full), F32)

        def one_micro(m, carry):
            for tw in range(2):
                size = sz.lens[tw]
                rows = window_rows(m, tw, sz)
                keys_ok = (sc_ref[1 + m] - tw * sz.frames) * sz.frame

                @pl.when(keys_ok > 0)
                def _(rows=rows, size=size, keys_ok=keys_ok):
                    row = lax.broadcasted_iota(jnp.int32, (size, 1), 0)
                    for head in range(sz.group):
                        lanes = slice(head * sz.head, (head + 1) * sz.head)
                        spot = [slice(n * gcols + lanes.start, n * gcols + lanes.stop) for n in range(3)]
                        query = qkv_ref[0, rows, lanes]
                        key = qkv_ref[1, rows, lanes]
                        value = qkv_ref[2, rows, lanes]
                        grad_out = grad_att[rows, lanes]
                        scores = dot_nt(key, query) + spread[head, :size, :size].astype(F32)
                        scores = jnp.where(row < keys_ok, scores, MASKED)
                        weight = jnp.exp(scores - jnp.max(scores, axis=0, keepdims=True))
                        probs = weight * (1.0 / jnp.sum(weight, axis=0, keepdims=True))
                        grad_probs = dot_nt(value, grad_out)
                        inner = jnp.sum(probs * grad_probs, axis=0, keepdims=True)
                        grad_scores = (probs * (grad_probs - inner)).astype(BF16)
                        pair_sum[head, :size, :size] += grad_scores.astype(F32)
                        parts[rows, spot[2]] = dot_nn(probs.astype(BF16), grad_out).astype(BF16)
                        parts[rows, spot[1]] = dot_nn(grad_scores, query).astype(BF16)
                        parts[rows, spot[0]] = (dot_tn(grad_scores, key) * scale).astype(BF16)

                @pl.when(keys_ok <= 0)
                def _(rows=rows, size=size):
                    parts[rows, :] = jnp.zeros((size, 3 * gcols), BF16)

            return carry

        lax.fori_loop(0, sz.micro, one_micro, 0)
        for head in range(sz.group):
            folded[...] = jnp.zeros_like(folded)
            for t in range(sz.frames):
                low = (sz.frames - 1 - t) * sz.frame
                folded[:, low : low + full] += pair_sum[head, t * sz.frame : (t + 1) * sz.frame, :]
            fold_ref[head] = folded[...].astype(BF16)
        for n in range(4):
            rows = slice(n * quarter, (n + 1) * quarter)
            give(gw_refs, n // 2, n % 2 * quarter, dot_nn(hidden_t[rows, :], parts[...]))
        total[...] += dot_nt(parts[...], w_ref[...])
        columns = pl.ds(pl.multiple_of(step * gcols, gcols), gcols)
        for n in range(4):
            rows = slice(n * quarter, (n + 1) * quarter)
            value = dot_nn(turned[rows, :], grad[:, columns])
            give(gwo_refs, n // 2, n % 2 * quarter, value, 3 * gcols if direct else 0)

        @pl.when(step == steps - 1)
        def _():
            for m in range(sz.micro):
                for f in range(sz.used):
                    at = m * sz.win_rows + f * sz.frame
                    ho_ref[m, f] = total[at : at + sz.half].astype(BF16)
                    hf_ref[m, f] = total[at + sz.half : at + sz.frame].astype(BF16)

    piece = (sz.micro, sz.used, sz.half, width)
    fixed = lambda g, s: (0, 0, 0, 0)
    flat = lambda g, s: (0, 0)
    cols = width // 2
    fold = (sz.frame, (2 * sz.frames - 1) * sz.frame)
    in_specs = [
        once(piece, fixed),
        once(piece, fixed),
        once(piece, fixed),
        once(piece, fixed),
        pl.BlockSpec((3, sz.rows, gcols), lambda g, s: (0, 0, g)),
        pl.BlockSpec((width, 3 * gcols), lambda g, s: (0, g)),
        pl.BlockSpec((gcols, width), lambda g, s: (g, 0)),
        pl.BlockSpec((sz.group,) + bias.shape[1:], lambda g, s: (g, 0, 0, 0)),
    ]
    along = lambda g, s: g
    wide = 4 * gcols if direct else 3 * gcols
    out_specs = grad_specs(direct, shard, width, wide, along)
    if not direct:
        out_specs += grad_specs(direct, shard, width, gcols, along)
    out_specs += [pl.BlockSpec((sz.group,) + fold, lambda g, s: (g, 0, 0))]
    out_specs += [pl.BlockSpec(piece, fixed)] * 2
    out_shape = grad_shapes(direct, shard, width, steps * wide)
    if not direct:
        out_shape += grad_shapes(direct, shard, width, width)
    out_shape += [jax.ShapeDtypeStruct((HEADS,) + fold, BF16)]
    out_shape += [jax.ShapeDtypeStruct(piece, BF16)] * 2
    scratch = [
        pltpu.VMEM((sz.rows, width), BF16),
        pltpu.VMEM((width, sz.rows), BF16),
        pltpu.VMEM((sz.rows, gcols), BF16),
        pltpu.VMEM((sz.rows, 3 * gcols), BF16),
        pltpu.VMEM((sz.group, sz.lens[0], sz.lens[0]), BF16),
        pltpu.VMEM((sz.group, sz.lens[0], sz.lens[0]), F32),
    ]
    args = [scalars, grad_own, grad_far, own, far, qkv, w_qkv, w_out, bias]
    flops = 16 * sz.rows * width * width + 10 * sz.rows * sz.lens[0] * width
    in_specs += [once((sz.rows, cols), flat)] * 2
    scratch += [pltpu.VMEM((sz.rows, width), F32), pltpu.VMEM((width, sz.rows), BF16)]
    scratch += [pltpu.VMEM(fold, F32)]
    args += list(atts)
    return pl.pallas_call(
        kernel,
        grid_spec=pltpu.PrefetchScalarGridSpec(
            num_scalar_prefetch=1,
            grid=(steps,),
            in_specs=in_specs,
            out_specs=out_specs,
            scratch_shapes=scratch,
        ),
        out_shape=out_shape,
        compiler_params=params(1),
        cost_estimate=cost(3 * flops, 24 * sz.rows * width),
        name="attention_back",
    )(*args)


GELU_A = math.sqrt(2.0 / math.pi)
GELU_B = 0.044715
MLP_TILES = 3
CHUNK = 512


def mlp(hidden, grad, weights, b_up, scalars, sz, shard, inner_first):
    chunk = CHUNK
    tiles = MLP_TILES
    tile = sz.rows // tiles
    inner = b_up.shape[1]
    steps = inner // chunk
    packed = len(weights) == 1
    direct = shard is not None
    rows, width = sz.rows, sz.width
    quarter = width // 4
    n_up = len(weights[0].arrays)
    copied = n_up > 1

    def kernel(sc_ref, h_ref, g_ref, bu_ref, *refs):
        refs = list(refs)
        take = lambda count: [refs.pop(0) for _ in range(count)]
        up_refs = take(n_up)
        down_refs = up_refs if packed else take(1)
        y_ref, t_ref, gbu_ref = take(3)
        if inner_first:
            (gbd_ref,) = take(1)
        gw_refs = take(2 if direct else 1)
        gwd_refs = gw_refs if packed else take(1)
        hidden_t, act_s, gpre_s = take(3)
        step = pl.program_id(0)
        key, z_here = sc_ref[1 + sz.micro], sc_ref[2 + sz.micro]

        @pl.when(step == 0)
        def _():
            turn(h_ref[...], hidden_t, sc_ref[0], shard)
            if inner_first:
                gbd_ref[...] = jnp.sum(g_ref[...].astype(F32), axis=0, keepdims=True)
            y_ref[...] = jnp.zeros_like(y_ref)
            t_ref[...] = jnp.zeros_like(t_ref)

        if packed:
            (wd_ref,) = take(1)
            place_inner(down_refs, key, z_here, wd_ref, slice(chunk, chunk + width // 2))
        else:
            wd_ref = down_refs[0]
        if copied:
            (wu_ref,) = take(1)
            place(up_refs, key, z_here, wu_ref, source=slice(0, chunk))
        else:
            wu_ref = up_refs[0]
        bias_sum = jnp.zeros((1, chunk), F32)
        for n in range(tiles):
            span = slice(n * tile, (n + 1) * tile)
            pre = dot_nn(h_ref[span], wu_ref[:, :chunk]) + bu_ref[...]
            grad_act = dot_nt(g_ref[span], wd_ref[...])
            square = pre * pre
            tanh = jnp.tanh(GELU_A * pre * (1.0 + GELU_B * square))
            half = 0.5 * (1.0 + tanh)
            act = (pre * half).astype(BF16)
            slope = half + (0.5 * GELU_A) * pre * (1.0 - tanh * tanh) * (
                1.0 + (3.0 * GELU_B) * square
            )
            grad_pre = (grad_act * slope).astype(BF16)
            act_s[0, span] = act[:, : chunk // 2]
            act_s[1, span] = act[:, chunk // 2 :]
            gpre_s[span] = grad_pre
            bias_sum = bias_sum + jnp.sum(grad_pre.astype(F32), axis=0, keepdims=True)
            y_ref[span] += dot_nn(act, wd_ref[...])
            t_ref[span] += dot_nt(grad_pre, wu_ref[:, :chunk])
        gbu_ref[...] = bias_sum
        for n in range(4):
            span = slice(n * quarter, (n + 1) * quarter)
            give(gw_refs, n // 2, n % 2 * quarter, dot_nn(hidden_t[span, :], gpre_s[...]))
        for n in range(2):
            source = sc_ref[0] ^ n if direct else n
            value = dot_tn(act_s[source], g_ref[...])
            if not packed:
                give(gwd_refs, n, 0, value)
                continue
            value = value.astype(BF16)
            cut = chunk // 32
            for half in range(2):
                part = value[:, half * width // 2 : (half + 1) * width // 2]
                if direct:
                    gw_refs[n][:, half * cut : (half + 1) * cut, chunk:] = part.reshape(
                        16, cut, width // 2
                    )
                    continue
                for k in range(16):
                    to = (2 * k + n) * 2 * cut + half * cut
                    gw_refs[0][to : to + cut, chunk:] = part[k * cut : (k + 1) * cut]

    fixed = lambda j, s: (0, 0)
    along = lambda j, s: j
    in_specs = [
        once((rows, width), fixed),
        once((rows, width), fixed),
        pl.BlockSpec((1, chunk), lambda j, s: (0, j)),
    ]
    args = [scalars, hidden, grad, b_up]
    out_specs = [
        pl.BlockSpec((rows, width), fixed),
        pl.BlockSpec((rows, width), fixed),
        pl.BlockSpec((1, chunk), lambda j, s: (0, j)),
    ]
    out_shape = [
        jax.ShapeDtypeStruct((rows, width), F32),
        jax.ShapeDtypeStruct((rows, width), F32),
        jax.ShapeDtypeStruct((1, inner), F32),
    ]
    if inner_first:
        out_specs += [pl.BlockSpec((1, width), fixed)]
        out_shape += [jax.ShapeDtypeStruct((1, width), F32)]
    if packed:
        wide = chunk + width // 2
        in_specs += weights[0].specs(wide, along)
        args += weights[0].arrays
        out_specs += grad_specs(direct, shard, width, wide, along)
        out_shape += grad_shapes(direct, shard, width, steps * wide)
    else:
        in_specs += weights[0].specs(chunk, along)
        in_specs += [pl.BlockSpec((chunk, width), lambda j, s: (j, 0))]
        args += [weights[0].arrays[0], weights[1].arrays[0]]
        out_specs += grad_specs(False, None, width, chunk, along)
        out_specs += [pl.BlockSpec((chunk, width), lambda j, s: (j, 0))]
        out_shape += grad_shapes(False, None, width, inner)
        out_shape += grad_shapes(False, None, inner, width)
    scratch = [
        pltpu.VMEM((width, rows), BF16),
        pltpu.VMEM((2, rows, chunk // 2), BF16),
        pltpu.VMEM((rows, chunk), BF16),
    ]
    if packed:
        scratch += [pltpu.VMEM((chunk, width), BF16)]
    if copied:
        scratch += [pltpu.VMEM((width, chunk), BF16)]
    return pl.pallas_call(
        kernel,
        grid_spec=pltpu.PrefetchScalarGridSpec(
            num_scalar_prefetch=1,
            grid=(steps,),
            in_specs=in_specs,
            out_specs=out_specs,
            scratch_shapes=scratch,
        ),
        out_shape=out_shape,
        compiler_params=params(1),
        cost_estimate=cost(14 * rows * width * inner, 16 * rows * width),
        name="mlp",
    )(*args)


def offset_onehot(core, sz):
    span = 2 * sz.side - 1
    place = jnp.arange(sz.frame, dtype=jnp.int32)
    row = ((place // sz.half) ^ core) * sz.strip_rows + place // sz.side % sz.strip_rows
    column = place % sz.side
    index = (row[:, None] - row[None, :] + sz.side - 1) * span
    index = index + column[:, None] - column[None, :] + sz.side - 1
    return (jnp.arange(span * span, dtype=jnp.int32)[:, None, None] == index[None]).astype(BF16)


def bucket_onehot(bucket, count):
    return (jnp.arange(count, dtype=jnp.int32)[:, None] == bucket[None, :]).astype(BF16)


def bias_blocks(table, bucket, places, sz):
    by_offset = dot_tn(table, bucket_onehot(bucket, table.shape[0])).astype(BF16)
    by_offset = by_offset.reshape(HEADS * (2 * sz.frames - 1), -1)
    blocks = dot_nn(by_offset, places.reshape(places.shape[0], -1)).astype(BF16)
    return blocks.reshape(HEADS, -1, sz.frame, sz.frame)


def split_low(value):
    high = value.astype(BF16)
    return high, (value - high.astype(F32)).astype(BF16)


def offset_grad(fold, places, sz):
    steps = 2 * sz.frames - 1
    fold = fold.reshape(-1, sz.frame, steps, sz.frame)
    made = jnp.einsum("hqkp,jpq->hkj", fold, places, preferred_element_type=F32)
    return made.reshape(fold.shape[0], -1)


def table_grad(by_offset, bucket, buckets):
    onehot = bucket_onehot(bucket, buckets)
    return sum(dot_nt(onehot, part) for part in split_low(by_offset))


class Net:
    AXES = ("clip", "win")
    X, Y, CORE = 2, 4, 1

    def __init__(self):
        self.count = lax.axis_size(self.AXES)
        self.direct = lax.axis_size("win") == 4 and self.count == 32
        self.deep = self.count // 8
        self.index = lax.axis_index(self.AXES)
        self.z = self.index // 8

    def bit(self, which):
        return self.index // which % 2

    def swap(self, value, which):
        return lax.ppermute(value, self.AXES, [(n, n ^ which) for n in range(self.count)])

    def from_z(self, value, step):
        move = lambda n: (n // 8 - step) % self.deep * 8 + n % 8
        return lax.ppermute(value, self.AXES, [(n, move(n)) for n in range(self.count)])

    def swap_sum(self, value, which):
        return value + self.swap(value, which)


    def gather_clips(self, value):
        along = jnp.stack([value] + [self.from_z(value, k) for k in range(1, self.deep)])
        return jnp.stack([along, self.swap(along, self.Y)], axis=1)

    def scatter_clips(self, value, notes):
        got = self.swap(value[:, 1], self.Y)
        notes.append(got)
        kept = value[:, 0] + got
        got = [self.from_z(kept[self.deep - k], k) for k in range(1, self.deep)]
        notes.append(got[-1])
        return kept[0] + sum(got)

    def share(self, value, count, scatter):
        deep = self.deep
        got = self.swap(value, self.Y)
        clips = jnp.stack([value[:count], got[:count]])
        rest = (value[count:] + got[count:]).reshape(deep, -1)
        pick = lambda at: lax.dynamic_index_in_dim(rest, at % deep, 0, keepdims=False)
        sends = [
            jnp.concatenate([clips.reshape(-1), pick(self.z + deep - k)]).astype(BF16)
            for k in range(1, deep)
        ]
        sends = tie2(sends, scatter.got[:1])
        got = [self.from_z(send, k).astype(F32) for k, send in enumerate(sends, 1)]
        clips = jnp.stack([clips] + [v[: 2 * count].reshape(2, count) for v in got])
        rest = (pick(self.z) + sum(v[2 * count :] for v in got)).reshape(8, -1)
        return clips, lax.dynamic_index_in_dim(rest, self.index % 8, 0, keepdims=False)

    def gather_pairs(self, value):
        parts = value
        for which in (self.X, self.CORE):
            parts = jnp.stack([parts, self.swap(parts, which)], axis=2 if which == self.X else 3)
        parts = parts.reshape(self.count, -1)
        place = jnp.arange(self.count, dtype=jnp.int32)
        holder = (self.z + place // 8) % self.deep * 8 + (place % 8 ^ self.index % 8)
        pick = (place[:, None] == holder[None, :]).astype(BF16)
        return dot_nn(pick, parts).astype(BF16)


def cut_rows(parts, widths):
    rows, columns = parts[0].shape
    half = rows // 2

    def kernel(*refs):
        ins, outs = refs[: len(parts)], refs[len(parts) :]
        for n, ref in enumerate(ins):
            low = 0
            for k, size in enumerate(widths):
                for side in range(2):
                    outs[2 * k + side][n] = ref[side * half : (side + 1) * half, low : low + size]
                low += size

    return pl.pallas_call(
        kernel,
        out_shape=[
            jax.ShapeDtypeStruct((len(parts), half, size), BF16) for size in widths for _ in range(2)
        ],
        compiler_params=pltpu.CompilerParams(vmem_limit_bytes=VMEM_LIMIT),
        cost_estimate=cost(0, 4 * len(parts) * rows * columns),
        name="cut_rows",
    )(*parts)


class Gather:
    def __init__(self, net, halves):
        self.net = net
        self.halves = list(halves)
        self.got = []

    @staticmethod
    def along_z(net, shards):
        both = jnp.concatenate(shards, axis=1)
        return Gather.cut(net, both, Gather.send_z(net, both), [v.shape[1] for v in shards])

    @staticmethod
    def send_z(net, shard):
        return [net.from_z(shard, k) for k in range(1, net.deep)]

    @staticmethod
    def cut(net, shard, got, widths):
        made = cut_rows([shard] + list(got), widths)
        return [Gather(net, made[2 * n : 2 * n + 2]) for n in range(len(widths))]

    def start(self, first):
        net = self.net
        order = (net.X, net.Y) if first else (net.Y, net.X)
        self.got = [net.swap(v, which) for v, which in zip(self.halves, order)]

    def join(self):
        self.halves = [jnp.stack(pair) for pair in zip(self.halves, self.got)]

    def tie(self, *others):
        self.got = list(lax.optimization_barrier((*self.got, *others))[: len(self.got)])

    def core(self):
        net = self.net
        self.halves = [v for pair in zip(self.halves, self.got) for v in pair]
        self.got = [net.swap(v, net.CORE) for v in self.halves]

    def pieces(self):
        near, far = self.halves, self.got
        return Pieces([*near[:2], *far[:2], *near[2:], *far[2:]])


def add_bf16(one, two):
    return (one.astype(F32) + two.astype(F32)).astype(BF16)


class Scatter:
    def __init__(self, net, pair):
        self.net = net
        keep, send = [v.reshape((net.deep, 4) + v.shape[1:]) for v in pair]
        self.keep = [keep]
        self.got = [net.swap(send, net.CORE)]
        self.bits = jnp.stack([net.bit(net.Y), net.bit(net.X), net.z])
        self.rows, self.columns = keep.shape[2:]

    def tie(self, *others):
        self.got = list(lax.optimization_barrier((*self.got, *others))[: len(self.got)])

    def tie_keep(self, *others):
        self.keep = list(lax.optimization_barrier((*self.keep, *others))[: len(self.keep)])

    def second(self):
        net, cut = self.net, self.rows // 2

        def kernel(sc_ref, keep, got, *outs):
            for half in range(2):
                span = slice(half * cut, (half + 1) * cut)
                for role in range(2):
                    for other in range(2):
                        near = sc_ref[half] ^ role
                        at = near * 2 + other if half == 0 else other * 2 + near
                        outs[2 * half + role][0, other] = add_bf16(keep[0, at, span], got[0, at, span])

        spans = 1
        block = (1,) + self.keep[0].shape[1:3] + (self.columns // spans,)
        out = (2, cut, self.columns // spans)
        made = pl.pallas_call(
            kernel,
            grid_spec=pltpu.PrefetchScalarGridSpec(
                num_scalar_prefetch=1,
                grid=(net.deep, spans),
                in_specs=[pl.BlockSpec(block, lambda z, n, s: (z, 0, 0, n))] * 2,
                out_specs=[pl.BlockSpec((1,) + out, lambda z, n, s: (z, 0, 0, n))] * 4,
            ),
            out_shape=[jax.ShapeDtypeStruct((net.deep, 2, cut, self.columns), BF16)] * 4,
            compiler_params=params(2),
            cost_estimate=cost(0, 6 * self.keep[0].size),
            name="add_cores",
        )(self.bits, *self.keep, *self.got)
        self.keep = [made[0], made[2]]
        self.got = [net.swap(made[1], net.Y), net.swap(made[3], net.X)]

    def third(self):
        net, cut = self.net, self.rows // 2

        def kernel(sc_ref, k0, k1, g0, g1, *outs):
            for half, (keep, got) in enumerate(((k0, g0), (k1, g1))):
                for role in range(2):
                    at = sc_ref[1 - half] ^ role
                    outs[2 * half + role][...] = add_bf16(keep[:, at], got[:, at])

        out = jax.ShapeDtypeStruct((net.deep, cut, self.columns), BF16)
        made = self.call(kernel, [*self.keep, *self.got], [out] * 4, "add_second")
        self.keep = [made[0], made[2]]
        self.got = [net.swap(made[1], net.X), net.swap(made[3], net.Y)]

    def fourth(self):
        net, rows, cut = self.net, self.rows, self.rows // 2

        def kernel(sc_ref, k0, k1, g0, g1, *outs):
            for away, out in enumerate(outs):
                at = (sc_ref[2] + net.deep - away) % net.deep
                out[:cut] = add_bf16(k0[at], g0[at])
                out[cut:] = add_bf16(k1[at], g1[at])

        out = jax.ShapeDtypeStruct((rows, self.columns), BF16)
        made = self.call(kernel, [*self.keep, *self.got], [out] * net.deep, "add_third")
        self.keep = [made[0]]
        self.got = [net.from_z(made[k], k) for k in range(1, net.deep)]

    def total(self):
        return self.keep[0].astype(F32) + sum(v.astype(F32) for v in self.got)

    def total_heads(self, sz):
        size = sz.gcols

        def kernel(sc_ref, own, g0, g1, g2, qkv_ref, out_ref):
            for g in range(sz.groups):
                for n in range(4):
                    low = (4 * g + n) * size
                    total = sum(v[:, low : low + size].astype(F32) for v in (own, g0, g1, g2))
                    if n < 3:
                        low = n * sz.width + g * size
                        qkv_ref[:, low : low + size] = total
                    else:
                        out_ref[:, g * size : (g + 1) * size] = total

        outs = [jax.ShapeDtypeStruct((self.rows, k * sz.width), F32) for k in (3, 1)]
        return self.call(kernel, [*self.keep, *self.got], outs, "total_heads")

    def call(self, kernel, args, outs, name):
        return pl.pallas_call(
            kernel,
            grid_spec=pltpu.PrefetchScalarGridSpec(
                num_scalar_prefetch=1,
                grid=(1,),
                in_specs=[pl.BlockSpec(memory_space=pltpu.VMEM)] * len(args),
                out_specs=[pl.BlockSpec(memory_space=pltpu.VMEM)] * len(outs),
            ),
            out_shape=outs,
            compiler_params=params(1),
            cost_estimate=cost(0, 6 * sum(v.size for v in args)),
            name=name,
        )(self.bits, *args)


def tie(value, *others):
    return lax.optimization_barrier((value,) + others)[0]


def tie2(values, others):
    return lax.optimization_barrier((*values, *others))[: len(values)]


def body(
    tokens, cond, lengths, ada_w, ada_b, w_qkv, w_out, w_up, b_up, w_down, b_down,
    rel_table, bucket, cotangent,
):
    axes = ("clip", "win")
    sz = Sizes(tokens)
    net = Net()
    devices, index = net.count, net.index
    clips = lax.axis_size("clip")
    width = sz.width
    core = lax.axis_index("win") % 2
    swap = [(n, n ^ 1) for n in range(lax.axis_size("win"))]
    place_in = jnp.arange(3 + sz.micro, dtype=jnp.int32)
    scalars = jnp.where(place_in == 0, core, jnp.where(place_in == 1 + sz.micro, index % 8, index // 8))
    for n in range(sz.micro):
        scalars = jnp.where(place_in == 1 + n, lengths[n, 0], scalars)
    strip = (sz.micro, 2, 2, sz.frames, sz.half, width)
    tok = tokens.reshape(strip)
    cot = cotangent.reshape(strip)

    cond_act = jax.nn.silu(cond[:, 0].astype(F32)).astype(BF16)
    rows = ada_w.shape[0]
    small = jnp.concatenate([b_up, b_down, rel_table.reshape(-1)])
    n_cond = cond_act.size
    if net.direct:
        early = jnp.concatenate([cond_act.reshape(-1), small])
        early = net.gather_clips(jnp.pad(early, (0, -early.size % 128)))
        cond_all = early[:, :, :n_cond].reshape(early.shape[:2] + cond_act.shape)
    else:
        cond_all = lax.all_gather(cond_act, "clip", axis=0)
    cond_mine = lax.dynamic_slice_in_dim(cond_all, index * rows, rows, cond_all.ndim - 1)
    lead = cond_mine.shape[:-1]
    cond_mine = cond_mine.reshape(clips * sz.micro, rows)
    mod_part = dot_nn(cond_mine, ada_w)
    spread_b = jnp.zeros((mod_part.shape[1],), F32)
    spread_b = lax.dynamic_update_slice(spread_b, ada_b.astype(F32), (index * ada_b.shape[0],))
    mod_part = (mod_part + spread_b[None, :]).reshape(lead + (6 * width,))
    notes = []
    if net.direct:
        mod = net.scatter_clips(mod_part, notes)
        mod = net.swap_sum(net.swap_sum(mod, net.CORE), net.X)
    else:
        mod = lax.psum_scatter(mod_part, "clip", scatter_dimension=0, tiled=False)
        mod = lax.psum(mod, "win")
    mod = mod.reshape(sz.micro, 6, width)

    cols = width // 2
    by_group = w_qkv.reshape(rows, 3, sz.groups, sz.gcols).transpose(0, 2, 1, 3)
    by_group = by_group.reshape(rows, 2, 3 * cols)
    shard_q = [by_group[:, n] for n in range(2)]
    inner = w_up.shape[1]
    per = w_down.shape[0] // 2
    thin = CHUNK // devices

    def inner_order(value):
        if not net.direct:
            value = value.reshape(-1, devices, 2, per).transpose(2, 0, 1, 3)
        else:
            value = value.reshape(-1, devices // 2, 2, 2, per // thin, thin)
            value = value.transpose(3, 0, 4, 2, 1, 5)
        return value.reshape(2, -1, inner // 2)

    def inner_back(halves):
        value = jnp.stack(halves)
        if not net.direct:
            value = value.reshape(2, -1, devices, per).transpose(1, 2, 0, 3)
        else:
            value = value.reshape(2, -1, per // thin, 2, devices // 2, thin)
            value = value.transpose(1, 4, 3, 0, 2, 5)
        return value.reshape(-1, inner)

    def pack_inner(up, down):
        down = down.reshape(per // thin, thin, 2, width // 2).transpose(2, 1, 0, 3)
        down = down.reshape(rows, per // thin, width // 2)
        return jnp.concatenate([up.reshape(rows, -1, CHUNK), down], axis=2).reshape(rows, -1)

    def unpack_inner(value):
        value = value.reshape(rows, per // thin, -1)
        down = value[:, :, CHUNK:].reshape(2, thin, per // thin, width // 2)
        return value[:, :, :CHUNK].reshape(rows, -1), down.transpose(2, 1, 0, 3).reshape(per, width)

    shard_u = inner_order(w_up)
    shard_d = [w_down[:per], w_down[per:]]
    gather = lambda v: lax.all_gather(v, axes, axis=0, tiled=True)
    if net.direct:
        packs = [
            shard_q[0],
            jnp.concatenate([shard_q[1], w_out], axis=1),
            pack_inner(shard_u[1], shard_d[1]),
            pack_inner(shard_u[0], shard_d[0]),
        ]
        rest_q = gather(packs[1])
        rest = gather(tie(packs[2], early))
        (one,) = Gather.along_z(net, [packs[0]])
        small = net.gather_pairs(tie(early[:, :, n_cond:], *notes))
        one.halves = tie2(one.halves, [mod_part])
        one.start(True)
        one.join()
        one.halves = tie2(one.halves, notes[:1])
        one.start(False)
        three_pack = tie(packs[3], notes[0])
        three_got = tie2(Gather.send_z(net, three_pack), one.got)
        (three,) = Gather.cut(net, three_pack, three_got, [packs[3].shape[1]])
        one.core()
        full_q = [one.pieces(), Pieces([rest_q])]
        full_out = full_q[1]
    else:
        full_q = [Pieces([gather(v)]) for v in shard_q]
        full_out = Pieces([gather(w_out)])
        full_i = [[Pieces([gather(u)]), Pieces([gather(d)])] for u, d in zip(shard_u, shard_d)]
        small = gather(small[None])
    n_up, n_down = b_up.shape[0], b_down.shape[0]
    n_small = n_up + n_down + rel_table.size
    full_bup = inner_order(small[:, :n_up].astype(F32).reshape(1, inner))
    full_bdown = small[:, n_up : n_up + n_down].astype(F32).reshape(1, width)
    table = small[:, n_up + n_down : n_small].reshape(-1, HEADS)
    places = offset_onehot(core, sz)
    bias = bias_blocks(table, bucket, places, sz)

    if net.direct:
        mod = tie(mod, bias, *three.halves)
    own, send = first_norm(tok, mod, scalars, sz)
    far = lax.ppermute(send, "win", swap)
    if net.direct:
        three.start(True)
    first = attention(0, own, far, full_q[0], bias, scalars, sz)
    if net.direct:
        three.tie(first[2])
        three.join()
        three.start(False)
        first = tie2(first, three.halves)
    qkv, wide, att_1, wide_out, branch_own, branch_send = attention(
        1, own, far, full_q[1], bias, scalars, sz, first, full_out
    )
    if net.direct:
        three.tie(branch_own)
        branch_send = tie(branch_send, *three.got)
    branch_far = lax.ppermute(branch_send, "win", swap)
    hidden_two, grad_mlp = second_norm(tok, cot, branch_own, branch_far, mod, scalars, sz)
    flat = (sz.rows, width)
    both = (2, sz.micro, sz.used, sz.half, width)
    hidden_two, grad_mlp = hidden_two.reshape(flat), grad_mlp.reshape(flat)
    if net.direct:
        three.tie(branch_far)
        three.halves = tie2(three.halves, [branch_far])
        three.core()
        full_i = [[three.pieces()], [Pieces([rest])]]
    mlps = []
    for n in range(2):
        shard = rows if net.direct and n == 1 else None
        mlps.append(
            mlp(hidden_two, grad_mlp, full_i[n], full_bup[n], scalars, sz, shard, n == 0)
        )
        if net.direct and n == 0:
            pack, hidden_two = lax.optimization_barrier((mlps[0][4], hidden_two))
            r_first = lax.psum_scatter(pack, axes, scatter_dimension=0, tiled=True).astype(F32)

    if net.direct:
        second = Scatter(net, mlps[1][3:5])
    output, grad_mid, grad_own, grad_send, sums_two = after_mlp(
        tok, cot, branch_own, branch_far, [v[0].reshape(both) for v in mlps],
        [v[1].reshape(both) for v in mlps], mod, full_bdown, scalars, sz,
    )
    grad_far = lax.ppermute(grad_send, "win", swap)
    if net.direct:
        second.tie(grad_own)
        second.second()
        grad_own = tie(grad_own, *second.keep)
    *g_att, fold, hid_own, hid_send = attention_back(
        grad_own, grad_far, own, far, qkv, (first[2], att_1), wide, wide_out, bias, scalars, sz,
        rows if net.direct else None,
    )
    if net.direct:
        second.tie(hid_own)
        g_att = tie2(g_att, second.got)
        hid_send = tie(hid_send, *second.got)
        heads = Scatter(net, g_att)
        hid_far = lax.ppermute(hid_send, "win", swap)
        second.third()
        heads.tie(*second.keep)
        heads.second()
        hid_far = tie(hid_far, *heads.keep)
    else:
        hid_far = lax.ppermute(hid_send, "win", swap)
    grad_in, sums_one = last_norm(tok, cot, grad_mid, hid_own, hid_far, mod, scalars, sz)
    if net.direct:
        second.tie(sums_one, r_first)
        second.fourth()
        sums_one, fold = lax.optimization_barrier((sums_one, fold, *second.keep))[:2]

    grad_mod = jnp.concatenate(
        [sums_one, sums_two[:, 3:4], sums_two[:, 0:3]], axis=1
    ).reshape(sz.micro, 6 * width)
    g_table = table_grad(offset_grad(fold, places, sz), bucket, table.shape[0]).reshape(devices, -1)
    if net.direct:
        heads.tie(g_table)
        heads.third()
        second.tie(*heads.keep)
        r_second = second.total()
        g_table = tie(g_table, r_second)
    g_bup = inner_back([v[2] for v in mlps]).reshape(devices, -1)
    g_bdown = mlps[0][3].reshape(devices, -1)
    g_small = jnp.concatenate([g_bup, g_bdown, g_table], axis=1)
    if net.direct:
        every = jnp.concatenate([grad_mod.reshape(-1), g_small.reshape(-1)])
        every = net.swap_sum(net.swap_sum(every, net.CORE), net.X)
        heads.tie(every)
        heads.fourth()
        mod_all, g_small = net.share(tie(every, *heads.keep), grad_mod.size, heads)
    else:
        mod_all = lax.all_gather(lax.psum(grad_mod, "win"), "clip", axis=0)
        g_small = lax.psum_scatter(g_small, axes, scatter_dimension=0, tiled=False)
    mod_all = mod_all.reshape(clips * sz.micro, -1)
    grad_ada_w = lax.dot_general(
        cond_mine.astype(F32), mod_all, (((0,), (0,)), ((), ())),
        precision=HIGHEST, preferred_element_type=F32,
    )
    grad_ada_b = lax.dynamic_slice_in_dim(
        jnp.sum(mod_all, axis=0), index * ada_b.shape[0], ada_b.shape[0]
    )
    if net.direct:
        r_u, r_d = zip(unpack_inner(r_first), unpack_inner(r_second))
        r_qkv, r_out = heads.total_heads(sz)
    else:
        scatter = lambda v: lax.psum_scatter(
            v.astype(F32), axes, scatter_dimension=0, tiled=True
        )
        r_u = [scatter(v[-2]) for v in mlps]
        r_d = [scatter(v[-1]) for v in mlps]
        r_qkv, r_out = scatter(g_att[0]), scatter(g_att[1])
        r_qkv = r_qkv.reshape(rows, sz.groups, 3, sz.gcols).transpose(0, 2, 1, 3)
        r_qkv = r_qkv.reshape(rows, 3 * width)
    r_up = inner_back(r_u)
    r_down = jnp.concatenate(r_d)
    return (
        output.reshape(tokens.shape), grad_in.reshape(tokens.shape), grad_ada_w, grad_ada_b,
        r_qkv, r_out, r_up, g_small[:n_up], r_down, g_small[n_up : n_up + n_down],
        g_small[n_up + n_down :].reshape(rel_table.shape),
    )


def solution(mesh):
    weights = P(("clip", "win"), None)
    vector = P(("clip", "win"))
    strips = P(None, "clip", "win", None, None, None, None, None)
    return jax.shard_map(
        body,
        mesh=mesh,
        in_specs=(
            strips, P(None, "clip", None), P(None, "clip"), weights, vector, weights, weights,
            weights, vector, weights, vector, weights, P(), strips,
        ),
        out_specs=(
            strips, strips, weights, vector, weights, weights, weights, vector, weights, vector,
            weights,
        ),
        check_vma=False,
    )
```

```python
import functools
import math

import jax
import jax.numpy as jnp
from jax import lax
from jax.experimental import pallas as pl
from jax.experimental.pallas import tpu as pltpu
from jax.sharding import PartitionSpec as P

HEADS = 16
EPSILON = 1e-06
MASKED = -1000000000.0
F32 = jnp.float32
BF16 = jnp.bfloat16
VMEM_LIMIT = 58 * 1024 * 1024
HIGHEST = lax.Precision.HIGHEST


def dot_nn(a, b):
    return lax.dot_general(a, b, (((1,), (0,)), ((), ())), preferred_element_type=F32)


def dot_nt(a, b):
    return lax.dot_general(a, b, (((1,), (1,)), ((), ())), preferred_element_type=F32)


def dot_tn(a, b):
    return lax.dot_general(a, b, (((0,), (0,)), ((), ())), preferred_element_type=F32)


def params(count):
    return pltpu.CompilerParams(
        dimension_semantics=("arbitrary",) * count, vmem_limit_bytes=VMEM_LIMIT
    )


def cost(flops, size):
    return pl.CostEstimate(flops=flops, bytes_accessed=size, transcendentals=0)


def once(shape, index_map):
    return pl.BlockSpec(shape, index_map, pipeline_mode=pl.Buffered(1))


def normalize(values):
    centered = values - jnp.mean(values, axis=-1, keepdims=True)
    inv = lax.rsqrt(jnp.mean(centered * centered, axis=-1, keepdims=True) + EPSILON)
    return centered * inv, inv


def norm_back(grad, normed, inv):
    return inv * (
        grad
        - jnp.mean(grad, axis=-1, keepdims=True)
        - normed * jnp.mean(grad * normed, axis=-1, keepdims=True)
    )


class Sizes:
    def __init__(self, tokens):
        self.micro, _, _, self.blocks, self.frames, rows, side, self.width = tokens.shape
        self.half = rows * side
        self.cols = self.blocks // 2
        self.strip_rows, self.side = rows, side
        self.used = 2 * self.frames - 1
        self.frame = 2 * self.half
        self.win_rows = self.used * self.frame
        self.rows = self.micro * self.win_rows
        self.lens = (self.frames * self.frame, (self.frames - 1) * self.frame)
        self.head = self.width // HEADS
        self.group = 4
        self.gcols = self.group * self.head
        self.groups = HEADS // self.group


def each_frame(body, sz):
    for tw in range(2):

        def step(t, carry, tw=tw):
            body(tw, t, tw * sz.frames + t)
            return carry

        lax.fori_loop(0, sz.frames - tw, step, 0, unroll=True)


def fold_rows(value):
    return jnp.sum(value.reshape(-1, 8, value.shape[-1]), axis=0)


def first_norm(tok, mod, core, sz):
    def kernel(sc_ref, x_ref, mod_ref, own_ref, far_ref):
        shift = mod_ref[0, 0:1, :]
        scale = 1.0 + mod_ref[0, 1:2, :]
        for slot, out_ref in enumerate((own_ref, far_ref)):
            column = sc_ref[0] ^ slot

            def one(tw, t, f, column=column, out_ref=out_ref):
                normed, _ = normalize(x_ref[0, tw, column, t].astype(F32))
                out_ref[0, f] = (normed * scale + shift).astype(BF16)

            each_frame(one, sz)

    strip = (1, 2, 2, sz.frames, sz.half, sz.width)
    piece = (1, sz.used, sz.half, sz.width)
    shape = jax.ShapeDtypeStruct((sz.micro,) + piece[1:], BF16)
    return pl.pallas_call(
        kernel,
        grid_spec=pltpu.PrefetchScalarGridSpec(
            num_scalar_prefetch=1,
            grid=(sz.micro,),
            in_specs=[
                pl.BlockSpec(strip, lambda m, s: (m, 0, 0, 0, 0, 0)),
                pl.BlockSpec((1, 6, sz.width), lambda m, s: (m, 0, 0)),
            ],
            out_specs=[pl.BlockSpec(piece, lambda m, s: (m, 0, 0, 0))] * 2,
        ),
        out_shape=[shape, shape],
        compiler_params=params(1),
        name="first_norm",
    )(core, tok, mod)


def second_norm(tok, cot, branch_own, branch_far, mod, scalars, sz):
    def kernel(sc_ref, x_ref, c_ref, bo_ref, bf_ref, mod_ref, h_ref, g_ref):
        length = sc_ref[1 + pl.program_id(0)]
        gate1 = mod_ref[0, 2:3, :]
        shift = mod_ref[0, 3:4, :]
        scale = 1.0 + mod_ref[0, 4:5, :]
        gate2 = mod_ref[0, 5:6, :]
        for slot, b_ref in enumerate((bo_ref, bf_ref)):
            column = sc_ref[0] ^ slot

            def one(tw, t, f, slot=slot, column=column, b_ref=b_ref):
                rows = x_ref[0, tw, column, t].astype(F32) + gate1 * b_ref[0, f].astype(F32)
                normed, _ = normalize(rows)
                h_ref[slot, 0, f] = (normed * scale + shift).astype(BF16)
                valid = (f < length).astype(F32)
                g_ref[slot, 0, f] = (c_ref[0, tw, column, t].astype(F32) * (valid * gate2)).astype(BF16)

            each_frame(one, sz)

    strip = (1, 2, 2, sz.frames, sz.half, sz.width)
    piece = (1, sz.used, sz.half, sz.width)
    both = (2, 1, sz.used, sz.half, sz.width)
    shape = jax.ShapeDtypeStruct((2, sz.micro, sz.used, sz.half, sz.width), BF16)
    return pl.pallas_call(
        kernel,
        grid_spec=pltpu.PrefetchScalarGridSpec(
            num_scalar_prefetch=1,
            grid=(sz.micro,),
            in_specs=[
                pl.BlockSpec(strip, lambda m, s: (m, 0, 0, 0, 0, 0)),
                pl.BlockSpec(strip, lambda m, s: (m, 0, 0, 0, 0, 0)),
                pl.BlockSpec(piece, lambda m, s: (m, 0, 0, 0)),
                pl.BlockSpec(piece, lambda m, s: (m, 0, 0, 0)),
                pl.BlockSpec((1, 6, sz.width), lambda m, s: (m, 0, 0)),
            ],
            out_specs=[pl.BlockSpec(both, lambda m, s: (0, m, 0, 0, 0))] * 2,
        ),
        out_shape=[shape, shape],
        compiler_params=params(1),
        name="second_norm",
    )(scalars, tok, cot, branch_own, branch_far, mod)


def after_mlp(tok, cot, branch_own, branch_far, mlps, grads, mod, b_down, scalars, sz):
    def kernel(
        sc_ref, x_ref, c_ref, bo_ref, bf_ref, y0_ref, y1_ref, t0_ref, t1_ref, mod_ref, bd_ref,
        out_ref, gm_ref, go_ref, gf_ref, sum_ref, sums,
    ):
        length = sc_ref[1 + pl.program_id(0)]
        gate1 = mod_ref[0, 2:3, :]
        scale = 1.0 + mod_ref[0, 4:5, :]
        gate2 = mod_ref[0, 5:6, :]
        sums[...] = jnp.zeros_like(sums)
        for slot, (b_ref, g_ref) in enumerate(((bo_ref, go_ref), (bf_ref, gf_ref))):
            column = sc_ref[0] ^ slot

            def one(tw, t, f, slot=slot, column=column, b_ref=b_ref, g_ref=g_ref):
                valid = (f < length).astype(F32)
                branch = b_ref[0, f].astype(F32)
                middle = x_ref[0, tw, column, t].astype(F32) + gate1 * branch
                normed, inv = normalize(middle)
                y = y0_ref[slot, 0, f] + y1_ref[slot, 0, f] + bd_ref[0:1, :]
                grad = c_ref[0, tw, column, t].astype(F32)
                out_ref[0, tw, column, t] = (middle + valid * gate2 * y).astype(BF16)
                two = t0_ref[slot, 0, f] + t1_ref[slot, 0, f]
                gm = grad + norm_back(two * scale, normed, inv)
                gm_ref[slot, 0, f] = gm.astype(BF16)
                g_ref[0, f] = (valid * (gm * gate1)).astype(BF16)
                for n, term in enumerate((two, two * normed, grad * valid * y, gm * branch)):
                    sums[n] += fold_rows(term)

            each_frame(one, sz)
            out_ref[0, 1, column, sz.frames - 1] = x_ref[0, 1, column, sz.frames - 1]
        for n in range(4):
            sum_ref[0, n : n + 1, :] = jnp.sum(sums[n], axis=0, keepdims=True)

    strip = (1, 2, 2, sz.frames, sz.half, sz.width)
    piece = (1, sz.used, sz.half, sz.width)
    both = (2, 1, sz.used, sz.half, sz.width)
    full = (sz.micro,) + piece[1:]
    at_strip = lambda m, s: (m, 0, 0, 0, 0, 0)
    at_piece = lambda m, s: (m, 0, 0, 0)
    at_both = lambda m, s: (0, m, 0, 0, 0)
    return pl.pallas_call(
        kernel,
        grid_spec=pltpu.PrefetchScalarGridSpec(
            num_scalar_prefetch=1,
            grid=(sz.micro,),
            in_specs=[
                pl.BlockSpec(strip, at_strip),
                pl.BlockSpec(strip, at_strip),
                pl.BlockSpec(piece, at_piece),
                pl.BlockSpec(piece, at_piece),
                pl.BlockSpec(both, at_both),
                pl.BlockSpec(both, at_both),
                pl.BlockSpec(both, at_both),
                pl.BlockSpec(both, at_both),
                pl.BlockSpec((1, 6, sz.width), lambda m, s: (m, 0, 0)),
                pl.BlockSpec((1, sz.width), lambda m, s: (0, 0)),
            ],
            out_specs=[
                pl.BlockSpec(strip, at_strip),
                pl.BlockSpec(both, at_both),
                pl.BlockSpec(piece, at_piece),
                pl.BlockSpec(piece, at_piece),
                pl.BlockSpec((1, 4, sz.width), lambda m, s: (m, 0, 0)),
            ],
            scratch_shapes=[pltpu.VMEM((4, 8, sz.width), F32)],
        ),
        out_shape=[
            jax.ShapeDtypeStruct(tok.shape, BF16),
            jax.ShapeDtypeStruct((2,) + full, BF16),
            jax.ShapeDtypeStruct(full, BF16),
            jax.ShapeDtypeStruct(full, BF16),
            jax.ShapeDtypeStruct((sz.micro, 4, sz.width), F32),
        ],
        compiler_params=params(1),
        name="after_mlp",
    )(scalars, tok, cot, branch_own, branch_far, *mlps, *grads, mod, b_down)


def last_norm(tok, cot, grad_mid, grad_own, grad_far, mod, scalars, sz):
    def kernel(sc_ref, x_ref, c_ref, gm_ref, go_ref, gf_ref, mod_ref, out_ref, sum_ref, sums):
        scale = 1.0 + mod_ref[0, 1:2, :]
        sums[...] = jnp.zeros_like(sums)
        for slot, g_ref in enumerate((go_ref, gf_ref)):
            column = sc_ref[0] ^ slot

            def one(tw, t, f, slot=slot, column=column, g_ref=g_ref):
                normed, inv = normalize(x_ref[0, tw, column, t].astype(F32))
                grad = g_ref[0, f].astype(F32)
                total = gm_ref[slot, 0, f].astype(F32) + norm_back(grad * scale, normed, inv)
                out_ref[0, tw, column, t] = total.astype(BF16)
                sums[0] += fold_rows(grad)
                sums[1] += fold_rows(grad * normed)

            each_frame(one, sz)
        for slot in range(2):
            out_ref[0, 1, slot, sz.frames - 1] = c_ref[0, 0, slot, 0]
        for n in range(2):
            sum_ref[0, n : n + 1, :] = jnp.sum(sums[n], axis=0, keepdims=True)

    strip = (1, 2, 2, sz.frames, sz.half, sz.width)
    tail = (1, 1, 2, 1, sz.half, sz.width)
    piece = (1, sz.used, sz.half, sz.width)
    both = (2, 1, sz.used, sz.half, sz.width)
    return pl.pallas_call(
        kernel,
        grid_spec=pltpu.PrefetchScalarGridSpec(
            num_scalar_prefetch=1,
            grid=(sz.micro,),
            in_specs=[
                pl.BlockSpec(strip, lambda m, s: (m, 0, 0, 0, 0, 0)),
                pl.BlockSpec(tail, lambda m, s: (m, 1, 0, sz.frames - 1, 0, 0)),
                pl.BlockSpec(both, lambda m, s: (0, m, 0, 0, 0)),
                pl.BlockSpec(piece, lambda m, s: (m, 0, 0, 0)),
                pl.BlockSpec(piece, lambda m, s: (m, 0, 0, 0)),
                pl.BlockSpec((1, 6, sz.width), lambda m, s: (m, 0, 0)),
            ],
            out_specs=[
                pl.BlockSpec(strip, lambda m, s: (m, 0, 0, 0, 0, 0)),
                pl.BlockSpec((1, 2, sz.width), lambda m, s: (m, 0, 0)),
            ],
            scratch_shapes=[pltpu.VMEM((2, 8, sz.width), F32)],
        ),
        out_shape=[
            jax.ShapeDtypeStruct(tok.shape, BF16),
            jax.ShapeDtypeStruct((sz.micro, 2, sz.width), F32),
        ],
        compiler_params=params(1),
        name="last_norm",
    )(scalars, tok, cot, grad_mid, grad_own, grad_far, mod)


class Pieces:
    def __init__(self, arrays):
        self.arrays = arrays
        self.whole = len(arrays) == 1

    def specs(self, columns, index_map):
        if self.whole:
            at = lambda *g: (0, index_map(*g))
            return [pl.BlockSpec((self.arrays[0].shape[0], columns), at)]
        at = lambda *g: (0, 0, 0, index_map(*g))
        shape = self.arrays[0].shape[:-1] + (columns,)
        return [pl.BlockSpec(shape, at)] * 8


def pieces_of(refs, key, z_here):
    depth = refs[0].shape[1]
    for z in range(depth):
        for n in range(8):
            half, far, i = n // 4, n // 2 % 2, n % 2
            for j in range(2):
                away = (i * 4 + j * 2 if half == 0 else i * 2 + j * 4) + far
                yield (z_here + z) % depth, key ^ away, half, refs[n].at[j, z]


def place(refs, key, z_here, out_ref, columns=slice(None), source=slice(None)):
    if len(refs) == 1:
        out_ref[:, columns] = refs[0][:, source]
        return
    for z, at, half, piece in pieces_of(refs, key, z_here):
        cut = piece.shape[0]
        row = pl.multiple_of((z * 8 + at) * (2 * cut) + half * cut, cut)
        out_ref[pl.ds(row, cut), columns] = piece[:, source]


def place_inner(refs, key, z_here, out_ref, source):
    size = source.stop - source.start
    if len(refs) == 1:
        cut = out_ref.shape[0] // 32
        for n in range(64):
            at, half = n // 2, n % 2
            to = (at % 2) * (16 * cut) + at // 2 * cut
            out_ref[to : to + cut, half * size : (half + 1) * size] = refs[0][
                n * cut : (n + 1) * cut, source
            ]
        return
    for z, at, half, piece in pieces_of(refs, key, z_here):
        cut = piece.shape[0]
        row = pl.multiple_of((at % 2) * (16 * cut) + (z * 4 + at // 2) * cut, cut)
        out_ref[pl.ds(row, cut), half * size : (half + 1) * size] = piece[:, source]


def turn(value, out_ref, core, shard, start=0):
    turned = value.T
    if shard is None:
        out_ref[start : start + turned.shape[0]] = turned
        return
    height = out_ref.shape[0]
    for n in range(turned.shape[0] // shard):
        at = start // shard + n
        at = (core ^ (at % 2)) * (height // 2) + at // 2 * shard
        out_ref[pl.ds(pl.multiple_of(at, shard), shard), :] = turned[n * shard : (n + 1) * shard]


def give(refs, half, low, value, start=0):
    value = value.astype(BF16)
    columns = slice(start, start + value.shape[1])
    if len(refs) == 1:
        low = half * (refs[0].shape[0] // 2) + low
        refs[0][low : low + value.shape[0], columns] = value
        return
    rows = refs[half].shape[1]
    refs[half][low // rows : (low + value.shape[0]) // rows, :, columns] = value.reshape(
        value.shape[0] // rows, rows, value.shape[1]
    )


def grad_shapes(direct, rows, height, columns):
    if not direct:
        return [jax.ShapeDtypeStruct((height, columns), BF16)]
    return [jax.ShapeDtypeStruct((height // (2 * rows), rows, columns), BF16)] * 2


def grad_specs(direct, rows, height, columns, at_column):
    if not direct:
        return [pl.BlockSpec((height, columns), lambda *g: (0, at_column(*g)))]
    shape = (height // (2 * rows), rows, columns)
    return [pl.BlockSpec(shape, lambda *g: (0, 0, at_column(*g)))] * 2


def join_frames(own_ref, far_ref, joined_ref, sz):
    for m in range(sz.micro):
        for f in range(sz.used):
            at = m * sz.win_rows + f * sz.frame
            joined_ref[at : at + sz.half] = own_ref[m, f]
            joined_ref[at + sz.half : at + sz.frame] = far_ref[m, f]


def spread_bias(block_ref, head, bias_ref, sz, turned=False):
    size = sz.frame
    for step in range(2 * sz.frames - 1):
        block = block_ref[head, step]
        if turned:
            block = block.T
        for key in range(sz.frames):
            query = key + step - (sz.frames - 1)
            if 0 <= query < sz.frames:
                row, column = (key, query) if turned else (query, key)
                bias_ref[row * size : (row + 1) * size, column * size : (column + 1) * size] = block


def window_rows(m, tw, sz):
    start = pl.multiple_of(m * sz.win_rows + tw * sz.lens[0], sz.frame)
    return pl.ds(start, sz.lens[tw])


def attention(half, own, far, w_qkv, bias, scalars, sz, first=None, w_out=None):
    scale = 1.0 / math.sqrt(sz.head)
    last = w_out is not None
    steps = sz.groups // 2
    gcols = sz.gcols
    joint = w_out is w_qkv
    n_out = 2 * len(w_qkv.arrays) if joint else 1

    def kernel(sc_ref, own_ref, far_ref, bias_ref, *refs):
        refs = list(refs)
        take = lambda count: [refs.pop(0) for _ in range(count)]
        w_refs = take(len(w_qkv.arrays))
        if last:
            (first_ref,) = take(1)
            out_refs = take(n_out)
            take(2)
        qkv_ref, w_ref, att_ref = take(3)
        if last:
            wo_ref, bo_ref, bf_ref = take(3)
        joined, spread = take(2)
        step = pl.program_id(0)
        key, z_here = sc_ref[1 + sz.micro], sc_ref[2 + sz.micro]

        @pl.when(step == 0)
        def _():
            join_frames(own_ref, far_ref, joined, sz)

        place(w_refs, key, z_here, w_ref)
        for n in range(3):
            part = dot_nn(joined[...], w_ref[:, n * gcols : (n + 1) * gcols]).astype(BF16)
            qkv_ref[n] = part * scale if n == 0 else part
        for head in range(sz.group):
            spread_bias(bias_ref, head, spread.at[head], sz)

        def one_micro(m, carry):
            for tw in range(2):
                size = sz.lens[tw]
                rows = window_rows(m, tw, sz)
                keys_ok = (sc_ref[1 + m] - tw * sz.frames) * sz.frame

                @pl.when(keys_ok > 0)
                def _(rows=rows, size=size, keys_ok=keys_ok):
                    column = lax.broadcasted_iota(jnp.int32, (1, size), 1)
                    for head in range(sz.group):
                        lanes = slice(head * sz.head, (head + 1) * sz.head)
                        scores = dot_nt(qkv_ref[0, rows, lanes], qkv_ref[1, rows, lanes])
                        scores = scores + spread[head, :size, :size].astype(F32)
                        scores = jnp.where(column < keys_ok, scores, MASKED)
                        top = jnp.max(scores, axis=-1, keepdims=True)
                        weight = jnp.exp(scores - top)
                        share = 1.0 / jnp.sum(weight, axis=-1, keepdims=True)
                        probs = (weight * share).astype(BF16)
                        att_ref[rows, lanes] = dot_nn(probs, qkv_ref[2, rows, lanes]).astype(BF16)

                @pl.when(keys_ok <= 0)
                def _(rows=rows, size=size):
                    att_ref[rows, :] = jnp.zeros((size, gcols), BF16)

            return carry

        lax.fori_loop(0, sz.micro, one_micro, 0)
        if not last:
            return
        kept, total = take(2)
        for n in range(steps):

            @pl.when(step == n)
            def _(n=n):
                kept[:, n * gcols : (n + 1) * gcols] = att_ref[...]

        @pl.when(step == steps - 1)
        def _():
            if joint:
                place(out_refs[: n_out // 2], key, z_here, wo_ref, slice(0, 2 * gcols))
                place(out_refs[n_out // 2 :], key, z_here, wo_ref, slice(2 * gcols, 4 * gcols))
            else:
                place(out_refs, key, z_here, wo_ref)
            middle = first_ref.shape[1]
            total[...] = dot_nn(first_ref[...], wo_ref[:middle]) + dot_nn(
                kept[...], wo_ref[middle:]
            )
            for m in range(sz.micro):
                for f in range(sz.used):
                    at = m * sz.win_rows + f * sz.frame
                    valid = (f < sc_ref[1 + m]).astype(F32)
                    bo_ref[m, f] = (total[at : at + sz.half] * valid).astype(BF16)
                    bf_ref[m, f] = (total[at + sz.half : at + sz.frame] * valid).astype(BF16)

    piece = (sz.micro, sz.used, sz.half, sz.width)
    fixed = lambda g, s: (0, 0, 0, 0)
    flat = lambda g, s: (0, 0)
    width, cols = sz.width, sz.width // 2
    in_specs = [
        once(piece, fixed),
        once(piece, fixed),
        pl.BlockSpec((sz.group,) + bias.shape[1:], lambda g, s: (half * steps + g, 0, 0, 0)),
    ] + w_qkv.specs(3 * gcols, lambda g, s: g)
    out_specs = [
        pl.BlockSpec((3, sz.rows, gcols), lambda g, s: (0, 0, half * steps + g)),
        pl.BlockSpec((width, 3 * gcols), lambda g, s: (0, half * steps + g)),
        pl.BlockSpec((sz.rows, gcols), lambda g, s: (0, g)),
    ]
    out_shape = [
        jax.ShapeDtypeStruct((3, sz.rows, width), BF16),
        jax.ShapeDtypeStruct((width, 3 * width), BF16),
        jax.ShapeDtypeStruct((sz.rows, cols), BF16),
    ]
    aliases = {}
    scratch = [
        pltpu.VMEM((sz.rows, width), BF16),
        pltpu.VMEM((sz.group, sz.lens[0], sz.lens[0]), BF16),
    ]
    args = [scalars, own, far, bias, *w_qkv.arrays]
    flops = 6 * sz.rows * width * cols + 4 * sz.rows * sz.lens[0] * cols
    if last:
        in_specs += [once((sz.rows, cols), flat)]
        if joint:
            low = w_out.arrays[0].shape[-1] // (2 * gcols) - 2
            in_specs += w_out.specs(2 * gcols, lambda g, s: low)
            in_specs += w_out.specs(2 * gcols, lambda g, s: low + 1)
            out_args = w_out.arrays * 2
        else:
            in_specs += w_out.specs(width, lambda g, s: 0)
            out_args = w_out.arrays
        out_specs += [pl.BlockSpec((width, width), flat)] + [pl.BlockSpec(piece, fixed)] * 2
        out_shape += [jax.ShapeDtypeStruct((width, width), BF16)]
        out_shape += [jax.ShapeDtypeStruct(piece, BF16)] * 2
        scratch += [pltpu.VMEM((sz.rows, cols), BF16), pltpu.VMEM((sz.rows, width), F32)]
        args += [first[2], *out_args]
        aliases = {len(args): 0, len(args) + 1: 1}
        in_specs += [pl.BlockSpec(memory_space=pl.ANY)] * 2
        args += first[:2]
        flops += 2 * sz.rows * width * width
    return pl.pallas_call(
        kernel,
        grid_spec=pltpu.PrefetchScalarGridSpec(
            num_scalar_prefetch=1,
            grid=(steps,),
            in_specs=in_specs,
            out_specs=out_specs,
            scratch_shapes=scratch,
        ),
        out_shape=out_shape,
        input_output_aliases=aliases,
        compiler_params=params(1),
        cost_estimate=cost(3 * flops, 16 * sz.rows * width),
        name="attention" + "_last" * last,
    )(*args)


def attention_back(grad_own, grad_far, own, far, qkv, atts, w_qkv, w_out, bias, scalars, sz, shard):
    scale = 1.0 / math.sqrt(sz.head)
    steps = sz.groups
    direct = shard is not None
    outs = 2 if direct else 1
    gcols, width = sz.gcols, sz.width
    quarter = width // 4

    def kernel(
        sc_ref, go_ref, gf_ref, own_ref, far_ref, qkv_ref, w_ref, wo_ref, bias_ref, *refs
    ):
        refs = list(refs)
        take = lambda count: [refs.pop(0) for _ in range(count)]
        att_refs = take(2)
        gw_refs = take(outs)
        gwo_refs = gw_refs if direct else take(1)
        fold_ref, ho_ref, hf_ref = take(3)
        grad, hidden_t, grad_att, parts, spread, pair_sum, total, turned = take(8)
        (folded,) = take(1)
        step = pl.program_id(0)

        @pl.when(step == 0)
        def _():
            join_frames(own_ref, far_ref, grad, sz)
            turn(grad[...], hidden_t, sc_ref[0], shard)
            join_frames(go_ref, gf_ref, grad, sz)
            total[...] = jnp.zeros_like(total)
            for n, a_ref in enumerate(att_refs):
                turn(a_ref[...], turned, sc_ref[0], shard, n * a_ref.shape[1])

        grad_att[...] = dot_nt(grad[...], wo_ref[...]).astype(BF16)
        full = sz.lens[0]
        for head in range(sz.group):
            spread_bias(bias_ref, head, spread.at[head], sz, True)
            pair_sum[head] = jnp.zeros((full, full), F32)

        def one_micro(m, carry):
            for tw in range(2):
                size = sz.lens[tw]
                rows = window_rows(m, tw, sz)
                keys_ok = (sc_ref[1 + m] - tw * sz.frames) * sz.frame

                @pl.when(keys_ok > 0)
                def _(rows=rows, size=size, keys_ok=keys_ok):
                    row = lax.broadcasted_iota(jnp.int32, (size, 1), 0)
                    for head in range(sz.group):
                        lanes = slice(head * sz.head, (head + 1) * sz.head)
                        spot = [slice(n * gcols + lanes.start, n * gcols + lanes.stop) for n in range(3)]
                        query = qkv_ref[0, rows, lanes]
                        key = qkv_ref[1, rows, lanes]
                        value = qkv_ref[2, rows, lanes]
                        grad_out = grad_att[rows, lanes]
                        scores = dot_nt(key, query) + spread[head, :size, :size].astype(F32)
                        scores = jnp.where(row < keys_ok, scores, MASKED)
                        weight = jnp.exp(scores - jnp.max(scores, axis=0, keepdims=True))
                        probs = weight * (1.0 / jnp.sum(weight, axis=0, keepdims=True))
                        grad_probs = dot_nt(value, grad_out)
                        inner = jnp.sum(probs * grad_probs, axis=0, keepdims=True)
                        grad_scores = (probs * (grad_probs - inner)).astype(BF16)
                        pair_sum[head, :size, :size] += grad_scores.astype(F32)
                        parts[rows, spot[2]] = dot_nn(probs.astype(BF16), grad_out).astype(BF16)
                        parts[rows, spot[1]] = dot_nn(grad_scores, query).astype(BF16)
                        parts[rows, spot[0]] = (dot_tn(grad_scores, key) * scale).astype(BF16)

                @pl.when(keys_ok <= 0)
                def _(rows=rows, size=size):
                    parts[rows, :] = jnp.zeros((size, 3 * gcols), BF16)

            return carry

        lax.fori_loop(0, sz.micro, one_micro, 0)
        for head in range(sz.group):
            folded[...] = jnp.zeros_like(folded)
            for t in range(sz.frames):
                low = (sz.frames - 1 - t) * sz.frame
                folded[:, low : low + full] += pair_sum[head, t * sz.frame : (t + 1) * sz.frame, :]
            fold_ref[head] = folded[...].astype(BF16)
        for n in range(4):
            rows = slice(n * quarter, (n + 1) * quarter)
            give(gw_refs, n // 2, n % 2 * quarter, dot_nn(hidden_t[rows, :], parts[...]))
        total[...] += dot_nt(parts[...], w_ref[...])
        columns = pl.ds(pl.multiple_of(step * gcols, gcols), gcols)
        for n in range(4):
            rows = slice(n * quarter, (n + 1) * quarter)
            value = dot_nn(turned[rows, :], grad[:, columns])
            give(gwo_refs, n // 2, n % 2 * quarter, value, 3 * gcols if direct else 0)

        @pl.when(step == steps - 1)
        def _():
            for m in range(sz.micro):
                for f in range(sz.used):
                    at = m * sz.win_rows + f * sz.frame
                    ho_ref[m, f] = total[at : at + sz.half].astype(BF16)
                    hf_ref[m, f] = total[at + sz.half : at + sz.frame].astype(BF16)

    piece = (sz.micro, sz.used, sz.half, width)
    fixed = lambda g, s: (0, 0, 0, 0)
    flat = lambda g, s: (0, 0)
    cols = width // 2
    fold = (sz.frame, (2 * sz.frames - 1) * sz.frame)
    in_specs = [
        once(piece, fixed),
        once(piece, fixed),
        once(piece, fixed),
        once(piece, fixed),
        pl.BlockSpec((3, sz.rows, gcols), lambda g, s: (0, 0, g)),
        pl.BlockSpec((width, 3 * gcols), lambda g, s: (0, g)),
        pl.BlockSpec((gcols, width), lambda g, s: (g, 0)),
        pl.BlockSpec((sz.group,) + bias.shape[1:], lambda g, s: (g, 0, 0, 0)),
    ]
    along = lambda g, s: g
    wide = 4 * gcols if direct else 3 * gcols
    out_specs = grad_specs(direct, shard, width, wide, along)
    if not direct:
        out_specs += grad_specs(direct, shard, width, gcols, along)
    out_specs += [pl.BlockSpec((sz.group,) + fold, lambda g, s: (g, 0, 0))]
    out_specs += [pl.BlockSpec(piece, fixed)] * 2
    out_shape = grad_shapes(direct, shard, width, steps * wide)
    if not direct:
        out_shape += grad_shapes(direct, shard, width, width)
    out_shape += [jax.ShapeDtypeStruct((HEADS,) + fold, BF16)]
    out_shape += [jax.ShapeDtypeStruct(piece, BF16)] * 2
    scratch = [
        pltpu.VMEM((sz.rows, width), BF16),
        pltpu.VMEM((width, sz.rows), BF16),
        pltpu.VMEM((sz.rows, gcols), BF16),
        pltpu.VMEM((sz.rows, 3 * gcols), BF16),
        pltpu.VMEM((sz.group, sz.lens[0], sz.lens[0]), BF16),
        pltpu.VMEM((sz.group, sz.lens[0], sz.lens[0]), F32),
    ]
    args = [scalars, grad_own, grad_far, own, far, qkv, w_qkv, w_out, bias]
    flops = 16 * sz.rows * width * width + 10 * sz.rows * sz.lens[0] * width
    in_specs += [once((sz.rows, cols), flat)] * 2
    scratch += [pltpu.VMEM((sz.rows, width), F32), pltpu.VMEM((width, sz.rows), BF16)]
    scratch += [pltpu.VMEM(fold, F32)]
    args += list(atts)
    return pl.pallas_call(
        kernel,
        grid_spec=pltpu.PrefetchScalarGridSpec(
            num_scalar_prefetch=1,
            grid=(steps,),
            in_specs=in_specs,
            out_specs=out_specs,
            scratch_shapes=scratch,
        ),
        out_shape=out_shape,
        compiler_params=params(1),
        cost_estimate=cost(3 * flops, 24 * sz.rows * width),
        name="attention_back",
    )(*args)


GELU_A = math.sqrt(2.0 / math.pi)
GELU_B = 0.044715
MLP_TILES = 3
CHUNK = 512


def mlp(hidden, grad, weights, b_up, scalars, sz, shard, inner_first):
    chunk = CHUNK
    tiles = MLP_TILES
    tile = sz.rows // tiles
    inner = b_up.shape[1]
    steps = inner // chunk
    packed = len(weights) == 1
    direct = shard is not None
    rows, width = sz.rows, sz.width
    quarter = width // 4
    n_up = len(weights[0].arrays)
    copied = n_up > 1

    def kernel(sc_ref, h_ref, g_ref, bu_ref, *refs):
        refs = list(refs)
        take = lambda count: [refs.pop(0) for _ in range(count)]
        up_refs = take(n_up)
        down_refs = up_refs if packed else take(1)
        y_ref, t_ref, gbu_ref = take(3)
        if inner_first:
            (gbd_ref,) = take(1)
        gw_refs = take(2 if direct else 1)
        gwd_refs = gw_refs if packed else take(1)
        hidden_t, act_s, gpre_s = take(3)
        step = pl.program_id(0)
        key, z_here = sc_ref[1 + sz.micro], sc_ref[2 + sz.micro]

        @pl.when(step == 0)
        def _():
            turn(h_ref[...], hidden_t, sc_ref[0], shard)
            if inner_first:
                gbd_ref[...] = jnp.sum(g_ref[...].astype(F32), axis=0, keepdims=True)
            y_ref[...] = jnp.zeros_like(y_ref)
            t_ref[...] = jnp.zeros_like(t_ref)

        if packed:
            (wd_ref,) = take(1)
            place_inner(down_refs, key, z_here, wd_ref, slice(chunk, chunk + width // 2))
        else:
            wd_ref = down_refs[0]
        if copied:
            (wu_ref,) = take(1)
            place(up_refs, key, z_here, wu_ref, source=slice(0, chunk))
        else:
            wu_ref = up_refs[0]
        bias_sum = jnp.zeros((1, chunk), F32)
        for n in range(tiles):
            span = slice(n * tile, (n + 1) * tile)
            pre = dot_nn(h_ref[span], wu_ref[:, :chunk]) + bu_ref[...]
            grad_act = dot_nt(g_ref[span], wd_ref[...])
            square = pre * pre
            tanh = jnp.tanh(GELU_A * pre * (1.0 + GELU_B * square))
            half = 0.5 * (1.0 + tanh)
            act = (pre * half).astype(BF16)
            slope = half + (0.5 * GELU_A) * pre * (1.0 - tanh * tanh) * (
                1.0 + (3.0 * GELU_B) * square
            )
            grad_pre = (grad_act * slope).astype(BF16)
            act_s[0, span] = act[:, : chunk // 2]
            act_s[1, span] = act[:, chunk // 2 :]
            gpre_s[span] = grad_pre
            bias_sum = bias_sum + jnp.sum(grad_pre.astype(F32), axis=0, keepdims=True)
            y_ref[span] += dot_nn(act, wd_ref[...])
            t_ref[span] += dot_nt(grad_pre, wu_ref[:, :chunk])
        gbu_ref[...] = bias_sum
        for n in range(4):
            span = slice(n * quarter, (n + 1) * quarter)
            give(gw_refs, n // 2, n % 2 * quarter, dot_nn(hidden_t[span, :], gpre_s[...]))
        for n in range(2):
            source = sc_ref[0] ^ n if direct else n
            value = dot_tn(act_s[source], g_ref[...])
            if not packed:
                give(gwd_refs, n, 0, value)
                continue
            value = value.astype(BF16)
            cut = chunk // 32
            for half in range(2):
                part = value[:, half * width // 2 : (half + 1) * width // 2]
                if direct:
                    gw_refs[n][:, half * cut : (half + 1) * cut, chunk:] = part.reshape(
                        16, cut, width // 2
                    )
                    continue
                for k in range(16):
                    to = (2 * k + n) * 2 * cut + half * cut
                    gw_refs[0][to : to + cut, chunk:] = part[k * cut : (k + 1) * cut]

    fixed = lambda j, s: (0, 0)
    along = lambda j, s: j
    in_specs = [
        once((rows, width), fixed),
        once((rows, width), fixed),
        pl.BlockSpec((1, chunk), lambda j, s: (0, j)),
    ]
    args = [scalars, hidden, grad, b_up]
    out_specs = [
        pl.BlockSpec((rows, width), fixed),
        pl.BlockSpec((rows, width), fixed),
        pl.BlockSpec((1, chunk), lambda j, s: (0, j)),
    ]
    out_shape = [
        jax.ShapeDtypeStruct((rows, width), F32),
        jax.ShapeDtypeStruct((rows, width), F32),
        jax.ShapeDtypeStruct((1, inner), F32),
    ]
    if inner_first:
        out_specs += [pl.BlockSpec((1, width), fixed)]
        out_shape += [jax.ShapeDtypeStruct((1, width), F32)]
    if packed:
        wide = chunk + width // 2
        in_specs += weights[0].specs(wide, along)
        args += weights[0].arrays
        out_specs += grad_specs(direct, shard, width, wide, along)
        out_shape += grad_shapes(direct, shard, width, steps * wide)
    else:
        in_specs += weights[0].specs(chunk, along)
        in_specs += [pl.BlockSpec((chunk, width), lambda j, s: (j, 0))]
        args += [weights[0].arrays[0], weights[1].arrays[0]]
        out_specs += grad_specs(False, None, width, chunk, along)
        out_specs += [pl.BlockSpec((chunk, width), lambda j, s: (j, 0))]
        out_shape += grad_shapes(False, None, width, inner)
        out_shape += grad_shapes(False, None, inner, width)
    scratch = [
        pltpu.VMEM((width, rows), BF16),
        pltpu.VMEM((2, rows, chunk // 2), BF16),
        pltpu.VMEM((rows, chunk), BF16),
    ]
    if packed:
        scratch += [pltpu.VMEM((chunk, width), BF16)]
    if copied:
        scratch += [pltpu.VMEM((width, chunk), BF16)]
    return pl.pallas_call(
        kernel,
        grid_spec=pltpu.PrefetchScalarGridSpec(
            num_scalar_prefetch=1,
            grid=(steps,),
            in_specs=in_specs,
            out_specs=out_specs,
            scratch_shapes=scratch,
        ),
        out_shape=out_shape,
        compiler_params=params(1),
        cost_estimate=cost(14 * rows * width * inner, 16 * rows * width),
        name="mlp",
    )(*args)


def offset_onehot(core, sz):
    span = 2 * sz.side - 1
    place = jnp.arange(sz.frame, dtype=jnp.int32)
    row = ((place // sz.half) ^ core) * sz.strip_rows + place // sz.side % sz.strip_rows
    column = place % sz.side
    index = (row[:, None] - row[None, :] + sz.side - 1) * span
    index = index + column[:, None] - column[None, :] + sz.side - 1
    return (jnp.arange(span * span, dtype=jnp.int32)[:, None, None] == index[None]).astype(BF16)


def bucket_onehot(bucket, count):
    return (jnp.arange(count, dtype=jnp.int32)[:, None] == bucket[None, :]).astype(BF16)


def bias_blocks(table, bucket, places, sz):
    by_offset = dot_tn(table, bucket_onehot(bucket, table.shape[0])).astype(BF16)
    by_offset = by_offset.reshape(HEADS * (2 * sz.frames - 1), -1)
    blocks = dot_nn(by_offset, places.reshape(places.shape[0], -1)).astype(BF16)
    return blocks.reshape(HEADS, -1, sz.frame, sz.frame)


def offset_grad(fold, places, sz):
    steps = 2 * sz.frames - 1
    fold = fold.reshape(-1, sz.frame, steps, sz.frame)
    made = jnp.einsum("hqkp,jpq->hkj", fold, places, preferred_element_type=F32)
    return made.reshape(fold.shape[0], -1)


def table_grad(by_offset, bucket, buckets):
    onehot = bucket_onehot(bucket, buckets)
    return dot_nt(onehot, by_offset.astype(BF16))


class Net:
    AXES = ("clip", "win")
    X, Y, CORE = 2, 4, 1

    def __init__(self):
        self.count = lax.axis_size(self.AXES)
        self.direct = lax.axis_size("win") == 4 and self.count == 32
        self.deep = self.count // 8
        self.index = lax.axis_index(self.AXES)
        self.z = self.index // 8

    def bit(self, which):
        return self.index // which % 2

    def swap(self, value, which):
        return lax.ppermute(value, self.AXES, [(n, n ^ which) for n in range(self.count)])

    def from_z(self, value, step):
        move = lambda n: (n // 8 - step) % self.deep * 8 + n % 8
        return lax.ppermute(value, self.AXES, [(n, move(n)) for n in range(self.count)])

    def swap_sum(self, value, which):
        return value + self.swap(value, which)


    def gather_clips(self, value):
        along = jnp.stack([value] + [self.from_z(value, k) for k in range(1, self.deep)])
        return jnp.stack([along, self.swap(along, self.Y)], axis=1)

    def scatter_clips(self, value, notes):
        got = self.swap(value[:, 1], self.Y)
        notes.append(got)
        kept = value[:, 0] + got
        got = [self.from_z(kept[self.deep - k], k) for k in range(1, self.deep)]
        notes.append(got[-1])
        return kept[0] + sum(got)

    def share(self, value, count, scatter):
        deep = self.deep
        got = self.swap(value, self.Y)
        clips = jnp.stack([value[:count], got[:count]])
        rest = (value[count:] + got[count:]).reshape(deep, -1)
        pick = lambda at: lax.dynamic_index_in_dim(rest, at % deep, 0, keepdims=False)
        sends = [
            jnp.concatenate([clips.reshape(-1), pick(self.z + deep - k)]).astype(BF16)
            for k in range(1, deep)
        ]
        sends = tie2(sends, scatter.got[:1])
        got = [self.from_z(send, k).astype(F32) for k, send in enumerate(sends, 1)]
        clips = jnp.stack([clips] + [v[: 2 * count].reshape(2, count) for v in got])
        rest = (pick(self.z) + sum(v[2 * count :] for v in got)).reshape(8, -1)
        return clips, lax.dynamic_index_in_dim(rest, self.index % 8, 0, keepdims=False)

    def gather_pairs(self, value):
        parts = value
        for which in (self.X, self.CORE):
            parts = jnp.stack([parts, self.swap(parts, which)], axis=2 if which == self.X else 3)
        parts = parts.reshape(self.count, -1)
        place = jnp.arange(self.count, dtype=jnp.int32)
        holder = (self.z + place // 8) % self.deep * 8 + (place % 8 ^ self.index % 8)
        pick = (place[:, None] == holder[None, :]).astype(BF16)
        return dot_nn(pick, parts).astype(BF16)


def cut_rows(parts, widths):
    rows, columns = parts[0].shape
    half = rows // 2

    def kernel(*refs):
        ins, outs = refs[: len(parts)], refs[len(parts) :]
        for n, ref in enumerate(ins):
            low = 0
            for k, size in enumerate(widths):
                for side in range(2):
                    outs[2 * k + side][n] = ref[side * half : (side + 1) * half, low : low + size]
                low += size

    return pl.pallas_call(
        kernel,
        out_shape=[
            jax.ShapeDtypeStruct((len(parts), half, size), BF16) for size in widths for _ in range(2)
        ],
        compiler_params=pltpu.CompilerParams(vmem_limit_bytes=VMEM_LIMIT),
        cost_estimate=cost(0, 4 * len(parts) * rows * columns),
        name="cut_rows",
    )(*parts)


class Gather:
    def __init__(self, net, halves):
        self.net = net
        self.halves = list(halves)
        self.got = []

    @staticmethod
    def along_z(net, shards):
        both = jnp.concatenate(shards, axis=1)
        return Gather.cut(net, both, Gather.send_z(net, both), [v.shape[1] for v in shards])

    @staticmethod
    def send_z(net, shard):
        return [net.from_z(shard, k) for k in range(1, net.deep)]

    @staticmethod
    def cut(net, shard, got, widths):
        made = cut_rows([shard] + list(got), widths)
        return [Gather(net, made[2 * n : 2 * n + 2]) for n in range(len(widths))]

    def start(self, first):
        net = self.net
        order = (net.X, net.Y) if first else (net.Y, net.X)
        self.got = [net.swap(v, which) for v, which in zip(self.halves, order)]

    def join(self):
        self.halves = [jnp.stack(pair) for pair in zip(self.halves, self.got)]

    def tie(self, *others):
        self.got = list(lax.optimization_barrier((*self.got, *others))[: len(self.got)])

    def core(self):
        net = self.net
        self.halves = [v for pair in zip(self.halves, self.got) for v in pair]
        self.got = [net.swap(v, net.CORE) for v in self.halves]

    def pieces(self):
        near, far = self.halves, self.got
        return Pieces([*near[:2], *far[:2], *near[2:], *far[2:]])


def add_bf16(one, two):
    return (one.astype(F32) + two.astype(F32)).astype(BF16)


class Scatter:
    def __init__(self, net, pair):
        self.net = net
        keep, send = [v.reshape((net.deep, 4) + v.shape[1:]) for v in pair]
        self.keep = [keep]
        self.got = [net.swap(send, net.CORE)]
        self.bits = jnp.stack([net.bit(net.Y), net.bit(net.X), net.z])
        self.rows, self.columns = keep.shape[2:]

    def tie(self, *others):
        self.got = list(lax.optimization_barrier((*self.got, *others))[: len(self.got)])

    def tie_keep(self, *others):
        self.keep = list(lax.optimization_barrier((*self.keep, *others))[: len(self.keep)])

    def second(self):
        net, cut = self.net, self.rows // 2

        def kernel(sc_ref, keep, got, *outs):
            for half in range(2):
                span = slice(half * cut, (half + 1) * cut)
                for role in range(2):
                    for other in range(2):
                        near = sc_ref[half] ^ role
                        at = near * 2 + other if half == 0 else other * 2 + near
                        outs[2 * half + role][0, other] = add_bf16(keep[0, at, span], got[0, at, span])

        spans = 1
        block = (1,) + self.keep[0].shape[1:3] + (self.columns // spans,)
        out = (2, cut, self.columns // spans)
        made = pl.pallas_call(
            kernel,
            grid_spec=pltpu.PrefetchScalarGridSpec(
                num_scalar_prefetch=1,
                grid=(net.deep, spans),
                in_specs=[pl.BlockSpec(block, lambda z, n, s: (z, 0, 0, n))] * 2,
                out_specs=[pl.BlockSpec((1,) + out, lambda z, n, s: (z, 0, 0, n))] * 4,
            ),
            out_shape=[jax.ShapeDtypeStruct((net.deep, 2, cut, self.columns), BF16)] * 4,
            compiler_params=params(2),
            cost_estimate=cost(0, 6 * self.keep[0].size),
            name="add_cores",
        )(self.bits, *self.keep, *self.got)
        self.keep = [made[0], made[2]]
        self.got = [net.swap(made[1], net.Y), net.swap(made[3], net.X)]

    def third(self):
        net, cut = self.net, self.rows // 2

        def kernel(sc_ref, k0, k1, g0, g1, *outs):
            for half, (keep, got) in enumerate(((k0, g0), (k1, g1))):
                for role in range(2):
                    at = sc_ref[1 - half] ^ role
                    outs[2 * half + role][...] = add_bf16(keep[:, at], got[:, at])

        out = jax.ShapeDtypeStruct((net.deep, cut, self.columns), BF16)
        made = self.call(kernel, [*self.keep, *self.got], [out] * 4, "add_second")
        self.keep = [made[0], made[2]]
        self.got = [net.swap(made[1], net.X), net.swap(made[3], net.Y)]

    def fourth(self):
        net, rows, cut = self.net, self.rows, self.rows // 2

        def kernel(sc_ref, k0, k1, g0, g1, *outs):
            for away, out in enumerate(outs):
                at = (sc_ref[2] + net.deep - away) % net.deep
                out[:cut] = add_bf16(k0[at], g0[at])
                out[cut:] = add_bf16(k1[at], g1[at])

        out = jax.ShapeDtypeStruct((rows, self.columns), BF16)
        made = self.call(kernel, [*self.keep, *self.got], [out] * net.deep, "add_third")
        self.keep = [made[0]]
        self.got = [net.from_z(made[k], k) for k in range(1, net.deep)]

    def total(self):
        return self.keep[0].astype(F32) + sum(v.astype(F32) for v in self.got)

    def total_heads(self, sz):
        size = sz.gcols

        def kernel(sc_ref, own, g0, g1, g2, qkv_ref, out_ref):
            for g in range(sz.groups):
                for n in range(4):
                    low = (4 * g + n) * size
                    total = sum(v[:, low : low + size].astype(F32) for v in (own, g0, g1, g2))
                    if n < 3:
                        low = n * sz.width + g * size
                        qkv_ref[:, low : low + size] = total
                    else:
                        out_ref[:, g * size : (g + 1) * size] = total

        outs = [jax.ShapeDtypeStruct((self.rows, k * sz.width), F32) for k in (3, 1)]
        return self.call(kernel, [*self.keep, *self.got], outs, "total_heads")

    def call(self, kernel, args, outs, name):
        return pl.pallas_call(
            kernel,
            grid_spec=pltpu.PrefetchScalarGridSpec(
                num_scalar_prefetch=1,
                grid=(1,),
                in_specs=[pl.BlockSpec(memory_space=pltpu.VMEM)] * len(args),
                out_specs=[pl.BlockSpec(memory_space=pltpu.VMEM)] * len(outs),
            ),
            out_shape=outs,
            compiler_params=params(1),
            cost_estimate=cost(0, 6 * sum(v.size for v in args)),
            name=name,
        )(self.bits, *args)


def tie(value, *others):
    return lax.optimization_barrier((value,) + others)[0]


def tie2(values, others):
    return lax.optimization_barrier((*values, *others))[: len(values)]


def body(
    tokens, cond, lengths, ada_w, ada_b, w_qkv, w_out, w_up, b_up, w_down, b_down,
    rel_table, bucket, cotangent,
):
    axes = ("clip", "win")
    sz = Sizes(tokens)
    net = Net()
    devices, index = net.count, net.index
    clips = lax.axis_size("clip")
    width = sz.width
    core = lax.axis_index("win") % 2
    swap = [(n, n ^ 1) for n in range(lax.axis_size("win"))]
    place_in = jnp.arange(3 + sz.micro, dtype=jnp.int32)
    scalars = jnp.where(place_in == 0, core, jnp.where(place_in == 1 + sz.micro, index % 8, index // 8))
    for n in range(sz.micro):
        scalars = jnp.where(place_in == 1 + n, lengths[n, 0], scalars)
    strip = (sz.micro, 2, 2, sz.frames, sz.half, width)
    tok = tokens.reshape(strip)
    cot = cotangent.reshape(strip)

    cond_act = jax.nn.silu(cond[:, 0].astype(F32)).astype(BF16)
    rows = ada_w.shape[0]
    small = jnp.concatenate([b_up, b_down, rel_table.reshape(-1)])
    n_cond = cond_act.size
    if net.direct:
        early = jnp.concatenate([cond_act.reshape(-1), small])
        early = net.gather_clips(jnp.pad(early, (0, -early.size % 128)))
        cond_all = early[:, :, :n_cond].reshape(early.shape[:2] + cond_act.shape)
    else:
        cond_all = lax.all_gather(cond_act, "clip", axis=0)
    cond_mine = lax.dynamic_slice_in_dim(cond_all, index * rows, rows, cond_all.ndim - 1)
    lead = cond_mine.shape[:-1]
    cond_mine = cond_mine.reshape(clips * sz.micro, rows)
    mod_part = dot_nn(cond_mine, ada_w)
    spread_b = jnp.zeros((mod_part.shape[1],), F32)
    spread_b = lax.dynamic_update_slice(spread_b, ada_b.astype(F32), (index * ada_b.shape[0],))
    mod_part = (mod_part + spread_b[None, :]).reshape(lead + (6 * width,))
    notes = []
    if net.direct:
        mod = net.scatter_clips(mod_part, notes)
        mod = net.swap_sum(net.swap_sum(mod, net.CORE), net.X)
    else:
        mod = lax.psum_scatter(mod_part, "clip", scatter_dimension=0, tiled=False)
        mod = lax.psum(mod, "win")
    mod = mod.reshape(sz.micro, 6, width)

    cols = width // 2
    by_group = w_qkv.reshape(rows, 3, sz.groups, sz.gcols).transpose(0, 2, 1, 3)
    by_group = by_group.reshape(rows, 2, 3 * cols)
    shard_q = [by_group[:, n] for n in range(2)]
    inner = w_up.shape[1]
    per = w_down.shape[0] // 2
    thin = CHUNK // devices

    def inner_order(value):
        if not net.direct:
            value = value.reshape(-1, devices, 2, per).transpose(2, 0, 1, 3)
        else:
            value = value.reshape(-1, devices // 2, 2, 2, per // thin, thin)
            value = value.transpose(3, 0, 4, 2, 1, 5)
        return value.reshape(2, -1, inner // 2)

    def inner_back(halves):
        value = jnp.stack(halves)
        if not net.direct:
            value = value.reshape(2, -1, devices, per).transpose(1, 2, 0, 3)
        else:
            value = value.reshape(2, -1, per // thin, 2, devices // 2, thin)
            value = value.transpose(1, 4, 3, 0, 2, 5)
        return value.reshape(-1, inner)

    def pack_inner(up, down):
        down = down.reshape(per // thin, thin, 2, width // 2).transpose(2, 1, 0, 3)
        down = down.reshape(rows, per // thin, width // 2)
        return jnp.concatenate([up.reshape(rows, -1, CHUNK), down], axis=2).reshape(rows, -1)

    def unpack_inner(value):
        value = value.reshape(rows, per // thin, -1)
        down = value[:, :, CHUNK:].reshape(2, thin, per // thin, width // 2)
        return value[:, :, :CHUNK].reshape(rows, -1), down.transpose(2, 1, 0, 3).reshape(per, width)

    shard_u = inner_order(w_up)
    shard_d = [w_down[:per], w_down[per:]]
    gather = lambda v: lax.all_gather(v, axes, axis=0, tiled=True)
    if net.direct:
        packs = [
            shard_q[0],
            jnp.concatenate([shard_q[1], w_out], axis=1),
            pack_inner(shard_u[1], shard_d[1]),
            pack_inner(shard_u[0], shard_d[0]),
        ]
        rest_q = gather(packs[1])
        rest = gather(tie(packs[2], early))
        (one,) = Gather.along_z(net, [packs[0]])
        small = net.gather_pairs(tie(early[:, :, n_cond:], *notes))
        one.halves = tie2(one.halves, [mod_part])
        one.start(True)
        one.join()
        one.halves = tie2(one.halves, notes[:1])
        one.start(False)
        three_pack = tie(packs[3], notes[0])
        three_got = tie2(Gather.send_z(net, three_pack), one.got)
        (three,) = Gather.cut(net, three_pack, three_got, [packs[3].shape[1]])
        one.core()
        full_q = [one.pieces(), Pieces([rest_q])]
        full_out = full_q[1]
    else:
        full_q = [Pieces([gather(v)]) for v in shard_q]
        full_out = Pieces([gather(w_out)])
        full_i = [[Pieces([gather(u)]), Pieces([gather(d)])] for u, d in zip(shard_u, shard_d)]
        small = gather(small[None])
    n_up, n_down = b_up.shape[0], b_down.shape[0]
    n_small = n_up + n_down + rel_table.size
    full_bup = inner_order(small[:, :n_up].astype(F32).reshape(1, inner))
    full_bdown = small[:, n_up : n_up + n_down].astype(F32).reshape(1, width)
    table = small[:, n_up + n_down : n_small].reshape(-1, HEADS)
    places = offset_onehot(core, sz)
    bias = bias_blocks(table, bucket, places, sz)

    if net.direct:
        mod = tie(mod, bias, *three.halves)
    own, send = first_norm(tok, mod, scalars, sz)
    far = lax.ppermute(send, "win", swap)
    if net.direct:
        three.start(True)
    first = attention(0, own, far, full_q[0], bias, scalars, sz)
    if net.direct:
        three.tie(first[2])
        three.join()
        three.start(False)
        first = tie2(first, three.halves)
    qkv, wide, att_1, wide_out, branch_own, branch_send = attention(
        1, own, far, full_q[1], bias, scalars, sz, first, full_out
    )
    if net.direct:
        three.tie(branch_own)
        branch_send = tie(branch_send, *three.got)
    branch_far = lax.ppermute(branch_send, "win", swap)
    hidden_two, grad_mlp = second_norm(tok, cot, branch_own, branch_far, mod, scalars, sz)
    flat = (sz.rows, width)
    both = (2, sz.micro, sz.used, sz.half, width)
    hidden_two, grad_mlp = hidden_two.reshape(flat), grad_mlp.reshape(flat)
    if net.direct:
        three.tie(branch_far)
        three.halves = tie2(three.halves, [branch_far])
        three.core()
        full_i = [[three.pieces()], [Pieces([rest])]]
    mlps = []
    for n in range(2):
        shard = rows if net.direct and n == 1 else None
        mlps.append(
            mlp(hidden_two, grad_mlp, full_i[n], full_bup[n], scalars, sz, shard, n == 0)
        )
        if net.direct and n == 0:
            pack, hidden_two = lax.optimization_barrier((mlps[0][4], hidden_two))
            r_first = lax.psum_scatter(pack, axes, scatter_dimension=0, tiled=True).astype(F32)

    if net.direct:
        second = Scatter(net, mlps[1][3:5])
    output, grad_mid, grad_own, grad_send, sums_two = after_mlp(
        tok, cot, branch_own, branch_far, [v[0].reshape(both) for v in mlps],
        [v[1].reshape(both) for v in mlps], mod, full_bdown, scalars, sz,
    )
    grad_far = lax.ppermute(grad_send, "win", swap)
    if net.direct:
        second.tie(grad_own)
        second.second()
        grad_own = tie(grad_own, *second.keep)
    *g_att, fold, hid_own, hid_send = attention_back(
        grad_own, grad_far, own, far, qkv, (first[2], att_1), wide, wide_out, bias, scalars, sz,
        rows if net.direct else None,
    )
    if net.direct:
        second.tie(hid_own)
        g_att = tie2(g_att, second.got)
        hid_send = tie(hid_send, *second.got)
        heads = Scatter(net, g_att)
        hid_far = lax.ppermute(hid_send, "win", swap)
        second.third()
        heads.tie(*second.keep)
        heads.second()
        hid_far = tie(hid_far, *heads.keep)
    else:
        hid_far = lax.ppermute(hid_send, "win", swap)
    grad_in, sums_one = last_norm(tok, cot, grad_mid, hid_own, hid_far, mod, scalars, sz)
    if net.direct:
        second.tie(sums_one, r_first)
        second.fourth()
        sums_one, fold = lax.optimization_barrier((sums_one, fold, *second.keep))[:2]

    grad_mod = jnp.concatenate(
        [sums_one, sums_two[:, 3:4], sums_two[:, 0:3]], axis=1
    ).reshape(sz.micro, 6 * width)
    g_table = table_grad(offset_grad(fold, places, sz), bucket, table.shape[0]).reshape(devices, -1)
    if net.direct:
        heads.tie(g_table)
        heads.third()
        second.tie(*heads.keep)
        r_second = second.total()
        g_table = tie(g_table, r_second)
    g_bup = inner_back([v[2] for v in mlps]).reshape(devices, -1)
    g_bdown = mlps[0][3].reshape(devices, -1)
    g_small = jnp.concatenate([g_bup, g_bdown, g_table], axis=1)
    if net.direct:
        every = jnp.concatenate([grad_mod.reshape(-1), g_small.reshape(-1)])
        every = net.swap_sum(net.swap_sum(every, net.CORE), net.X)
        heads.tie(every)
        heads.fourth()
        mod_all, g_small = net.share(tie(every, *heads.keep), grad_mod.size, heads)
    else:
        mod_all = lax.all_gather(lax.psum(grad_mod, "win"), "clip", axis=0)
        g_small = lax.psum_scatter(g_small, axes, scatter_dimension=0, tiled=False)
    mod_all = mod_all.reshape(clips * sz.micro, -1)
    grad_ada_w = lax.dot_general(
        cond_mine.astype(F32), mod_all, (((0,), (0,)), ((), ())),
        precision=HIGHEST, preferred_element_type=F32,
    )
    grad_ada_b = lax.dynamic_slice_in_dim(
        jnp.sum(mod_all, axis=0), index * ada_b.shape[0], ada_b.shape[0]
    )
    if net.direct:
        r_u, r_d = zip(unpack_inner(r_first), unpack_inner(r_second))
        r_qkv, r_out = heads.total_heads(sz)
    else:
        scatter = lambda v: lax.psum_scatter(
            v.astype(F32), axes, scatter_dimension=0, tiled=True
        )
        r_u = [scatter(v[-2]) for v in mlps]
        r_d = [scatter(v[-1]) for v in mlps]
        r_qkv, r_out = scatter(g_att[0]), scatter(g_att[1])
        r_qkv = r_qkv.reshape(rows, sz.groups, 3, sz.gcols).transpose(0, 2, 1, 3)
        r_qkv = r_qkv.reshape(rows, 3 * width)
    r_up = inner_back(r_u)
    r_down = jnp.concatenate(r_d)
    return (
        output.reshape(tokens.shape), grad_in.reshape(tokens.shape), grad_ada_w, grad_ada_b,
        r_qkv, r_out, r_up, g_small[:n_up], r_down, g_small[n_up : n_up + n_down],
        g_small[n_up + n_down :].reshape(rel_table.shape),
    )


def solution(mesh):
    weights = P(("clip", "win"), None)
    vector = P(("clip", "win"))
    strips = P(None, "clip", "win", None, None, None, None, None)
    return jax.shard_map(
        body,
        mesh=mesh,
        in_specs=(
            strips, P(None, "clip", None), P(None, "clip"), weights, vector, weights, weights,
            weights, vector, weights, vector, weights, P(), strips,
        ),
        out_specs=(
            strips, strips, weights, vector, weights, weights, weights, vector, weights, vector,
            weights,
        ),
        check_vma=False,
    )
```
